512 devices in a mesh: row: 64 (over y_hi, x, z), col: 8 (over y_lo, core).
Axes of the slice: x: 4, y: 8 (y_hi: 2, y_lo: 4; y = y_hi * 4 + y_lo), z: 8, core: 2. Of those that a mesh axis runs over, the one named last changes fastest.
Arguments:
- features: bfloat16 [131072, 256], P(('row', 'col')), may hold values from -6 to 6
- weight: bfloat16 [256, 256], replicated, may hold values from -0.375 to 0.375
- weight_self: bfloat16 [256, 256], replicated, may hold values from -0.375 to 0.375
- tile_values: bfloat16 [64, 256, 128, 128], P('row', 'col'), may hold values from -0.125 to 0.125
- tile_rows: int32 [64, 256], P('row', 'col'), may hold values from 0 to 1
- tile_cols: int32 [64, 256], P('row', 'col'), may hold values from 0 to 47
- tile_count: int32 [64, 8], P('row', 'col'), may hold values from 1 to 32, as said below
- cotangent: bfloat16 [131072, 256], P(('row', 'col')), may hold values from -6 to 6
Outputs:
- activations: bfloat16 [131072, 256], P(('row', 'col'))
- feature_grad: bfloat16 [131072, 256], P(('row', 'col'))
- weight_grad: float32 [256, 256], replicated
- self_grad: float32 [256, 256], replicated
The draws below stay inside these ranges and needn't reach their ends.
Inputs may be any that keep to these rules, and one draw needn't show every extreme that they name: Slots 0 to tile_count - 1 of a node block are live, the others are ignored; some node block has all 32 slots live.
All inputs are finite; a program needn't handle non-finite values.
Results may differ from the reference program's by a relative error of at most 0.0052.
Values may be sent and summed in bfloat16 or wider, within the bound.
A program may use at most 64 MiB of HBM per device.

```python
import math
import jax
import jax.numpy as jnp
from jax import lax

F = 256
TILE = 128
NODE_DEV = 256
TILES_DEV = 32
TPB = 2
EXT = 48
NODES = 131072
N_ROW = 64
N_COL = 8


def draw_tile_count(key, part):
    first_key, second_key, third_key = jax.random.split(jax.random.fold_in(key, 17), 3)
    shape_all = (N_ROW, N_COL)
    first = jax.random.randint(first_key, shape_all, 0, TILES_DEV)
    second = jax.random.randint(second_key, shape_all, 0, TILES_DEV)
    counts = 1 + first * second // TILES_DEV
    chosen = jax.random.randint(third_key, (), 0, N_ROW * N_COL)
    flat = counts.reshape(-1)
    positions = jnp.arange(N_ROW * N_COL, dtype=jnp.int32)
    flat = jnp.where(positions == chosen, TILES_DEV, flat)
    return flat.reshape(shape_all).astype(jnp.int32)


def set_ends(drawn, stream_key, least, top_value):
    dims = drawn.shape
    index_at = [jax.random.randint(jax.random.fold_in(stream_key, axis), (), 0, dims[axis]) for axis in range(len(dims))]
    drawn = drawn.at[tuple(index_at)].set(least)
    longest = dims.index(max(dims))
    index_at[longest] = (index_at[longest] + 1) % dims[longest]
    return drawn.at[tuple(index_at)].set(top_value)


def block_scale(stream_key, shape, shards, least, largest):
    def one(axis_at, blocks):
        draws = jax.random.uniform(jax.random.fold_in(jax.random.fold_in(stream_key, 6), axis_at), (blocks,), jnp.float32, least / len(shards), largest / len(shards))
        return jnp.repeat(jnp.exp(draws), shape[axis_at] // blocks).reshape((-1,) + (1,) * (len(shape) - axis_at - 1))

    gain = one(*shards[0])
    for cut in shards[1:]:
        gain = gain * one(*cut)
    return gain


def gaussian(own_key, shape, spread, limit, shards=(), held_as=jnp.bfloat16):
    factor_of = block_scale(own_key, shape, shards, -0.22, 0.18) if shards else 1.0
    drawn = jax.random.normal(own_key, shape, jnp.float32) * spread * factor_of
    return jnp.minimum(jnp.maximum(drawn, -limit), limit).astype(held_as)


def setup_inputs(seed: int = 0) -> dict:
    key_list = jax.random.split(jax.random.key(seed), 9)
    return {
        "features": gaussian(key_list[0], (NODES, F), 1.0, 6.0, ((0, 512),)),
        "weight": gaussian(key_list[1], (F, F), F ** -0.5, 0.375),
        "weight_self": gaussian(key_list[2], (F, F), F ** -0.5, 0.375),
        "tile_values": gaussian(key_list[3], (N_ROW, N_COL * TILES_DEV, TILE, TILE), (TILE * TILES_DEV // 2) ** -0.5, 0.125, ((0, 64), (1, 8))),
        "tile_rows": set_ends(jax.random.randint(key_list[4], (N_ROW, N_COL * TILES_DEV), 0, TPB), jax.random.fold_in(key_list[4], 1), 0, TPB - 1).astype(jnp.int32),
        "tile_cols": set_ends(jax.random.randint(key_list[5], (N_ROW, N_COL * TILES_DEV), 0, EXT), jax.random.fold_in(key_list[5], 1), 0, EXT - 1).astype(jnp.int32),
        "tile_count": draw_tile_count(jax.random.fold_in(key_list[8], 71), 0),
        "cotangent": gaussian(key_list[7], (NODES, F), 1.0, 6.0, ((0, 512),)),
    }


def reference(features, weight, weight_self, tile_values, tile_rows, tile_cols, tile_count, cotangent):
    per_block = NODE_DEV // TILE
    span = N_COL * per_block
    blocks_all = N_ROW * N_COL
    tile_sets = tile_values.reshape(blocks_all, TILES_DEV, TILE, TILE)
    row_sets = tile_rows.reshape(blocks_all, TILES_DEV)
    col_sets = tile_cols.reshape(blocks_all, TILES_DEV)
    counts = tile_count.reshape(blocks_all)
    slot_ids = jnp.arange(TILES_DEV, dtype=jnp.int32)

    def placing(block):
        row_group = block // N_COL
        group = col_sets[block] // span
        within = col_sets[block] % span
        return ((row_group + group - 1) % N_ROW * span + within).astype(jnp.int32)
    feature_tiles = features.reshape(NODES // TILE, TILE, F).astype(jnp.float32)

    def forward_one(block):
        target_cols = placing(block)
        live_mask = (slot_ids < counts[block]).astype(jnp.float32)
        picked = feature_tiles[target_cols]
        products = jnp.einsum('tij,tjf->tif', tile_sets[block].astype(jnp.float32), picked)
        products = products * live_mask[:, None, None]
        return jnp.zeros((per_block, TILE, F), jnp.float32).at[row_sets[block]].add(products)
    block_ids = jnp.arange(blocks_all, dtype=jnp.int32)
    aggregated = lax.map(forward_one, block_ids).reshape(NODES, F).astype(jnp.bfloat16)
    pre_act = jnp.dot(aggregated, weight, preferred_element_type=jnp.float32) + jnp.dot(features, weight_self, preferred_element_type=jnp.float32)
    activations = jax.nn.silu(pre_act).astype(jnp.bfloat16)
    sigma = jax.nn.sigmoid(pre_act)
    grad_pre = (cotangent.astype(jnp.float32) * sigma * (1.0 + pre_act * (1.0 - sigma))).astype(jnp.bfloat16)
    factor = 1.0 / math.sqrt(NODES)
    weight_grad = jnp.dot(aggregated.T, grad_pre, preferred_element_type=jnp.float32) * factor
    self_grad = jnp.dot(features.T, grad_pre, preferred_element_type=jnp.float32) * factor
    grad_aggregated = jnp.dot(grad_pre, weight.T, preferred_element_type=jnp.float32).astype(jnp.bfloat16)
    grad_tiles = grad_aggregated.reshape(NODES // TILE, TILE, F).astype(jnp.float32)

    def backward_one(total, block):
        target_cols = placing(block)
        live_mask = (slot_ids < counts[block]).astype(jnp.float32)
        picked = grad_tiles[block * per_block + row_sets[block]]
        products = jnp.einsum('tij,tif->tjf', tile_sets[block].astype(jnp.float32), picked)
        products = products * live_mask[:, None, None]
        return (total.at[target_cols].add(products), None)
    total, _ = lax.scan(backward_one, jnp.zeros((NODES // TILE, TILE, F), jnp.float32), block_ids)
    self_part = jnp.dot(grad_pre, weight_self.T, preferred_element_type=jnp.float32)
    feature_grad = (total.reshape(NODES, F) + self_part).astype(jnp.bfloat16)
    return (activations, feature_grad, weight_grad, self_grad)
```

```python
import functools
import math

import jax
import jax.numpy as jnp
from jax import lax
from jax.experimental import pallas as pl
from jax.experimental.pallas import tpu as pltpu
from jax.sharding import PartitionSpec as P

MESH = pl.DeviceIdType.MESH


def flip(index, stride):
    bit = (index // stride) % 2
    return index + stride - 2 * stride * bit, bit


def allreduce_kernel(n_row, n_col, x_ref, o_ref, part, gath, rsend, rrecv, dsend, drecv, gsend, grecv):
    row = lax.axis_index("row")
    col = lax.axis_index("col")
    col_bits = n_col.bit_length() - 1
    row_bits = n_row.bit_length() - 1
    partners = []
    for k in range(col_bits):
        partners.append((row, flip(col, 1 << k)[0]))
    for k in range(row_bits):
        partners.append((flip(row, 1 << k)[0], col))
    barrier = pltpu.get_barrier_semaphore()
    for device in partners:
        pl.semaphore_signal(barrier, inc=1, device_id=device, device_id_type=MESH)
    pl.semaphore_wait(barrier, len(partners))

    rows = x_ref.shape[0]
    src = x_ref
    base = 0
    size = rows
    for k in range(col_bits):
        other, bit = flip(col, 1 << k)
        half = size // 2
        keep = base + bit * half
        give = base + (1 - bit) * half
        copy = pltpu.make_async_remote_copy(
            src_ref=src.at[pl.ds(pl.multiple_of(give, 8), half)],
            dst_ref=part.at[k, pl.ds(0, half)],
            send_sem=rsend.at[k],
            recv_sem=rrecv.at[k],
            device_id=(row, other),
            device_id_type=MESH,
        )
        copy.start()
        copy.wait()
        mine = src[pl.ds(pl.multiple_of(keep, 8), half), :] + part[k, pl.ds(0, half), :]
        gath[k, pl.ds(pl.multiple_of(keep, 8), half), :] = mine
        src = gath.at[k]
        base = keep
        size = half
    chunk = size
    total = gath[col_bits - 1, pl.ds(pl.multiple_of(base, 8), chunk), :]
    for k in range(row_bits):
        other, _ = flip(row, 1 << k)
        hold = o_ref.at[pl.ds(0, chunk)]
        hold[...] = total
        copy = pltpu.make_async_remote_copy(
            src_ref=hold,
            dst_ref=part.at[col_bits + k, pl.ds(0, chunk)],
            send_sem=dsend.at[k],
            recv_sem=drecv.at[k],
            device_id=(other, col),
            device_id_type=MESH,
        )
        copy.start()
        copy.wait()
        total = total + part[col_bits + k, pl.ds(0, chunk), :]
    final = gath.at[col_bits]
    final[pl.ds(pl.multiple_of(base, 8), chunk), :] = total
    size = chunk
    for k in reversed(range(col_bits)):
        other, bit = flip(col, 1 << k)
        start = base - bit * size
        copy = pltpu.make_async_remote_copy(
            src_ref=final.at[pl.ds(pl.multiple_of(base, 8), size)],
            dst_ref=final.at[pl.ds(pl.multiple_of(base, 8), size)],
            send_sem=gsend.at[k],
            recv_sem=grecv.at[k],
            device_id=(row, other),
            device_id_type=MESH,
        )
        copy.start()
        copy.wait()
        base = start
        size = size * 2
    o_ref[...] = final[...]


def all_reduce(stacked, n_row, n_col):
    rows, width = stacked.shape
    col_bits = n_col.bit_length() - 1
    row_bits = n_row.bit_length() - 1
    return pl.pallas_call(
        functools.partial(allreduce_kernel, n_row, n_col),
        out_shape=jax.ShapeDtypeStruct((rows, width), jnp.float32),
        in_specs=[pl.BlockSpec(memory_space=pltpu.VMEM)],
        out_specs=pl.BlockSpec(memory_space=pltpu.VMEM),
        scratch_shapes=[
            pltpu.VMEM((col_bits + row_bits, rows // 2, width), jnp.float32),
            pltpu.VMEM((col_bits + 1, rows, width), jnp.float32),
            pltpu.SemaphoreType.DMA((col_bits,)),
            pltpu.SemaphoreType.DMA((col_bits,)),
            pltpu.SemaphoreType.DMA((row_bits,)),
            pltpu.SemaphoreType.DMA((row_bits,)),
            pltpu.SemaphoreType.DMA((col_bits,)),
            pltpu.SemaphoreType.DMA((col_bits,)),
        ],
        compiler_params=pltpu.CompilerParams(collective_id=0, has_side_effects=True),
    )(stacked)


def with_halo(cells, sides, width):
    for axis, dim in sides:
        count = lax.axis_size(axis)
        head = lax.slice_in_dim(cells, 0, width, axis=dim)
        tail = lax.slice_in_dim(cells, cells.shape[dim] - width, cells.shape[dim], axis=dim)
        cells = jnp.concatenate(
            [
                lax.ppermute(tail, axis, [(i, (i + 1) % count) for i in range(count)]),
                cells,
                lax.ppermute(head, axis, [((i + 1) % count, i) for i in range(count)]),
            ],
            axis=dim,
        )
    return cells


def passed_along(value, axis, steps):
    count = lax.axis_size(axis)
    pairs = [(source, (source + steps) % count) for source in range(count)]
    return lax.ppermute(value, axis, pairs)


def shards(features, weight, weight_self, tile_values, tile_rows, tile_cols, tile_count, cotangent):
    tile_block = tile_values[0]
    slot_rows = tile_rows[0]
    slot_cols = tile_cols[0]
    live_count = tile_count[0, 0]
    slot_total = tile_block.shape[0]
    tile_side = tile_block.shape[-1]
    node_rows = features.shape[0]
    width = features.shape[1]
    per_block = node_rows // tile_side
    col_count = lax.axis_size("col")
    row_count = lax.axis_size("row")
    span = col_count * per_block
    group = lax.all_gather(features, "col", axis=0, tiled=True)
    window = with_halo(group, (("row", 0),), group.shape[0])
    window_tiles = window.reshape(-1, tile_side, width)
    row_ids = jnp.arange(per_block, dtype=jnp.int32)
    tiles_part = tile_block
    rows_part = slot_rows
    live_part = jnp.arange(slot_total, dtype=jnp.int32) < live_count
    feat_tiles = window_tiles[slot_cols]
    selector = ((rows_part[None, :] == row_ids[:, None]) & live_part[None, :]).astype(jnp.bfloat16)
    masked = tiles_part[None, :, :, :] * selector[:, :, None, None]
    summed = jnp.einsum("ktij,tjf->kif", masked, feat_tiles, preferred_element_type=jnp.float32)
    aggregated = summed.reshape(node_rows, width).astype(jnp.bfloat16)
    pre_act = jnp.dot(aggregated, weight, preferred_element_type=jnp.float32) + jnp.dot(
        features, weight_self, preferred_element_type=jnp.float32
    )
    activations = jax.nn.silu(pre_act).astype(jnp.bfloat16)
    sigma = jax.nn.sigmoid(pre_act)
    grad_pre = (cotangent.astype(jnp.float32) * sigma * (1.0 + pre_act * (1.0 - sigma))).astype(
        jnp.bfloat16
    )
    weight_part = jnp.einsum("nf,ng->fg", aggregated, grad_pre, preferred_element_type=jnp.float32)
    self_part = jnp.einsum("nf,ng->fg", features, grad_pre, preferred_element_type=jnp.float32)
    grad_aggregated = jnp.einsum(
        "ng,fg->nf", grad_pre, weight, preferred_element_type=jnp.float32
    ).astype(jnp.bfloat16)
    self_feature = jnp.einsum(
        "ng,fg->nf", grad_pre, weight_self, preferred_element_type=jnp.float32
    )
    grad_tiles = grad_aggregated.reshape(per_block, tile_side, width)
    spread_zero = jnp.zeros((3 * span, tile_side, width), jnp.float32)
    tiles_part = tile_block
    rows_part = slot_rows
    live_part = (jnp.arange(slot_total, dtype=jnp.int32) < live_count).astype(jnp.float32)
    picked = grad_tiles[rows_part]
    products = jnp.einsum("tij,tif->tjf", tiles_part, picked, preferred_element_type=jnp.float32)
    spread = spread_zero.at[slot_cols].add(products * live_part[:, None, None])
    spread = spread.reshape(3, col_count * node_rows, width)
    middle = spread[1]
    for offset in (1, -1):
        outgoing = spread[2] if offset == 1 else spread[0]
        middle = middle + passed_along(outgoing, "row", offset)
    own_share = lax.psum_scatter(middle, "col", scatter_dimension=0, tiled=True)
    feature_grad = (own_share + self_feature).astype(jnp.bfloat16)
    summed_parts = all_reduce(
        jnp.concatenate([weight_part, self_part], axis=0), row_count, col_count
    )
    weight_total, self_total = summed_parts[:width], summed_parts[width:]
    factor = 1.0 / math.sqrt(node_rows * col_count * row_count)
    return (activations, feature_grad, weight_total * factor, self_total * factor)


def solution(mesh):
    placed = (
        P(("row", "col"), None),
        P(),
        P(),
        P("row", "col", None, None),
        P("row", "col"),
        P("row", "col"),
        P("row", "col"),
        P(("row", "col"), None),
    )
    return jax.shard_map(
        shards,
        mesh=mesh,
        in_specs=placed,
        out_specs=(P(("row", "col"), None), P(("row", "col"), None), P(), P()),
        check_vma=False,
    )
```

```python
import functools
import math

import jax
import jax.numpy as jnp
from jax import lax
from jax.experimental import pallas as pl
from jax.experimental.pallas import tpu as pltpu
from jax.sharding import PartitionSpec as P

MESH = pl.DeviceIdType.MESH


def flip(index, stride):
    bit = (index // stride) % 2
    return index + stride - 2 * stride * bit, bit


def allreduce_kernel(n_row, n_col, x_ref, o_ref, part, gath, rsend, rrecv, dsend, drecv, gsend, grecv):
    row = lax.axis_index("row")
    col = lax.axis_index("col")
    col_bits = n_col.bit_length() - 1
    row_bits = n_row.bit_length() - 1
    partners = []
    for k in range(col_bits):
        partners.append((row, flip(col, 1 << k)[0]))
    for k in range(row_bits):
        partners.append((flip(row, 1 << k)[0], col))
    barrier = pltpu.get_barrier_semaphore()
    for device in partners:
        pl.semaphore_signal(barrier, inc=1, device_id=device, device_id_type=MESH)
    pl.semaphore_wait(barrier, len(partners))

    rows = x_ref.shape[0]
    src = x_ref
    base = 0
    size = rows
    for k in range(col_bits):
        other, bit = flip(col, 1 << k)
        half = size // 2
        keep = base + bit * half
        give = base + (1 - bit) * half
        copy = pltpu.make_async_remote_copy(
            src_ref=src.at[pl.ds(pl.multiple_of(give, 8), half)],
            dst_ref=part.at[k, pl.ds(0, half)],
            send_sem=rsend.at[k],
            recv_sem=rrecv.at[k],
            device_id=(row, other),
            device_id_type=MESH,
        )
        copy.start()
        copy.wait()
        mine = src[pl.ds(pl.multiple_of(keep, 8), half), :] + part[k, pl.ds(0, half), :]
        gath[k, pl.ds(pl.multiple_of(keep, 8), half), :] = mine
        src = gath.at[k]
        base = keep
        size = half
    chunk = size
    total = gath[col_bits - 1, pl.ds(pl.multiple_of(base, 8), chunk), :]
    for k in range(row_bits):
        other, _ = flip(row, 1 << k)
        hold = o_ref.at[pl.ds(0, chunk)]
        hold[...] = total
        copy = pltpu.make_async_remote_copy(
            src_ref=hold,
            dst_ref=part.at[col_bits + k, pl.ds(0, chunk)],
            send_sem=dsend.at[k],
            recv_sem=drecv.at[k],
            device_id=(other, col),
            device_id_type=MESH,
        )
        copy.start()
        copy.wait()
        total = total + part[col_bits + k, pl.ds(0, chunk), :]
    final = gath.at[col_bits]
    final[pl.ds(pl.multiple_of(base, 8), chunk), :] = total
    size = chunk
    for k in reversed(range(col_bits)):
        other, bit = flip(col, 1 << k)
        start = base - bit * size
        copy = pltpu.make_async_remote_copy(
            src_ref=final.at[pl.ds(pl.multiple_of(base, 8), size)],
            dst_ref=final.at[pl.ds(pl.multiple_of(base, 8), size)],
            send_sem=gsend.at[k],
            recv_sem=grecv.at[k],
            device_id=(row, other),
            device_id_type=MESH,
        )
        copy.start()
        copy.wait()
        base = start
        size = size * 2
    o_ref[...] = final[...]


def ring_position(col, n):
    core = col % 2
    y = col // 2
    return y + core * (n - 1 - 2 * y)


def ring_col(p, n):
    q = p // (n // 2)
    y = p + q * (n - 1 - 2 * p)
    return 2 * y + q


def gather_kernel(n_row, n_col, x_ref, w_ref, ring_send, ring_recv, up_send, up_recv, down_send, down_recv, local_sem):
    row = lax.axis_index("row")
    col = lax.axis_index("col")
    p = ring_position(col, n_col)
    succ = ring_col((p + 1) % n_col, n_col)
    pred = ring_col((p + n_col - 1) % n_col, n_col)
    up = (row + 1) % n_row
    down = (row + n_row - 1) % n_row
    barrier = pltpu.get_barrier_semaphore()
    for device in ((row, succ), (row, pred), (up, col), (down, col)):
        pl.semaphore_signal(barrier, inc=1, device_id=device, device_id_type=MESH)
    pl.semaphore_wait(barrier, 4)
    local = pltpu.make_async_copy(x_ref, w_ref.at[1, col], local_sem.at[0])
    local.start()
    halos = []

    def halo(src, block, step):
        for target, slot, send, recv in ((up, 0, up_send, up_recv), (down, 2, down_send, down_recv)):
            copy = pltpu.make_async_remote_copy(
                src_ref=src,
                dst_ref=w_ref.at[slot, block],
                send_sem=send.at[step],
                recv_sem=recv.at[step],
                device_id=(target, col),
                device_id_type=MESH,
            )
            copy.start()
            halos.append(copy)

    halo(x_ref, col, 0)
    src = x_ref
    sent = col
    for step in range(1, n_col):
        got = ring_col((p - step + n_col) % n_col, n_col)
        copy = pltpu.make_async_remote_copy(
            src_ref=src,
            dst_ref=w_ref.at[1, sent],
            send_sem=ring_send.at[step - 1],
            recv_sem=ring_recv.at[step - 1],
            device_id=(row, succ),
            device_id_type=MESH,
        )
        copy.start()
        copy.wait()
        src = w_ref.at[1, got]
        sent = got
        halo(src, got, step)
    for copy in halos:
        copy.wait()
    local.wait()


def gather_window(block, n_row, n_col):
    rows, width = block.shape
    return pl.pallas_call(
        functools.partial(gather_kernel, n_row, n_col),
        out_shape=jax.ShapeDtypeStruct((3, n_col, rows, width), block.dtype),
        in_specs=[pl.BlockSpec(memory_space=pltpu.VMEM)],
        out_specs=pl.BlockSpec(memory_space=pltpu.VMEM),
        scratch_shapes=[
            pltpu.SemaphoreType.DMA((n_col - 1,)),
            pltpu.SemaphoreType.DMA((n_col - 1,)),
            pltpu.SemaphoreType.DMA((n_col,)),
            pltpu.SemaphoreType.DMA((n_col,)),
            pltpu.SemaphoreType.DMA((n_col,)),
            pltpu.SemaphoreType.DMA((n_col,)),
            pltpu.SemaphoreType.DMA((1,)),
        ],
        compiler_params=pltpu.CompilerParams(collective_id=1, has_side_effects=True),
    )(block)


def all_reduce(stacked, n_row, n_col):
    rows, width = stacked.shape
    col_bits = n_col.bit_length() - 1
    row_bits = n_row.bit_length() - 1
    return pl.pallas_call(
        functools.partial(allreduce_kernel, n_row, n_col),
        out_shape=jax.ShapeDtypeStruct((rows, width), jnp.float32),
        in_specs=[pl.BlockSpec(memory_space=pltpu.VMEM)],
        out_specs=pl.BlockSpec(memory_space=pltpu.VMEM),
        scratch_shapes=[
            pltpu.VMEM((col_bits + row_bits, rows // 2, width), jnp.float32),
            pltpu.VMEM((col_bits + 1, rows, width), jnp.float32),
            pltpu.SemaphoreType.DMA((col_bits,)),
            pltpu.SemaphoreType.DMA((col_bits,)),
            pltpu.SemaphoreType.DMA((row_bits,)),
            pltpu.SemaphoreType.DMA((row_bits,)),
            pltpu.SemaphoreType.DMA((col_bits,)),
            pltpu.SemaphoreType.DMA((col_bits,)),
        ],
        compiler_params=pltpu.CompilerParams(collective_id=0, has_side_effects=True),
    )(stacked)


def with_halo(cells, sides, width):
    for axis, dim in sides:
        count = lax.axis_size(axis)
        head = lax.slice_in_dim(cells, 0, width, axis=dim)
        tail = lax.slice_in_dim(cells, cells.shape[dim] - width, cells.shape[dim], axis=dim)
        cells = jnp.concatenate(
            [
                lax.ppermute(tail, axis, [(i, (i + 1) % count) for i in range(count)]),
                cells,
                lax.ppermute(head, axis, [((i + 1) % count, i) for i in range(count)]),
            ],
            axis=dim,
        )
    return cells


def passed_along(value, axis, steps):
    count = lax.axis_size(axis)
    pairs = [(source, (source + steps) % count) for source in range(count)]
    return lax.ppermute(value, axis, pairs)


def shards(features, weight, weight_self, tile_values, tile_rows, tile_cols, tile_count, cotangent):
    tile_block = tile_values[0]
    slot_rows = tile_rows[0]
    slot_cols = tile_cols[0]
    live_count = tile_count[0, 0]
    slot_total = tile_block.shape[0]
    tile_side = tile_block.shape[-1]
    node_rows = features.shape[0]
    width = features.shape[1]
    per_block = node_rows // tile_side
    col_count = lax.axis_size("col")
    row_count = lax.axis_size("row")
    span = col_count * per_block
    window = gather_window(features, row_count, col_count)
    window_tiles = window.reshape(-1, tile_side, width)
    row_ids = jnp.arange(per_block, dtype=jnp.int32)
    tiles_part = tile_block
    rows_part = slot_rows
    live_part = jnp.arange(slot_total, dtype=jnp.int32) < live_count
    feat_tiles = window_tiles[slot_cols]
    selector = ((rows_part[None, :] == row_ids[:, None]) & live_part[None, :]).astype(jnp.bfloat16)
    masked = tiles_part[None, :, :, :] * selector[:, :, None, None]
    summed = jnp.einsum("ktij,tjf->kif", masked, feat_tiles, preferred_element_type=jnp.float32)
    aggregated = summed.reshape(node_rows, width).astype(jnp.bfloat16)
    pre_act = jnp.dot(aggregated, weight, preferred_element_type=jnp.float32) + jnp.dot(
        features, weight_self, preferred_element_type=jnp.float32
    )
    activations = jax.nn.silu(pre_act).astype(jnp.bfloat16)
    sigma = jax.nn.sigmoid(pre_act)
    grad_pre = (cotangent.astype(jnp.float32) * sigma * (1.0 + pre_act * (1.0 - sigma))).astype(
        jnp.bfloat16
    )
    weight_part = jnp.einsum("nf,ng->fg", aggregated, grad_pre, preferred_element_type=jnp.float32)
    self_part = jnp.einsum("nf,ng->fg", features, grad_pre, preferred_element_type=jnp.float32)
    grad_aggregated = jnp.einsum(
        "ng,fg->nf", grad_pre, weight, preferred_element_type=jnp.float32
    ).astype(jnp.bfloat16)
    self_feature = jnp.einsum(
        "ng,fg->nf", grad_pre, weight_self, preferred_element_type=jnp.float32
    )
    grad_tiles = grad_aggregated.reshape(per_block, tile_side, width)
    spread_zero = jnp.zeros((3 * span, tile_side, width), jnp.float32)
    tiles_part = tile_block
    rows_part = slot_rows
    live_part = (jnp.arange(slot_total, dtype=jnp.int32) < live_count).astype(jnp.float32)
    picked = grad_tiles[rows_part]
    products = jnp.einsum("tij,tif->tjf", tiles_part, picked, preferred_element_type=jnp.float32)
    spread = spread_zero.at[slot_cols].add(products * live_part[:, None, None])
    spread = spread.reshape(3, col_count * node_rows, width)
    middle = spread[1]
    for offset in (1, -1):
        outgoing = spread[2] if offset == 1 else spread[0]
        middle = middle + passed_along(outgoing, "row", offset)
    own_share = lax.psum_scatter(middle, "col", scatter_dimension=0, tiled=True)
    feature_grad = (own_share + self_feature).astype(jnp.bfloat16)
    summed_parts = all_reduce(
        jnp.concatenate([weight_part, self_part], axis=0), row_count, col_count
    )
    weight_total, self_total = summed_parts[:width], summed_parts[width:]
    factor = 1.0 / math.sqrt(node_rows * col_count * row_count)
    return (activations, feature_grad, weight_total * factor, self_total * factor)


def solution(mesh):
    placed = (
        P(("row", "col"), None),
        P(),
        P(),
        P("row", "col", None, None),
        P("row", "col"),
        P("row", "col"),
        P("row", "col"),
        P(("row", "col"), None),
    )
    return jax.shard_map(
        shards,
        mesh=mesh,
        in_specs=placed,
        out_specs=(P(("row", "col"), None), P(("row", "col"), None), P(), P()),
        check_vma=False,
    )
```

```python
import functools
import math

import jax
import jax.numpy as jnp
from jax import lax
from jax.experimental import pallas as pl
from jax.experimental.pallas import tpu as pltpu
from jax.sharding import PartitionSpec as P

MESH = pl.DeviceIdType.MESH


def flip(index, stride):
    bit = (index // stride) % 2
    return index + stride - 2 * stride * bit, bit


def allreduce_kernel(n_row, n_col, x_ref, o_ref, part, gath, rsend, rrecv, dsend, drecv, gsend, grecv):
    row = lax.axis_index("row")
    col = lax.axis_index("col")
    col_bits = n_col.bit_length() - 1
    row_bits = n_row.bit_length() - 1
    partners = []
    for k in range(col_bits):
        partners.append((row, flip(col, 1 << k)[0]))
    for k in range(row_bits):
        partners.append((flip(row, 1 << k)[0], col))
    barrier = pltpu.get_barrier_semaphore()
    for device in partners:
        pl.semaphore_signal(barrier, inc=1, device_id=device, device_id_type=MESH)
    pl.semaphore_wait(barrier, len(partners))

    rows = x_ref.shape[0]
    src = x_ref
    base = 0
    size = rows
    for k in range(col_bits):
        other, bit = flip(col, 1 << k)
        half = size // 2
        keep = base + bit * half
        give = base + (1 - bit) * half
        copy = pltpu.make_async_remote_copy(
            src_ref=src.at[pl.ds(pl.multiple_of(give, 8), half)],
            dst_ref=part.at[k, pl.ds(0, half)],
            send_sem=rsend.at[k],
            recv_sem=rrecv.at[k],
            device_id=(row, other),
            device_id_type=MESH,
        )
        copy.start()
        copy.wait()
        mine = src[pl.ds(pl.multiple_of(keep, 8), half), :] + part[k, pl.ds(0, half), :]
        gath[k, pl.ds(pl.multiple_of(keep, 8), half), :] = mine
        src = gath.at[k]
        base = keep
        size = half
    chunk = size
    total = gath[col_bits - 1, pl.ds(pl.multiple_of(base, 8), chunk), :]
    for k in range(row_bits):
        other, _ = flip(row, 1 << k)
        hold = o_ref.at[pl.ds(0, chunk)]
        hold[...] = total
        copy = pltpu.make_async_remote_copy(
            src_ref=hold,
            dst_ref=part.at[col_bits + k, pl.ds(0, chunk)],
            send_sem=dsend.at[k],
            recv_sem=drecv.at[k],
            device_id=(other, col),
            device_id_type=MESH,
        )
        copy.start()
        copy.wait()
        total = total + part[col_bits + k, pl.ds(0, chunk), :]
    final = gath.at[col_bits]
    final[pl.ds(pl.multiple_of(base, 8), chunk), :] = total
    size = chunk
    for k in reversed(range(col_bits)):
        other, bit = flip(col, 1 << k)
        start = base - bit * size
        copy = pltpu.make_async_remote_copy(
            src_ref=final.at[pl.ds(pl.multiple_of(base, 8), size)],
            dst_ref=final.at[pl.ds(pl.multiple_of(base, 8), size)],
            send_sem=gsend.at[k],
            recv_sem=grecv.at[k],
            device_id=(row, other),
            device_id_type=MESH,
        )
        copy.start()
        copy.wait()
        base = start
        size = size * 2
    o_ref[...] = final[...]


def ring_position(col, n):
    core = col % 2
    y = col // 2
    return y + core * (n - 1 - 2 * y)


def ring_col(p, n):
    q = p // (n // 2)
    y = p + q * (n - 1 - 2 * p)
    return 2 * y + q


def gather_kernel(n_row, n_col, x_ref, w_ref, ring_send, ring_recv, up_send, up_recv, down_send, down_recv, local_sem):
    row = lax.axis_index("row")
    col = lax.axis_index("col")
    p = ring_position(col, n_col)
    succ = ring_col((p + 1) % n_col, n_col)
    pred = ring_col((p + n_col - 1) % n_col, n_col)
    up = (row + 1) % n_row
    down = (row + n_row - 1) % n_row
    barrier = pltpu.get_barrier_semaphore()
    for device in ((row, succ), (row, pred), (up, col), (down, col)):
        pl.semaphore_signal(barrier, inc=1, device_id=device, device_id_type=MESH)
    pl.semaphore_wait(barrier, 4)
    local = pltpu.make_async_copy(x_ref, w_ref.at[1, col], local_sem.at[0])
    local.start()
    halos = []

    def halo(src, block, step):
        for target, slot, send, recv in ((up, 0, up_send, up_recv), (down, 2, down_send, down_recv)):
            copy = pltpu.make_async_remote_copy(
                src_ref=src,
                dst_ref=w_ref.at[slot, block],
                send_sem=send.at[step],
                recv_sem=recv.at[step],
                device_id=(target, col),
                device_id_type=MESH,
            )
            copy.start()
            halos.append(copy)

    halo(x_ref, col, 0)
    src = x_ref
    sent = col
    for step in range(1, n_col):
        got = ring_col((p - step + n_col) % n_col, n_col)
        copy = pltpu.make_async_remote_copy(
            src_ref=src,
            dst_ref=w_ref.at[1, sent],
            send_sem=ring_send.at[step - 1],
            recv_sem=ring_recv.at[step - 1],
            device_id=(row, succ),
            device_id_type=MESH,
        )
        copy.start()
        copy.wait()
        src = w_ref.at[1, got]
        sent = got
        halo(src, got, step)
    for copy in halos:
        copy.wait()
    local.wait()


def gather_window(block, n_row, n_col):
    rows, width = block.shape
    return pl.pallas_call(
        functools.partial(gather_kernel, n_row, n_col),
        out_shape=jax.ShapeDtypeStruct((3, n_col, rows, width), block.dtype),
        in_specs=[pl.BlockSpec(memory_space=pltpu.VMEM)],
        out_specs=pl.BlockSpec(memory_space=pltpu.VMEM),
        scratch_shapes=[
            pltpu.SemaphoreType.DMA((n_col - 1,)),
            pltpu.SemaphoreType.DMA((n_col - 1,)),
            pltpu.SemaphoreType.DMA((n_col,)),
            pltpu.SemaphoreType.DMA((n_col,)),
            pltpu.SemaphoreType.DMA((n_col,)),
            pltpu.SemaphoreType.DMA((n_col,)),
            pltpu.SemaphoreType.DMA((1,)),
        ],
        compiler_params=pltpu.CompilerParams(collective_id=1, has_side_effects=True),
    )(block)


def spread_kernel(n_row, n_col, mid_ref, up_ref, down_ref, o_ref, from_down, from_up, ring_in, ring_out,
                  up_send, down_send, from_down_sem, from_up_sem, ring_send, ring_recv):
    row = lax.axis_index("row")
    col = lax.axis_index("col")
    p = ring_position(col, n_col)
    succ = ring_col((p + 1) % n_col, n_col)
    pred = ring_col((p + n_col - 1) % n_col, n_col)
    up = (row + 1) % n_row
    down = (row + n_row - 1) % n_row
    barrier = pltpu.get_barrier_semaphore()
    for device in ((row, succ), (row, pred), (up, col), (down, col)):
        pl.semaphore_signal(barrier, inc=1, device_id=device, device_id_type=MESH)
    pl.semaphore_wait(barrier, 4)
    halos = []
    for step in range(1, n_col + 1):
        block = ring_col((p - step + 2 * n_col) % n_col, n_col)
        pair = []
        for src, dst, target, send, recv in (
            (up_ref, from_down, up, up_send, from_down_sem),
            (down_ref, from_up, down, down_send, from_up_sem),
        ):
            copy = pltpu.make_async_remote_copy(
                src_ref=src.at[block],
                dst_ref=dst.at[block],
                send_sem=send.at[step - 1],
                recv_sem=recv.at[step - 1],
                device_id=(target, col),
                device_id_type=MESH,
            )
            copy.start()
            pair.append(copy)
        halos.append((block, pair))

    def local_total(index):
        block, pair = halos[index]
        for copy in pair:
            copy.wait_recv()
        return (
            mid_ref[block]
            + from_down[block].astype(jnp.float32)
            + from_up[block].astype(jnp.float32)
        )

    for step in range(1, n_col):
        value = local_total(step - 1)
        if step > 1:
            value = value + ring_in[step - 2]
        ring_out[step - 1] = value
        copy = pltpu.make_async_remote_copy(
            src_ref=ring_out.at[step - 1],
            dst_ref=ring_in.at[step - 1],
            send_sem=ring_send.at[step - 1],
            recv_sem=ring_recv.at[step - 1],
            device_id=(row, succ),
            device_id_type=MESH,
        )
        copy.start()
        copy.wait()
    o_ref[...] = local_total(n_col - 1) + ring_in[n_col - 2]
    for _, pair in halos:
        for copy in pair:
            copy.wait_send()


def reduce_spread(mid, up_part, down_part, n_row, n_col):
    _, rows, width = mid.shape
    return pl.pallas_call(
        functools.partial(spread_kernel, n_row, n_col),
        out_shape=jax.ShapeDtypeStruct((rows, width), jnp.float32),
        in_specs=[pl.BlockSpec(memory_space=pltpu.VMEM)] * 3,
        out_specs=pl.BlockSpec(memory_space=pltpu.VMEM),
        scratch_shapes=[
            pltpu.VMEM((n_col, rows, width), up_part.dtype),
            pltpu.VMEM((n_col, rows, width), up_part.dtype),
            pltpu.VMEM((n_col - 1, rows, width), jnp.float32),
            pltpu.VMEM((n_col - 1, rows, width), jnp.float32),
            pltpu.SemaphoreType.DMA((n_col,)),
            pltpu.SemaphoreType.DMA((n_col,)),
            pltpu.SemaphoreType.DMA((n_col,)),
            pltpu.SemaphoreType.DMA((n_col,)),
            pltpu.SemaphoreType.DMA((n_col - 1,)),
            pltpu.SemaphoreType.DMA((n_col - 1,)),
        ],
        compiler_params=pltpu.CompilerParams(collective_id=2, has_side_effects=True),
    )(mid, up_part, down_part)


def all_reduce(stacked, n_row, n_col):
    rows, width = stacked.shape
    col_bits = n_col.bit_length() - 1
    row_bits = n_row.bit_length() - 1
    return pl.pallas_call(
        functools.partial(allreduce_kernel, n_row, n_col),
        out_shape=jax.ShapeDtypeStruct((rows, width), jnp.float32),
        in_specs=[pl.BlockSpec(memory_space=pltpu.VMEM)],
        out_specs=pl.BlockSpec(memory_space=pltpu.VMEM),
        scratch_shapes=[
            pltpu.VMEM((col_bits + row_bits, rows // 2, width), jnp.float32),
            pltpu.VMEM((col_bits + 1, rows, width), jnp.float32),
            pltpu.SemaphoreType.DMA((col_bits,)),
            pltpu.SemaphoreType.DMA((col_bits,)),
            pltpu.SemaphoreType.DMA((row_bits,)),
            pltpu.SemaphoreType.DMA((row_bits,)),
            pltpu.SemaphoreType.DMA((col_bits,)),
            pltpu.SemaphoreType.DMA((col_bits,)),
        ],
        compiler_params=pltpu.CompilerParams(collective_id=0, has_side_effects=True),
    )(stacked)


def with_halo(cells, sides, width):
    for axis, dim in sides:
        count = lax.axis_size(axis)
        head = lax.slice_in_dim(cells, 0, width, axis=dim)
        tail = lax.slice_in_dim(cells, cells.shape[dim] - width, cells.shape[dim], axis=dim)
        cells = jnp.concatenate(
            [
                lax.ppermute(tail, axis, [(i, (i + 1) % count) for i in range(count)]),
                cells,
                lax.ppermute(head, axis, [((i + 1) % count, i) for i in range(count)]),
            ],
            axis=dim,
        )
    return cells


def passed_along(value, axis, steps):
    count = lax.axis_size(axis)
    pairs = [(source, (source + steps) % count) for source in range(count)]
    return lax.ppermute(value, axis, pairs)


def shards(features, weight, weight_self, tile_values, tile_rows, tile_cols, tile_count, cotangent):
    tile_block = tile_values[0]
    slot_rows = tile_rows[0]
    slot_cols = tile_cols[0]
    live_count = tile_count[0, 0]
    slot_total = tile_block.shape[0]
    tile_side = tile_block.shape[-1]
    node_rows = features.shape[0]
    width = features.shape[1]
    per_block = node_rows // tile_side
    col_count = lax.axis_size("col")
    row_count = lax.axis_size("row")
    span = col_count * per_block
    window = gather_window(features, row_count, col_count)
    window_tiles = window.reshape(-1, tile_side, width)
    row_ids = jnp.arange(per_block, dtype=jnp.int32)
    tiles_part = tile_block
    rows_part = slot_rows
    live_part = jnp.arange(slot_total, dtype=jnp.int32) < live_count
    feat_tiles = window_tiles[slot_cols]
    selector = ((rows_part[None, :] == row_ids[:, None]) & live_part[None, :]).astype(jnp.bfloat16)
    masked = tiles_part[None, :, :, :] * selector[:, :, None, None]
    summed = jnp.einsum("ktij,tjf->kif", masked, feat_tiles, preferred_element_type=jnp.float32)
    aggregated = summed.reshape(node_rows, width).astype(jnp.bfloat16)
    pre_act = jnp.dot(aggregated, weight, preferred_element_type=jnp.float32) + jnp.dot(
        features, weight_self, preferred_element_type=jnp.float32
    )
    activations = jax.nn.silu(pre_act).astype(jnp.bfloat16)
    sigma = jax.nn.sigmoid(pre_act)
    grad_pre = (cotangent.astype(jnp.float32) * sigma * (1.0 + pre_act * (1.0 - sigma))).astype(
        jnp.bfloat16
    )
    weight_part = jnp.einsum("nf,ng->fg", aggregated, grad_pre, preferred_element_type=jnp.float32)
    self_part = jnp.einsum("nf,ng->fg", features, grad_pre, preferred_element_type=jnp.float32)
    grad_aggregated = jnp.einsum(
        "ng,fg->nf", grad_pre, weight, preferred_element_type=jnp.float32
    ).astype(jnp.bfloat16)
    self_feature = jnp.einsum(
        "ng,fg->nf", grad_pre, weight_self, preferred_element_type=jnp.float32
    )
    grad_tiles = grad_aggregated.reshape(per_block, tile_side, width)
    spread_zero = jnp.zeros((3 * span, tile_side, width), jnp.float32)
    tiles_part = tile_block
    rows_part = slot_rows
    live_part = (jnp.arange(slot_total, dtype=jnp.int32) < live_count).astype(jnp.float32)
    picked = grad_tiles[rows_part]
    products = jnp.einsum("tij,tif->tjf", tiles_part, picked, preferred_element_type=jnp.float32)
    spread = spread_zero.at[slot_cols].add(products * live_part[:, None, None])
    spread = spread.reshape(3, col_count, node_rows, width)
    own_share = reduce_spread(
        spread[1],
        spread[2].astype(jnp.bfloat16),
        spread[0].astype(jnp.bfloat16),
        row_count,
        col_count,
    )
    feature_grad = (own_share + self_feature).astype(jnp.bfloat16)
    summed_parts = all_reduce(
        jnp.concatenate([weight_part, self_part], axis=0), row_count, col_count
    )
    weight_total, self_total = summed_parts[:width], summed_parts[width:]
    factor = 1.0 / math.sqrt(node_rows * col_count * row_count)
    return (activations, feature_grad, weight_total * factor, self_total * factor)


def solution(mesh):
    placed = (
        P(("row", "col"), None),
        P(),
        P(),
        P("row", "col", None, None),
        P("row", "col"),
        P("row", "col"),
        P("row", "col"),
        P(("row", "col"), None),
    )
    return jax.shard_map(
        shards,
        mesh=mesh,
        in_specs=placed,
        out_specs=(P(("row", "col"), None), P(("row", "col"), None), P(), P()),
        check_vma=False,
    )
```

```python
import functools
import math

import jax
import jax.numpy as jnp
from jax import lax
from jax.experimental import pallas as pl
from jax.experimental.pallas import tpu as pltpu
from jax.sharding import PartitionSpec as P

MESH = pl.DeviceIdType.MESH


def flip(index, stride):
    bit = (index // stride) % 2
    return index + stride - 2 * stride * bit, bit


def allreduce_kernel(n_row, n_col, x_ref, o_ref, part, gath, rsend, rrecv, dsend, drecv, gsend, grecv):
    row = lax.axis_index("row")
    col = lax.axis_index("col")
    col_bits = n_col.bit_length() - 1
    row_bits = n_row.bit_length() - 1
    partners = []
    for k in range(col_bits):
        partners.append((row, flip(col, 1 << k)[0]))
    for k in range(row_bits):
        partners.append((flip(row, 1 << k)[0], col))
    barrier = pltpu.get_barrier_semaphore()
    for device in partners:
        pl.semaphore_signal(barrier, inc=1, device_id=device, device_id_type=MESH)
    pl.semaphore_wait(barrier, len(partners))

    rows = x_ref.shape[0]
    src = x_ref
    base = 0
    size = rows
    for k in range(col_bits):
        other, bit = flip(col, 1 << k)
        half = size // 2
        keep = base + bit * half
        give = base + (1 - bit) * half
        copy = pltpu.make_async_remote_copy(
            src_ref=src.at[pl.ds(pl.multiple_of(give, 8), half)],
            dst_ref=part.at[k, pl.ds(0, half)],
            send_sem=rsend.at[k],
            recv_sem=rrecv.at[k],
            device_id=(row, other),
            device_id_type=MESH,
        )
        copy.start()
        copy.wait()
        mine = src[pl.ds(pl.multiple_of(keep, 8), half), :] + part[k, pl.ds(0, half), :]
        gath[k, pl.ds(pl.multiple_of(keep, 8), half), :] = mine
        src = gath.at[k]
        base = keep
        size = half
    chunk = size
    total = gath[col_bits - 1, pl.ds(pl.multiple_of(base, 8), chunk), :]
    for k in range(row_bits):
        other, _ = flip(row, 1 << k)
        hold = o_ref.at[pl.ds(0, chunk)]
        hold[...] = total
        copy = pltpu.make_async_remote_copy(
            src_ref=hold,
            dst_ref=part.at[col_bits + k, pl.ds(0, chunk)],
            send_sem=dsend.at[k],
            recv_sem=drecv.at[k],
            device_id=(other, col),
            device_id_type=MESH,
        )
        copy.start()
        copy.wait()
        total = total + part[col_bits + k, pl.ds(0, chunk), :]
    final = gath.at[col_bits]
    final[pl.ds(pl.multiple_of(base, 8), chunk), :] = total
    size = chunk
    for k in reversed(range(col_bits)):
        other, bit = flip(col, 1 << k)
        start = base - bit * size
        copy = pltpu.make_async_remote_copy(
            src_ref=final.at[pl.ds(pl.multiple_of(base, 8), size)],
            dst_ref=final.at[pl.ds(pl.multiple_of(base, 8), size)],
            send_sem=gsend.at[k],
            recv_sem=grecv.at[k],
            device_id=(row, other),
            device_id_type=MESH,
        )
        copy.start()
        copy.wait()
        base = start
        size = size * 2
    o_ref[...] = final[...]


def ring_position(col, n):
    core = col % 2
    y = col // 2
    return y + core * (n - 1 - 2 * y)


def ring_col(p, n):
    q = p // (n // 2)
    y = p + q * (n - 1 - 2 * p)
    return 2 * y + q


def gather_kernel(n_row, n_col, x_ref, w_ref, ring_send, ring_recv, up_send, up_recv, down_send, down_recv, local_sem):
    row = lax.axis_index("row")
    col = lax.axis_index("col")
    p = ring_position(col, n_col)
    succ = ring_col((p + 1) % n_col, n_col)
    pred = ring_col((p + n_col - 1) % n_col, n_col)
    up = (row + 1) % n_row
    down = (row + n_row - 1) % n_row
    barrier = pltpu.get_barrier_semaphore()
    for device in ((row, succ), (row, pred), (up, col), (down, col)):
        pl.semaphore_signal(barrier, inc=1, device_id=device, device_id_type=MESH)
    pl.semaphore_wait(barrier, 4)
    local = pltpu.make_async_copy(x_ref, w_ref.at[1, col], local_sem.at[0])
    local.start()
    halos = []

    def halo(src, block, step):
        for target, slot, send, recv in ((up, 0, up_send, up_recv), (down, 2, down_send, down_recv)):
            copy = pltpu.make_async_remote_copy(
                src_ref=src,
                dst_ref=w_ref.at[slot, block],
                send_sem=send.at[step],
                recv_sem=recv.at[step],
                device_id=(target, col),
                device_id_type=MESH,
            )
            copy.start()
            halos.append(copy)

    halo(x_ref, col, 0)
    src = x_ref
    sent = col
    for step in range(1, n_col):
        got = ring_col((p - step + n_col) % n_col, n_col)
        copy = pltpu.make_async_remote_copy(
            src_ref=src,
            dst_ref=w_ref.at[1, sent],
            send_sem=ring_send.at[step - 1],
            recv_sem=ring_recv.at[step - 1],
            device_id=(row, succ),
            device_id_type=MESH,
        )
        copy.start()
        copy.wait()
        src = w_ref.at[1, got]
        sent = got
        halo(src, got, step)
    for copy in halos:
        copy.wait()
    local.wait()


def gather_window(block, n_row, n_col):
    rows, width = block.shape
    return pl.pallas_call(
        functools.partial(gather_kernel, n_row, n_col),
        out_shape=jax.ShapeDtypeStruct((3, n_col, rows, width), block.dtype),
        in_specs=[pl.BlockSpec(memory_space=pltpu.VMEM)],
        out_specs=pl.BlockSpec(memory_space=pltpu.VMEM),
        scratch_shapes=[
            pltpu.SemaphoreType.DMA((n_col - 1,)),
            pltpu.SemaphoreType.DMA((n_col - 1,)),
            pltpu.SemaphoreType.DMA((n_col,)),
            pltpu.SemaphoreType.DMA((n_col,)),
            pltpu.SemaphoreType.DMA((n_col,)),
            pltpu.SemaphoreType.DMA((n_col,)),
            pltpu.SemaphoreType.DMA((1,)),
        ],
        compiler_params=pltpu.CompilerParams(collective_id=1, has_side_effects=True),
    )(block)


def spread_kernel(n_row, n_col, mid_ref, up_ref, down_ref, o_ref, from_down, from_up, ring_in, ring_out,
                  up_send, down_send, from_down_sem, from_up_sem, ring_send, ring_recv):
    row = lax.axis_index("row")
    col = lax.axis_index("col")
    p = ring_position(col, n_col)
    succ = ring_col((p + 1) % n_col, n_col)
    pred = ring_col((p + n_col - 1) % n_col, n_col)
    up = (row + 1) % n_row
    down = (row + n_row - 1) % n_row
    barrier = pltpu.get_barrier_semaphore()
    for device in ((row, succ), (row, pred), (up, col), (down, col)):
        pl.semaphore_signal(barrier, inc=1, device_id=device, device_id_type=MESH)
    pl.semaphore_wait(barrier, 4)
    halos = []
    for step in range(1, n_col + 1):
        block = ring_col((p - step + 2 * n_col) % n_col, n_col)
        pair = []
        for src, dst, target, send, recv in (
            (up_ref, from_down, up, up_send, from_down_sem),
            (down_ref, from_up, down, down_send, from_up_sem),
        ):
            copy = pltpu.make_async_remote_copy(
                src_ref=src.at[block],
                dst_ref=dst.at[block],
                send_sem=send.at[step - 1],
                recv_sem=recv.at[step - 1],
                device_id=(target, col),
                device_id_type=MESH,
            )
            copy.start()
            pair.append(copy)
        halos.append((block, pair))

    def local_total(index):
        block, pair = halos[index]
        for copy in pair:
            copy.wait_recv()
        return (
            mid_ref[block]
            + from_down[block].astype(jnp.float32)
            + from_up[block].astype(jnp.float32)
        )

    for step in range(1, n_col):
        value = local_total(step - 1)
        if step > 1:
            value = value + ring_in[step - 2]
        ring_out[step - 1] = value
        copy = pltpu.make_async_remote_copy(
            src_ref=ring_out.at[step - 1],
            dst_ref=ring_in.at[step - 1],
            send_sem=ring_send.at[step - 1],
            recv_sem=ring_recv.at[step - 1],
            device_id=(row, succ),
            device_id_type=MESH,
        )
        copy.start()
        copy.wait()
    o_ref[...] = local_total(n_col - 1) + ring_in[n_col - 2]
    for _, pair in halos:
        for copy in pair:
            copy.wait_send()


def reduce_spread(mid, up_part, down_part, n_row, n_col):
    _, rows, width = mid.shape
    return pl.pallas_call(
        functools.partial(spread_kernel, n_row, n_col),
        out_shape=jax.ShapeDtypeStruct((rows, width), jnp.float32),
        in_specs=[pl.BlockSpec(memory_space=pltpu.VMEM)] * 3,
        out_specs=pl.BlockSpec(memory_space=pltpu.VMEM),
        scratch_shapes=[
            pltpu.VMEM((n_col, rows, width), up_part.dtype),
            pltpu.VMEM((n_col, rows, width), up_part.dtype),
            pltpu.VMEM((n_col - 1, rows, width), jnp.float32),
            pltpu.VMEM((n_col - 1, rows, width), jnp.float32),
            pltpu.SemaphoreType.DMA((n_col,)),
            pltpu.SemaphoreType.DMA((n_col,)),
            pltpu.SemaphoreType.DMA((n_col,)),
            pltpu.SemaphoreType.DMA((n_col,)),
            pltpu.SemaphoreType.DMA((n_col - 1,)),
            pltpu.SemaphoreType.DMA((n_col - 1,)),
        ],
        compiler_params=pltpu.CompilerParams(collective_id=2, has_side_effects=True),
    )(mid, up_part, down_part)


def local_kernel(rows_ref, cols_ref, count_ref, window_ref, tiles_ref, feat_ref, w_ref, ws_ref, cot_ref,
                 act_ref, parts_ref, self_ref, mid_ref, up_ref, down_ref, acc, grad_agg, spread):
    tile = tiles_ref.shape[-1]
    nodes = acc.shape[0]
    span = mid_ref.shape[0]
    count = jnp.minimum(count_ref[0], tiles_ref.shape[0])
    acc[...] = jnp.zeros_like(acc)

    def forward(j, carry):
        at = pl.multiple_of(rows_ref[j] * tile, tile)
        acc[pl.ds(at, tile), :] += jnp.dot(
            tiles_ref[j], window_ref[cols_ref[j]], preferred_element_type=jnp.float32
        )
        return carry

    lax.fori_loop(0, count, forward, 0)
    aggregated = acc[...].astype(jnp.bfloat16)
    features = feat_ref[...]
    pre_act = jnp.dot(aggregated, w_ref[...], preferred_element_type=jnp.float32) + jnp.dot(
        features, ws_ref[...], preferred_element_type=jnp.float32
    )
    sigma = jax.nn.sigmoid(pre_act)
    act_ref[...] = (pre_act * sigma).astype(act_ref.dtype)
    grad_pre = (cot_ref[...].astype(jnp.float32) * sigma * (1.0 + pre_act * (1.0 - sigma))).astype(
        jnp.bfloat16
    )
    over_nodes = (((0,), (0,)), ((), ()))
    parts_ref[pl.ds(0, nodes), :] = lax.dot_general(
        aggregated, grad_pre, over_nodes, preferred_element_type=jnp.float32
    )
    parts_ref[pl.ds(nodes, nodes), :] = lax.dot_general(
        features, grad_pre, over_nodes, preferred_element_type=jnp.float32
    )
    by_rows = (((1,), (1,)), ((), ()))
    grad_agg[...] = lax.dot_general(
        grad_pre, w_ref[...], by_rows, preferred_element_type=jnp.float32
    ).astype(jnp.bfloat16)
    self_ref[...] = lax.dot_general(grad_pre, ws_ref[...], by_rows, preferred_element_type=jnp.float32)
    spread[...] = jnp.zeros_like(spread)

    def backward(j, carry):
        at = pl.multiple_of(rows_ref[j] * tile, tile)
        column = cols_ref[j]
        spread[column] += lax.dot_general(
            tiles_ref[j], grad_agg[pl.ds(at, tile), :], over_nodes, preferred_element_type=jnp.float32
        )
        return carry

    lax.fori_loop(0, count, backward, 0)
    mid_ref[...] = spread[pl.ds(span, span)]
    up_ref[...] = spread[pl.ds(2 * span, span)].astype(up_ref.dtype)
    down_ref[...] = spread[pl.ds(0, span)].astype(down_ref.dtype)


def local_math(slot_rows, slot_cols, count, window, tiles, features, weight, weight_self, cotangent):
    nodes, width = features.shape
    span = window.shape[0] // 3
    tile = tiles.shape[-1]
    smem = pl.BlockSpec(memory_space=pltpu.SMEM)
    vmem = pl.BlockSpec(memory_space=pltpu.VMEM)
    return pl.pallas_call(
        local_kernel,
        out_shape=(
            jax.ShapeDtypeStruct((nodes, width), jnp.bfloat16),
            jax.ShapeDtypeStruct((2 * width, width), jnp.float32),
            jax.ShapeDtypeStruct((nodes, width), jnp.float32),
            jax.ShapeDtypeStruct((span, tile, width), jnp.float32),
            jax.ShapeDtypeStruct((span, tile, width), jnp.bfloat16),
            jax.ShapeDtypeStruct((span, tile, width), jnp.bfloat16),
        ),
        in_specs=[smem, smem, smem] + [vmem] * 6,
        out_specs=(vmem,) * 6,
        scratch_shapes=[
            pltpu.VMEM((nodes, width), jnp.float32),
            pltpu.VMEM((nodes, width), jnp.bfloat16),
            pltpu.VMEM((3 * span, tile, width), jnp.float32),
        ],
    )(slot_rows, slot_cols, count, window, tiles, features, weight, weight_self, cotangent)


def all_reduce(stacked, n_row, n_col):
    rows, width = stacked.shape
    col_bits = n_col.bit_length() - 1
    row_bits = n_row.bit_length() - 1
    return pl.pallas_call(
        functools.partial(allreduce_kernel, n_row, n_col),
        out_shape=jax.ShapeDtypeStruct((rows, width), jnp.float32),
        in_specs=[pl.BlockSpec(memory_space=pltpu.VMEM)],
        out_specs=pl.BlockSpec(memory_space=pltpu.VMEM),
        scratch_shapes=[
            pltpu.VMEM((col_bits + row_bits, rows // 2, width), jnp.float32),
            pltpu.VMEM((col_bits + 1, rows, width), jnp.float32),
            pltpu.SemaphoreType.DMA((col_bits,)),
            pltpu.SemaphoreType.DMA((col_bits,)),
            pltpu.SemaphoreType.DMA((row_bits,)),
            pltpu.SemaphoreType.DMA((row_bits,)),
            pltpu.SemaphoreType.DMA((col_bits,)),
            pltpu.SemaphoreType.DMA((col_bits,)),
        ],
        compiler_params=pltpu.CompilerParams(collective_id=0, has_side_effects=True),
    )(stacked)


def with_halo(cells, sides, width):
    for axis, dim in sides:
        count = lax.axis_size(axis)
        head = lax.slice_in_dim(cells, 0, width, axis=dim)
        tail = lax.slice_in_dim(cells, cells.shape[dim] - width, cells.shape[dim], axis=dim)
        cells = jnp.concatenate(
            [
                lax.ppermute(tail, axis, [(i, (i + 1) % count) for i in range(count)]),
                cells,
                lax.ppermute(head, axis, [((i + 1) % count, i) for i in range(count)]),
            ],
            axis=dim,
        )
    return cells


def passed_along(value, axis, steps):
    count = lax.axis_size(axis)
    pairs = [(source, (source + steps) % count) for source in range(count)]
    return lax.ppermute(value, axis, pairs)


def shards(features, weight, weight_self, tile_values, tile_rows, tile_cols, tile_count, cotangent):
    tile_block = tile_values[0]
    slot_rows = tile_rows[0]
    slot_cols = tile_cols[0]
    live_count = tile_count[0, 0]
    slot_total = tile_block.shape[0]
    tile_side = tile_block.shape[-1]
    node_rows = features.shape[0]
    width = features.shape[1]
    per_block = node_rows // tile_side
    col_count = lax.axis_size("col")
    row_count = lax.axis_size("row")
    span = col_count * per_block
    window = gather_window(features, row_count, col_count)
    window_tiles = window.reshape(-1, tile_side, width)
    activations, parts, self_feature, mid, up_part, down_part = local_math(
        slot_rows,
        slot_cols,
        tile_count[0],
        window_tiles,
        tile_block,
        features,
        weight,
        weight_self,
        cotangent,
    )
    own_share = reduce_spread(
        mid.reshape(col_count, node_rows, width),
        up_part.reshape(col_count, node_rows, width),
        down_part.reshape(col_count, node_rows, width),
        row_count,
        col_count,
    )
    feature_grad = (own_share + self_feature).astype(jnp.bfloat16)
    summed_parts = all_reduce(parts, row_count, col_count)
    weight_total, self_total = summed_parts[:width], summed_parts[width:]
    factor = 1.0 / math.sqrt(node_rows * col_count * row_count)
    return (activations, feature_grad, weight_total * factor, self_total * factor)


def solution(mesh):
    placed = (
        P(("row", "col"), None),
        P(),
        P(),
        P("row", "col", None, None),
        P("row", "col"),
        P("row", "col"),
        P("row", "col"),
        P(("row", "col"), None),
    )
    return jax.shard_map(
        shards,
        mesh=mesh,
        in_specs=placed,
        out_specs=(P(("row", "col"), None), P(("row", "col"), None), P(), P()),
        check_vma=False,
    )
```

```python
import functools
import math

import jax
import jax.numpy as jnp
from jax import lax
from jax.experimental import pallas as pl
from jax.experimental.pallas import tpu as pltpu
from jax.sharding import PartitionSpec as P

MESH = pl.DeviceIdType.MESH


def flip(index, stride):
    bit = (index // stride) % 2
    return index + stride - 2 * stride * bit, bit


def allreduce_partners(n_row, n_col, row, col):
    partners = []
    for k in range(n_col.bit_length() - 1):
        partners.append((row, flip(col, 1 << k)[0]))
    for k in range(n_row.bit_length() - 1):
        partners.append((flip(row, 1 << k)[0], col))
    return partners


def allreduce_steps(n_row, n_col, row, col, x_ref, o_ref, part, gath, rsend, rrecv, dsend, drecv, gsend, grecv):
    col_bits = n_col.bit_length() - 1
    row_bits = n_row.bit_length() - 1
    rows = x_ref.shape[0]
    src = x_ref
    base = 0
    size = rows
    for k in range(col_bits):
        other, bit = flip(col, 1 << k)
        half = size // 2
        keep = base + bit * half
        give = base + (1 - bit) * half
        copy = pltpu.make_async_remote_copy(
            src_ref=src.at[pl.ds(pl.multiple_of(give, 8), half)],
            dst_ref=part.at[k, pl.ds(0, half)],
            send_sem=rsend.at[k],
            recv_sem=rrecv.at[k],
            device_id=(row, other),
            device_id_type=MESH,
        )
        copy.start()
        yield copy
        mine = src[pl.ds(pl.multiple_of(keep, 8), half), :] + part[k, pl.ds(0, half), :]
        gath[k, pl.ds(pl.multiple_of(keep, 8), half), :] = mine
        src = gath.at[k]
        base = keep
        size = half
    chunk = size
    total = gath[col_bits - 1, pl.ds(pl.multiple_of(base, 8), chunk), :]
    for k in range(row_bits):
        other, _ = flip(row, 1 << k)
        hold = o_ref.at[pl.ds(0, chunk)]
        hold[...] = total
        copy = pltpu.make_async_remote_copy(
            src_ref=hold,
            dst_ref=part.at[col_bits + k, pl.ds(0, chunk)],
            send_sem=dsend.at[k],
            recv_sem=drecv.at[k],
            device_id=(other, col),
            device_id_type=MESH,
        )
        copy.start()
        yield copy
        total = total + part[col_bits + k, pl.ds(0, chunk), :]
    final = gath.at[col_bits]
    final[pl.ds(pl.multiple_of(base, 8), chunk), :] = total
    size = chunk
    for k in reversed(range(col_bits)):
        other, bit = flip(col, 1 << k)
        start = base - bit * size
        copy = pltpu.make_async_remote_copy(
            src_ref=final.at[pl.ds(pl.multiple_of(base, 8), size)],
            dst_ref=final.at[pl.ds(pl.multiple_of(base, 8), size)],
            send_sem=gsend.at[k],
            recv_sem=grecv.at[k],
            device_id=(row, other),
            device_id_type=MESH,
        )
        copy.start()
        yield copy
        base = start
        size = size * 2
    o_ref[...] = final[...]


def run_together(*chains):
    active = list(chains)
    while active:
        copies, kept = [], []
        for chain in active:
            try:
                copies.append(next(chain))
                kept.append(chain)
            except StopIteration:
                pass
        for copy in copies:
            copy.wait()
        active = kept


def ring_position(col, n):
    core = col % 2
    y = col // 2
    return y + core * (n - 1 - 2 * y)


def ring_col(p, n):
    q = p // (n // 2)
    y = p + q * (n - 1 - 2 * p)
    return 2 * y + q


def gather_kernel(n_row, n_col, x_ref, w_ref, ring_send, ring_recv, up_send, up_recv, down_send, down_recv, local_sem):
    row = lax.axis_index("row")
    col = lax.axis_index("col")
    p = ring_position(col, n_col)
    succ = ring_col((p + 1) % n_col, n_col)
    pred = ring_col((p + n_col - 1) % n_col, n_col)
    up = (row + 1) % n_row
    down = (row + n_row - 1) % n_row
    barrier = pltpu.get_barrier_semaphore()
    for device in ((row, succ), (row, pred), (up, col), (down, col)):
        pl.semaphore_signal(barrier, inc=1, device_id=device, device_id_type=MESH)
    pl.semaphore_wait(barrier, 4)
    local = pltpu.make_async_copy(x_ref, w_ref.at[1, col], local_sem.at[0])
    local.start()
    halos = []

    def halo(src, block, step):
        for target, slot, send, recv in ((up, 0, up_send, up_recv), (down, 2, down_send, down_recv)):
            copy = pltpu.make_async_remote_copy(
                src_ref=src,
                dst_ref=w_ref.at[slot, block],
                send_sem=send.at[step],
                recv_sem=recv.at[step],
                device_id=(target, col),
                device_id_type=MESH,
            )
            copy.start()
            halos.append(copy)

    halo(x_ref, col, 0)
    src = x_ref
    sent = col
    for step in range(1, n_col):
        got = ring_col((p - step + n_col) % n_col, n_col)
        copy = pltpu.make_async_remote_copy(
            src_ref=src,
            dst_ref=w_ref.at[1, sent],
            send_sem=ring_send.at[step - 1],
            recv_sem=ring_recv.at[step - 1],
            device_id=(row, succ),
            device_id_type=MESH,
        )
        copy.start()
        copy.wait()
        src = w_ref.at[1, got]
        sent = got
        halo(src, got, step)
    for copy in halos:
        copy.wait()
    local.wait()


def gather_window(block, n_row, n_col):
    rows, width = block.shape
    return pl.pallas_call(
        functools.partial(gather_kernel, n_row, n_col),
        out_shape=jax.ShapeDtypeStruct((3, n_col, rows, width), block.dtype),
        in_specs=[pl.BlockSpec(memory_space=pltpu.VMEM)],
        out_specs=pl.BlockSpec(memory_space=pltpu.VMEM),
        scratch_shapes=[
            pltpu.SemaphoreType.DMA((n_col - 1,)),
            pltpu.SemaphoreType.DMA((n_col - 1,)),
            pltpu.SemaphoreType.DMA((n_col,)),
            pltpu.SemaphoreType.DMA((n_col,)),
            pltpu.SemaphoreType.DMA((n_col,)),
            pltpu.SemaphoreType.DMA((n_col,)),
            pltpu.SemaphoreType.DMA((1,)),
        ],
        compiler_params=pltpu.CompilerParams(collective_id=1, has_side_effects=True),
    )(block)


def spread_kernel(n_row, n_col, mid_ref, up_ref, down_ref, parts_ref, o_ref, sums_ref, from_down, from_up,
                  ring_in, ring_out, up_send, down_send, from_down_sem, from_up_sem, ring_send, ring_recv,
                  part, gath, rsend, rrecv, dsend, drecv, gsend, grecv):
    row = lax.axis_index("row")
    col = lax.axis_index("col")
    p = ring_position(col, n_col)
    succ = ring_col((p + 1) % n_col, n_col)
    pred = ring_col((p + n_col - 1) % n_col, n_col)
    up = (row + 1) % n_row
    down = (row + n_row - 1) % n_row
    partners = [(row, succ), (row, pred), (up, col), (down, col)]
    partners += allreduce_partners(n_row, n_col, row, col)
    barrier = pltpu.get_barrier_semaphore()
    for device in partners:
        pl.semaphore_signal(barrier, inc=1, device_id=device, device_id_type=MESH)
    pl.semaphore_wait(barrier, len(partners))
    halos = []
    for step in range(1, n_col + 1):
        block = ring_col((p - step + 2 * n_col) % n_col, n_col)
        pair = []
        for src, dst, target, send, recv in (
            (up_ref, from_down, up, up_send, from_down_sem),
            (down_ref, from_up, down, down_send, from_up_sem),
        ):
            copy = pltpu.make_async_remote_copy(
                src_ref=src.at[block],
                dst_ref=dst.at[block],
                send_sem=send.at[step - 1],
                recv_sem=recv.at[step - 1],
                device_id=(target, col),
                device_id_type=MESH,
            )
            copy.start()
            pair.append(copy)
        halos.append((block, pair))

    def local_total(index):
        block, pair = halos[index]
        for copy in pair:
            copy.wait_recv()
        return (
            mid_ref[block]
            + from_down[block].astype(jnp.float32)
            + from_up[block].astype(jnp.float32)
        )

    def ring_steps():
        for step in range(1, n_col):
            value = local_total(step - 1)
            if step > 1:
                value = value + ring_in[step - 2]
            ring_out[step - 1] = value
            copy = pltpu.make_async_remote_copy(
                src_ref=ring_out.at[step - 1],
                dst_ref=ring_in.at[step - 1],
                send_sem=ring_send.at[step - 1],
                recv_sem=ring_recv.at[step - 1],
                device_id=(row, succ),
                device_id_type=MESH,
            )
            copy.start()
            yield copy
        o_ref[...] = local_total(n_col - 1) + ring_in[n_col - 2]

    run_together(
        allreduce_steps(n_row, n_col, row, col, parts_ref, sums_ref, part, gath,
                        rsend, rrecv, dsend, drecv, gsend, grecv),
        ring_steps(),
    )
    for _, pair in halos:
        for copy in pair:
            copy.wait_send()


def reduce_spread(mid, up_part, down_part, parts, n_row, n_col):
    _, rows, width = mid.shape
    col_bits = n_col.bit_length() - 1
    row_bits = n_row.bit_length() - 1
    stacked, _ = parts.shape
    return pl.pallas_call(
        functools.partial(spread_kernel, n_row, n_col),
        out_shape=(
            jax.ShapeDtypeStruct((rows, width), jnp.float32),
            jax.ShapeDtypeStruct(parts.shape, jnp.float32),
        ),
        in_specs=[pl.BlockSpec(memory_space=pltpu.VMEM)] * 4,
        out_specs=(pl.BlockSpec(memory_space=pltpu.VMEM),) * 2,
        scratch_shapes=[
            pltpu.VMEM((n_col, rows, width), up_part.dtype),
            pltpu.VMEM((n_col, rows, width), up_part.dtype),
            pltpu.VMEM((n_col - 1, rows, width), jnp.float32),
            pltpu.VMEM((n_col - 1, rows, width), jnp.float32),
            pltpu.SemaphoreType.DMA((n_col,)),
            pltpu.SemaphoreType.DMA((n_col,)),
            pltpu.SemaphoreType.DMA((n_col,)),
            pltpu.SemaphoreType.DMA((n_col,)),
            pltpu.SemaphoreType.DMA((n_col - 1,)),
            pltpu.SemaphoreType.DMA((n_col - 1,)),
            pltpu.VMEM((col_bits + row_bits, stacked // 2, width), jnp.float32),
            pltpu.VMEM((col_bits + 1, stacked, width), jnp.float32),
            pltpu.SemaphoreType.DMA((col_bits,)),
            pltpu.SemaphoreType.DMA((col_bits,)),
            pltpu.SemaphoreType.DMA((row_bits,)),
            pltpu.SemaphoreType.DMA((row_bits,)),
            pltpu.SemaphoreType.DMA((col_bits,)),
            pltpu.SemaphoreType.DMA((col_bits,)),
        ],
        compiler_params=pltpu.CompilerParams(collective_id=2, has_side_effects=True),
    )(mid, up_part, down_part, parts)


def local_kernel(rows_ref, cols_ref, count_ref, window_ref, tiles_ref, feat_ref, w_ref, ws_ref, cot_ref,
                 act_ref, parts_ref, self_ref, mid_ref, up_ref, down_ref, acc, grad_agg, spread):
    tile = tiles_ref.shape[-1]
    nodes = acc.shape[0]
    span = mid_ref.shape[0]
    count = jnp.minimum(count_ref[0], tiles_ref.shape[0])
    acc[...] = jnp.zeros_like(acc)

    def forward(j, carry):
        at = pl.multiple_of(rows_ref[j] * tile, tile)
        acc[pl.ds(at, tile), :] += jnp.dot(
            tiles_ref[j], window_ref[cols_ref[j]], preferred_element_type=jnp.float32
        )
        return carry

    lax.fori_loop(0, count, forward, 0)
    aggregated = acc[...].astype(jnp.bfloat16)
    features = feat_ref[...]
    pre_act = jnp.dot(aggregated, w_ref[...], preferred_element_type=jnp.float32) + jnp.dot(
        features, ws_ref[...], preferred_element_type=jnp.float32
    )
    sigma = jax.nn.sigmoid(pre_act)
    act_ref[...] = (pre_act * sigma).astype(act_ref.dtype)
    grad_pre = (cot_ref[...].astype(jnp.float32) * sigma * (1.0 + pre_act * (1.0 - sigma))).astype(
        jnp.bfloat16
    )
    over_nodes = (((0,), (0,)), ((), ()))
    parts_ref[pl.ds(0, nodes), :] = lax.dot_general(
        aggregated, grad_pre, over_nodes, preferred_element_type=jnp.float32
    )
    parts_ref[pl.ds(nodes, nodes), :] = lax.dot_general(
        features, grad_pre, over_nodes, preferred_element_type=jnp.float32
    )
    by_rows = (((1,), (1,)), ((), ()))
    grad_agg[...] = lax.dot_general(
        grad_pre, w_ref[...], by_rows, preferred_element_type=jnp.float32
    ).astype(jnp.bfloat16)
    self_ref[...] = lax.dot_general(grad_pre, ws_ref[...], by_rows, preferred_element_type=jnp.float32)
    spread[...] = jnp.zeros_like(spread)

    def backward(j, carry):
        at = pl.multiple_of(rows_ref[j] * tile, tile)
        column = cols_ref[j]
        spread[column] += lax.dot_general(
            tiles_ref[j], grad_agg[pl.ds(at, tile), :], over_nodes, preferred_element_type=jnp.float32
        )
        return carry

    lax.fori_loop(0, count, backward, 0)
    mid_ref[...] = spread[pl.ds(span, span)]
    up_ref[...] = spread[pl.ds(2 * span, span)].astype(up_ref.dtype)
    down_ref[...] = spread[pl.ds(0, span)].astype(down_ref.dtype)


def local_math(slot_rows, slot_cols, count, window, tiles, features, weight, weight_self, cotangent):
    nodes, width = features.shape
    span = window.shape[0] // 3
    tile = tiles.shape[-1]
    smem = pl.BlockSpec(memory_space=pltpu.SMEM)
    vmem = pl.BlockSpec(memory_space=pltpu.VMEM)
    return pl.pallas_call(
        local_kernel,
        out_shape=(
            jax.ShapeDtypeStruct((nodes, width), jnp.bfloat16),
            jax.ShapeDtypeStruct((2 * width, width), jnp.float32),
            jax.ShapeDtypeStruct((nodes, width), jnp.float32),
            jax.ShapeDtypeStruct((span, tile, width), jnp.float32),
            jax.ShapeDtypeStruct((span, tile, width), jnp.bfloat16),
            jax.ShapeDtypeStruct((span, tile, width), jnp.bfloat16),
        ),
        in_specs=[smem, smem, smem] + [vmem] * 6,
        out_specs=(vmem,) * 6,
        scratch_shapes=[
            pltpu.VMEM((nodes, width), jnp.float32),
            pltpu.VMEM((nodes, width), jnp.bfloat16),
            pltpu.VMEM((3 * span, tile, width), jnp.float32),
        ],
    )(slot_rows, slot_cols, count, window, tiles, features, weight, weight_self, cotangent)


def shards(features, weight, weight_self, tile_values, tile_rows, tile_cols, tile_count, cotangent):
    tile_block = tile_values[0]
    slot_rows = tile_rows[0]
    slot_cols = tile_cols[0]
    live_count = tile_count[0, 0]
    slot_total = tile_block.shape[0]
    tile_side = tile_block.shape[-1]
    node_rows = features.shape[0]
    width = features.shape[1]
    per_block = node_rows // tile_side
    col_count = lax.axis_size("col")
    row_count = lax.axis_size("row")
    span = col_count * per_block
    window = gather_window(features, row_count, col_count)
    window_tiles = window.reshape(-1, tile_side, width)
    activations, parts, self_feature, mid, up_part, down_part = local_math(
        slot_rows,
        slot_cols,
        tile_count[0],
        window_tiles,
        tile_block,
        features,
        weight,
        weight_self,
        cotangent,
    )
    own_share, summed_parts = reduce_spread(
        mid.reshape(col_count, node_rows, width),
        up_part.reshape(col_count, node_rows, width),
        down_part.reshape(col_count, node_rows, width),
        parts,
        row_count,
        col_count,
    )
    feature_grad = (own_share + self_feature).astype(jnp.bfloat16)
    weight_total, self_total = summed_parts[:width], summed_parts[width:]
    factor = 1.0 / math.sqrt(node_rows * col_count * row_count)
    return (activations, feature_grad, weight_total * factor, self_total * factor)


def solution(mesh):
    placed = (
        P(("row", "col"), None),
        P(),
        P(),
        P("row", "col", None, None),
        P("row", "col"),
        P("row", "col"),
        P("row", "col"),
        P(("row", "col"), None),
    )
    return jax.shard_map(
        shards,
        mesh=mesh,
        in_specs=placed,
        out_specs=(P(("row", "col"), None), P(("row", "col"), None), P(), P()),
        check_vma=False,
    )
```

```python
import functools
import math

import jax
import jax.numpy as jnp
from jax import lax
from jax.experimental import pallas as pl
from jax.experimental.pallas import tpu as pltpu
from jax.sharding import PartitionSpec as P

MESH = pl.DeviceIdType.MESH


def flip(index, stride):
    bit = (index // stride) % 2
    return index + stride - 2 * stride * bit, bit


def allreduce_partners(n_row, n_col, row, col):
    partners = []
    for k in range(n_col.bit_length() - 1):
        partners.append((row, flip(col, 1 << k)[0]))
    for k in range(n_row.bit_length() - 1):
        partners.append((flip(row, 1 << k)[0], col))
    return partners


def allreduce_steps(n_row, n_col, row, col, x_ref, o_ref, part, gath, rsend, rrecv, dsend, drecv, gsend, grecv):
    col_bits = n_col.bit_length() - 1
    row_bits = n_row.bit_length() - 1
    rows = x_ref.shape[0]
    src = x_ref
    base = 0
    size = rows
    for k in range(col_bits):
        other, bit = flip(col, 1 << k)
        half = size // 2
        keep = base + bit * half
        give = base + (1 - bit) * half
        copy = pltpu.make_async_remote_copy(
            src_ref=src.at[pl.ds(pl.multiple_of(give, 8), half)],
            dst_ref=part.at[k, pl.ds(0, half)],
            send_sem=rsend.at[k],
            recv_sem=rrecv.at[k],
            device_id=(row, other),
            device_id_type=MESH,
        )
        copy.start()
        yield copy
        mine = src[pl.ds(pl.multiple_of(keep, 8), half), :] + part[k, pl.ds(0, half), :]
        gath[k, pl.ds(pl.multiple_of(keep, 8), half), :] = mine
        src = gath.at[k]
        base = keep
        size = half
    chunk = size
    total = gath[col_bits - 1, pl.ds(pl.multiple_of(base, 8), chunk), :]
    for k in range(row_bits):
        other, _ = flip(row, 1 << k)
        hold = o_ref.at[pl.ds(0, chunk)]
        hold[...] = total
        copy = pltpu.make_async_remote_copy(
            src_ref=hold,
            dst_ref=part.at[col_bits + k, pl.ds(0, chunk)],
            send_sem=dsend.at[k],
            recv_sem=drecv.at[k],
            device_id=(other, col),
            device_id_type=MESH,
        )
        copy.start()
        yield copy
        total = total + part[col_bits + k, pl.ds(0, chunk), :]
    final = gath.at[col_bits]
    final[pl.ds(pl.multiple_of(base, 8), chunk), :] = total
    size = chunk
    for k in reversed(range(col_bits)):
        other, bit = flip(col, 1 << k)
        start = base - bit * size
        copy = pltpu.make_async_remote_copy(
            src_ref=final.at[pl.ds(pl.multiple_of(base, 8), size)],
            dst_ref=final.at[pl.ds(pl.multiple_of(base, 8), size)],
            send_sem=gsend.at[k],
            recv_sem=grecv.at[k],
            device_id=(row, other),
            device_id_type=MESH,
        )
        copy.start()
        yield copy
        base = start
        size = size * 2
    o_ref[...] = final[...]


def run_together(*chains):
    active = list(chains)
    while active:
        copies, kept = [], []
        for chain in active:
            try:
                copies.append(next(chain))
                kept.append(chain)
            except StopIteration:
                pass
        for copy in copies:
            copy.wait()
        active = kept


def ring_position(col, n):
    core = col % 2
    y = col // 2
    return y + core * (n - 1 - 2 * y)


def ring_col(p, n):
    q = p // (n // 2)
    y = p + q * (n - 1 - 2 * p)
    return 2 * y + q


def gather_kernel(n_row, n_col, x_ref, w_ref, ring_send, ring_recv, halo_send, halo_recv, local_sem):
    row = lax.axis_index("row")
    col = lax.axis_index("col")
    p = ring_position(col, n_col)
    succ = ring_col((p + 1) % n_col, n_col)
    pred = ring_col((p + n_col - 1) % n_col, n_col)
    up = (row + 1) % n_row
    down = (row + n_row - 1) % n_row
    barrier = pltpu.get_barrier_semaphore()
    for device in ((row, succ), (row, pred), (up, col), (down, col)):
        pl.semaphore_signal(barrier, inc=1, device_id=device, device_id_type=MESH)
    pl.semaphore_wait(barrier, 4)
    local = pltpu.make_async_copy(x_ref, w_ref.at[1, col], local_sem.at[0])
    local.start()
    halos = {}
    for target, slot in ((up, 0), (down, 2)):
        copy = pltpu.make_async_remote_copy(
            src_ref=x_ref,
            dst_ref=w_ref.at[slot, col],
            send_sem=halo_send.at[slot // 2],
            recv_sem=halo_recv.at[slot // 2],
            device_id=(target, col),
            device_id_type=MESH,
        )
        copy.start()
        halos[slot] = copy
    sent = col
    for step in range(1, n_col):
        copies = []
        for group in (1, 0, 2):
            if step == 1 and group != 1:
                halos[group].wait_recv()
            src = x_ref if (step == 1 and group == 1) else w_ref.at[group, sent]
            copy = pltpu.make_async_remote_copy(
                src_ref=src,
                dst_ref=w_ref.at[group, sent],
                send_sem=ring_send.at[group, step - 1],
                recv_sem=ring_recv.at[group, step - 1],
                device_id=(row, succ),
                device_id_type=MESH,
            )
            copy.start()
            copies.append(copy)
        for copy in copies:
            copy.wait()
        sent = ring_col((p - step + n_col) % n_col, n_col)
    for copy in halos.values():
        copy.wait_send()
    local.wait()


def gather_window(block, n_row, n_col):
    rows, width = block.shape
    return pl.pallas_call(
        functools.partial(gather_kernel, n_row, n_col),
        out_shape=jax.ShapeDtypeStruct((3, n_col, rows, width), block.dtype),
        in_specs=[pl.BlockSpec(memory_space=pltpu.VMEM)],
        out_specs=pl.BlockSpec(memory_space=pltpu.VMEM),
        scratch_shapes=[
            pltpu.SemaphoreType.DMA((3, n_col - 1)),
            pltpu.SemaphoreType.DMA((3, n_col - 1)),
            pltpu.SemaphoreType.DMA((2,)),
            pltpu.SemaphoreType.DMA((2,)),
            pltpu.SemaphoreType.DMA((1,)),
        ],
        compiler_params=pltpu.CompilerParams(collective_id=1, has_side_effects=True),
    )(block)


def spread_kernel(n_row, n_col, mid_ref, up_ref, down_ref, parts_ref, o_ref, sums_ref, from_down, from_up,
                  ring_in, ring_out, up_send, down_send, from_down_sem, from_up_sem, ring_send, ring_recv,
                  part, gath, rsend, rrecv, dsend, drecv, gsend, grecv):
    row = lax.axis_index("row")
    col = lax.axis_index("col")
    p = ring_position(col, n_col)
    succ = ring_col((p + 1) % n_col, n_col)
    pred = ring_col((p + n_col - 1) % n_col, n_col)
    up = (row + 1) % n_row
    down = (row + n_row - 1) % n_row
    partners = [(row, succ), (row, pred), (up, col), (down, col)]
    partners += allreduce_partners(n_row, n_col, row, col)
    barrier = pltpu.get_barrier_semaphore()
    for device in partners:
        pl.semaphore_signal(barrier, inc=1, device_id=device, device_id_type=MESH)
    pl.semaphore_wait(barrier, len(partners))
    halos = []
    for step in range(1, n_col + 1):
        block = ring_col((p - step + 2 * n_col) % n_col, n_col)
        pair = []
        for src, dst, target, send, recv in (
            (up_ref, from_down, up, up_send, from_down_sem),
            (down_ref, from_up, down, down_send, from_up_sem),
        ):
            copy = pltpu.make_async_remote_copy(
                src_ref=src.at[block],
                dst_ref=dst.at[block],
                send_sem=send.at[step - 1],
                recv_sem=recv.at[step - 1],
                device_id=(target, col),
                device_id_type=MESH,
            )
            copy.start()
            pair.append(copy)
        halos.append((block, pair))

    def local_total(index):
        block, pair = halos[index]
        for copy in pair:
            copy.wait_recv()
        return (
            mid_ref[block]
            + from_down[block].astype(jnp.float32)
            + from_up[block].astype(jnp.float32)
        )

    def ring_steps():
        for step in range(1, n_col):
            value = local_total(step - 1)
            if step > 1:
                value = value + ring_in[step - 2]
            ring_out[step - 1] = value
            copy = pltpu.make_async_remote_copy(
                src_ref=ring_out.at[step - 1],
                dst_ref=ring_in.at[step - 1],
                send_sem=ring_send.at[step - 1],
                recv_sem=ring_recv.at[step - 1],
                device_id=(row, succ),
                device_id_type=MESH,
            )
            copy.start()
            yield copy
        o_ref[...] = local_total(n_col - 1) + ring_in[n_col - 2]

    run_together(
        allreduce_steps(n_row, n_col, row, col, parts_ref, sums_ref, part, gath,
                        rsend, rrecv, dsend, drecv, gsend, grecv),
        ring_steps(),
    )
    for _, pair in halos:
        for copy in pair:
            copy.wait_send()


def reduce_spread(mid, up_part, down_part, parts, n_row, n_col):
    _, rows, width = mid.shape
    col_bits = n_col.bit_length() - 1
    row_bits = n_row.bit_length() - 1
    stacked, _ = parts.shape
    return pl.pallas_call(
        functools.partial(spread_kernel, n_row, n_col),
        out_shape=(
            jax.ShapeDtypeStruct((rows, width), jnp.float32),
            jax.ShapeDtypeStruct(parts.shape, jnp.float32),
        ),
        in_specs=[pl.BlockSpec(memory_space=pltpu.VMEM)] * 4,
        out_specs=(pl.BlockSpec(memory_space=pltpu.VMEM),) * 2,
        scratch_shapes=[
            pltpu.VMEM((n_col, rows, width), up_part.dtype),
            pltpu.VMEM((n_col, rows, width), up_part.dtype),
            pltpu.VMEM((n_col - 1, rows, width), jnp.float32),
            pltpu.VMEM((n_col - 1, rows, width), jnp.float32),
            pltpu.SemaphoreType.DMA((n_col,)),
            pltpu.SemaphoreType.DMA((n_col,)),
            pltpu.SemaphoreType.DMA((n_col,)),
            pltpu.SemaphoreType.DMA((n_col,)),
            pltpu.SemaphoreType.DMA((n_col - 1,)),
            pltpu.SemaphoreType.DMA((n_col - 1,)),
            pltpu.VMEM((col_bits + row_bits, stacked // 2, width), jnp.float32),
            pltpu.VMEM((col_bits + 1, stacked, width), jnp.float32),
            pltpu.SemaphoreType.DMA((col_bits,)),
            pltpu.SemaphoreType.DMA((col_bits,)),
            pltpu.SemaphoreType.DMA((row_bits,)),
            pltpu.SemaphoreType.DMA((row_bits,)),
            pltpu.SemaphoreType.DMA((col_bits,)),
            pltpu.SemaphoreType.DMA((col_bits,)),
        ],
        compiler_params=pltpu.CompilerParams(collective_id=2, has_side_effects=True),
    )(mid, up_part, down_part, parts)


def local_kernel(rows_ref, cols_ref, count_ref, window_ref, tiles_ref, feat_ref, w_ref, ws_ref, cot_ref,
                 act_ref, parts_ref, self_ref, mid_ref, up_ref, down_ref, acc, grad_agg, spread):
    tile = tiles_ref.shape[-1]
    nodes = acc.shape[0]
    span = mid_ref.shape[0]
    count = jnp.minimum(count_ref[0], tiles_ref.shape[0])
    acc[...] = jnp.zeros_like(acc)

    def forward(j, carry):
        at = pl.multiple_of(rows_ref[j] * tile, tile)
        acc[pl.ds(at, tile), :] += jnp.dot(
            tiles_ref[j], window_ref[cols_ref[j]], preferred_element_type=jnp.float32
        )
        return carry

    lax.fori_loop(0, count, forward, 0)
    aggregated = acc[...].astype(jnp.bfloat16)
    features = feat_ref[...]
    pre_act = jnp.dot(aggregated, w_ref[...], preferred_element_type=jnp.float32) + jnp.dot(
        features, ws_ref[...], preferred_element_type=jnp.float32
    )
    sigma = jax.nn.sigmoid(pre_act)
    act_ref[...] = (pre_act * sigma).astype(act_ref.dtype)
    grad_pre = (cot_ref[...].astype(jnp.float32) * sigma * (1.0 + pre_act * (1.0 - sigma))).astype(
        jnp.bfloat16
    )
    over_nodes = (((0,), (0,)), ((), ()))
    parts_ref[pl.ds(0, nodes), :] = lax.dot_general(
        aggregated, grad_pre, over_nodes, preferred_element_type=jnp.float32
    )
    parts_ref[pl.ds(nodes, nodes), :] = lax.dot_general(
        features, grad_pre, over_nodes, preferred_element_type=jnp.float32
    )
    by_rows = (((1,), (1,)), ((), ()))
    grad_agg[...] = lax.dot_general(
        grad_pre, w_ref[...], by_rows, preferred_element_type=jnp.float32
    ).astype(jnp.bfloat16)
    self_ref[...] = lax.dot_general(grad_pre, ws_ref[...], by_rows, preferred_element_type=jnp.float32)
    spread[...] = jnp.zeros_like(spread)

    def backward(j, carry):
        at = pl.multiple_of(rows_ref[j] * tile, tile)
        column = cols_ref[j]
        spread[column] += lax.dot_general(
            tiles_ref[j], grad_agg[pl.ds(at, tile), :], over_nodes, preferred_element_type=jnp.float32
        )
        return carry

    lax.fori_loop(0, count, backward, 0)
    mid_ref[...] = spread[pl.ds(span, span)]
    up_ref[...] = spread[pl.ds(2 * span, span)].astype(up_ref.dtype)
    down_ref[...] = spread[pl.ds(0, span)].astype(down_ref.dtype)


def local_math(slot_rows, slot_cols, count, window, tiles, features, weight, weight_self, cotangent):
    nodes, width = features.shape
    span = window.shape[0] // 3
    tile = tiles.shape[-1]
    smem = pl.BlockSpec(memory_space=pltpu.SMEM)
    vmem = pl.BlockSpec(memory_space=pltpu.VMEM)
    return pl.pallas_call(
        local_kernel,
        out_shape=(
            jax.ShapeDtypeStruct((nodes, width), jnp.bfloat16),
            jax.ShapeDtypeStruct((2 * width, width), jnp.float32),
            jax.ShapeDtypeStruct((nodes, width), jnp.float32),
            jax.ShapeDtypeStruct((span, tile, width), jnp.float32),
            jax.ShapeDtypeStruct((span, tile, width), jnp.bfloat16),
            jax.ShapeDtypeStruct((span, tile, width), jnp.bfloat16),
        ),
        in_specs=[smem, smem, smem] + [vmem] * 6,
        out_specs=(vmem,) * 6,
        scratch_shapes=[
            pltpu.VMEM((nodes, width), jnp.float32),
            pltpu.VMEM((nodes, width), jnp.bfloat16),
            pltpu.VMEM((3 * span, tile, width), jnp.float32),
        ],
    )(slot_rows, slot_cols, count, window, tiles, features, weight, weight_self, cotangent)


def shards(features, weight, weight_self, tile_values, tile_rows, tile_cols, tile_count, cotangent):
    tile_block = tile_values[0]
    slot_rows = tile_rows[0]
    slot_cols = tile_cols[0]
    live_count = tile_count[0, 0]
    slot_total = tile_block.shape[0]
    tile_side = tile_block.shape[-1]
    node_rows = features.shape[0]
    width = features.shape[1]
    per_block = node_rows // tile_side
    col_count = lax.axis_size("col")
    row_count = lax.axis_size("row")
    span = col_count * per_block
    window = gather_window(features, row_count, col_count)
    window_tiles = window.reshape(-1, tile_side, width)
    activations, parts, self_feature, mid, up_part, down_part = local_math(
        slot_rows,
        slot_cols,
        tile_count[0],
        window_tiles,
        tile_block,
        features,
        weight,
        weight_self,
        cotangent,
    )
    own_share, summed_parts = reduce_spread(
        mid.reshape(col_count, node_rows, width),
        up_part.reshape(col_count, node_rows, width),
        down_part.reshape(col_count, node_rows, width),
        parts,
        row_count,
        col_count,
    )
    feature_grad = (own_share + self_feature).astype(jnp.bfloat16)
    weight_total, self_total = summed_parts[:width], summed_parts[width:]
    factor = 1.0 / math.sqrt(node_rows * col_count * row_count)
    return (activations, feature_grad, weight_total * factor, self_total * factor)


def solution(mesh):
    placed = (
        P(("row", "col"), None),
        P(),
        P(),
        P("row", "col", None, None),
        P("row", "col"),
        P("row", "col"),
        P("row", "col"),
        P(("row", "col"), None),
    )
    return jax.shard_map(
        shards,
        mesh=mesh,
        in_specs=placed,
        out_specs=(P(("row", "col"), None), P(("row", "col"), None), P(), P()),
        check_vma=False,
    )
```

```python
import functools
import math

import jax
import jax.numpy as jnp
from jax import lax
from jax.experimental import pallas as pl
from jax.experimental.pallas import tpu as pltpu
from jax.sharding import PartitionSpec as P

MESH = pl.DeviceIdType.MESH


def flip(index, stride):
    bit = (index // stride) % 2
    return index + stride - 2 * stride * bit, bit


def allreduce_partners(n_row, n_col, row, col):
    partners = []
    for k in range(n_col.bit_length() - 1):
        partners.append((row, flip(col, 1 << k)[0]))
    for k in range(n_row.bit_length() - 1):
        partners.append((flip(row, 1 << k)[0], col))
    return partners


def allreduce_steps(n_row, n_col, row, col, x_ref, o_ref, part, gath, rsend, rrecv, dsend, drecv, gsend, grecv):
    col_bits = n_col.bit_length() - 1
    row_bits = n_row.bit_length() - 1
    rows = x_ref.shape[0]
    src = x_ref
    base = 0
    size = rows
    for k in range(col_bits):
        other, bit = flip(col, 1 << k)
        half = size // 2
        keep = base + bit * half
        give = base + (1 - bit) * half
        copy = pltpu.make_async_remote_copy(
            src_ref=src.at[pl.ds(pl.multiple_of(give, 8), half)],
            dst_ref=part.at[k, pl.ds(0, half)],
            send_sem=rsend.at[k],
            recv_sem=rrecv.at[k],
            device_id=(row, other),
            device_id_type=MESH,
        )
        copy.start()
        yield copy
        mine = src[pl.ds(pl.multiple_of(keep, 8), half), :] + part[k, pl.ds(0, half), :]
        gath[k, pl.ds(pl.multiple_of(keep, 8), half), :] = mine
        src = gath.at[k]
        base = keep
        size = half
    chunk = size
    total = gath[col_bits - 1, pl.ds(pl.multiple_of(base, 8), chunk), :]
    for k in range(row_bits):
        other, _ = flip(row, 1 << k)
        hold = o_ref.at[pl.ds(0, chunk)]
        hold[...] = total
        copy = pltpu.make_async_remote_copy(
            src_ref=hold,
            dst_ref=part.at[col_bits + k, pl.ds(0, chunk)],
            send_sem=dsend.at[k],
            recv_sem=drecv.at[k],
            device_id=(other, col),
            device_id_type=MESH,
        )
        copy.start()
        yield copy
        total = total + part[col_bits + k, pl.ds(0, chunk), :]
    final = gath.at[col_bits]
    final[pl.ds(pl.multiple_of(base, 8), chunk), :] = total
    size = chunk
    for k in reversed(range(col_bits)):
        other, bit = flip(col, 1 << k)
        start = base - bit * size
        copy = pltpu.make_async_remote_copy(
            src_ref=final.at[pl.ds(pl.multiple_of(base, 8), size)],
            dst_ref=final.at[pl.ds(pl.multiple_of(base, 8), size)],
            send_sem=gsend.at[k],
            recv_sem=grecv.at[k],
            device_id=(row, other),
            device_id_type=MESH,
        )
        copy.start()
        yield copy
        base = start
        size = size * 2
    o_ref[...] = final[...]


def run_together(*chains):
    active = list(chains)
    while active:
        copies, kept = [], []
        for chain in active:
            try:
                copies.append(next(chain))
                kept.append(chain)
            except StopIteration:
                pass
        for copy in copies:
            copy.wait()
        active = kept


def ring_position(col, n):
    core = col % 2
    y = col // 2
    return y + core * (n - 1 - 2 * y)


def ring_col(p, n):
    q = p // (n // 2)
    y = p + q * (n - 1 - 2 * p)
    return 2 * y + q


def gather_kernel(n_row, n_col, x_ref, w_ref, ring_send, ring_recv, halo_send, halo_recv, local_sem):
    row = lax.axis_index("row")
    col = lax.axis_index("col")
    p = ring_position(col, n_col)
    succ = ring_col((p + 1) % n_col, n_col)
    pred = ring_col((p + n_col - 1) % n_col, n_col)
    up = (row + 1) % n_row
    down = (row + n_row - 1) % n_row
    half = max(n_row // 2, 1)
    far = {0: row % half == 0, 2: (row + 1) % half == 0}
    barrier = pltpu.get_barrier_semaphore()
    for device in ((row, succ), (row, pred), (up, col), (down, col)):
        pl.semaphore_signal(barrier, inc=1, device_id=device, device_id_type=MESH)
    pl.semaphore_wait(barrier, 4)
    local = pltpu.make_async_copy(x_ref, w_ref.at[1, col], local_sem.at[0])
    local.start()

    def halo(src, block, index):
        copies = {}
        for target, slot in ((up, 0), (down, 2)):
            copies[slot] = pltpu.make_async_remote_copy(
                src_ref=src,
                dst_ref=w_ref.at[slot, block],
                send_sem=halo_send.at[slot // 2, index],
                recv_sem=halo_recv.at[slot // 2, index],
                device_id=(target, col),
                device_id_type=MESH,
            )
        return copies

    halos = [(col, halo(x_ref, col, 0))]
    for copy in halos[0][1].values():
        copy.start()
    sent = col
    for step in range(1, n_col):
        copies = {}
        for group in (1, 0, 2):
            src = x_ref if (step == 1 and group == 1) else w_ref.at[group, sent]
            copies[group] = pltpu.make_async_remote_copy(
                src_ref=src,
                dst_ref=w_ref.at[group, sent],
                send_sem=ring_send.at[group, step - 1],
                recv_sem=ring_recv.at[group, step - 1],
                device_id=(row, succ),
                device_id_type=MESH,
            )
        copies[1].start()
        for group in (0, 2):
            @pl.when(far[group])
            def _():
                if step == 1:
                    halos[0][1][group].wait_recv()
                copies[group].start()
        copies[1].wait()
        for group in (0, 2):
            @pl.when(far[group])
            def _():
                copies[group].wait()
        sent = ring_col((p - step + n_col) % n_col, n_col)
        forward = halo(w_ref.at[1, sent], sent, step)
        halos.append((sent, forward))
        for slot in (0, 2):
            @pl.when(jnp.logical_not(far[2 - slot]))
            def _():
                forward[slot].start()
    for copy in halos[0][1].values():
        copy.wait_send()
    for slot in (0, 2):
        @pl.when(jnp.logical_not(far[slot]))
        def _():
            halos[0][1][slot].wait_recv()
    for _, copies in halos[1:]:
        for slot in (0, 2):
            @pl.when(jnp.logical_not(far[2 - slot]))
            def _():
                copies[slot].wait_send()

            @pl.when(jnp.logical_not(far[slot]))
            def _():
                copies[slot].wait_recv()
    local.wait()


def gather_window(block, n_row, n_col):
    rows, width = block.shape
    return pl.pallas_call(
        functools.partial(gather_kernel, n_row, n_col),
        out_shape=jax.ShapeDtypeStruct((3, n_col, rows, width), block.dtype),
        in_specs=[pl.BlockSpec(memory_space=pltpu.VMEM)],
        out_specs=pl.BlockSpec(memory_space=pltpu.VMEM),
        scratch_shapes=[
            pltpu.SemaphoreType.DMA((3, n_col - 1)),
            pltpu.SemaphoreType.DMA((3, n_col - 1)),
            pltpu.SemaphoreType.DMA((2, n_col)),
            pltpu.SemaphoreType.DMA((2, n_col)),
            pltpu.SemaphoreType.DMA((1,)),
        ],
        compiler_params=pltpu.CompilerParams(collective_id=1, has_side_effects=True),
    )(block)


def spread_kernel(n_row, n_col, mid_ref, up_ref, down_ref, parts_ref, o_ref, sums_ref, from_down, from_up,
                  ring_in, ring_out, up_send, down_send, from_down_sem, from_up_sem, ring_send, ring_recv,
                  part, gath, rsend, rrecv, dsend, drecv, gsend, grecv):
    row = lax.axis_index("row")
    col = lax.axis_index("col")
    p = ring_position(col, n_col)
    succ = ring_col((p + 1) % n_col, n_col)
    pred = ring_col((p + n_col - 1) % n_col, n_col)
    up = (row + 1) % n_row
    down = (row + n_row - 1) % n_row
    partners = [(row, succ), (row, pred), (up, col), (down, col)]
    partners += allreduce_partners(n_row, n_col, row, col)
    barrier = pltpu.get_barrier_semaphore()
    for device in partners:
        pl.semaphore_signal(barrier, inc=1, device_id=device, device_id_type=MESH)
    pl.semaphore_wait(barrier, len(partners))
    halos = []
    for step in range(1, n_col + 1):
        block = ring_col((p - step + 2 * n_col) % n_col, n_col)
        pair = []
        for src, dst, target, send, recv in (
            (up_ref, from_down, up, up_send, from_down_sem),
            (down_ref, from_up, down, down_send, from_up_sem),
        ):
            copy = pltpu.make_async_remote_copy(
                src_ref=src.at[block],
                dst_ref=dst.at[block],
                send_sem=send.at[step - 1],
                recv_sem=recv.at[step - 1],
                device_id=(target, col),
                device_id_type=MESH,
            )
            copy.start()
            pair.append(copy)
        halos.append((block, pair))

    def local_total(index):
        block, pair = halos[index]
        for copy in pair:
            copy.wait_recv()
        return (
            mid_ref[block]
            + from_down[block].astype(jnp.float32)
            + from_up[block].astype(jnp.float32)
        )

    def ring_steps():
        for step in range(1, n_col):
            value = local_total(step - 1)
            if step > 1:
                value = value + ring_in[step - 2]
            ring_out[step - 1] = value
            copy = pltpu.make_async_remote_copy(
                src_ref=ring_out.at[step - 1],
                dst_ref=ring_in.at[step - 1],
                send_sem=ring_send.at[step - 1],
                recv_sem=ring_recv.at[step - 1],
                device_id=(row, succ),
                device_id_type=MESH,
            )
            copy.start()
            yield copy
        o_ref[...] = local_total(n_col - 1) + ring_in[n_col - 2]

    run_together(
        allreduce_steps(n_row, n_col, row, col, parts_ref, sums_ref, part, gath,
                        rsend, rrecv, dsend, drecv, gsend, grecv),
        ring_steps(),
    )
    for _, pair in halos:
        for copy in pair:
            copy.wait_send()


def reduce_spread(mid, up_part, down_part, parts, n_row, n_col):
    _, rows, width = mid.shape
    col_bits = n_col.bit_length() - 1
    row_bits = n_row.bit_length() - 1
    stacked, _ = parts.shape
    return pl.pallas_call(
        functools.partial(spread_kernel, n_row, n_col),
        out_shape=(
            jax.ShapeDtypeStruct((rows, width), jnp.float32),
            jax.ShapeDtypeStruct(parts.shape, jnp.float32),
        ),
        in_specs=[pl.BlockSpec(memory_space=pltpu.VMEM)] * 4,
        out_specs=(pl.BlockSpec(memory_space=pltpu.VMEM),) * 2,
        scratch_shapes=[
            pltpu.VMEM((n_col, rows, width), up_part.dtype),
            pltpu.VMEM((n_col, rows, width), up_part.dtype),
            pltpu.VMEM((n_col - 1, rows, width), jnp.float32),
            pltpu.VMEM((n_col - 1, rows, width), jnp.float32),
            pltpu.SemaphoreType.DMA((n_col,)),
            pltpu.SemaphoreType.DMA((n_col,)),
            pltpu.SemaphoreType.DMA((n_col,)),
            pltpu.SemaphoreType.DMA((n_col,)),
            pltpu.SemaphoreType.DMA((n_col - 1,)),
            pltpu.SemaphoreType.DMA((n_col - 1,)),
            pltpu.VMEM((col_bits + row_bits, stacked // 2, width), jnp.float32),
            pltpu.VMEM((col_bits + 1, stacked, width), jnp.float32),
            pltpu.SemaphoreType.DMA((col_bits,)),
            pltpu.SemaphoreType.DMA((col_bits,)),
            pltpu.SemaphoreType.DMA((row_bits,)),
            pltpu.SemaphoreType.DMA((row_bits,)),
            pltpu.SemaphoreType.DMA((col_bits,)),
            pltpu.SemaphoreType.DMA((col_bits,)),
        ],
        compiler_params=pltpu.CompilerParams(collective_id=2, has_side_effects=True),
    )(mid, up_part, down_part, parts)


def local_kernel(rows_ref, cols_ref, count_ref, window_ref, tiles_ref, feat_ref, w_ref, ws_ref, cot_ref,
                 act_ref, parts_ref, self_ref, mid_ref, up_ref, down_ref, acc, grad_agg, spread):
    tile = tiles_ref.shape[-1]
    nodes = acc.shape[0]
    span = mid_ref.shape[0]
    count = jnp.minimum(count_ref[0], tiles_ref.shape[0])
    acc[...] = jnp.zeros_like(acc)

    def forward(j, carry):
        at = pl.multiple_of(rows_ref[j] * tile, tile)
        acc[pl.ds(at, tile), :] += jnp.dot(
            tiles_ref[j], window_ref[cols_ref[j]], preferred_element_type=jnp.float32
        )
        return carry

    lax.fori_loop(0, count, forward, 0)
    aggregated = acc[...].astype(jnp.bfloat16)
    features = feat_ref[...]
    pre_act = jnp.dot(aggregated, w_ref[...], preferred_element_type=jnp.float32) + jnp.dot(
        features, ws_ref[...], preferred_element_type=jnp.float32
    )
    sigma = jax.nn.sigmoid(pre_act)
    act_ref[...] = (pre_act * sigma).astype(act_ref.dtype)
    grad_pre = (cot_ref[...].astype(jnp.float32) * sigma * (1.0 + pre_act * (1.0 - sigma))).astype(
        jnp.bfloat16
    )
    over_nodes = (((0,), (0,)), ((), ()))
    parts_ref[pl.ds(0, nodes), :] = lax.dot_general(
        aggregated, grad_pre, over_nodes, preferred_element_type=jnp.float32
    )
    parts_ref[pl.ds(nodes, nodes), :] = lax.dot_general(
        features, grad_pre, over_nodes, preferred_element_type=jnp.float32
    )
    by_rows = (((1,), (1,)), ((), ()))
    grad_agg[...] = lax.dot_general(
        grad_pre, w_ref[...], by_rows, preferred_element_type=jnp.float32
    ).astype(jnp.bfloat16)
    self_ref[...] = lax.dot_general(grad_pre, ws_ref[...], by_rows, preferred_element_type=jnp.float32)
    spread[...] = jnp.zeros_like(spread)

    def backward(j, carry):
        at = pl.multiple_of(rows_ref[j] * tile, tile)
        column = cols_ref[j]
        spread[column] += lax.dot_general(
            tiles_ref[j], grad_agg[pl.ds(at, tile), :], over_nodes, preferred_element_type=jnp.float32
        )
        return carry

    lax.fori_loop(0, count, backward, 0)
    mid_ref[...] = spread[pl.ds(span, span)]
    up_ref[...] = spread[pl.ds(2 * span, span)].astype(up_ref.dtype)
    down_ref[...] = spread[pl.ds(0, span)].astype(down_ref.dtype)


def local_math(slot_rows, slot_cols, count, window, tiles, features, weight, weight_self, cotangent):
    nodes, width = features.shape
    span = window.shape[0] // 3
    tile = tiles.shape[-1]
    smem = pl.BlockSpec(memory_space=pltpu.SMEM)
    vmem = pl.BlockSpec(memory_space=pltpu.VMEM)
    return pl.pallas_call(
        local_kernel,
        out_shape=(
            jax.ShapeDtypeStruct((nodes, width), jnp.bfloat16),
            jax.ShapeDtypeStruct((2 * width, width), jnp.float32),
            jax.ShapeDtypeStruct((nodes, width), jnp.float32),
            jax.ShapeDtypeStruct((span, tile, width), jnp.float32),
            jax.ShapeDtypeStruct((span, tile, width), jnp.bfloat16),
            jax.ShapeDtypeStruct((span, tile, width), jnp.bfloat16),
        ),
        in_specs=[smem, smem, smem] + [vmem] * 6,
        out_specs=(vmem,) * 6,
        scratch_shapes=[
            pltpu.VMEM((nodes, width), jnp.float32),
            pltpu.VMEM((nodes, width), jnp.bfloat16),
            pltpu.VMEM((3 * span, tile, width), jnp.float32),
        ],
    )(slot_rows, slot_cols, count, window, tiles, features, weight, weight_self, cotangent)


def shards(features, weight, weight_self, tile_values, tile_rows, tile_cols, tile_count, cotangent):
    tile_block = tile_values[0]
    slot_rows = tile_rows[0]
    slot_cols = tile_cols[0]
    live_count = tile_count[0, 0]
    slot_total = tile_block.shape[0]
    tile_side = tile_block.shape[-1]
    node_rows = features.shape[0]
    width = features.shape[1]
    per_block = node_rows // tile_side
    col_count = lax.axis_size("col")
    row_count = lax.axis_size("row")
    span = col_count * per_block
    window = gather_window(features, row_count, col_count)
    window_tiles = window.reshape(-1, tile_side, width)
    activations, parts, self_feature, mid, up_part, down_part = local_math(
        slot_rows,
        slot_cols,
        tile_count[0],
        window_tiles,
        tile_block,
        features,
        weight,
        weight_self,
        cotangent,
    )
    own_share, summed_parts = reduce_spread(
        mid.reshape(col_count, node_rows, width),
        up_part.reshape(col_count, node_rows, width),
        down_part.reshape(col_count, node_rows, width),
        parts,
        row_count,
        col_count,
    )
    feature_grad = (own_share + self_feature).astype(jnp.bfloat16)
    weight_total, self_total = summed_parts[:width], summed_parts[width:]
    factor = 1.0 / math.sqrt(node_rows * col_count * row_count)
    return (activations, feature_grad, weight_total * factor, self_total * factor)


def solution(mesh):
    placed = (
        P(("row", "col"), None),
        P(),
        P(),
        P("row", "col", None, None),
        P("row", "col"),
        P("row", "col"),
        P("row", "col"),
        P(("row", "col"), None),
    )
    return jax.shard_map(
        shards,
        mesh=mesh,
        in_specs=placed,
        out_specs=(P(("row", "col"), None), P(("row", "col"), None), P(), P()),
        check_vma=False,
    )
```

```python
import functools
import math

import jax
import jax.numpy as jnp
from jax import lax
from jax.experimental import pallas as pl
from jax.experimental.pallas import tpu as pltpu
from jax.sharding import PartitionSpec as P

MESH = pl.DeviceIdType.MESH


def flip(index, stride):
    bit = (index // stride) % 2
    return index + stride - 2 * stride * bit, bit


def allreduce_partners(n_row, n_col, row, col):
    partners = []
    for k in range(n_col.bit_length() - 1):
        partners.append((row, flip(col, 1 << k)[0]))
    for k in range(n_row.bit_length() - 1):
        partners.append((flip(row, 1 << k)[0], col))
    return partners


def allreduce_steps(n_row, n_col, row, col, x_ref, o_ref, part, gath, rsend, rrecv, dsend, drecv, gsend, grecv):
    col_bits = n_col.bit_length() - 1
    row_bits = n_row.bit_length() - 1
    rows = x_ref.shape[0]
    src = x_ref
    base = 0
    size = rows
    for k in range(col_bits):
        other, bit = flip(col, 1 << k)
        half = size // 2
        keep = base + bit * half
        give = base + (1 - bit) * half
        copy = pltpu.make_async_remote_copy(
            src_ref=src.at[pl.ds(pl.multiple_of(give, 8), half)],
            dst_ref=part.at[k, pl.ds(0, half)],
            send_sem=rsend.at[k],
            recv_sem=rrecv.at[k],
            device_id=(row, other),
            device_id_type=MESH,
        )
        copy.start()
        yield copy
        mine = src[pl.ds(pl.multiple_of(keep, 8), half), :] + part[k, pl.ds(0, half), :]
        gath[k, pl.ds(pl.multiple_of(keep, 8), half), :] = mine
        src = gath.at[k]
        base = keep
        size = half
    chunk = size
    total = gath[col_bits - 1, pl.ds(pl.multiple_of(base, 8), chunk), :]
    for k in range(row_bits):
        other, _ = flip(row, 1 << k)
        hold = o_ref.at[pl.ds(0, chunk)]
        hold[...] = total
        copy = pltpu.make_async_remote_copy(
            src_ref=hold,
            dst_ref=part.at[col_bits + k, pl.ds(0, chunk)],
            send_sem=dsend.at[k],
            recv_sem=drecv.at[k],
            device_id=(other, col),
            device_id_type=MESH,
        )
        copy.start()
        yield copy
        total = total + part[col_bits + k, pl.ds(0, chunk), :]
    final = gath.at[col_bits]
    final[pl.ds(pl.multiple_of(base, 8), chunk), :] = total
    size = chunk
    for k in reversed(range(col_bits)):
        other, bit = flip(col, 1 << k)
        start = base - bit * size
        copy = pltpu.make_async_remote_copy(
            src_ref=final.at[pl.ds(pl.multiple_of(base, 8), size)],
            dst_ref=final.at[pl.ds(pl.multiple_of(base, 8), size)],
            send_sem=gsend.at[k],
            recv_sem=grecv.at[k],
            device_id=(row, other),
            device_id_type=MESH,
        )
        copy.start()
        yield copy
        base = start
        size = size * 2
    o_ref[...] = final[...]


def run_together(*chains):
    active = list(chains)
    while active:
        copies, kept = [], []
        for chain in active:
            try:
                copies.append(next(chain))
                kept.append(chain)
            except StopIteration:
                pass
        for copy in copies:
            copy.wait()
        active = kept


def ring_position(col, n):
    core = col % 2
    y = col // 2
    return y + core * (n - 1 - 2 * y)


def ring_col(p, n):
    q = p // (n // 2)
    y = p + q * (n - 1 - 2 * p)
    return 2 * y + q


def gather_kernel(n_row, n_col, x_ref, w_ref, ring_send, ring_recv, halo_send, halo_recv, local_sem):
    row = lax.axis_index("row")
    col = lax.axis_index("col")
    p = ring_position(col, n_col)
    succ = ring_col((p + 1) % n_col, n_col)
    pred = ring_col((p + n_col - 1) % n_col, n_col)
    up = (row + 1) % n_row
    down = (row + n_row - 1) % n_row
    half = max(n_row // 2, 1)
    far = {0: row % half == 0, 2: (row + 1) % half == 0}
    barrier = pltpu.get_barrier_semaphore()
    for device in ((row, succ), (row, pred), (up, col), (down, col)):
        pl.semaphore_signal(barrier, inc=1, device_id=device, device_id_type=MESH)
    pl.semaphore_wait(barrier, 4)
    local = pltpu.make_async_copy(x_ref, w_ref.at[1, col], local_sem.at[0])
    local.start()

    def halo(src, block, index):
        copies = {}
        for target, slot in ((up, 0), (down, 2)):
            copies[slot] = pltpu.make_async_remote_copy(
                src_ref=src,
                dst_ref=w_ref.at[slot, block],
                send_sem=halo_send.at[slot // 2, index],
                recv_sem=halo_recv.at[slot // 2, index],
                device_id=(target, col),
                device_id_type=MESH,
            )
        return copies

    halos = [(col, halo(x_ref, col, 0))]
    for copy in halos[0][1].values():
        copy.start()
    sent = col
    for step in range(1, n_col):
        copies = {}
        for group in (1, 0, 2):
            src = x_ref if (step == 1 and group == 1) else w_ref.at[group, sent]
            copies[group] = pltpu.make_async_remote_copy(
                src_ref=src,
                dst_ref=w_ref.at[group, sent],
                send_sem=ring_send.at[group, step - 1],
                recv_sem=ring_recv.at[group, step - 1],
                device_id=(row, succ),
                device_id_type=MESH,
            )
        copies[1].start()
        for group in (0, 2):
            @pl.when(far[group])
            def _():
                if step == 1:
                    halos[0][1][group].wait_recv()
                copies[group].start()
        copies[1].wait()
        for group in (0, 2):
            @pl.when(far[group])
            def _():
                copies[group].wait()
        sent = ring_col((p - step + n_col) % n_col, n_col)
        forward = halo(w_ref.at[1, sent], sent, step)
        halos.append((sent, forward))
        for slot in (0, 2):
            @pl.when(jnp.logical_not(far[2 - slot]))
            def _():
                forward[slot].start()
    for copy in halos[0][1].values():
        copy.wait_send()
    for slot in (0, 2):
        @pl.when(jnp.logical_not(far[slot]))
        def _():
            halos[0][1][slot].wait_recv()
    for _, copies in halos[1:]:
        for slot in (0, 2):
            @pl.when(jnp.logical_not(far[2 - slot]))
            def _():
                copies[slot].wait_send()

            @pl.when(jnp.logical_not(far[slot]))
            def _():
                copies[slot].wait_recv()
    local.wait()


def gather_window(block, n_row, n_col):
    rows, width = block.shape
    return pl.pallas_call(
        functools.partial(gather_kernel, n_row, n_col),
        out_shape=jax.ShapeDtypeStruct((3, n_col, rows, width), block.dtype),
        in_specs=[pl.BlockSpec(memory_space=pltpu.VMEM)],
        out_specs=pl.BlockSpec(memory_space=pltpu.VMEM),
        scratch_shapes=[
            pltpu.SemaphoreType.DMA((3, n_col - 1)),
            pltpu.SemaphoreType.DMA((3, n_col - 1)),
            pltpu.SemaphoreType.DMA((2, n_col)),
            pltpu.SemaphoreType.DMA((2, n_col)),
            pltpu.SemaphoreType.DMA((1,)),
        ],
        compiler_params=pltpu.CompilerParams(collective_id=1, has_side_effects=True),
    )(block)


class Gated:
    def __init__(self, copy, cond):
        self.copy = copy
        self.cond = cond

    def wait(self):
        pl.when(self.cond)(self.copy.wait)


def spread_kernel(n_row, n_col, mid_ref, up_ref, down_ref, parts_ref, o_ref, sums_ref, up_bf, down_bf,
                  from_down, from_up, ring_in, ring_out, far_in, far_out, far_from, up_send, down_send,
                  from_down_sem, from_up_sem, ring_send, ring_recv, far_send, far_recv, last_send, last_recv,
                  part, gath, rsend, rrecv, dsend, drecv, gsend, grecv):
    row = lax.axis_index("row")
    col = lax.axis_index("col")
    p = ring_position(col, n_col)
    succ = ring_col((p + 1) % n_col, n_col)
    pred = ring_col((p + n_col - 1) % n_col, n_col)
    up = (row + 1) % n_row
    down = (row + n_row - 1) % n_row
    half = max(n_row // 2, 1)
    far_down = row % half == 0
    far_up = (row + 1) % half == 0
    partners = [(row, succ), (row, pred), (up, col), (down, col)]
    partners += allreduce_partners(n_row, n_col, row, col)
    barrier = pltpu.get_barrier_semaphore()
    for device in partners:
        pl.semaphore_signal(barrier, inc=1, device_id=device, device_id_type=MESH)
    pl.semaphore_wait(barrier, len(partners))
    up_bf[...] = up_ref[...].astype(up_bf.dtype)
    down_bf[...] = down_ref[...].astype(down_bf.dtype)
    halos = []
    for step in range(1, n_col + 1):
        block = ring_col((p - step + 2 * n_col) % n_col, n_col)
        pair = []
        for src, dst, target, send, recv, far in (
            (up_bf, from_down, up, up_send, from_down_sem, far_up),
            (down_bf, from_up, down, down_send, from_up_sem, far_down),
        ):
            copy = pltpu.make_async_remote_copy(
                src_ref=src.at[block],
                dst_ref=dst.at[block],
                send_sem=send.at[step - 1],
                recv_sem=recv.at[step - 1],
                device_id=(target, col),
                device_id_type=MESH,
            )
            pl.when(jnp.logical_not(far))(copy.start)
            pair.append(copy)
        halos.append((block, pair))

    def local_total(index):
        block, (from_below, from_above) = halos[index]
        pl.when(jnp.logical_not(far_down))(from_below.wait_recv)
        pl.when(jnp.logical_not(far_up))(from_above.wait_recv)
        zero = jnp.zeros(mid_ref.shape[1:], jnp.float32)
        return (
            mid_ref[block]
            + jnp.where(far_down, zero, from_down[block].astype(jnp.float32))
            + jnp.where(far_up, zero, from_up[block].astype(jnp.float32))
        )

    def ring_steps():
        for step in range(1, n_col):
            value = local_total(step - 1)
            if step > 1:
                value = value + ring_in[step - 2]
            ring_out[step - 1] = value
            copy = pltpu.make_async_remote_copy(
                src_ref=ring_out.at[step - 1],
                dst_ref=ring_in.at[step - 1],
                send_sem=ring_send.at[step - 1],
                recv_sem=ring_recv.at[step - 1],
                device_id=(row, succ),
                device_id_type=MESH,
            )
            copy.start()
            yield copy
        o_ref[...] = local_total(n_col - 1) + ring_in[n_col - 2]

    def far_steps(side, part_ref, far):
        for step in range(1, n_col):
            block = ring_col((p - step + 2 * n_col) % n_col, n_col)
            copy = pltpu.make_async_remote_copy(
                src_ref=far_out.at[side, step - 1],
                dst_ref=far_in.at[side, step - 1],
                send_sem=far_send.at[side, step - 1],
                recv_sem=far_recv.at[side, step - 1],
                device_id=(row, succ),
                device_id_type=MESH,
            )

            def send(step=step, block=block, copy=copy):
                value = part_ref[block]
                if step > 1:
                    value = value + far_in[side, step - 2]
                far_out[side, step - 1] = value
                copy.start()

            pl.when(far)(send)
            yield Gated(copy, far)

        def finish():
            far_out[side, n_col - 1] = part_ref[col] + far_in[side, n_col - 2]

        pl.when(far)(finish)

    run_together(
        allreduce_steps(n_row, n_col, row, col, parts_ref, sums_ref, part, gath,
                        rsend, rrecv, dsend, drecv, gsend, grecv),
        ring_steps(),
        far_steps(0, up_ref, far_up),
        far_steps(1, down_ref, far_down),
    )
    lasts = []
    for side, target, slot, far in ((0, up, 0, far_up), (1, down, 1, far_down)):
        copy = pltpu.make_async_remote_copy(
            src_ref=far_out.at[side, n_col - 1],
            dst_ref=far_from.at[slot],
            send_sem=last_send.at[side],
            recv_sem=last_recv.at[slot],
            device_id=(target, col),
            device_id_type=MESH,
        )
        pl.when(far)(copy.start)
        lasts.append(copy)
    pl.when(far_up)(lasts[0].wait_send)
    pl.when(far_down)(lasts[1].wait_send)
    pl.when(far_down)(lasts[0].wait_recv)
    pl.when(far_up)(lasts[1].wait_recv)
    zero = jnp.zeros(o_ref.shape, jnp.float32)
    o_ref[...] = (
        o_ref[...]
        + jnp.where(far_down, far_from[0], zero)
        + jnp.where(far_up, far_from[1], zero)
    )
    for _, (to_up, to_down) in halos:
        pl.when(jnp.logical_not(far_up))(to_up.wait_send)
        pl.when(jnp.logical_not(far_down))(to_down.wait_send)


def reduce_spread(mid, up_part, down_part, parts, n_row, n_col):
    _, rows, width = mid.shape
    col_bits = n_col.bit_length() - 1
    row_bits = n_row.bit_length() - 1
    stacked, _ = parts.shape
    return pl.pallas_call(
        functools.partial(spread_kernel, n_row, n_col),
        out_shape=(
            jax.ShapeDtypeStruct((rows, width), jnp.float32),
            jax.ShapeDtypeStruct(parts.shape, jnp.float32),
        ),
        in_specs=[pl.BlockSpec(memory_space=pltpu.VMEM)] * 4,
        out_specs=(pl.BlockSpec(memory_space=pltpu.VMEM),) * 2,
        scratch_shapes=[
            pltpu.VMEM((n_col, rows, width), jnp.bfloat16),
            pltpu.VMEM((n_col, rows, width), jnp.bfloat16),
            pltpu.VMEM((n_col, rows, width), jnp.bfloat16),
            pltpu.VMEM((n_col, rows, width), jnp.bfloat16),
            pltpu.VMEM((n_col - 1, rows, width), jnp.float32),
            pltpu.VMEM((n_col - 1, rows, width), jnp.float32),
            pltpu.VMEM((2, n_col - 1, rows, width), jnp.float32),
            pltpu.VMEM((2, n_col, rows, width), jnp.float32),
            pltpu.VMEM((2, rows, width), jnp.float32),
            pltpu.SemaphoreType.DMA((n_col,)),
            pltpu.SemaphoreType.DMA((n_col,)),
            pltpu.SemaphoreType.DMA((n_col,)),
            pltpu.SemaphoreType.DMA((n_col,)),
            pltpu.SemaphoreType.DMA((n_col - 1,)),
            pltpu.SemaphoreType.DMA((n_col - 1,)),
            pltpu.SemaphoreType.DMA((2, n_col - 1)),
            pltpu.SemaphoreType.DMA((2, n_col - 1)),
            pltpu.SemaphoreType.DMA((2,)),
            pltpu.SemaphoreType.DMA((2,)),
            pltpu.VMEM((col_bits + row_bits, stacked // 2, width), jnp.float32),
            pltpu.VMEM((col_bits + 1, stacked, width), jnp.float32),
            pltpu.SemaphoreType.DMA((col_bits,)),
            pltpu.SemaphoreType.DMA((col_bits,)),
            pltpu.SemaphoreType.DMA((row_bits,)),
            pltpu.SemaphoreType.DMA((row_bits,)),
            pltpu.SemaphoreType.DMA((col_bits,)),
            pltpu.SemaphoreType.DMA((col_bits,)),
        ],
        compiler_params=pltpu.CompilerParams(collective_id=2, has_side_effects=True),
    )(mid, up_part, down_part, parts)


def local_kernel(rows_ref, cols_ref, count_ref, window_ref, tiles_ref, feat_ref, w_ref, ws_ref, cot_ref,
                 act_ref, parts_ref, self_ref, mid_ref, up_ref, down_ref, acc, grad_agg, spread):
    tile = tiles_ref.shape[-1]
    nodes = acc.shape[0]
    span = mid_ref.shape[0]
    count = jnp.minimum(count_ref[0], tiles_ref.shape[0])
    acc[...] = jnp.zeros_like(acc)

    def forward(j, carry):
        at = pl.multiple_of(rows_ref[j] * tile, tile)
        acc[pl.ds(at, tile), :] += jnp.dot(
            tiles_ref[j], window_ref[cols_ref[j]], preferred_element_type=jnp.float32
        )
        return carry

    lax.fori_loop(0, count, forward, 0)
    aggregated = acc[...].astype(jnp.bfloat16)
    features = feat_ref[...]
    pre_act = jnp.dot(aggregated, w_ref[...], preferred_element_type=jnp.float32) + jnp.dot(
        features, ws_ref[...], preferred_element_type=jnp.float32
    )
    sigma = jax.nn.sigmoid(pre_act)
    act_ref[...] = (pre_act * sigma).astype(act_ref.dtype)
    grad_pre = (cot_ref[...].astype(jnp.float32) * sigma * (1.0 + pre_act * (1.0 - sigma))).astype(
        jnp.bfloat16
    )
    over_nodes = (((0,), (0,)), ((), ()))
    parts_ref[pl.ds(0, nodes), :] = lax.dot_general(
        aggregated, grad_pre, over_nodes, preferred_element_type=jnp.float32
    )
    parts_ref[pl.ds(nodes, nodes), :] = lax.dot_general(
        features, grad_pre, over_nodes, preferred_element_type=jnp.float32
    )
    by_rows = (((1,), (1,)), ((), ()))
    grad_agg[...] = lax.dot_general(
        grad_pre, w_ref[...], by_rows, preferred_element_type=jnp.float32
    ).astype(jnp.bfloat16)
    self_ref[...] = lax.dot_general(grad_pre, ws_ref[...], by_rows, preferred_element_type=jnp.float32)
    spread[...] = jnp.zeros_like(spread)

    def backward(j, carry):
        at = pl.multiple_of(rows_ref[j] * tile, tile)
        column = cols_ref[j]
        spread[column] += lax.dot_general(
            tiles_ref[j], grad_agg[pl.ds(at, tile), :], over_nodes, preferred_element_type=jnp.float32
        )
        return carry

    lax.fori_loop(0, count, backward, 0)
    mid_ref[...] = spread[pl.ds(span, span)]
    up_ref[...] = spread[pl.ds(2 * span, span)].astype(up_ref.dtype)
    down_ref[...] = spread[pl.ds(0, span)].astype(down_ref.dtype)


def local_math(slot_rows, slot_cols, count, window, tiles, features, weight, weight_self, cotangent):
    nodes, width = features.shape
    span = window.shape[0] // 3
    tile = tiles.shape[-1]
    smem = pl.BlockSpec(memory_space=pltpu.SMEM)
    vmem = pl.BlockSpec(memory_space=pltpu.VMEM)
    return pl.pallas_call(
        local_kernel,
        out_shape=(
            jax.ShapeDtypeStruct((nodes, width), jnp.bfloat16),
            jax.ShapeDtypeStruct((2 * width, width), jnp.float32),
            jax.ShapeDtypeStruct((nodes, width), jnp.float32),
            jax.ShapeDtypeStruct((span, tile, width), jnp.float32),
            jax.ShapeDtypeStruct((span, tile, width), jnp.float32),
            jax.ShapeDtypeStruct((span, tile, width), jnp.float32),
        ),
        in_specs=[smem, smem, smem] + [vmem] * 6,
        out_specs=(vmem,) * 6,
        scratch_shapes=[
            pltpu.VMEM((nodes, width), jnp.float32),
            pltpu.VMEM((nodes, width), jnp.bfloat16),
            pltpu.VMEM((3 * span, tile, width), jnp.float32),
        ],
    )(slot_rows, slot_cols, count, window, tiles, features, weight, weight_self, cotangent)


def shards(features, weight, weight_self, tile_values, tile_rows, tile_cols, tile_count, cotangent):
    tile_block = tile_values[0]
    slot_rows = tile_rows[0]
    slot_cols = tile_cols[0]
    live_count = tile_count[0, 0]
    slot_total = tile_block.shape[0]
    tile_side = tile_block.shape[-1]
    node_rows = features.shape[0]
    width = features.shape[1]
    per_block = node_rows // tile_side
    col_count = lax.axis_size("col")
    row_count = lax.axis_size("row")
    span = col_count * per_block
    window = gather_window(features, row_count, col_count)
    window_tiles = window.reshape(-1, tile_side, width)
    activations, parts, self_feature, mid, up_part, down_part = local_math(
        slot_rows,
        slot_cols,
        tile_count[0],
        window_tiles,
        tile_block,
        features,
        weight,
        weight_self,
        cotangent,
    )
    own_share, summed_parts = reduce_spread(
        mid.reshape(col_count, node_rows, width),
        up_part.reshape(col_count, node_rows, width),
        down_part.reshape(col_count, node_rows, width),
        parts,
        row_count,
        col_count,
    )
    feature_grad = (own_share + self_feature).astype(jnp.bfloat16)
    weight_total, self_total = summed_parts[:width], summed_parts[width:]
    factor = 1.0 / math.sqrt(node_rows * col_count * row_count)
    return (activations, feature_grad, weight_total * factor, self_total * factor)


def solution(mesh):
    placed = (
        P(("row", "col"), None),
        P(),
        P(),
        P("row", "col", None, None),
        P("row", "col"),
        P("row", "col"),
        P("row", "col"),
        P(("row", "col"), None),
    )
    return jax.shard_map(
        shards,
        mesh=mesh,
        in_specs=placed,
        out_specs=(P(("row", "col"), None), P(("row", "col"), None), P(), P()),
        check_vma=False,
    )
```

```python
import functools
import math

import jax
import jax.numpy as jnp
from jax import lax
from jax.experimental import pallas as pl
from jax.experimental.pallas import tpu as pltpu
from jax.sharding import PartitionSpec as P

MESH = pl.DeviceIdType.MESH


def flip(index, stride):
    bit = (index // stride) % 2
    return index + stride - 2 * stride * bit, bit


def allreduce_partners(n_row, n_col, row, col):
    partners = [(row, peer) for peer in range(n_col)]
    for k in range(n_row.bit_length() - 1):
        partners.append((flip(row, 1 << k)[0], col))
    return partners


class Group:
    def __init__(self, copies, receipts, col):
        self.copies = copies
        self.receipts = receipts
        self.col = col

    def wait(self):
        for peer, (copy, receipt) in enumerate(zip(self.copies, self.receipts)):
            @pl.when(peer != self.col)
            def _():
                copy.wait_send()
                receipt.wait_recv()


def allreduce_steps(n_row, n_col, row, col, x_ref, o_ref, part, gath, rsend, rrecv, dsend, drecv, gsend, grecv):
    row_bits = n_row.bit_length() - 1
    chunk = x_ref.shape[0] // n_col
    mine = pl.ds(pl.multiple_of(col * chunk, 8), chunk)
    copies, receipts = [], []
    for peer in range(n_col):
        copies.append(pltpu.make_async_remote_copy(
            src_ref=x_ref.at[pl.ds(peer * chunk, chunk)],
            dst_ref=gath.at[0, col],
            send_sem=rsend.at[peer],
            recv_sem=rrecv.at[col],
            device_id=(row, peer),
            device_id_type=MESH,
        ))
        receipts.append(pltpu.make_async_remote_copy(
            src_ref=x_ref.at[pl.ds(peer * chunk, chunk)],
            dst_ref=gath.at[0, peer],
            send_sem=rsend.at[peer],
            recv_sem=rrecv.at[peer],
            device_id=(row, peer),
            device_id_type=MESH,
        ))
        pl.when(peer != col)(copies[-1].start)
    yield Group(copies, receipts, col)
    total = x_ref[mine, :]
    for peer in range(n_col):
        total = total + jnp.where(peer == col, jnp.zeros_like(total), gath[0, peer])
    for k in range(row_bits):
        other, _ = flip(row, 1 << k)
        hold = part.at[2 * k]
        hold[...] = total
        copy = pltpu.make_async_remote_copy(
            src_ref=hold,
            dst_ref=part.at[2 * k + 1],
            send_sem=dsend.at[k],
            recv_sem=drecv.at[k],
            device_id=(other, col),
            device_id_type=MESH,
        )
        copy.start()
        yield copy
        total = total + part[2 * k + 1]
    o_ref[mine, :] = total
    copies, receipts = [], []
    for peer in range(n_col):
        copies.append(pltpu.make_async_remote_copy(
            src_ref=o_ref.at[mine],
            dst_ref=o_ref.at[mine],
            send_sem=gsend.at[peer],
            recv_sem=grecv.at[col],
            device_id=(row, peer),
            device_id_type=MESH,
        ))
        receipts.append(pltpu.make_async_remote_copy(
            src_ref=o_ref.at[mine],
            dst_ref=o_ref.at[pl.ds(peer * chunk, chunk)],
            send_sem=gsend.at[peer],
            recv_sem=grecv.at[peer],
            device_id=(row, peer),
            device_id_type=MESH,
        ))
        pl.when(peer != col)(copies[-1].start)
    yield Group(copies, receipts, col)


def run_together(*chains):
    active = list(chains)
    while active:
        copies, kept = [], []
        for chain in active:
            try:
                copies.append(next(chain))
                kept.append(chain)
            except StopIteration:
                pass
        for copy in copies:
            copy.wait()
        active = kept


def ring_position(col, n):
    core = col % 2
    y = col // 2
    return y + core * (n - 1 - 2 * y)


def ring_col(p, n):
    q = p // (n // 2)
    y = p + q * (n - 1 - 2 * p)
    return 2 * y + q


def gather_kernel(n_row, n_col, x_ref, w_ref, ring_send, ring_recv, halo_send, halo_recv, local_sem):
    row = lax.axis_index("row")
    col = lax.axis_index("col")
    p = ring_position(col, n_col)
    succ = ring_col((p + 1) % n_col, n_col)
    pred = ring_col((p + n_col - 1) % n_col, n_col)
    up = (row + 1) % n_row
    down = (row + n_row - 1) % n_row
    half = max(n_row // 2, 1)
    far = {0: row % half == 0, 2: (row + 1) % half == 0}
    barrier = pltpu.get_barrier_semaphore()
    for device in ((row, succ), (row, pred), (up, col), (down, col)):
        pl.semaphore_signal(barrier, inc=1, device_id=device, device_id_type=MESH)
    pl.semaphore_wait(barrier, 4)
    local = pltpu.make_async_copy(x_ref, w_ref.at[1, col], local_sem.at[0])
    local.start()

    def halo(src, block, index):
        copies = {}
        for target, slot in ((up, 0), (down, 2)):
            copies[slot] = pltpu.make_async_remote_copy(
                src_ref=src,
                dst_ref=w_ref.at[slot, block],
                send_sem=halo_send.at[slot // 2, index],
                recv_sem=halo_recv.at[slot // 2, index],
                device_id=(target, col),
                device_id_type=MESH,
            )
        return copies

    halos = [(col, halo(x_ref, col, 0))]
    for copy in halos[0][1].values():
        copy.start()
    sent = col
    for step in range(1, n_col):
        copies = {}
        for group in (1, 0, 2):
            src = x_ref if (step == 1 and group == 1) else w_ref.at[group, sent]
            copies[group] = pltpu.make_async_remote_copy(
                src_ref=src,
                dst_ref=w_ref.at[group, sent],
                send_sem=ring_send.at[group, step - 1],
                recv_sem=ring_recv.at[group, step - 1],
                device_id=(row, succ),
                device_id_type=MESH,
            )
        copies[1].start()
        for group in (0, 2):
            @pl.when(far[group])
            def _():
                if step == 1:
                    halos[0][1][group].wait_recv()
                copies[group].start()
        copies[1].wait()
        for group in (0, 2):
            @pl.when(far[group])
            def _():
                copies[group].wait()
        sent = ring_col((p - step + n_col) % n_col, n_col)
        forward = halo(w_ref.at[1, sent], sent, step)
        halos.append((sent, forward))
        for slot in (0, 2):
            @pl.when(jnp.logical_not(far[2 - slot]))
            def _():
                forward[slot].start()
    for copy in halos[0][1].values():
        copy.wait_send()
    for slot in (0, 2):
        @pl.when(jnp.logical_not(far[slot]))
        def _():
            halos[0][1][slot].wait_recv()
    for _, copies in halos[1:]:
        for slot in (0, 2):
            @pl.when(jnp.logical_not(far[2 - slot]))
            def _():
                copies[slot].wait_send()

            @pl.when(jnp.logical_not(far[slot]))
            def _():
                copies[slot].wait_recv()
    local.wait()


def gather_window(block, n_row, n_col):
    rows, width = block.shape
    return pl.pallas_call(
        functools.partial(gather_kernel, n_row, n_col),
        out_shape=jax.ShapeDtypeStruct((3, n_col, rows, width), block.dtype),
        in_specs=[pl.BlockSpec(memory_space=pltpu.VMEM)],
        out_specs=pl.BlockSpec(memory_space=pltpu.VMEM),
        scratch_shapes=[
            pltpu.SemaphoreType.DMA((3, n_col - 1)),
            pltpu.SemaphoreType.DMA((3, n_col - 1)),
            pltpu.SemaphoreType.DMA((2, n_col)),
            pltpu.SemaphoreType.DMA((2, n_col)),
            pltpu.SemaphoreType.DMA((1,)),
        ],
        compiler_params=pltpu.CompilerParams(collective_id=1, has_side_effects=True),
    )(block)


class Gated:
    def __init__(self, copy, cond):
        self.copy = copy
        self.cond = cond

    def wait(self):
        pl.when(self.cond)(self.copy.wait)


def spread_kernel(n_row, n_col, mid_ref, up_ref, down_ref, parts_ref, o_ref, sums_ref, up_bf, down_bf,
                  from_down, from_up, ring_in, ring_out, far_in, far_out, far_from, up_send, down_send,
                  from_down_sem, from_up_sem, ring_send, ring_recv, far_send, far_recv, last_send, last_recv,
                  part, gath, rsend, rrecv, dsend, drecv, gsend, grecv):
    row = lax.axis_index("row")
    col = lax.axis_index("col")
    p = ring_position(col, n_col)
    succ = ring_col((p + 1) % n_col, n_col)
    pred = ring_col((p + n_col - 1) % n_col, n_col)
    up = (row + 1) % n_row
    down = (row + n_row - 1) % n_row
    half = max(n_row // 2, 1)
    far_down = row % half == 0
    far_up = (row + 1) % half == 0
    partners = [(row, succ), (row, pred), (up, col), (down, col)]
    partners += allreduce_partners(n_row, n_col, row, col)
    barrier = pltpu.get_barrier_semaphore()
    for device in partners:
        def signal(device=device):
            pl.semaphore_signal(barrier, inc=1, device_id=device, device_id_type=MESH)

        pl.when(jnp.logical_or(device[0] != row, device[1] != col))(signal)
    pl.semaphore_wait(barrier, len(partners) - 1)
    up_bf[...] = up_ref[...].astype(up_bf.dtype)
    down_bf[...] = down_ref[...].astype(down_bf.dtype)
    halos = []
    for step in range(1, n_col + 1):
        block = ring_col((p - step + 2 * n_col) % n_col, n_col)
        pair = []
        for src, dst, target, send, recv, far in (
            (up_bf, from_down, up, up_send, from_down_sem, far_up),
            (down_bf, from_up, down, down_send, from_up_sem, far_down),
        ):
            copy = pltpu.make_async_remote_copy(
                src_ref=src.at[block],
                dst_ref=dst.at[block],
                send_sem=send.at[step - 1],
                recv_sem=recv.at[step - 1],
                device_id=(target, col),
                device_id_type=MESH,
            )
            pl.when(jnp.logical_not(far))(copy.start)
            pair.append(copy)
        halos.append((block, pair))

    def local_total(index):
        block, (from_below, from_above) = halos[index]
        pl.when(jnp.logical_not(far_down))(from_below.wait_recv)
        pl.when(jnp.logical_not(far_up))(from_above.wait_recv)
        zero = jnp.zeros(mid_ref.shape[1:], jnp.float32)
        return (
            mid_ref[block]
            + jnp.where(far_down, zero, from_down[block].astype(jnp.float32))
            + jnp.where(far_up, zero, from_up[block].astype(jnp.float32))
        )

    def ring_steps():
        for step in range(1, n_col):
            value = local_total(step - 1)
            if step > 1:
                value = value + ring_in[step - 2]
            ring_out[step - 1] = value
            copy = pltpu.make_async_remote_copy(
                src_ref=ring_out.at[step - 1],
                dst_ref=ring_in.at[step - 1],
                send_sem=ring_send.at[step - 1],
                recv_sem=ring_recv.at[step - 1],
                device_id=(row, succ),
                device_id_type=MESH,
            )
            copy.start()
            yield copy
        o_ref[...] = local_total(n_col - 1) + ring_in[n_col - 2]

    def far_steps(side, part_ref, far):
        for step in range(1, n_col):
            block = ring_col((p - step + 2 * n_col) % n_col, n_col)
            copy = pltpu.make_async_remote_copy(
                src_ref=far_out.at[side, step - 1],
                dst_ref=far_in.at[side, step - 1],
                send_sem=far_send.at[side, step - 1],
                recv_sem=far_recv.at[side, step - 1],
                device_id=(row, succ),
                device_id_type=MESH,
            )

            def send(step=step, block=block, copy=copy):
                value = part_ref[block]
                if step > 1:
                    value = value + far_in[side, step - 2]
                far_out[side, step - 1] = value
                copy.start()

            pl.when(far)(send)
            yield Gated(copy, far)

        def finish():
            far_out[side, n_col - 1] = part_ref[col] + far_in[side, n_col - 2]

        pl.when(far)(finish)

    run_together(
        allreduce_steps(n_row, n_col, row, col, parts_ref, sums_ref, part, gath,
                        rsend, rrecv, dsend, drecv, gsend, grecv),
        ring_steps(),
        far_steps(0, up_ref, far_up),
        far_steps(1, down_ref, far_down),
    )
    lasts = []
    for side, target, slot, far in ((0, up, 0, far_up), (1, down, 1, far_down)):
        copy = pltpu.make_async_remote_copy(
            src_ref=far_out.at[side, n_col - 1],
            dst_ref=far_from.at[slot],
            send_sem=last_send.at[side],
            recv_sem=last_recv.at[slot],
            device_id=(target, col),
            device_id_type=MESH,
        )
        pl.when(far)(copy.start)
        lasts.append(copy)
    pl.when(far_up)(lasts[0].wait_send)
    pl.when(far_down)(lasts[1].wait_send)
    pl.when(far_down)(lasts[0].wait_recv)
    pl.when(far_up)(lasts[1].wait_recv)
    zero = jnp.zeros(o_ref.shape, jnp.float32)
    o_ref[...] = (
        o_ref[...]
        + jnp.where(far_down, far_from[0], zero)
        + jnp.where(far_up, far_from[1], zero)
    )
    for _, (to_up, to_down) in halos:
        pl.when(jnp.logical_not(far_up))(to_up.wait_send)
        pl.when(jnp.logical_not(far_down))(to_down.wait_send)


def reduce_spread(mid, up_part, down_part, parts, n_row, n_col):
    _, rows, width = mid.shape
    col_bits = n_col.bit_length() - 1
    row_bits = n_row.bit_length() - 1
    stacked, _ = parts.shape
    return pl.pallas_call(
        functools.partial(spread_kernel, n_row, n_col),
        out_shape=(
            jax.ShapeDtypeStruct((rows, width), jnp.float32),
            jax.ShapeDtypeStruct(parts.shape, jnp.float32),
        ),
        in_specs=[pl.BlockSpec(memory_space=pltpu.VMEM)] * 4,
        out_specs=(pl.BlockSpec(memory_space=pltpu.VMEM),) * 2,
        scratch_shapes=[
            pltpu.VMEM((n_col, rows, width), jnp.bfloat16),
            pltpu.VMEM((n_col, rows, width), jnp.bfloat16),
            pltpu.VMEM((n_col, rows, width), jnp.bfloat16),
            pltpu.VMEM((n_col, rows, width), jnp.bfloat16),
            pltpu.VMEM((n_col - 1, rows, width), jnp.float32),
            pltpu.VMEM((n_col - 1, rows, width), jnp.float32),
            pltpu.VMEM((2, n_col - 1, rows, width), jnp.float32),
            pltpu.VMEM((2, n_col, rows, width), jnp.float32),
            pltpu.VMEM((2, rows, width), jnp.float32),
            pltpu.SemaphoreType.DMA((n_col,)),
            pltpu.SemaphoreType.DMA((n_col,)),
            pltpu.SemaphoreType.DMA((n_col,)),
            pltpu.SemaphoreType.DMA((n_col,)),
            pltpu.SemaphoreType.DMA((n_col - 1,)),
            pltpu.SemaphoreType.DMA((n_col - 1,)),
            pltpu.SemaphoreType.DMA((2, n_col - 1)),
            pltpu.SemaphoreType.DMA((2, n_col - 1)),
            pltpu.SemaphoreType.DMA((2,)),
            pltpu.SemaphoreType.DMA((2,)),
            pltpu.VMEM((2 * row_bits, stacked // n_col, width), jnp.float32),
            pltpu.VMEM((1, n_col, stacked // n_col, width), jnp.float32),
            pltpu.SemaphoreType.DMA((n_col,)),
            pltpu.SemaphoreType.DMA((n_col,)),
            pltpu.SemaphoreType.DMA((row_bits,)),
            pltpu.SemaphoreType.DMA((row_bits,)),
            pltpu.SemaphoreType.DMA((n_col,)),
            pltpu.SemaphoreType.DMA((n_col,)),
        ],
        compiler_params=pltpu.CompilerParams(collective_id=2, has_side_effects=True),
    )(mid, up_part, down_part, parts)


def local_kernel(rows_ref, cols_ref, count_ref, window_ref, tiles_ref, feat_ref, w_ref, ws_ref, cot_ref,
                 act_ref, parts_ref, self_ref, mid_ref, up_ref, down_ref, acc, grad_agg, spread):
    tile = tiles_ref.shape[-1]
    nodes = acc.shape[0]
    span = mid_ref.shape[0]
    count = jnp.minimum(count_ref[0], tiles_ref.shape[0])
    acc[...] = jnp.zeros_like(acc)

    def forward(j, carry):
        at = pl.multiple_of(rows_ref[j] * tile, tile)
        acc[pl.ds(at, tile), :] += jnp.dot(
            tiles_ref[j], window_ref[cols_ref[j]], preferred_element_type=jnp.float32
        )
        return carry

    lax.fori_loop(0, count, forward, 0)
    aggregated = acc[...].astype(jnp.bfloat16)
    features = feat_ref[...]
    pre_act = jnp.dot(aggregated, w_ref[...], preferred_element_type=jnp.float32) + jnp.dot(
        features, ws_ref[...], preferred_element_type=jnp.float32
    )
    sigma = jax.nn.sigmoid(pre_act)
    act_ref[...] = (pre_act * sigma).astype(act_ref.dtype)
    grad_pre = (cot_ref[...].astype(jnp.float32) * sigma * (1.0 + pre_act * (1.0 - sigma))).astype(
        jnp.bfloat16
    )
    over_nodes = (((0,), (0,)), ((), ()))
    parts_ref[pl.ds(0, nodes), :] = lax.dot_general(
        aggregated, grad_pre, over_nodes, preferred_element_type=jnp.float32
    )
    parts_ref[pl.ds(nodes, nodes), :] = lax.dot_general(
        features, grad_pre, over_nodes, preferred_element_type=jnp.float32
    )
    by_rows = (((1,), (1,)), ((), ()))
    grad_agg[...] = lax.dot_general(
        grad_pre, w_ref[...], by_rows, preferred_element_type=jnp.float32
    ).astype(jnp.bfloat16)
    self_ref[...] = lax.dot_general(grad_pre, ws_ref[...], by_rows, preferred_element_type=jnp.float32)
    spread[...] = jnp.zeros_like(spread)

    def backward(j, carry):
        at = pl.multiple_of(rows_ref[j] * tile, tile)
        column = cols_ref[j]
        spread[column] += lax.dot_general(
            tiles_ref[j], grad_agg[pl.ds(at, tile), :], over_nodes, preferred_element_type=jnp.float32
        )
        return carry

    lax.fori_loop(0, count, backward, 0)
    mid_ref[...] = spread[pl.ds(span, span)]
    up_ref[...] = spread[pl.ds(2 * span, span)].astype(up_ref.dtype)
    down_ref[...] = spread[pl.ds(0, span)].astype(down_ref.dtype)


def local_math(slot_rows, slot_cols, count, window, tiles, features, weight, weight_self, cotangent):
    nodes, width = features.shape
    span = window.shape[0] // 3
    tile = tiles.shape[-1]
    smem = pl.BlockSpec(memory_space=pltpu.SMEM)
    vmem = pl.BlockSpec(memory_space=pltpu.VMEM)
    return pl.pallas_call(
        local_kernel,
        out_shape=(
            jax.ShapeDtypeStruct((nodes, width), jnp.bfloat16),
            jax.ShapeDtypeStruct((2 * width, width), jnp.float32),
            jax.ShapeDtypeStruct((nodes, width), jnp.float32),
            jax.ShapeDtypeStruct((span, tile, width), jnp.float32),
            jax.ShapeDtypeStruct((span, tile, width), jnp.float32),
            jax.ShapeDtypeStruct((span, tile, width), jnp.float32),
        ),
        in_specs=[smem, smem, smem] + [vmem] * 6,
        out_specs=(vmem,) * 6,
        scratch_shapes=[
            pltpu.VMEM((nodes, width), jnp.float32),
            pltpu.VMEM((nodes, width), jnp.bfloat16),
            pltpu.VMEM((3 * span, tile, width), jnp.float32),
        ],
    )(slot_rows, slot_cols, count, window, tiles, features, weight, weight_self, cotangent)


def shards(features, weight, weight_self, tile_values, tile_rows, tile_cols, tile_count, cotangent):
    tile_block = tile_values[0]
    slot_rows = tile_rows[0]
    slot_cols = tile_cols[0]
    live_count = tile_count[0, 0]
    slot_total = tile_block.shape[0]
    tile_side = tile_block.shape[-1]
    node_rows = features.shape[0]
    width = features.shape[1]
    per_block = node_rows // tile_side
    col_count = lax.axis_size("col")
    row_count = lax.axis_size("row")
    span = col_count * per_block
    window = gather_window(features, row_count, col_count)
    window_tiles = window.reshape(-1, tile_side, width)
    activations, parts, self_feature, mid, up_part, down_part = local_math(
        slot_rows,
        slot_cols,
        tile_count[0],
        window_tiles,
        tile_block,
        features,
        weight,
        weight_self,
        cotangent,
    )
    own_share, summed_parts = reduce_spread(
        mid.reshape(col_count, node_rows, width),
        up_part.reshape(col_count, node_rows, width),
        down_part.reshape(col_count, node_rows, width),
        parts,
        row_count,
        col_count,
    )
    feature_grad = (own_share + self_feature).astype(jnp.bfloat16)
    weight_total, self_total = summed_parts[:width], summed_parts[width:]
    factor = 1.0 / math.sqrt(node_rows * col_count * row_count)
    return (activations, feature_grad, weight_total * factor, self_total * factor)


def solution(mesh):
    placed = (
        P(("row", "col"), None),
        P(),
        P(),
        P("row", "col", None, None),
        P("row", "col"),
        P("row", "col"),
        P("row", "col"),
        P(("row", "col"), None),
    )
    return jax.shard_map(
        shards,
        mesh=mesh,
        in_specs=placed,
        out_specs=(P(("row", "col"), None), P(("row", "col"), None), P(), P()),
        check_vma=False,
    )
```

```python
import functools
import math

import jax
import jax.numpy as jnp
from jax import lax
from jax.experimental import pallas as pl
from jax.experimental.pallas import tpu as pltpu
from jax.sharding import PartitionSpec as P

MESH = pl.DeviceIdType.MESH


def flip(index, stride):
    bit = (index // stride) % 2
    return index + stride - 2 * stride * bit, bit


def allreduce_partners(n_row, n_col, row, col):
    partners = [(row, peer) for peer in range(n_col)]
    for k in range(n_row.bit_length() - 1):
        partners.append((flip(row, 1 << k)[0], col))
    return partners


class Group:
    def __init__(self, copies, receipts, col):
        self.copies = copies
        self.receipts = receipts
        self.col = col

    def wait(self):
        for peer, (copy, receipt) in enumerate(zip(self.copies, self.receipts)):
            @pl.when(peer != self.col)
            def _():
                copy.wait_send()
                receipt.wait_recv()


def allreduce_steps(n_row, n_col, row, col, x_ref, o_ref, part, gath, rsend, rrecv, dsend, drecv, gsend, grecv):
    row_bits = n_row.bit_length() - 1
    chunk = x_ref.shape[0] // n_col
    mine = pl.ds(pl.multiple_of(col * chunk, 8), chunk)
    copies, receipts = [], []
    for peer in range(n_col):
        copies.append(pltpu.make_async_remote_copy(
            src_ref=x_ref.at[pl.ds(peer * chunk, chunk)],
            dst_ref=gath.at[0, col],
            send_sem=rsend.at[peer],
            recv_sem=rrecv.at[col],
            device_id=(row, peer),
            device_id_type=MESH,
        ))
        receipts.append(pltpu.make_async_remote_copy(
            src_ref=x_ref.at[pl.ds(peer * chunk, chunk)],
            dst_ref=gath.at[0, peer],
            send_sem=rsend.at[peer],
            recv_sem=rrecv.at[peer],
            device_id=(row, peer),
            device_id_type=MESH,
        ))
        pl.when(peer != col)(copies[-1].start)
    yield Group(copies, receipts, col)
    total = x_ref[mine, :]
    for peer in range(n_col):
        total = total + jnp.where(peer == col, jnp.zeros_like(total), gath[0, peer])
    for k in range(row_bits):
        other, _ = flip(row, 1 << k)
        hold = part.at[2 * k]
        hold[...] = total
        copy = pltpu.make_async_remote_copy(
            src_ref=hold,
            dst_ref=part.at[2 * k + 1],
            send_sem=dsend.at[k],
            recv_sem=drecv.at[k],
            device_id=(other, col),
            device_id_type=MESH,
        )
        copy.start()
        yield copy
        total = total + part[2 * k + 1]
    o_ref[mine, :] = total
    copies, receipts = [], []
    for peer in range(n_col):
        copies.append(pltpu.make_async_remote_copy(
            src_ref=o_ref.at[mine],
            dst_ref=o_ref.at[mine],
            send_sem=gsend.at[peer],
            recv_sem=grecv.at[col],
            device_id=(row, peer),
            device_id_type=MESH,
        ))
        receipts.append(pltpu.make_async_remote_copy(
            src_ref=o_ref.at[mine],
            dst_ref=o_ref.at[pl.ds(peer * chunk, chunk)],
            send_sem=gsend.at[peer],
            recv_sem=grecv.at[peer],
            device_id=(row, peer),
            device_id_type=MESH,
        ))
        pl.when(peer != col)(copies[-1].start)
    yield Group(copies, receipts, col)


def run_together(*chains):
    active = list(chains)
    while active:
        copies, kept = [], []
        for chain in active:
            try:
                copies.append(next(chain))
                kept.append(chain)
            except StopIteration:
                pass
        for copy in copies:
            copy.wait()
        active = kept


def ring_position(col, n):
    core = col % 2
    y = col // 2
    return y + core * (n - 1 - 2 * y)


def ring_col(p, n):
    q = p // (n // 2)
    y = p + q * (n - 1 - 2 * p)
    return 2 * y + q


def gather_kernel(n_row, n_col, x_ref, w_ref, ring_send, ring_recv, halo_send, halo_recv, local_sem):
    row = lax.axis_index("row")
    col = lax.axis_index("col")
    p = ring_position(col, n_col)
    succ = ring_col((p + 1) % n_col, n_col)
    pred = ring_col((p + n_col - 1) % n_col, n_col)
    up = (row + 1) % n_row
    down = (row + n_row - 1) % n_row
    half = max(n_row // 2, 1)
    far = {0: row % half == 0, 2: (row + 1) % half == 0}
    barrier = pltpu.get_barrier_semaphore()
    for device in ((row, succ), (row, pred), (up, col), (down, col)):
        pl.semaphore_signal(barrier, inc=1, device_id=device, device_id_type=MESH)
    pl.semaphore_wait(barrier, 4)
    local = pltpu.make_async_copy(x_ref, w_ref.at[1, col], local_sem.at[0])
    local.start()

    def halo(src, block, index):
        copies = {}
        for target, slot in ((up, 0), (down, 2)):
            copies[slot] = pltpu.make_async_remote_copy(
                src_ref=src,
                dst_ref=w_ref.at[slot, block],
                send_sem=halo_send.at[slot // 2, index],
                recv_sem=halo_recv.at[slot // 2, index],
                device_id=(target, col),
                device_id_type=MESH,
            )
        return copies

    halos = [(col, halo(x_ref, col, 0))]
    for copy in halos[0][1].values():
        copy.start()
    sent = col
    for step in range(1, n_col):
        copies = {}
        for group in (1, 0, 2):
            src = x_ref if (step == 1 and group == 1) else w_ref.at[group, sent]
            copies[group] = pltpu.make_async_remote_copy(
                src_ref=src,
                dst_ref=w_ref.at[group, sent],
                send_sem=ring_send.at[group, step - 1],
                recv_sem=ring_recv.at[group, step - 1],
                device_id=(row, succ),
                device_id_type=MESH,
            )
        copies[1].start()
        for group in (0, 2):
            @pl.when(far[group])
            def _():
                if step == 1:
                    halos[0][1][group].wait_recv()
                copies[group].start()
        copies[1].wait()
        for group in (0, 2):
            @pl.when(far[group])
            def _():
                copies[group].wait()
        sent = ring_col((p - step + n_col) % n_col, n_col)
        forward = halo(w_ref.at[1, sent], sent, step)
        halos.append((sent, forward))
        for slot in (0, 2):
            @pl.when(jnp.logical_not(far[2 - slot]))
            def _():
                forward[slot].start()
    for copy in halos[0][1].values():
        copy.wait_send()
    for slot in (0, 2):
        @pl.when(jnp.logical_not(far[slot]))
        def _():
            halos[0][1][slot].wait_recv()
    for _, copies in halos[1:]:
        for slot in (0, 2):
            @pl.when(jnp.logical_not(far[2 - slot]))
            def _():
                copies[slot].wait_send()

            @pl.when(jnp.logical_not(far[slot]))
            def _():
                copies[slot].wait_recv()
    local.wait()


def gather_window(block, n_row, n_col):
    rows, width = block.shape
    return pl.pallas_call(
        functools.partial(gather_kernel, n_row, n_col),
        out_shape=jax.ShapeDtypeStruct((3, n_col, rows, width), block.dtype),
        in_specs=[pl.BlockSpec(memory_space=pltpu.VMEM)],
        out_specs=pl.BlockSpec(memory_space=pltpu.VMEM),
        scratch_shapes=[
            pltpu.SemaphoreType.DMA((3, n_col - 1)),
            pltpu.SemaphoreType.DMA((3, n_col - 1)),
            pltpu.SemaphoreType.DMA((2, n_col)),
            pltpu.SemaphoreType.DMA((2, n_col)),
            pltpu.SemaphoreType.DMA((1,)),
        ],
        compiler_params=pltpu.CompilerParams(collective_id=1, has_side_effects=True),
    )(block)


class Gated:
    def __init__(self, copy, cond):
        self.copy = copy
        self.cond = cond

    def wait(self):
        pl.when(self.cond)(self.copy.wait)


def spread_kernel(n_row, n_col, scale, mid_ref, up_ref, down_ref, parts_ref, self_ref, o_ref, sums_ref, own,
                  up_bf, down_bf,
                  from_down, from_up, ring_in, ring_out, far_in, far_out, far_from, up_send, down_send,
                  from_down_sem, from_up_sem, ring_send, ring_recv, far_send, far_recv, last_send, last_recv,
                  part, gath, rsend, rrecv, dsend, drecv, gsend, grecv):
    row = lax.axis_index("row")
    col = lax.axis_index("col")
    p = ring_position(col, n_col)
    succ = ring_col((p + 1) % n_col, n_col)
    pred = ring_col((p + n_col - 1) % n_col, n_col)
    up = (row + 1) % n_row
    down = (row + n_row - 1) % n_row
    half = max(n_row // 2, 1)
    far_down = row % half == 0
    far_up = (row + 1) % half == 0
    partners = [(row, succ), (row, pred), (up, col), (down, col)]
    partners += allreduce_partners(n_row, n_col, row, col)
    barrier = pltpu.get_barrier_semaphore()
    for device in partners:
        def signal(device=device):
            pl.semaphore_signal(barrier, inc=1, device_id=device, device_id_type=MESH)

        pl.when(jnp.logical_or(device[0] != row, device[1] != col))(signal)
    pl.semaphore_wait(barrier, len(partners) - 1)
    up_bf[...] = up_ref[...].astype(up_bf.dtype)
    down_bf[...] = down_ref[...].astype(down_bf.dtype)
    halos = []
    for step in range(1, n_col + 1):
        block = ring_col((p - step + 2 * n_col) % n_col, n_col)
        pair = []
        for src, dst, target, send, recv, far in (
            (up_bf, from_down, up, up_send, from_down_sem, far_up),
            (down_bf, from_up, down, down_send, from_up_sem, far_down),
        ):
            copy = pltpu.make_async_remote_copy(
                src_ref=src.at[block],
                dst_ref=dst.at[block],
                send_sem=send.at[step - 1],
                recv_sem=recv.at[step - 1],
                device_id=(target, col),
                device_id_type=MESH,
            )
            pl.when(jnp.logical_not(far))(copy.start)
            pair.append(copy)
        halos.append((block, pair))

    def local_total(index):
        block, (from_below, from_above) = halos[index]
        pl.when(jnp.logical_not(far_down))(from_below.wait_recv)
        pl.when(jnp.logical_not(far_up))(from_above.wait_recv)
        zero = jnp.zeros(mid_ref.shape[1:], jnp.float32)
        return (
            mid_ref[block]
            + jnp.where(far_down, zero, from_down[block].astype(jnp.float32))
            + jnp.where(far_up, zero, from_up[block].astype(jnp.float32))
        )

    def ring_steps():
        for step in range(1, n_col):
            value = local_total(step - 1)
            if step > 1:
                value = value + ring_in[step - 2].astype(jnp.float32)
            ring_out[step - 1] = value.astype(ring_out.dtype)
            copy = pltpu.make_async_remote_copy(
                src_ref=ring_out.at[step - 1],
                dst_ref=ring_in.at[step - 1],
                send_sem=ring_send.at[step - 1],
                recv_sem=ring_recv.at[step - 1],
                device_id=(row, succ),
                device_id_type=MESH,
            )
            copy.start()
            yield copy
        own[...] = local_total(n_col - 1) + ring_in[n_col - 2].astype(jnp.float32)

    def far_steps(side, part_ref, far):
        for step in range(1, n_col):
            block = ring_col((p - step + 2 * n_col) % n_col, n_col)
            copy = pltpu.make_async_remote_copy(
                src_ref=far_out.at[side, step - 1],
                dst_ref=far_in.at[side, step - 1],
                send_sem=far_send.at[side, step - 1],
                recv_sem=far_recv.at[side, step - 1],
                device_id=(row, succ),
                device_id_type=MESH,
            )

            def send(step=step, block=block, copy=copy):
                value = part_ref[block]
                if step > 1:
                    value = value + far_in[side, step - 2]
                far_out[side, step - 1] = value
                copy.start()

            pl.when(far)(send)
            yield Gated(copy, far)

        def finish():
            far_out[side, n_col - 1] = part_ref[col] + far_in[side, n_col - 2]

        pl.when(far)(finish)

    run_together(
        allreduce_steps(n_row, n_col, row, col, parts_ref, sums_ref, part, gath,
                        rsend, rrecv, dsend, drecv, gsend, grecv),
        ring_steps(),
        far_steps(0, up_ref, far_up),
        far_steps(1, down_ref, far_down),
    )
    lasts = []
    for side, target, slot, far in ((0, up, 0, far_up), (1, down, 1, far_down)):
        copy = pltpu.make_async_remote_copy(
            src_ref=far_out.at[side, n_col - 1],
            dst_ref=far_from.at[slot],
            send_sem=last_send.at[side],
            recv_sem=last_recv.at[slot],
            device_id=(target, col),
            device_id_type=MESH,
        )
        pl.when(far)(copy.start)
        lasts.append(copy)
    pl.when(far_up)(lasts[0].wait_send)
    pl.when(far_down)(lasts[1].wait_send)
    pl.when(far_down)(lasts[0].wait_recv)
    pl.when(far_up)(lasts[1].wait_recv)
    zero = jnp.zeros(o_ref.shape, jnp.float32)
    total = own[...] + jnp.where(far_down, far_from[0], zero) + jnp.where(far_up, far_from[1], zero)
    o_ref[...] = (total + self_ref[...]).astype(o_ref.dtype)
    sums_ref[...] = sums_ref[...] * scale
    for _, (to_up, to_down) in halos:
        pl.when(jnp.logical_not(far_up))(to_up.wait_send)
        pl.when(jnp.logical_not(far_down))(to_down.wait_send)


def reduce_spread(mid, up_part, down_part, parts, self_feature, scale, n_row, n_col):
    _, rows, width = mid.shape
    col_bits = n_col.bit_length() - 1
    row_bits = n_row.bit_length() - 1
    stacked, _ = parts.shape
    return pl.pallas_call(
        functools.partial(spread_kernel, n_row, n_col, scale),
        out_shape=(
            jax.ShapeDtypeStruct((rows, width), jnp.bfloat16),
            jax.ShapeDtypeStruct(parts.shape, jnp.float32),
        ),
        in_specs=[pl.BlockSpec(memory_space=pltpu.VMEM)] * 5,
        out_specs=(pl.BlockSpec(memory_space=pltpu.VMEM),) * 2,
        scratch_shapes=[
            pltpu.VMEM((rows, width), jnp.float32),
            pltpu.VMEM((n_col, rows, width), jnp.bfloat16),
            pltpu.VMEM((n_col, rows, width), jnp.bfloat16),
            pltpu.VMEM((n_col, rows, width), jnp.bfloat16),
            pltpu.VMEM((n_col, rows, width), jnp.bfloat16),
            pltpu.VMEM((n_col - 1, rows, width), jnp.bfloat16),
            pltpu.VMEM((n_col - 1, rows, width), jnp.bfloat16),
            pltpu.VMEM((2, n_col - 1, rows, width), jnp.float32),
            pltpu.VMEM((2, n_col, rows, width), jnp.float32),
            pltpu.VMEM((2, rows, width), jnp.float32),
            pltpu.SemaphoreType.DMA((n_col,)),
            pltpu.SemaphoreType.DMA((n_col,)),
            pltpu.SemaphoreType.DMA((n_col,)),
            pltpu.SemaphoreType.DMA((n_col,)),
            pltpu.SemaphoreType.DMA((n_col - 1,)),
            pltpu.SemaphoreType.DMA((n_col - 1,)),
            pltpu.SemaphoreType.DMA((2, n_col - 1)),
            pltpu.SemaphoreType.DMA((2, n_col - 1)),
            pltpu.SemaphoreType.DMA((2,)),
            pltpu.SemaphoreType.DMA((2,)),
            pltpu.VMEM((2 * row_bits, stacked // n_col, width), jnp.float32),
            pltpu.VMEM((1, n_col, stacked // n_col, width), jnp.float32),
            pltpu.SemaphoreType.DMA((n_col,)),
            pltpu.SemaphoreType.DMA((n_col,)),
            pltpu.SemaphoreType.DMA((row_bits,)),
            pltpu.SemaphoreType.DMA((row_bits,)),
            pltpu.SemaphoreType.DMA((n_col,)),
            pltpu.SemaphoreType.DMA((n_col,)),
        ],
        compiler_params=pltpu.CompilerParams(collective_id=2, has_side_effects=True),
    )(mid, up_part, down_part, parts, self_feature)


def local_kernel(rows_ref, cols_ref, count_ref, window_ref, tiles_ref, feat_ref, w_ref, ws_ref, cot_ref,
                 act_ref, parts_ref, self_ref, mid_ref, up_ref, down_ref, acc, grad_agg, spread):
    tile = tiles_ref.shape[-1]
    nodes = acc.shape[0]
    span = mid_ref.shape[0]
    count = jnp.minimum(count_ref[0], tiles_ref.shape[0])
    acc[...] = jnp.zeros_like(acc)

    def forward(j, carry):
        at = pl.multiple_of(rows_ref[j] * tile, tile)
        acc[pl.ds(at, tile), :] += jnp.dot(
            tiles_ref[j], window_ref[cols_ref[j]], preferred_element_type=jnp.float32
        )
        return carry

    lax.fori_loop(0, count, forward, 0)
    aggregated = acc[...].astype(jnp.bfloat16)
    features = feat_ref[...]
    pre_act = jnp.dot(aggregated, w_ref[...], preferred_element_type=jnp.float32) + jnp.dot(
        features, ws_ref[...], preferred_element_type=jnp.float32
    )
    sigma = jax.nn.sigmoid(pre_act)
    act_ref[...] = (pre_act * sigma).astype(act_ref.dtype)
    grad_pre = (cot_ref[...].astype(jnp.float32) * sigma * (1.0 + pre_act * (1.0 - sigma))).astype(
        jnp.bfloat16
    )
    over_nodes = (((0,), (0,)), ((), ()))
    parts_ref[pl.ds(0, nodes), :] = lax.dot_general(
        aggregated, grad_pre, over_nodes, preferred_element_type=jnp.float32
    )
    parts_ref[pl.ds(nodes, nodes), :] = lax.dot_general(
        features, grad_pre, over_nodes, preferred_element_type=jnp.float32
    )
    by_rows = (((1,), (1,)), ((), ()))
    grad_agg[...] = lax.dot_general(
        grad_pre, w_ref[...], by_rows, preferred_element_type=jnp.float32
    ).astype(jnp.bfloat16)
    self_ref[...] = lax.dot_general(grad_pre, ws_ref[...], by_rows, preferred_element_type=jnp.float32)
    spread[...] = jnp.zeros_like(spread)

    def backward(j, carry):
        at = pl.multiple_of(rows_ref[j] * tile, tile)
        column = cols_ref[j]
        spread[column] += lax.dot_general(
            tiles_ref[j], grad_agg[pl.ds(at, tile), :], over_nodes, preferred_element_type=jnp.float32
        )
        return carry

    lax.fori_loop(0, count, backward, 0)
    mid_ref[...] = spread[pl.ds(span, span)]
    up_ref[...] = spread[pl.ds(2 * span, span)].astype(up_ref.dtype)
    down_ref[...] = spread[pl.ds(0, span)].astype(down_ref.dtype)


def local_math(slot_rows, slot_cols, count, window, tiles, features, weight, weight_self, cotangent):
    nodes, width = features.shape
    span = window.shape[0] // 3
    tile = tiles.shape[-1]
    smem = pl.BlockSpec(memory_space=pltpu.SMEM)
    vmem = pl.BlockSpec(memory_space=pltpu.VMEM)
    return pl.pallas_call(
        local_kernel,
        out_shape=(
            jax.ShapeDtypeStruct((nodes, width), jnp.bfloat16),
            jax.ShapeDtypeStruct((2 * width, width), jnp.float32),
            jax.ShapeDtypeStruct((nodes, width), jnp.float32),
            jax.ShapeDtypeStruct((span, tile, width), jnp.float32),
            jax.ShapeDtypeStruct((span, tile, width), jnp.float32),
            jax.ShapeDtypeStruct((span, tile, width), jnp.float32),
        ),
        in_specs=[smem, smem, smem] + [vmem] * 6,
        out_specs=(vmem,) * 6,
        scratch_shapes=[
            pltpu.VMEM((nodes, width), jnp.float32),
            pltpu.VMEM((nodes, width), jnp.bfloat16),
            pltpu.VMEM((3 * span, tile, width), jnp.float32),
        ],
    )(slot_rows, slot_cols, count, window, tiles, features, weight, weight_self, cotangent)


def shards(features, weight, weight_self, tile_values, tile_rows, tile_cols, tile_count, cotangent):
    tile_block = tile_values[0]
    slot_rows = tile_rows[0]
    slot_cols = tile_cols[0]
    live_count = tile_count[0, 0]
    slot_total = tile_block.shape[0]
    tile_side = tile_block.shape[-1]
    node_rows = features.shape[0]
    width = features.shape[1]
    per_block = node_rows // tile_side
    col_count = lax.axis_size("col")
    row_count = lax.axis_size("row")
    span = col_count * per_block
    window = gather_window(features, row_count, col_count)
    window_tiles = window.reshape(-1, tile_side, width)
    activations, parts, self_feature, mid, up_part, down_part = local_math(
        slot_rows,
        slot_cols,
        tile_count[0],
        window_tiles,
        tile_block,
        features,
        weight,
        weight_self,
        cotangent,
    )
    factor = 1.0 / math.sqrt(node_rows * col_count * row_count)
    feature_grad, summed_parts = reduce_spread(
        mid.reshape(col_count, node_rows, width),
        up_part.reshape(col_count, node_rows, width),
        down_part.reshape(col_count, node_rows, width),
        parts,
        self_feature,
        factor,
        row_count,
        col_count,
    )
    weight_total, self_total = summed_parts[:width], summed_parts[width:]
    return (activations, feature_grad, weight_total, self_total)


def solution(mesh):
    placed = (
        P(("row", "col"), None),
        P(),
        P(),
        P("row", "col", None, None),
        P("row", "col"),
        P("row", "col"),
        P("row", "col"),
        P(("row", "col"), None),
    )
    return jax.shard_map(
        shards,
        mesh=mesh,
        in_specs=placed,
        out_specs=(P(("row", "col"), None), P(("row", "col"), None), P(), P()),
        check_vma=False,
    )
```

```python
import functools
import math

import jax
import jax.numpy as jnp
from jax import lax
from jax.experimental import pallas as pl
from jax.experimental.pallas import tpu as pltpu
from jax.sharding import PartitionSpec as P

MESH = pl.DeviceIdType.MESH


def flip(index, stride):
    bit = (index // stride) % 2
    return index + stride - 2 * stride * bit, bit


def allreduce_partners(n_row, n_col, row, col):
    partners = [(row, peer) for peer in range(n_col)]
    for k in range(n_row.bit_length() - 1):
        partners.append((flip(row, 1 << k)[0], col))
    return partners


class Group:
    def __init__(self, copies, receipts, col):
        self.copies = copies
        self.receipts = receipts
        self.col = col

    def wait(self):
        for peer, (copy, receipt) in enumerate(zip(self.copies, self.receipts)):
            @pl.when(peer != self.col)
            def _():
                copy.wait_send()
                receipt.wait_recv()


def allreduce_steps(n_row, n_col, row, col, x_ref, o_ref, part, gath, rsend, rrecv, dsend, drecv, gsend, grecv):
    row_bits = n_row.bit_length() - 1
    chunk = x_ref.shape[0] // n_col
    mine = pl.ds(pl.multiple_of(col * chunk, 8), chunk)
    copies, receipts = [], []
    for peer in range(n_col):
        copies.append(pltpu.make_async_remote_copy(
            src_ref=x_ref.at[pl.ds(peer * chunk, chunk)],
            dst_ref=gath.at[0, col],
            send_sem=rsend.at[peer],
            recv_sem=rrecv.at[col],
            device_id=(row, peer),
            device_id_type=MESH,
        ))
        receipts.append(pltpu.make_async_remote_copy(
            src_ref=x_ref.at[pl.ds(peer * chunk, chunk)],
            dst_ref=gath.at[0, peer],
            send_sem=rsend.at[peer],
            recv_sem=rrecv.at[peer],
            device_id=(row, peer),
            device_id_type=MESH,
        ))
        pl.when(peer != col)(copies[-1].start)
    yield Group(copies, receipts, col)
    total = x_ref[mine, :]
    for peer in range(n_col):
        total = total + jnp.where(peer == col, jnp.zeros_like(total), gath[0, peer])
    for k in range(row_bits):
        other, _ = flip(row, 1 << k)
        hold = part.at[2 * k]
        hold[...] = total
        copy = pltpu.make_async_remote_copy(
            src_ref=hold,
            dst_ref=part.at[2 * k + 1],
            send_sem=dsend.at[k],
            recv_sem=drecv.at[k],
            device_id=(other, col),
            device_id_type=MESH,
        )
        copy.start()
        yield copy
        total = total + part[2 * k + 1]
    o_ref[mine, :] = total
    copies, receipts = [], []
    for peer in range(n_col):
        copies.append(pltpu.make_async_remote_copy(
            src_ref=o_ref.at[mine],
            dst_ref=o_ref.at[mine],
            send_sem=gsend.at[peer],
            recv_sem=grecv.at[col],
            device_id=(row, peer),
            device_id_type=MESH,
        ))
        receipts.append(pltpu.make_async_remote_copy(
            src_ref=o_ref.at[mine],
            dst_ref=o_ref.at[pl.ds(peer * chunk, chunk)],
            send_sem=gsend.at[peer],
            recv_sem=grecv.at[peer],
            device_id=(row, peer),
            device_id_type=MESH,
        ))
        pl.when(peer != col)(copies[-1].start)
    yield Group(copies, receipts, col)


def run_together(*chains):
    active = list(chains)
    while active:
        copies, kept = [], []
        for chain in active:
            try:
                copies.append(next(chain))
                kept.append(chain)
            except StopIteration:
                pass
        for copy in copies:
            copy.wait()
        active = kept


def ring_position(col, n):
    core = col % 2
    y = col // 2
    return y + core * (n - 1 - 2 * y)


def ring_col(p, n):
    q = p // (n // 2)
    y = p + q * (n - 1 - 2 * p)
    return 2 * y + q


def gather_kernel(n_row, n_col, x_ref, w_ref, ring_send, ring_recv, halo_send, halo_recv, local_sem):
    row = lax.axis_index("row")
    col = lax.axis_index("col")
    p = ring_position(col, n_col)
    succ = ring_col((p + 1) % n_col, n_col)
    pred = ring_col((p + n_col - 1) % n_col, n_col)
    up = (row + 1) % n_row
    down = (row + n_row - 1) % n_row
    half = 8 if n_row % 8 == 0 else n_row
    far = {0: row % half == 0, 2: (row + 1) % half == 0}
    barrier = pltpu.get_barrier_semaphore()
    for device in ((row, succ), (row, pred), (up, col), (down, col)):
        pl.semaphore_signal(barrier, inc=1, device_id=device, device_id_type=MESH)
    pl.semaphore_wait(barrier, 4)
    local = pltpu.make_async_copy(x_ref, w_ref.at[1, col], local_sem.at[0])
    local.start()

    def halo(src, block, index):
        copies = {}
        for target, slot in ((up, 0), (down, 2)):
            copies[slot] = pltpu.make_async_remote_copy(
                src_ref=src,
                dst_ref=w_ref.at[slot, block],
                send_sem=halo_send.at[slot // 2, index],
                recv_sem=halo_recv.at[slot // 2, index],
                device_id=(target, col),
                device_id_type=MESH,
            )
        return copies

    halos = [(col, halo(x_ref, col, 0))]
    for copy in halos[0][1].values():
        copy.start()
    sent = col
    for step in range(1, n_col):
        copies = {}
        for group in (1, 0, 2):
            src = x_ref if (step == 1 and group == 1) else w_ref.at[group, sent]
            copies[group] = pltpu.make_async_remote_copy(
                src_ref=src,
                dst_ref=w_ref.at[group, sent],
                send_sem=ring_send.at[group, step - 1],
                recv_sem=ring_recv.at[group, step - 1],
                device_id=(row, succ),
                device_id_type=MESH,
            )
        copies[1].start()
        for group in (0, 2):
            @pl.when(far[group])
            def _():
                if step == 1:
                    halos[0][1][group].wait_recv()
                copies[group].start()
        copies[1].wait()
        for group in (0, 2):
            @pl.when(far[group])
            def _():
                copies[group].wait()
        sent = ring_col((p - step + n_col) % n_col, n_col)
        forward = halo(w_ref.at[1, sent], sent, step)
        halos.append((sent, forward))
        for slot in (0, 2):
            @pl.when(jnp.logical_not(far[2 - slot]))
            def _():
                forward[slot].start()
    for copy in halos[0][1].values():
        copy.wait_send()
    for slot in (0, 2):
        @pl.when(jnp.logical_not(far[slot]))
        def _():
            halos[0][1][slot].wait_recv()
    for _, copies in halos[1:]:
        for slot in (0, 2):
            @pl.when(jnp.logical_not(far[2 - slot]))
            def _():
                copies[slot].wait_send()

            @pl.when(jnp.logical_not(far[slot]))
            def _():
                copies[slot].wait_recv()
    local.wait()


def gather_window(block, n_row, n_col):
    rows, width = block.shape
    return pl.pallas_call(
        functools.partial(gather_kernel, n_row, n_col),
        out_shape=jax.ShapeDtypeStruct((3, n_col, rows, width), block.dtype),
        in_specs=[pl.BlockSpec(memory_space=pltpu.VMEM)],
        out_specs=pl.BlockSpec(memory_space=pltpu.VMEM),
        scratch_shapes=[
            pltpu.SemaphoreType.DMA((3, n_col - 1)),
            pltpu.SemaphoreType.DMA((3, n_col - 1)),
            pltpu.SemaphoreType.DMA((2, n_col)),
            pltpu.SemaphoreType.DMA((2, n_col)),
            pltpu.SemaphoreType.DMA((1,)),
        ],
        compiler_params=pltpu.CompilerParams(collective_id=1, has_side_effects=True),
    )(block)


class Gated:
    def __init__(self, copy, cond):
        self.copy = copy
        self.cond = cond

    def wait(self):
        pl.when(self.cond)(self.copy.wait)


def spread_kernel(n_row, n_col, scale, mid_ref, up_ref, down_ref, parts_ref, self_ref, o_ref, sums_ref, own,
                  up_bf, down_bf,
                  from_down, from_up, ring_in, ring_out, far_in, far_out, far_from, up_send, down_send,
                  from_down_sem, from_up_sem, ring_send, ring_recv, far_send, far_recv, last_send, last_recv,
                  part, gath, rsend, rrecv, dsend, drecv, gsend, grecv):
    row = lax.axis_index("row")
    col = lax.axis_index("col")
    p = ring_position(col, n_col)
    succ = ring_col((p + 1) % n_col, n_col)
    pred = ring_col((p + n_col - 1) % n_col, n_col)
    up = (row + 1) % n_row
    down = (row + n_row - 1) % n_row
    half = 8 if n_row % 8 == 0 else n_row
    far_down = row % half == 0
    far_up = (row + 1) % half == 0
    partners = [(row, succ), (row, pred), (up, col), (down, col)]
    partners += allreduce_partners(n_row, n_col, row, col)
    barrier = pltpu.get_barrier_semaphore()
    for device in partners:
        def signal(device=device):
            pl.semaphore_signal(barrier, inc=1, device_id=device, device_id_type=MESH)

        pl.when(jnp.logical_or(device[0] != row, device[1] != col))(signal)
    pl.semaphore_wait(barrier, len(partners) - 1)
    up_bf[...] = up_ref[...].astype(up_bf.dtype)
    down_bf[...] = down_ref[...].astype(down_bf.dtype)
    halos = []
    for step in range(1, n_col + 1):
        block = ring_col((p - step + 2 * n_col) % n_col, n_col)
        pair = []
        for src, dst, target, send, recv, far in (
            (up_bf, from_down, up, up_send, from_down_sem, far_up),
            (down_bf, from_up, down, down_send, from_up_sem, far_down),
        ):
            copy = pltpu.make_async_remote_copy(
                src_ref=src.at[block],
                dst_ref=dst.at[block],
                send_sem=send.at[step - 1],
                recv_sem=recv.at[step - 1],
                device_id=(target, col),
                device_id_type=MESH,
            )
            pl.when(jnp.logical_not(far))(copy.start)
            pair.append(copy)
        halos.append((block, pair))

    def local_total(index):
        block, (from_below, from_above) = halos[index]
        pl.when(jnp.logical_not(far_down))(from_below.wait_recv)
        pl.when(jnp.logical_not(far_up))(from_above.wait_recv)
        zero = jnp.zeros(mid_ref.shape[1:], jnp.float32)
        return (
            mid_ref[block]
            + jnp.where(far_down, zero, from_down[block].astype(jnp.float32))
            + jnp.where(far_up, zero, from_up[block].astype(jnp.float32))
        )

    def ring_steps():
        for step in range(1, n_col):
            value = local_total(step - 1)
            if step > 1:
                value = value + ring_in[step - 2].astype(jnp.float32)
            ring_out[step - 1] = value.astype(ring_out.dtype)
            copy = pltpu.make_async_remote_copy(
                src_ref=ring_out.at[step - 1],
                dst_ref=ring_in.at[step - 1],
                send_sem=ring_send.at[step - 1],
                recv_sem=ring_recv.at[step - 1],
                device_id=(row, succ),
                device_id_type=MESH,
            )
            copy.start()
            yield copy
        own[...] = local_total(n_col - 1) + ring_in[n_col - 2].astype(jnp.float32)

    def far_steps(side, part_ref, far):
        for step in range(1, n_col):
            block = ring_col((p - step + 2 * n_col) % n_col, n_col)
            copy = pltpu.make_async_remote_copy(
                src_ref=far_out.at[side, step - 1],
                dst_ref=far_in.at[side, step - 1],
                send_sem=far_send.at[side, step - 1],
                recv_sem=far_recv.at[side, step - 1],
                device_id=(row, succ),
                device_id_type=MESH,
            )

            def send(step=step, block=block, copy=copy):
                value = part_ref[block]
                if step > 1:
                    value = value + far_in[side, step - 2]
                far_out[side, step - 1] = value
                copy.start()

            pl.when(far)(send)
            yield Gated(copy, far)

        def finish():
            far_out[side, n_col - 1] = part_ref[col] + far_in[side, n_col - 2]

        pl.when(far)(finish)

    run_together(
        allreduce_steps(n_row, n_col, row, col, parts_ref, sums_ref, part, gath,
                        rsend, rrecv, dsend, drecv, gsend, grecv),
        ring_steps(),
        far_steps(0, up_ref, far_up),
        far_steps(1, down_ref, far_down),
    )
    lasts = []
    for side, target, slot, far in ((0, up, 0, far_up), (1, down, 1, far_down)):
        copy = pltpu.make_async_remote_copy(
            src_ref=far_out.at[side, n_col - 1],
            dst_ref=far_from.at[slot],
            send_sem=last_send.at[side],
            recv_sem=last_recv.at[slot],
            device_id=(target, col),
            device_id_type=MESH,
        )
        pl.when(far)(copy.start)
        lasts.append(copy)
    pl.when(far_up)(lasts[0].wait_send)
    pl.when(far_down)(lasts[1].wait_send)
    pl.when(far_down)(lasts[0].wait_recv)
    pl.when(far_up)(lasts[1].wait_recv)
    zero = jnp.zeros(o_ref.shape, jnp.float32)
    total = own[...] + jnp.where(far_down, far_from[0], zero) + jnp.where(far_up, far_from[1], zero)
    o_ref[...] = (total + self_ref[...]).astype(o_ref.dtype)
    sums_ref[...] = sums_ref[...] * scale
    for _, (to_up, to_down) in halos:
        pl.when(jnp.logical_not(far_up))(to_up.wait_send)
        pl.when(jnp.logical_not(far_down))(to_down.wait_send)


def reduce_spread(mid, up_part, down_part, parts, self_feature, scale, n_row, n_col):
    _, rows, width = mid.shape
    col_bits = n_col.bit_length() - 1
    row_bits = n_row.bit_length() - 1
    stacked, _ = parts.shape
    return pl.pallas_call(
        functools.partial(spread_kernel, n_row, n_col, scale),
        out_shape=(
            jax.ShapeDtypeStruct((rows, width), jnp.bfloat16),
            jax.ShapeDtypeStruct(parts.shape, jnp.float32),
        ),
        in_specs=[pl.BlockSpec(memory_space=pltpu.VMEM)] * 5,
        out_specs=(pl.BlockSpec(memory_space=pltpu.VMEM),) * 2,
        scratch_shapes=[
            pltpu.VMEM((rows, width), jnp.float32),
            pltpu.VMEM((n_col, rows, width), jnp.bfloat16),
            pltpu.VMEM((n_col, rows, width), jnp.bfloat16),
            pltpu.VMEM((n_col, rows, width), jnp.bfloat16),
            pltpu.VMEM((n_col, rows, width), jnp.bfloat16),
            pltpu.VMEM((n_col - 1, rows, width), jnp.bfloat16),
            pltpu.VMEM((n_col - 1, rows, width), jnp.bfloat16),
            pltpu.VMEM((2, n_col - 1, rows, width), jnp.float32),
            pltpu.VMEM((2, n_col, rows, width), jnp.float32),
            pltpu.VMEM((2, rows, width), jnp.float32),
            pltpu.SemaphoreType.DMA((n_col,)),
            pltpu.SemaphoreType.DMA((n_col,)),
            pltpu.SemaphoreType.DMA((n_col,)),
            pltpu.SemaphoreType.DMA((n_col,)),
            pltpu.SemaphoreType.DMA((n_col - 1,)),
            pltpu.SemaphoreType.DMA((n_col - 1,)),
            pltpu.SemaphoreType.DMA((2, n_col - 1)),
            pltpu.SemaphoreType.DMA((2, n_col - 1)),
            pltpu.SemaphoreType.DMA((2,)),
            pltpu.SemaphoreType.DMA((2,)),
            pltpu.VMEM((2 * row_bits, stacked // n_col, width), jnp.float32),
            pltpu.VMEM((1, n_col, stacked // n_col, width), jnp.float32),
            pltpu.SemaphoreType.DMA((n_col,)),
            pltpu.SemaphoreType.DMA((n_col,)),
            pltpu.SemaphoreType.DMA((row_bits,)),
            pltpu.SemaphoreType.DMA((row_bits,)),
            pltpu.SemaphoreType.DMA((n_col,)),
            pltpu.SemaphoreType.DMA((n_col,)),
        ],
        compiler_params=pltpu.CompilerParams(collective_id=2, has_side_effects=True),
    )(mid, up_part, down_part, parts, self_feature)


def local_kernel(rows_ref, cols_ref, count_ref, window_ref, tiles_ref, feat_ref, w_ref, ws_ref, cot_ref,
                 act_ref, parts_ref, self_ref, mid_ref, up_ref, down_ref, acc, grad_agg, spread):
    tile = tiles_ref.shape[-1]
    nodes = acc.shape[0]
    span = mid_ref.shape[0]
    count = jnp.minimum(count_ref[0], tiles_ref.shape[0])
    acc[...] = jnp.zeros_like(acc)

    def forward(j, carry):
        at = pl.multiple_of(rows_ref[j] * tile, tile)
        acc[pl.ds(at, tile), :] += jnp.dot(
            tiles_ref[j], window_ref[cols_ref[j]], preferred_element_type=jnp.float32
        )
        return carry

    lax.fori_loop(0, count, forward, 0)
    aggregated = acc[...].astype(jnp.bfloat16)
    features = feat_ref[...]
    pre_act = jnp.dot(aggregated, w_ref[...], preferred_element_type=jnp.float32) + jnp.dot(
        features, ws_ref[...], preferred_element_type=jnp.float32
    )
    sigma = jax.nn.sigmoid(pre_act)
    act_ref[...] = (pre_act * sigma).astype(act_ref.dtype)
    grad_pre = (cot_ref[...].astype(jnp.float32) * sigma * (1.0 + pre_act * (1.0 - sigma))).astype(
        jnp.bfloat16
    )
    over_nodes = (((0,), (0,)), ((), ()))
    parts_ref[pl.ds(0, nodes), :] = lax.dot_general(
        aggregated, grad_pre, over_nodes, preferred_element_type=jnp.float32
    )
    parts_ref[pl.ds(nodes, nodes), :] = lax.dot_general(
        features, grad_pre, over_nodes, preferred_element_type=jnp.float32
    )
    by_rows = (((1,), (1,)), ((), ()))
    grad_agg[...] = lax.dot_general(
        grad_pre, w_ref[...], by_rows, preferred_element_type=jnp.float32
    ).astype(jnp.bfloat16)
    self_ref[...] = lax.dot_general(grad_pre, ws_ref[...], by_rows, preferred_element_type=jnp.float32)
    spread[...] = jnp.zeros_like(spread)

    def backward(j, carry):
        at = pl.multiple_of(rows_ref[j] * tile, tile)
        column = cols_ref[j]
        spread[column] += lax.dot_general(
            tiles_ref[j], grad_agg[pl.ds(at, tile), :], over_nodes, preferred_element_type=jnp.float32
        )
        return carry

    lax.fori_loop(0, count, backward, 0)
    mid_ref[...] = spread[pl.ds(span, span)]
    up_ref[...] = spread[pl.ds(2 * span, span)].astype(up_ref.dtype)
    down_ref[...] = spread[pl.ds(0, span)].astype(down_ref.dtype)


def local_math(slot_rows, slot_cols, count, window, tiles, features, weight, weight_self, cotangent):
    nodes, width = features.shape
    span = window.shape[0] // 3
    tile = tiles.shape[-1]
    smem = pl.BlockSpec(memory_space=pltpu.SMEM)
    vmem = pl.BlockSpec(memory_space=pltpu.VMEM)
    return pl.pallas_call(
        local_kernel,
        out_shape=(
            jax.ShapeDtypeStruct((nodes, width), jnp.bfloat16),
            jax.ShapeDtypeStruct((2 * width, width), jnp.float32),
            jax.ShapeDtypeStruct((nodes, width), jnp.float32),
            jax.ShapeDtypeStruct((span, tile, width), jnp.float32),
            jax.ShapeDtypeStruct((span, tile, width), jnp.float32),
            jax.ShapeDtypeStruct((span, tile, width), jnp.float32),
        ),
        in_specs=[smem, smem, smem] + [vmem] * 6,
        out_specs=(vmem,) * 6,
        scratch_shapes=[
            pltpu.VMEM((nodes, width), jnp.float32),
            pltpu.VMEM((nodes, width), jnp.bfloat16),
            pltpu.VMEM((3 * span, tile, width), jnp.float32),
        ],
    )(slot_rows, slot_cols, count, window, tiles, features, weight, weight_self, cotangent)


def shards(features, weight, weight_self, tile_values, tile_rows, tile_cols, tile_count, cotangent):
    tile_block = tile_values[0]
    slot_rows = tile_rows[0]
    slot_cols = tile_cols[0]
    live_count = tile_count[0, 0]
    slot_total = tile_block.shape[0]
    tile_side = tile_block.shape[-1]
    node_rows = features.shape[0]
    width = features.shape[1]
    per_block = node_rows // tile_side
    col_count = lax.axis_size("col")
    row_count = lax.axis_size("row")
    span = col_count * per_block
    window = gather_window(features, row_count, col_count)
    window_tiles = window.reshape(-1, tile_side, width)
    activations, parts, self_feature, mid, up_part, down_part = local_math(
        slot_rows,
        slot_cols,
        tile_count[0],
        window_tiles,
        tile_block,
        features,
        weight,
        weight_self,
        cotangent,
    )
    factor = 1.0 / math.sqrt(node_rows * col_count * row_count)
    feature_grad, summed_parts = reduce_spread(
        mid.reshape(col_count, node_rows, width),
        up_part.reshape(col_count, node_rows, width),
        down_part.reshape(col_count, node_rows, width),
        parts,
        self_feature,
        factor,
        row_count,
        col_count,
    )
    weight_total, self_total = summed_parts[:width], summed_parts[width:]
    return (activations, feature_grad, weight_total, self_total)


def solution(mesh):
    placed = (
        P(("row", "col"), None),
        P(),
        P(),
        P("row", "col", None, None),
        P("row", "col"),
        P("row", "col"),
        P("row", "col"),
        P(("row", "col"), None),
    )
    return jax.shard_map(
        shards,
        mesh=mesh,
        in_specs=placed,
        out_specs=(P(("row", "col"), None), P(("row", "col"), None), P(), P()),
        check_vma=False,
    )
```

```python
import functools
import math

import jax
import jax.numpy as jnp
from jax import lax
from jax.experimental import pallas as pl
from jax.experimental.pallas import tpu as pltpu
from jax.sharding import PartitionSpec as P

MESH = pl.DeviceIdType.MESH


def flip(index, stride):
    bit = (index // stride) % 2
    return index + stride - 2 * stride * bit, bit


def allreduce_partners(n_row, n_col, row, col):
    partners = [(row, peer) for peer in range(n_col)]
    for k in range(n_row.bit_length() - 1):
        partners.append((flip(row, 1 << k)[0], col))
    return partners


class Group:
    def __init__(self, copies, receipts, col):
        self.copies = copies
        self.receipts = receipts
        self.col = col

    def wait(self):
        for peer, (copy, receipt) in enumerate(zip(self.copies, self.receipts)):
            @pl.when(peer != self.col)
            def _():
                copy.wait_send()
                receipt.wait_recv()


def allreduce_steps(n_row, n_col, row, col, x_ref, o_ref, part, gath, rsend, rrecv, dsend, drecv, gsend, grecv):
    row_bits = n_row.bit_length() - 1
    chunk = x_ref.shape[0] // n_col
    mine = pl.ds(pl.multiple_of(col * chunk, 8), chunk)
    copies, receipts = [], []
    for peer in range(n_col):
        copies.append(pltpu.make_async_remote_copy(
            src_ref=x_ref.at[pl.ds(peer * chunk, chunk)],
            dst_ref=gath.at[0, col],
            send_sem=rsend.at[peer],
            recv_sem=rrecv.at[col],
            device_id=(row, peer),
            device_id_type=MESH,
        ))
        receipts.append(pltpu.make_async_remote_copy(
            src_ref=x_ref.at[pl.ds(peer * chunk, chunk)],
            dst_ref=gath.at[0, peer],
            send_sem=rsend.at[peer],
            recv_sem=rrecv.at[peer],
            device_id=(row, peer),
            device_id_type=MESH,
        ))
        pl.when(peer != col)(copies[-1].start)
    yield Group(copies, receipts, col)
    total = x_ref[mine, :]
    for peer in range(n_col):
        total = total + jnp.where(peer == col, jnp.zeros_like(total), gath[0, peer])
    for k in range(row_bits):
        other, _ = flip(row, 1 << k)
        hold = part.at[2 * k]
        hold[...] = total
        copy = pltpu.make_async_remote_copy(
            src_ref=hold,
            dst_ref=part.at[2 * k + 1],
            send_sem=dsend.at[k],
            recv_sem=drecv.at[k],
            device_id=(other, col),
            device_id_type=MESH,
        )
        copy.start()
        yield copy
        total = total + part[2 * k + 1]
    o_ref[mine, :] = total
    copies, receipts = [], []
    for peer in range(n_col):
        copies.append(pltpu.make_async_remote_copy(
            src_ref=o_ref.at[mine],
            dst_ref=o_ref.at[mine],
            send_sem=gsend.at[peer],
            recv_sem=grecv.at[col],
            device_id=(row, peer),
            device_id_type=MESH,
        ))
        receipts.append(pltpu.make_async_remote_copy(
            src_ref=o_ref.at[mine],
            dst_ref=o_ref.at[pl.ds(peer * chunk, chunk)],
            send_sem=gsend.at[peer],
            recv_sem=grecv.at[peer],
            device_id=(row, peer),
            device_id_type=MESH,
        ))
        pl.when(peer != col)(copies[-1].start)
    yield Group(copies, receipts, col)


def run_together(*chains):
    active = list(chains)
    while active:
        copies, kept = [], []
        for chain in active:
            try:
                copies.append(next(chain))
                kept.append(chain)
            except StopIteration:
                pass
        for copy in copies:
            copy.wait()
        active = kept


def ring_position(col, n):
    core = col % 2
    y = col // 2
    return y + core * (n - 1 - 2 * y)


def ring_col(p, n):
    q = p // (n // 2)
    y = p + q * (n - 1 - 2 * p)
    return 2 * y + q


def gather_kernel(n_row, n_col, x_ref, w_ref, ring_send, ring_recv, halo_send, halo_recv, local_sem):
    row = lax.axis_index("row")
    col = lax.axis_index("col")
    p = ring_position(col, n_col)
    succ = ring_col((p + 1) % n_col, n_col)
    pred = ring_col((p + n_col - 1) % n_col, n_col)
    up = (row + 1) % n_row
    down = (row + n_row - 1) % n_row
    half = max(n_row // 2, 1)
    far = {0: row % half == 0, 2: (row + 1) % half == 0}
    barrier = pltpu.get_barrier_semaphore()
    for device in ((row, succ), (row, pred), (up, col), (down, col)):
        pl.semaphore_signal(barrier, inc=1, device_id=device, device_id_type=MESH)
    pl.semaphore_wait(barrier, 4)
    local = pltpu.make_async_copy(x_ref, w_ref.at[1, col], local_sem.at[0])
    local.start()

    def halo(src, block, index):
        copies = {}
        for target, slot in ((up, 0), (down, 2)):
            copies[slot] = pltpu.make_async_remote_copy(
                src_ref=src,
                dst_ref=w_ref.at[slot, block],
                send_sem=halo_send.at[slot // 2, index],
                recv_sem=halo_recv.at[slot // 2, index],
                device_id=(target, col),
                device_id_type=MESH,
            )
        return copies

    halos = [(col, halo(x_ref, col, 0))]
    for copy in halos[0][1].values():
        copy.start()
    sent = col
    for step in range(1, n_col):
        copies = {}
        for group in (1, 0, 2):
            src = x_ref if (step == 1 and group == 1) else w_ref.at[group, sent]
            copies[group] = pltpu.make_async_remote_copy(
                src_ref=src,
                dst_ref=w_ref.at[group, sent],
                send_sem=ring_send.at[group, step - 1],
                recv_sem=ring_recv.at[group, step - 1],
                device_id=(row, succ),
                device_id_type=MESH,
            )
        copies[1].start()
        for group in (0, 2):
            @pl.when(far[group])
            def _():
                if step == 1:
                    halos[0][1][group].wait_recv()
                copies[group].start()
        copies[1].wait()
        for group in (0, 2):
            @pl.when(far[group])
            def _():
                copies[group].wait()
        sent = ring_col((p - step + n_col) % n_col, n_col)
        forward = halo(w_ref.at[1, sent], sent, step)
        halos.append((sent, forward))
        for slot in (0, 2):
            @pl.when(jnp.logical_not(far[2 - slot]))
            def _():
                forward[slot].start()
    for copy in halos[0][1].values():
        copy.wait_send()
    for slot in (0, 2):
        @pl.when(jnp.logical_not(far[slot]))
        def _():
            halos[0][1][slot].wait_recv()
    for _, copies in halos[1:]:
        for slot in (0, 2):
            @pl.when(jnp.logical_not(far[2 - slot]))
            def _():
                copies[slot].wait_send()

            @pl.when(jnp.logical_not(far[slot]))
            def _():
                copies[slot].wait_recv()
    local.wait()


def gather_window(block, n_row, n_col):
    rows, width = block.shape
    return pl.pallas_call(
        functools.partial(gather_kernel, n_row, n_col),
        out_shape=jax.ShapeDtypeStruct((3, n_col, rows, width), block.dtype),
        in_specs=[pl.BlockSpec(memory_space=pltpu.VMEM)],
        out_specs=pl.BlockSpec(memory_space=pltpu.VMEM),
        scratch_shapes=[
            pltpu.SemaphoreType.DMA((3, n_col - 1)),
            pltpu.SemaphoreType.DMA((3, n_col - 1)),
            pltpu.SemaphoreType.DMA((2, n_col)),
            pltpu.SemaphoreType.DMA((2, n_col)),
            pltpu.SemaphoreType.DMA((1,)),
        ],
        compiler_params=pltpu.CompilerParams(collective_id=1, has_side_effects=True),
    )(block)


class Gated:
    def __init__(self, copy, cond):
        self.copy = copy
        self.cond = cond

    def wait(self):
        pl.when(self.cond)(self.copy.wait)


def spread_kernel(n_row, n_col, scale, mid_ref, up_ref, down_ref, parts_ref, self_ref, o_ref, sums_ref, own,
                  up_bf, down_bf,
                  from_down, from_up, ring_in, ring_out, far_in, far_out, far_from, up_send, down_send,
                  from_down_sem, from_up_sem, ring_send, ring_recv, far_send, far_recv, last_send, last_recv,
                  part, gath, rsend, rrecv, dsend, drecv, gsend, grecv):
    row = lax.axis_index("row")
    col = lax.axis_index("col")
    p = ring_position(col, n_col)
    succ = ring_col((p + 1) % n_col, n_col)
    pred = ring_col((p + n_col - 1) % n_col, n_col)
    up = (row + 1) % n_row
    down = (row + n_row - 1) % n_row
    half = max(n_row // 2, 1)
    far_down = row % half == 0
    far_up = (row + 1) % half == 0
    partners = [(row, succ), (row, pred), (up, col), (down, col)]
    partners += allreduce_partners(n_row, n_col, row, col)
    barrier = pltpu.get_barrier_semaphore()
    for device in partners:
        def signal(device=device):
            pl.semaphore_signal(barrier, inc=1, device_id=device, device_id_type=MESH)

        pl.when(jnp.logical_or(device[0] != row, device[1] != col))(signal)
    pl.semaphore_wait(barrier, len(partners) - 1)
    up_bf[...] = up_ref[...].astype(up_bf.dtype)
    down_bf[...] = down_ref[...].astype(down_bf.dtype)
    halos = []
    starts = []
    lead = 2
    for step in range(1, n_col + 1):
        block = ring_col((p - step + 2 * n_col) % n_col, n_col)
        pair = []
        for src, dst, target, send, recv, far in (
            (up_bf, from_down, up, up_send, from_down_sem, far_up),
            (down_bf, from_up, down, down_send, from_up_sem, far_down),
        ):
            copy = pltpu.make_async_remote_copy(
                src_ref=src.at[block],
                dst_ref=dst.at[block],
                send_sem=send.at[step - 1],
                recv_sem=recv.at[step - 1],
                device_id=(target, col),
                device_id_type=MESH,
            )
            pair.append((copy, far))
        halos.append((block, [copy for copy, _ in pair]))
        starts.append(pair)

    def start_halo(index):
        if index < len(starts):
            for copy, far in starts[index]:
                pl.when(jnp.logical_not(far))(copy.start)

    for index in range(lead):
        start_halo(index)

    def local_total(index):
        block, (from_below, from_above) = halos[index]
        pl.when(jnp.logical_not(far_down))(from_below.wait_recv)
        pl.when(jnp.logical_not(far_up))(from_above.wait_recv)
        zero = jnp.zeros(mid_ref.shape[1:], jnp.float32)
        return (
            mid_ref[block]
            + jnp.where(far_down, zero, from_down[block].astype(jnp.float32))
            + jnp.where(far_up, zero, from_up[block].astype(jnp.float32))
        )

    def ring_steps():
        for step in range(1, n_col):
            start_halo(step - 1 + lead)
            value = local_total(step - 1)
            if step > 1:
                value = value + ring_in[step - 2].astype(jnp.float32)
            ring_out[step - 1] = value.astype(ring_out.dtype)
            copy = pltpu.make_async_remote_copy(
                src_ref=ring_out.at[step - 1],
                dst_ref=ring_in.at[step - 1],
                send_sem=ring_send.at[step - 1],
                recv_sem=ring_recv.at[step - 1],
                device_id=(row, succ),
                device_id_type=MESH,
            )
            copy.start()
            yield copy
        start_halo(n_col - 1 + lead)
        own[...] = local_total(n_col - 1) + ring_in[n_col - 2].astype(jnp.float32)

    def far_steps(side, part_ref, far):
        for step in range(1, n_col):
            block = ring_col((p - step + 2 * n_col) % n_col, n_col)
            copy = pltpu.make_async_remote_copy(
                src_ref=far_out.at[side, step - 1],
                dst_ref=far_in.at[side, step - 1],
                send_sem=far_send.at[side, step - 1],
                recv_sem=far_recv.at[side, step - 1],
                device_id=(row, succ),
                device_id_type=MESH,
            )

            def send(step=step, block=block, copy=copy):
                value = part_ref[block]
                if step > 1:
                    value = value + far_in[side, step - 2]
                far_out[side, step - 1] = value
                copy.start()

            pl.when(far)(send)
            yield Gated(copy, far)

        def finish():
            far_out[side, n_col - 1] = part_ref[col] + far_in[side, n_col - 2]

        pl.when(far)(finish)

    run_together(
        allreduce_steps(n_row, n_col, row, col, parts_ref, sums_ref, part, gath,
                        rsend, rrecv, dsend, drecv, gsend, grecv),
        ring_steps(),
        far_steps(0, up_ref, far_up),
        far_steps(1, down_ref, far_down),
    )
    lasts = []
    for side, target, slot, far in ((0, up, 0, far_up), (1, down, 1, far_down)):
        copy = pltpu.make_async_remote_copy(
            src_ref=far_out.at[side, n_col - 1],
            dst_ref=far_from.at[slot],
            send_sem=last_send.at[side],
            recv_sem=last_recv.at[slot],
            device_id=(target, col),
            device_id_type=MESH,
        )
        pl.when(far)(copy.start)
        lasts.append(copy)
    pl.when(far_up)(lasts[0].wait_send)
    pl.when(far_down)(lasts[1].wait_send)
    pl.when(far_down)(lasts[0].wait_recv)
    pl.when(far_up)(lasts[1].wait_recv)
    zero = jnp.zeros(o_ref.shape, jnp.float32)
    total = own[...] + jnp.where(far_down, far_from[0], zero) + jnp.where(far_up, far_from[1], zero)
    o_ref[...] = (total + self_ref[...]).astype(o_ref.dtype)
    sums_ref[...] = sums_ref[...] * scale
    for _, (to_up, to_down) in halos:
        pl.when(jnp.logical_not(far_up))(to_up.wait_send)
        pl.when(jnp.logical_not(far_down))(to_down.wait_send)


def reduce_spread(mid, up_part, down_part, parts, self_feature, scale, n_row, n_col):
    _, rows, width = mid.shape
    col_bits = n_col.bit_length() - 1
    row_bits = n_row.bit_length() - 1
    stacked, _ = parts.shape
    return pl.pallas_call(
        functools.partial(spread_kernel, n_row, n_col, scale),
        out_shape=(
            jax.ShapeDtypeStruct((rows, width), jnp.bfloat16),
            jax.ShapeDtypeStruct(parts.shape, jnp.float32),
        ),
        in_specs=[pl.BlockSpec(memory_space=pltpu.VMEM)] * 5,
        out_specs=(pl.BlockSpec(memory_space=pltpu.VMEM),) * 2,
        scratch_shapes=[
            pltpu.VMEM((rows, width), jnp.float32),
            pltpu.VMEM((n_col, rows, width), jnp.bfloat16),
            pltpu.VMEM((n_col, rows, width), jnp.bfloat16),
            pltpu.VMEM((n_col, rows, width), jnp.bfloat16),
            pltpu.VMEM((n_col, rows, width), jnp.bfloat16),
            pltpu.VMEM((n_col - 1, rows, width), jnp.bfloat16),
            pltpu.VMEM((n_col - 1, rows, width), jnp.bfloat16),
            pltpu.VMEM((2, n_col - 1, rows, width), jnp.float32),
            pltpu.VMEM((2, n_col, rows, width), jnp.float32),
            pltpu.VMEM((2, rows, width), jnp.float32),
            pltpu.SemaphoreType.DMA((n_col,)),
            pltpu.SemaphoreType.DMA((n_col,)),
            pltpu.SemaphoreType.DMA((n_col,)),
            pltpu.SemaphoreType.DMA((n_col,)),
            pltpu.SemaphoreType.DMA((n_col - 1,)),
            pltpu.SemaphoreType.DMA((n_col - 1,)),
            pltpu.SemaphoreType.DMA((2, n_col - 1)),
            pltpu.SemaphoreType.DMA((2, n_col - 1)),
            pltpu.SemaphoreType.DMA((2,)),
            pltpu.SemaphoreType.DMA((2,)),
            pltpu.VMEM((2 * row_bits, stacked // n_col, width), jnp.float32),
            pltpu.VMEM((1, n_col, stacked // n_col, width), jnp.float32),
            pltpu.SemaphoreType.DMA((n_col,)),
            pltpu.SemaphoreType.DMA((n_col,)),
            pltpu.SemaphoreType.DMA((row_bits,)),
            pltpu.SemaphoreType.DMA((row_bits,)),
            pltpu.SemaphoreType.DMA((n_col,)),
            pltpu.SemaphoreType.DMA((n_col,)),
        ],
        compiler_params=pltpu.CompilerParams(collective_id=2, has_side_effects=True),
    )(mid, up_part, down_part, parts, self_feature)


def local_kernel(rows_ref, cols_ref, count_ref, window_ref, tiles_ref, feat_ref, w_ref, ws_ref, cot_ref,
                 act_ref, parts_ref, self_ref, mid_ref, up_ref, down_ref, acc, grad_agg, spread):
    tile = tiles_ref.shape[-1]
    nodes = acc.shape[0]
    span = mid_ref.shape[0]
    count = jnp.minimum(count_ref[0], tiles_ref.shape[0])
    acc[...] = jnp.zeros_like(acc)

    def forward(j, carry):
        at = pl.multiple_of(rows_ref[j] * tile, tile)
        acc[pl.ds(at, tile), :] += jnp.dot(
            tiles_ref[j], window_ref[cols_ref[j]], preferred_element_type=jnp.float32
        )
        return carry

    lax.fori_loop(0, count, forward, 0)
    aggregated = acc[...].astype(jnp.bfloat16)
    features = feat_ref[...]
    pre_act = jnp.dot(aggregated, w_ref[...], preferred_element_type=jnp.float32) + jnp.dot(
        features, ws_ref[...], preferred_element_type=jnp.float32
    )
    sigma = jax.nn.sigmoid(pre_act)
    act_ref[...] = (pre_act * sigma).astype(act_ref.dtype)
    grad_pre = (cot_ref[...].astype(jnp.float32) * sigma * (1.0 + pre_act * (1.0 - sigma))).astype(
        jnp.bfloat16
    )
    over_nodes = (((0,), (0,)), ((), ()))
    parts_ref[pl.ds(0, nodes), :] = lax.dot_general(
        aggregated, grad_pre, over_nodes, preferred_element_type=jnp.float32
    )
    parts_ref[pl.ds(nodes, nodes), :] = lax.dot_general(
        features, grad_pre, over_nodes, preferred_element_type=jnp.float32
    )
    by_rows = (((1,), (1,)), ((), ()))
    grad_agg[...] = lax.dot_general(
        grad_pre, w_ref[...], by_rows, preferred_element_type=jnp.float32
    ).astype(jnp.bfloat16)
    self_ref[...] = lax.dot_general(grad_pre, ws_ref[...], by_rows, preferred_element_type=jnp.float32)
    spread[...] = jnp.zeros_like(spread)

    def backward(j, carry):
        at = pl.multiple_of(rows_ref[j] * tile, tile)
        column = cols_ref[j]
        spread[column] += lax.dot_general(
            tiles_ref[j], grad_agg[pl.ds(at, tile), :], over_nodes, preferred_element_type=jnp.float32
        )
        return carry

    lax.fori_loop(0, count, backward, 0)
    mid_ref[...] = spread[pl.ds(span, span)]
    up_ref[...] = spread[pl.ds(2 * span, span)].astype(up_ref.dtype)
    down_ref[...] = spread[pl.ds(0, span)].astype(down_ref.dtype)


def local_math(slot_rows, slot_cols, count, window, tiles, features, weight, weight_self, cotangent):
    nodes, width = features.shape
    span = window.shape[0] // 3
    tile = tiles.shape[-1]
    smem = pl.BlockSpec(memory_space=pltpu.SMEM)
    vmem = pl.BlockSpec(memory_space=pltpu.VMEM)
    return pl.pallas_call(
        local_kernel,
        out_shape=(
            jax.ShapeDtypeStruct((nodes, width), jnp.bfloat16),
            jax.ShapeDtypeStruct((2 * width, width), jnp.float32),
            jax.ShapeDtypeStruct((nodes, width), jnp.float32),
            jax.ShapeDtypeStruct((span, tile, width), jnp.float32),
            jax.ShapeDtypeStruct((span, tile, width), jnp.float32),
            jax.ShapeDtypeStruct((span, tile, width), jnp.float32),
        ),
        in_specs=[smem, smem, smem] + [vmem] * 6,
        out_specs=(vmem,) * 6,
        scratch_shapes=[
            pltpu.VMEM((nodes, width), jnp.float32),
            pltpu.VMEM((nodes, width), jnp.bfloat16),
            pltpu.VMEM((3 * span, tile, width), jnp.float32),
        ],
    )(slot_rows, slot_cols, count, window, tiles, features, weight, weight_self, cotangent)


def shards(features, weight, weight_self, tile_values, tile_rows, tile_cols, tile_count, cotangent):
    tile_block = tile_values[0]
    slot_rows = tile_rows[0]
    slot_cols = tile_cols[0]
    live_count = tile_count[0, 0]
    slot_total = tile_block.shape[0]
    tile_side = tile_block.shape[-1]
    node_rows = features.shape[0]
    width = features.shape[1]
    per_block = node_rows // tile_side
    col_count = lax.axis_size("col")
    row_count = lax.axis_size("row")
    span = col_count * per_block
    window = gather_window(features, row_count, col_count)
    window_tiles = window.reshape(-1, tile_side, width)
    activations, parts, self_feature, mid, up_part, down_part = local_math(
        slot_rows,
        slot_cols,
        tile_count[0],
        window_tiles,
        tile_block,
        features,
        weight,
        weight_self,
        cotangent,
    )
    factor = 1.0 / math.sqrt(node_rows * col_count * row_count)
    feature_grad, summed_parts = reduce_spread(
        mid.reshape(col_count, node_rows, width),
        up_part.reshape(col_count, node_rows, width),
        down_part.reshape(col_count, node_rows, width),
        parts,
        self_feature,
        factor,
        row_count,
        col_count,
    )
    weight_total, self_total = summed_parts[:width], summed_parts[width:]
    return (activations, feature_grad, weight_total, self_total)


def solution(mesh):
    placed = (
        P(("row", "col"), None),
        P(),
        P(),
        P("row", "col", None, None),
        P("row", "col"),
        P("row", "col"),
        P("row", "col"),
        P(("row", "col"), None),
    )
    return jax.shard_map(
        shards,
        mesh=mesh,
        in_specs=placed,
        out_specs=(P(("row", "col"), None), P(("row", "col"), None), P(), P()),
        check_vma=False,
    )
```

```python
import functools
import math

import jax
import jax.numpy as jnp
from jax import lax
from jax.experimental import pallas as pl
from jax.experimental.pallas import tpu as pltpu
from jax.sharding import PartitionSpec as P

MESH = pl.DeviceIdType.MESH


def flip(index, stride):
    bit = (index // stride) % 2
    return index + stride - 2 * stride * bit, bit


def allreduce_partners(n_row, n_col, row, col):
    partners = [(row, peer) for peer in range(n_col)]
    for k in range(n_row.bit_length() - 1):
        partners.append((flip(row, 1 << k)[0], col))
    return partners


class Group:
    def __init__(self, copies, receipts, col):
        self.copies = copies
        self.receipts = receipts
        self.col = col

    def wait(self):
        for peer, (copy, receipt) in enumerate(zip(self.copies, self.receipts)):
            @pl.when(peer != self.col)
            def _():
                copy.wait_send()
                receipt.wait_recv()


def allreduce_steps(n_row, n_col, row, col, x_ref, o_ref, part, gath, rsend, rrecv, dsend, drecv, gsend, grecv):
    row_bits = n_row.bit_length() - 1
    chunk = x_ref.shape[0] // n_col
    mine = pl.ds(pl.multiple_of(col * chunk, 8), chunk)
    copies, receipts = [], []
    for peer in range(n_col):
        copies.append(pltpu.make_async_remote_copy(
            src_ref=x_ref.at[pl.ds(peer * chunk, chunk)],
            dst_ref=gath.at[0, col],
            send_sem=rsend.at[peer],
            recv_sem=rrecv.at[col],
            device_id=(row, peer),
            device_id_type=MESH,
        ))
        receipts.append(pltpu.make_async_remote_copy(
            src_ref=x_ref.at[pl.ds(peer * chunk, chunk)],
            dst_ref=gath.at[0, peer],
            send_sem=rsend.at[peer],
            recv_sem=rrecv.at[peer],
            device_id=(row, peer),
            device_id_type=MESH,
        ))
        pl.when(peer != col)(copies[-1].start)
    yield Group(copies, receipts, col)
    total = x_ref[mine, :]
    for peer in range(n_col):
        total = total + jnp.where(peer == col, jnp.zeros_like(total), gath[0, peer])
    for k in range(row_bits):
        other, _ = flip(row, 1 << k)
        hold = part.at[2 * k]
        hold[...] = total
        copy = pltpu.make_async_remote_copy(
            src_ref=hold,
            dst_ref=part.at[2 * k + 1],
            send_sem=dsend.at[k],
            recv_sem=drecv.at[k],
            device_id=(other, col),
            device_id_type=MESH,
        )
        copy.start()
        yield copy
        total = total + part[2 * k + 1]
    o_ref[mine, :] = total
    copies, receipts = [], []
    for peer in range(n_col):
        copies.append(pltpu.make_async_remote_copy(
            src_ref=o_ref.at[mine],
            dst_ref=o_ref.at[mine],
            send_sem=gsend.at[peer],
            recv_sem=grecv.at[col],
            device_id=(row, peer),
            device_id_type=MESH,
        ))
        receipts.append(pltpu.make_async_remote_copy(
            src_ref=o_ref.at[mine],
            dst_ref=o_ref.at[pl.ds(peer * chunk, chunk)],
            send_sem=gsend.at[peer],
            recv_sem=grecv.at[peer],
            device_id=(row, peer),
            device_id_type=MESH,
        ))
        pl.when(peer != col)(copies[-1].start)
    yield Group(copies, receipts, col)


def run_together(*chains):
    active = list(chains)
    while active:
        copies, kept = [], []
        for chain in active:
            try:
                copies.append(next(chain))
                kept.append(chain)
            except StopIteration:
                pass
        for copy in copies:
            copy.wait()
        active = kept


def ring_position(col, n):
    core = col % 2
    y = col // 2
    return y + core * (n - 1 - 2 * y)


def ring_col(p, n):
    q = p // (n // 2)
    y = p + q * (n - 1 - 2 * p)
    return 2 * y + q


def gather_kernel(n_row, n_col, x_ref, w_ref, ring_send, ring_recv, halo_send, halo_recv, local_sem):
    row = lax.axis_index("row")
    col = lax.axis_index("col")
    p = ring_position(col, n_col)
    succ = ring_col((p + 1) % n_col, n_col)
    pred = ring_col((p + n_col - 1) % n_col, n_col)
    up = (row + 1) % n_row
    down = (row + n_row - 1) % n_row
    half = max(n_row // 2, 1)
    far = {0: row % half == 0, 2: (row + 1) % half == 0}
    barrier = pltpu.get_barrier_semaphore()
    for device in ((row, succ), (row, pred), (up, col), (down, col)):
        pl.semaphore_signal(barrier, inc=1, device_id=device, device_id_type=MESH)
    pl.semaphore_wait(barrier, 4)
    local = pltpu.make_async_copy(x_ref, w_ref.at[1, col], local_sem.at[0])
    local.start()

    def halo(src, block, index):
        copies = {}
        for target, slot in ((up, 0), (down, 2)):
            copies[slot] = pltpu.make_async_remote_copy(
                src_ref=src,
                dst_ref=w_ref.at[slot, block],
                send_sem=halo_send.at[slot // 2, index],
                recv_sem=halo_recv.at[slot // 2, index],
                device_id=(target, col),
                device_id_type=MESH,
            )
        return copies

    halos = [(col, halo(x_ref, col, 0))]
    for copy in halos[0][1].values():
        copy.start()
    sent = col
    for step in range(1, n_col):
        copies = {}
        for group in (1, 0, 2):
            src = x_ref if (step == 1 and group == 1) else w_ref.at[group, sent]
            copies[group] = pltpu.make_async_remote_copy(
                src_ref=src,
                dst_ref=w_ref.at[group, sent],
                send_sem=ring_send.at[group, step - 1],
                recv_sem=ring_recv.at[group, step - 1],
                device_id=(row, succ),
                device_id_type=MESH,
            )
        copies[1].start()
        for group in (0, 2):
            @pl.when(far[group])
            def _():
                if step == 1:
                    halos[0][1][group].wait_recv()
                copies[group].start()
        copies[1].wait()
        for group in (0, 2):
            @pl.when(far[group])
            def _():
                copies[group].wait()
        sent = ring_col((p - step + n_col) % n_col, n_col)
        forward = halo(w_ref.at[1, sent], sent, step)
        halos.append((sent, forward))
        for slot in (0, 2):
            @pl.when(jnp.logical_not(far[2 - slot]))
            def _():
                forward[slot].start()
    for copy in halos[0][1].values():
        copy.wait_send()
    for slot in (0, 2):
        @pl.when(jnp.logical_not(far[slot]))
        def _():
            halos[0][1][slot].wait_recv()
    for _, copies in halos[1:]:
        for slot in (0, 2):
            @pl.when(jnp.logical_not(far[2 - slot]))
            def _():
                copies[slot].wait_send()

            @pl.when(jnp.logical_not(far[slot]))
            def _():
                copies[slot].wait_recv()
    local.wait()


def gather_window(block, n_row, n_col):
    rows, width = block.shape
    return pl.pallas_call(
        functools.partial(gather_kernel, n_row, n_col),
        out_shape=jax.ShapeDtypeStruct((3, n_col, rows, width), block.dtype),
        in_specs=[pl.BlockSpec(memory_space=pltpu.VMEM)],
        out_specs=pl.BlockSpec(memory_space=pltpu.VMEM),
        scratch_shapes=[
            pltpu.SemaphoreType.DMA((3, n_col - 1)),
            pltpu.SemaphoreType.DMA((3, n_col - 1)),
            pltpu.SemaphoreType.DMA((2, n_col)),
            pltpu.SemaphoreType.DMA((2, n_col)),
            pltpu.SemaphoreType.DMA((1,)),
        ],
        compiler_params=pltpu.CompilerParams(collective_id=1, has_side_effects=True),
    )(block)


class Gated:
    def __init__(self, copy, cond):
        self.copy = copy
        self.cond = cond

    def wait(self):
        pl.when(self.cond)(self.copy.wait)


def spread_kernel(n_row, n_col, scale, spread_ref, parts_ref, self_ref, o_ref, sums_ref, own,
                  up_bf, down_bf,
                  from_down, from_up, ring_in, ring_out, far_in, far_out, far_from, up_send, down_send,
                  from_down_sem, from_up_sem, ring_send, ring_recv, far_send, far_recv, last_send, last_recv,
                  part, gath, rsend, rrecv, dsend, drecv, gsend, grecv):
    row = lax.axis_index("row")
    col = lax.axis_index("col")
    p = ring_position(col, n_col)
    succ = ring_col((p + 1) % n_col, n_col)
    pred = ring_col((p + n_col - 1) % n_col, n_col)
    up = (row + 1) % n_row
    down = (row + n_row - 1) % n_row
    half = max(n_row // 2, 1)
    far_down = row % half == 0
    far_up = (row + 1) % half == 0
    partners = [(row, succ), (row, pred), (up, col), (down, col)]
    partners += allreduce_partners(n_row, n_col, row, col)
    barrier = pltpu.get_barrier_semaphore()
    for device in partners:
        def signal(device=device):
            pl.semaphore_signal(barrier, inc=1, device_id=device, device_id_type=MESH)

        pl.when(jnp.logical_or(device[0] != row, device[1] != col))(signal)
    pl.semaphore_wait(barrier, len(partners) - 1)
    mid_ref, up_ref, down_ref = spread_ref.at[1], spread_ref.at[2], spread_ref.at[0]
    up_bf[...] = up_ref[...].astype(up_bf.dtype)
    down_bf[...] = down_ref[...].astype(down_bf.dtype)
    halos = []
    starts = []
    lead = 2
    for step in range(1, n_col + 1):
        block = ring_col((p - step + 2 * n_col) % n_col, n_col)
        pair = []
        for src, dst, target, send, recv, far in (
            (up_bf, from_down, up, up_send, from_down_sem, far_up),
            (down_bf, from_up, down, down_send, from_up_sem, far_down),
        ):
            copy = pltpu.make_async_remote_copy(
                src_ref=src.at[block],
                dst_ref=dst.at[block],
                send_sem=send.at[step - 1],
                recv_sem=recv.at[step - 1],
                device_id=(target, col),
                device_id_type=MESH,
            )
            pair.append((copy, far))
        halos.append((block, [copy for copy, _ in pair]))
        starts.append(pair)

    def start_halo(index):
        if index < len(starts):
            for copy, far in starts[index]:
                pl.when(jnp.logical_not(far))(copy.start)

    for index in range(lead):
        start_halo(index)

    def local_total(index):
        block, (from_below, from_above) = halos[index]
        pl.when(jnp.logical_not(far_down))(from_below.wait_recv)
        pl.when(jnp.logical_not(far_up))(from_above.wait_recv)
        zero = jnp.zeros(mid_ref.shape[1:], jnp.float32)
        return (
            mid_ref[block]
            + jnp.where(far_down, zero, from_down[block].astype(jnp.float32))
            + jnp.where(far_up, zero, from_up[block].astype(jnp.float32))
        )

    def ring_steps():
        for step in range(1, n_col):
            start_halo(step - 1 + lead)
            value = local_total(step - 1)
            if step > 1:
                value = value + ring_in[step - 2].astype(jnp.float32)
            ring_out[step - 1] = value.astype(ring_out.dtype)
            copy = pltpu.make_async_remote_copy(
                src_ref=ring_out.at[step - 1],
                dst_ref=ring_in.at[step - 1],
                send_sem=ring_send.at[step - 1],
                recv_sem=ring_recv.at[step - 1],
                device_id=(row, succ),
                device_id_type=MESH,
            )
            copy.start()
            yield copy
        start_halo(n_col - 1 + lead)
        own[...] = local_total(n_col - 1) + ring_in[n_col - 2].astype(jnp.float32)

    def far_steps(side, part_ref, far):
        for step in range(1, n_col):
            block = ring_col((p - step + 2 * n_col) % n_col, n_col)
            copy = pltpu.make_async_remote_copy(
                src_ref=far_out.at[side, step - 1],
                dst_ref=far_in.at[side, step - 1],
                send_sem=far_send.at[side, step - 1],
                recv_sem=far_recv.at[side, step - 1],
                device_id=(row, succ),
                device_id_type=MESH,
            )

            def send(step=step, block=block, copy=copy):
                value = part_ref[block]
                if step > 1:
                    value = value + far_in[side, step - 2]
                far_out[side, step - 1] = value
                copy.start()

            pl.when(far)(send)
            yield Gated(copy, far)

        def finish():
            far_out[side, n_col - 1] = part_ref[col] + far_in[side, n_col - 2]

        pl.when(far)(finish)

    run_together(
        allreduce_steps(n_row, n_col, row, col, parts_ref, sums_ref, part, gath,
                        rsend, rrecv, dsend, drecv, gsend, grecv),
        ring_steps(),
        far_steps(0, up_ref, far_up),
        far_steps(1, down_ref, far_down),
    )
    lasts = []
    for side, target, slot, far in ((0, up, 0, far_up), (1, down, 1, far_down)):
        copy = pltpu.make_async_remote_copy(
            src_ref=far_out.at[side, n_col - 1],
            dst_ref=far_from.at[slot],
            send_sem=last_send.at[side],
            recv_sem=last_recv.at[slot],
            device_id=(target, col),
            device_id_type=MESH,
        )
        pl.when(far)(copy.start)
        lasts.append(copy)
    pl.when(far_up)(lasts[0].wait_send)
    pl.when(far_down)(lasts[1].wait_send)
    pl.when(far_down)(lasts[0].wait_recv)
    pl.when(far_up)(lasts[1].wait_recv)
    zero = jnp.zeros(o_ref.shape, jnp.float32)
    total = own[...] + jnp.where(far_down, far_from[0], zero) + jnp.where(far_up, far_from[1], zero)
    o_ref[...] = (total + self_ref[...]).astype(o_ref.dtype)
    sums_ref[...] = sums_ref[...] * scale
    for _, (to_up, to_down) in halos:
        pl.when(jnp.logical_not(far_up))(to_up.wait_send)
        pl.when(jnp.logical_not(far_down))(to_down.wait_send)


def reduce_spread(spread, parts, self_feature, scale, n_row, n_col):
    _, _, rows, width = spread.shape
    col_bits = n_col.bit_length() - 1
    row_bits = n_row.bit_length() - 1
    stacked, _ = parts.shape
    return pl.pallas_call(
        functools.partial(spread_kernel, n_row, n_col, scale),
        out_shape=(
            jax.ShapeDtypeStruct((rows, width), jnp.bfloat16),
            jax.ShapeDtypeStruct(parts.shape, jnp.float32),
        ),
        in_specs=[pl.BlockSpec(memory_space=pltpu.VMEM)] * 3,
        out_specs=(pl.BlockSpec(memory_space=pltpu.VMEM),) * 2,
        scratch_shapes=[
            pltpu.VMEM((rows, width), jnp.float32),
            pltpu.VMEM((n_col, rows, width), jnp.bfloat16),
            pltpu.VMEM((n_col, rows, width), jnp.bfloat16),
            pltpu.VMEM((n_col, rows, width), jnp.bfloat16),
            pltpu.VMEM((n_col, rows, width), jnp.bfloat16),
            pltpu.VMEM((n_col - 1, rows, width), jnp.bfloat16),
            pltpu.VMEM((n_col - 1, rows, width), jnp.bfloat16),
            pltpu.VMEM((2, n_col - 1, rows, width), jnp.float32),
            pltpu.VMEM((2, n_col, rows, width), jnp.float32),
            pltpu.VMEM((2, rows, width), jnp.float32),
            pltpu.SemaphoreType.DMA((n_col,)),
            pltpu.SemaphoreType.DMA((n_col,)),
            pltpu.SemaphoreType.DMA((n_col,)),
            pltpu.SemaphoreType.DMA((n_col,)),
            pltpu.SemaphoreType.DMA((n_col - 1,)),
            pltpu.SemaphoreType.DMA((n_col - 1,)),
            pltpu.SemaphoreType.DMA((2, n_col - 1)),
            pltpu.SemaphoreType.DMA((2, n_col - 1)),
            pltpu.SemaphoreType.DMA((2,)),
            pltpu.SemaphoreType.DMA((2,)),
            pltpu.VMEM((2 * row_bits, stacked // n_col, width), jnp.float32),
            pltpu.VMEM((1, n_col, stacked // n_col, width), jnp.float32),
            pltpu.SemaphoreType.DMA((n_col,)),
            pltpu.SemaphoreType.DMA((n_col,)),
            pltpu.SemaphoreType.DMA((row_bits,)),
            pltpu.SemaphoreType.DMA((row_bits,)),
            pltpu.SemaphoreType.DMA((n_col,)),
            pltpu.SemaphoreType.DMA((n_col,)),
        ],
        compiler_params=pltpu.CompilerParams(collective_id=2, has_side_effects=True),
    )(spread, parts, self_feature)


def local_kernel(rows_ref, cols_ref, count_ref, window_ref, tiles_ref, feat_ref, w_ref, ws_ref, cot_ref,
                 act_ref, parts_ref, self_ref, spread, acc, grad_agg):
    tile = tiles_ref.shape[-1]
    nodes = acc.shape[0]
    count = jnp.minimum(count_ref[0], tiles_ref.shape[0])
    acc[...] = jnp.zeros_like(acc)

    def forward(j, carry):
        at = pl.multiple_of(rows_ref[j] * tile, tile)
        acc[pl.ds(at, tile), :] += jnp.dot(
            tiles_ref[j], window_ref[cols_ref[j]], preferred_element_type=jnp.float32
        )
        return carry

    lax.fori_loop(0, count, forward, 0)
    aggregated = acc[...].astype(jnp.bfloat16)
    features = feat_ref[...]
    pre_act = jnp.dot(aggregated, w_ref[...], preferred_element_type=jnp.float32) + jnp.dot(
        features, ws_ref[...], preferred_element_type=jnp.float32
    )
    sigma = jax.nn.sigmoid(pre_act)
    act_ref[...] = (pre_act * sigma).astype(act_ref.dtype)
    grad_pre = (cot_ref[...].astype(jnp.float32) * sigma * (1.0 + pre_act * (1.0 - sigma))).astype(
        jnp.bfloat16
    )
    over_nodes = (((0,), (0,)), ((), ()))
    parts_ref[pl.ds(0, nodes), :] = lax.dot_general(
        aggregated, grad_pre, over_nodes, preferred_element_type=jnp.float32
    )
    parts_ref[pl.ds(nodes, nodes), :] = lax.dot_general(
        features, grad_pre, over_nodes, preferred_element_type=jnp.float32
    )
    by_rows = (((1,), (1,)), ((), ()))
    grad_agg[...] = lax.dot_general(
        grad_pre, w_ref[...], by_rows, preferred_element_type=jnp.float32
    ).astype(jnp.bfloat16)
    self_ref[...] = lax.dot_general(grad_pre, ws_ref[...], by_rows, preferred_element_type=jnp.float32)
    spread[...] = jnp.zeros_like(spread)

    def backward(j, carry):
        at = pl.multiple_of(rows_ref[j] * tile, tile)
        column = cols_ref[j]
        spread[column] += lax.dot_general(
            tiles_ref[j], grad_agg[pl.ds(at, tile), :], over_nodes, preferred_element_type=jnp.float32
        )
        return carry

    lax.fori_loop(0, count, backward, 0)


def local_math(slot_rows, slot_cols, count, window, tiles, features, weight, weight_self, cotangent):
    nodes, width = features.shape
    span = window.shape[0] // 3
    tile = tiles.shape[-1]
    smem = pl.BlockSpec(memory_space=pltpu.SMEM)
    vmem = pl.BlockSpec(memory_space=pltpu.VMEM)
    return pl.pallas_call(
        local_kernel,
        out_shape=(
            jax.ShapeDtypeStruct((nodes, width), jnp.bfloat16),
            jax.ShapeDtypeStruct((2 * width, width), jnp.float32),
            jax.ShapeDtypeStruct((nodes, width), jnp.float32),
            jax.ShapeDtypeStruct((3 * span, tile, width), jnp.float32),
        ),
        in_specs=[smem, smem, smem] + [vmem] * 6,
        out_specs=(vmem,) * 4,
        scratch_shapes=[
            pltpu.VMEM((nodes, width), jnp.float32),
            pltpu.VMEM((nodes, width), jnp.bfloat16),
        ],
    )(slot_rows, slot_cols, count, window, tiles, features, weight, weight_self, cotangent)


def shards(features, weight, weight_self, tile_values, tile_rows, tile_cols, tile_count, cotangent):
    tile_block = tile_values[0]
    slot_rows = tile_rows[0]
    slot_cols = tile_cols[0]
    live_count = tile_count[0, 0]
    slot_total = tile_block.shape[0]
    tile_side = tile_block.shape[-1]
    node_rows = features.shape[0]
    width = features.shape[1]
    per_block = node_rows // tile_side
    col_count = lax.axis_size("col")
    row_count = lax.axis_size("row")
    span = col_count * per_block
    window = gather_window(features, row_count, col_count)
    window_tiles = window.reshape(-1, tile_side, width)
    activations, parts, self_feature, spread = local_math(
        slot_rows,
        slot_cols,
        tile_count[0],
        window_tiles,
        tile_block,
        features,
        weight,
        weight_self,
        cotangent,
    )
    factor = 1.0 / math.sqrt(node_rows * col_count * row_count)
    feature_grad, summed_parts = reduce_spread(
        spread.reshape(3, col_count, node_rows, width),
        parts,
        self_feature,
        factor,
        row_count,
        col_count,
    )
    weight_total, self_total = summed_parts[:width], summed_parts[width:]
    return (activations, feature_grad, weight_total, self_total)


def solution(mesh):
    placed = (
        P(("row", "col"), None),
        P(),
        P(),
        P("row", "col", None, None),
        P("row", "col"),
        P("row", "col"),
        P("row", "col"),
        P(("row", "col"), None),
    )
    return jax.shard_map(
        shards,
        mesh=mesh,
        in_specs=placed,
        out_specs=(P(("row", "col"), None), P(("row", "col"), None), P(), P()),
        check_vma=False,
    )
```

```python
import functools
import math

import jax
import jax.numpy as jnp
from jax import lax
from jax.experimental import pallas as pl
from jax.experimental.pallas import tpu as pltpu
from jax.sharding import PartitionSpec as P

MESH = pl.DeviceIdType.MESH


def flip(index, stride):
    bit = (index // stride) % 2
    return index + stride - 2 * stride * bit, bit


def allreduce_partners(n_row, n_col, row, col):
    partners = [(row, peer) for peer in range(n_col)]
    for k in range(n_row.bit_length() - 1):
        partners.append((flip(row, 1 << k)[0], col))
    return partners


class Group:
    def __init__(self, copies, receipts, col):
        self.copies = copies
        self.receipts = receipts
        self.col = col

    def wait(self):
        for peer, (copy, receipt) in enumerate(zip(self.copies, self.receipts)):
            @pl.when(peer != self.col)
            def _():
                copy.wait_send()
                receipt.wait_recv()


def allreduce_steps(n_row, n_col, row, col, x_ref, o_ref, part, gath, rsend, rrecv, dsend, drecv, gsend, grecv):
    row_bits = n_row.bit_length() - 1
    chunk = x_ref.shape[0] // n_col
    mine = pl.ds(pl.multiple_of(col * chunk, 8), chunk)
    copies, receipts = [], []
    for peer in range(n_col):
        copies.append(pltpu.make_async_remote_copy(
            src_ref=x_ref.at[pl.ds(peer * chunk, chunk)],
            dst_ref=gath.at[0, col],
            send_sem=rsend.at[peer],
            recv_sem=rrecv.at[col],
            device_id=(row, peer),
            device_id_type=MESH,
        ))
        receipts.append(pltpu.make_async_remote_copy(
            src_ref=x_ref.at[pl.ds(peer * chunk, chunk)],
            dst_ref=gath.at[0, peer],
            send_sem=rsend.at[peer],
            recv_sem=rrecv.at[peer],
            device_id=(row, peer),
            device_id_type=MESH,
        ))
        pl.when(peer != col)(copies[-1].start)
    yield Group(copies, receipts, col)
    total = x_ref[mine, :]
    for peer in range(n_col):
        total = total + jnp.where(peer == col, jnp.zeros_like(total), gath[0, peer])
    for k in range(row_bits):
        other, _ = flip(row, 1 << k)
        hold = part.at[2 * k]
        hold[...] = total
        copy = pltpu.make_async_remote_copy(
            src_ref=hold,
            dst_ref=part.at[2 * k + 1],
            send_sem=dsend.at[k],
            recv_sem=drecv.at[k],
            device_id=(other, col),
            device_id_type=MESH,
        )
        copy.start()
        yield copy
        total = total + part[2 * k + 1]
    o_ref[mine, :] = total
    copies, receipts = [], []
    for peer in range(n_col):
        copies.append(pltpu.make_async_remote_copy(
            src_ref=o_ref.at[mine],
            dst_ref=o_ref.at[mine],
            send_sem=gsend.at[peer],
            recv_sem=grecv.at[col],
            device_id=(row, peer),
            device_id_type=MESH,
        ))
        receipts.append(pltpu.make_async_remote_copy(
            src_ref=o_ref.at[mine],
            dst_ref=o_ref.at[pl.ds(peer * chunk, chunk)],
            send_sem=gsend.at[peer],
            recv_sem=grecv.at[peer],
            device_id=(row, peer),
            device_id_type=MESH,
        ))
        pl.when(peer != col)(copies[-1].start)
    yield Group(copies, receipts, col)


def run_together(*chains):
    active = list(chains)
    while active:
        copies, kept = [], []
        for chain in active:
            try:
                copies.append(next(chain))
                kept.append(chain)
            except StopIteration:
                pass
        for copy in copies:
            copy.wait()
        active = kept


def ring_position(col, n):
    core = col % 2
    y = col // 2
    return y + core * (n - 1 - 2 * y)


def ring_col(p, n):
    q = p // (n // 2)
    y = p + q * (n - 1 - 2 * p)
    return 2 * y + q


def gather_kernel(n_row, n_col, x_ref, w_ref, ring_send, ring_recv, halo_send, halo_recv, local_sem):
    row = lax.axis_index("row")
    col = lax.axis_index("col")
    p = ring_position(col, n_col)
    succ = ring_col((p + 1) % n_col, n_col)
    pred = ring_col((p + n_col - 1) % n_col, n_col)
    up = (row + 1) % n_row
    down = (row + n_row - 1) % n_row
    half = max(n_row // 2, 1)
    far = {0: row % half == 0, 2: (row + 1) % half == 0}
    barrier = pltpu.get_barrier_semaphore()
    for device in ((row, succ), (row, pred), (up, col), (down, col)):
        pl.semaphore_signal(barrier, inc=1, device_id=device, device_id_type=MESH)
    pl.semaphore_wait(barrier, 4)
    local = pltpu.make_async_copy(x_ref, w_ref.at[1, col], local_sem.at[0])
    local.start()

    def halo(src, block, index):
        copies = {}
        for target, slot in ((up, 0), (down, 2)):
            copies[slot] = pltpu.make_async_remote_copy(
                src_ref=src,
                dst_ref=w_ref.at[slot, block],
                send_sem=halo_send.at[slot // 2, index],
                recv_sem=halo_recv.at[slot // 2, index],
                device_id=(target, col),
                device_id_type=MESH,
            )
        return copies

    halos = [(col, halo(x_ref, col, 0))]
    for copy in halos[0][1].values():
        copy.start()
    sent = col
    pending = []
    for step in range(1, n_col):
        copies = {}
        for group in (1, 0, 2):
            src = x_ref if (step == 1 and group == 1) else w_ref.at[group, sent]
            copies[group] = pltpu.make_async_remote_copy(
                src_ref=src,
                dst_ref=w_ref.at[group, sent],
                send_sem=ring_send.at[group, step - 1],
                recv_sem=ring_recv.at[group, step - 1],
                device_id=(row, succ),
                device_id_type=MESH,
            )
        copies[1].start()
        for group in (0, 2):
            @pl.when(far[group])
            def _():
                if step == 1:
                    halos[0][1][group].wait_recv()
                copies[group].start()
        copies[1].wait_recv()
        pending.append((copies[1], None))
        for group in (0, 2):
            pl.when(far[group])(copies[group].wait_recv)
            pending.append((copies[group], far[group]))
        sent = ring_col((p - step + n_col) % n_col, n_col)
        forward = halo(w_ref.at[1, sent], sent, step)
        halos.append((sent, forward))
        for slot in (0, 2):
            @pl.when(jnp.logical_not(far[2 - slot]))
            def _():
                forward[slot].start()
    for copy, cond in pending:
        if cond is None:
            copy.wait_send()
        else:
            pl.when(cond)(copy.wait_send)
    for copy in halos[0][1].values():
        copy.wait_send()
    for slot in (0, 2):
        @pl.when(jnp.logical_not(far[slot]))
        def _():
            halos[0][1][slot].wait_recv()
    for _, copies in halos[1:]:
        for slot in (0, 2):
            @pl.when(jnp.logical_not(far[2 - slot]))
            def _():
                copies[slot].wait_send()

            @pl.when(jnp.logical_not(far[slot]))
            def _():
                copies[slot].wait_recv()
    local.wait()


def gather_window(block, n_row, n_col):
    rows, width = block.shape
    return pl.pallas_call(
        functools.partial(gather_kernel, n_row, n_col),
        out_shape=jax.ShapeDtypeStruct((3, n_col, rows, width), block.dtype),
        in_specs=[pl.BlockSpec(memory_space=pltpu.VMEM)],
        out_specs=pl.BlockSpec(memory_space=pltpu.VMEM),
        scratch_shapes=[
            pltpu.SemaphoreType.DMA((3, n_col - 1)),
            pltpu.SemaphoreType.DMA((3, n_col - 1)),
            pltpu.SemaphoreType.DMA((2, n_col)),
            pltpu.SemaphoreType.DMA((2, n_col)),
            pltpu.SemaphoreType.DMA((1,)),
        ],
        compiler_params=pltpu.CompilerParams(collective_id=1, has_side_effects=True),
    )(block)


class Gated:
    def __init__(self, copy, cond, pending):
        self.copy = copy
        self.cond = cond
        self.pending = pending

    def wait(self):
        pl.when(self.cond)(self.copy.wait_recv)
        self.pending.append(self)

    def finish(self):
        pl.when(self.cond)(self.copy.wait_send)


def spread_kernel(n_row, n_col, scale, spread_ref, parts_ref, self_ref, o_ref, sums_ref, own,
                  up_bf, down_bf,
                  from_down, from_up, ring_in, ring_out, far_in, far_out, far_from, up_send, down_send,
                  from_down_sem, from_up_sem, ring_send, ring_recv, far_send, far_recv, last_send, last_recv,
                  part, gath, rsend, rrecv, dsend, drecv, gsend, grecv):
    row = lax.axis_index("row")
    col = lax.axis_index("col")
    p = ring_position(col, n_col)
    succ = ring_col((p + 1) % n_col, n_col)
    pred = ring_col((p + n_col - 1) % n_col, n_col)
    up = (row + 1) % n_row
    down = (row + n_row - 1) % n_row
    half = max(n_row // 2, 1)
    far_down = row % half == 0
    far_up = (row + 1) % half == 0
    partners = [(row, succ), (row, pred), (up, col), (down, col)]
    partners += allreduce_partners(n_row, n_col, row, col)
    barrier = pltpu.get_barrier_semaphore()
    for device in partners:
        def signal(device=device):
            pl.semaphore_signal(barrier, inc=1, device_id=device, device_id_type=MESH)

        pl.when(jnp.logical_or(device[0] != row, device[1] != col))(signal)
    pl.semaphore_wait(barrier, len(partners) - 1)
    mid_ref, up_ref, down_ref = spread_ref.at[1], spread_ref.at[2], spread_ref.at[0]
    up_bf[...] = up_ref[...].astype(up_bf.dtype)
    down_bf[...] = down_ref[...].astype(down_bf.dtype)
    halos = []
    starts = []
    lead = 2
    for step in range(1, n_col + 1):
        block = ring_col((p - step + 2 * n_col) % n_col, n_col)
        pair = []
        for src, dst, target, send, recv, far in (
            (up_bf, from_down, up, up_send, from_down_sem, far_up),
            (down_bf, from_up, down, down_send, from_up_sem, far_down),
        ):
            copy = pltpu.make_async_remote_copy(
                src_ref=src.at[block],
                dst_ref=dst.at[block],
                send_sem=send.at[step - 1],
                recv_sem=recv.at[step - 1],
                device_id=(target, col),
                device_id_type=MESH,
            )
            pair.append((copy, far))
        halos.append((block, [copy for copy, _ in pair]))
        starts.append(pair)

    def start_halo(index):
        if index < len(starts):
            for copy, far in starts[index]:
                pl.when(jnp.logical_not(far))(copy.start)

    for index in range(lead):
        start_halo(index)

    def local_total(index):
        block, (from_below, from_above) = halos[index]
        pl.when(jnp.logical_not(far_down))(from_below.wait_recv)
        pl.when(jnp.logical_not(far_up))(from_above.wait_recv)
        zero = jnp.zeros(mid_ref.shape[1:], jnp.float32)
        return (
            mid_ref[block]
            + jnp.where(far_down, zero, from_down[block].astype(jnp.float32))
            + jnp.where(far_up, zero, from_up[block].astype(jnp.float32))
        )

    def ring_steps():
        for step in range(1, n_col):
            start_halo(step - 1 + lead)
            value = local_total(step - 1)
            if step > 1:
                value = value + ring_in[step - 2].astype(jnp.float32)
            ring_out[step - 1] = value.astype(ring_out.dtype)
            copy = pltpu.make_async_remote_copy(
                src_ref=ring_out.at[step - 1],
                dst_ref=ring_in.at[step - 1],
                send_sem=ring_send.at[step - 1],
                recv_sem=ring_recv.at[step - 1],
                device_id=(row, succ),
                device_id_type=MESH,
            )
            copy.start()
            yield Gated(copy, True, pending)
        start_halo(n_col - 1 + lead)
        own[...] = local_total(n_col - 1) + ring_in[n_col - 2].astype(jnp.float32)

    def far_steps(side, part_ref, far):
        for step in range(1, n_col):
            block = ring_col((p - step + 2 * n_col) % n_col, n_col)
            copy = pltpu.make_async_remote_copy(
                src_ref=far_out.at[side, step - 1],
                dst_ref=far_in.at[side, step - 1],
                send_sem=far_send.at[side, step - 1],
                recv_sem=far_recv.at[side, step - 1],
                device_id=(row, succ),
                device_id_type=MESH,
            )

            def send(step=step, block=block, copy=copy):
                value = part_ref[block]
                if step > 1:
                    value = value + far_in[side, step - 2]
                far_out[side, step - 1] = value
                copy.start()

            pl.when(far)(send)
            yield Gated(copy, far, pending)

        def finish():
            far_out[side, n_col - 1] = part_ref[col] + far_in[side, n_col - 2]

        pl.when(far)(finish)

    pending = []
    run_together(
        allreduce_steps(n_row, n_col, row, col, parts_ref, sums_ref, part, gath,
                        rsend, rrecv, dsend, drecv, gsend, grecv),
        ring_steps(),
        far_steps(0, up_ref, far_up),
        far_steps(1, down_ref, far_down),
    )
    for item in pending:
        item.finish()
    lasts = []
    for side, target, slot, far in ((0, up, 0, far_up), (1, down, 1, far_down)):
        copy = pltpu.make_async_remote_copy(
            src_ref=far_out.at[side, n_col - 1],
            dst_ref=far_from.at[slot],
            send_sem=last_send.at[side],
            recv_sem=last_recv.at[slot],
            device_id=(target, col),
            device_id_type=MESH,
        )
        pl.when(far)(copy.start)
        lasts.append(copy)
    pl.when(far_up)(lasts[0].wait_send)
    pl.when(far_down)(lasts[1].wait_send)
    pl.when(far_down)(lasts[0].wait_recv)
    pl.when(far_up)(lasts[1].wait_recv)
    zero = jnp.zeros(o_ref.shape, jnp.float32)
    total = own[...] + jnp.where(far_down, far_from[0], zero) + jnp.where(far_up, far_from[1], zero)
    o_ref[...] = (total + self_ref[...]).astype(o_ref.dtype)
    sums_ref[...] = sums_ref[...] * scale
    for _, (to_up, to_down) in halos:
        pl.when(jnp.logical_not(far_up))(to_up.wait_send)
        pl.when(jnp.logical_not(far_down))(to_down.wait_send)


def reduce_spread(spread, parts, self_feature, scale, n_row, n_col):
    _, _, rows, width = spread.shape
    col_bits = n_col.bit_length() - 1
    row_bits = n_row.bit_length() - 1
    stacked, _ = parts.shape
    return pl.pallas_call(
        functools.partial(spread_kernel, n_row, n_col, scale),
        out_shape=(
            jax.ShapeDtypeStruct((rows, width), jnp.bfloat16),
            jax.ShapeDtypeStruct(parts.shape, jnp.float32),
        ),
        in_specs=[pl.BlockSpec(memory_space=pltpu.VMEM)] * 3,
        out_specs=(pl.BlockSpec(memory_space=pltpu.VMEM),) * 2,
        scratch_shapes=[
            pltpu.VMEM((rows, width), jnp.float32),
            pltpu.VMEM((n_col, rows, width), jnp.bfloat16),
            pltpu.VMEM((n_col, rows, width), jnp.bfloat16),
            pltpu.VMEM((n_col, rows, width), jnp.bfloat16),
            pltpu.VMEM((n_col, rows, width), jnp.bfloat16),
            pltpu.VMEM((n_col - 1, rows, width), jnp.bfloat16),
            pltpu.VMEM((n_col - 1, rows, width), jnp.bfloat16),
            pltpu.VMEM((2, n_col - 1, rows, width), jnp.float32),
            pltpu.VMEM((2, n_col, rows, width), jnp.float32),
            pltpu.VMEM((2, rows, width), jnp.float32),
            pltpu.SemaphoreType.DMA((n_col,)),
            pltpu.SemaphoreType.DMA((n_col,)),
            pltpu.SemaphoreType.DMA((n_col,)),
            pltpu.SemaphoreType.DMA((n_col,)),
            pltpu.SemaphoreType.DMA((n_col - 1,)),
            pltpu.SemaphoreType.DMA((n_col - 1,)),
            pltpu.SemaphoreType.DMA((2, n_col - 1)),
            pltpu.SemaphoreType.DMA((2, n_col - 1)),
            pltpu.SemaphoreType.DMA((2,)),
            pltpu.SemaphoreType.DMA((2,)),
            pltpu.VMEM((2 * row_bits, stacked // n_col, width), jnp.float32),
            pltpu.VMEM((1, n_col, stacked // n_col, width), jnp.float32),
            pltpu.SemaphoreType.DMA((n_col,)),
            pltpu.SemaphoreType.DMA((n_col,)),
            pltpu.SemaphoreType.DMA((row_bits,)),
            pltpu.SemaphoreType.DMA((row_bits,)),
            pltpu.SemaphoreType.DMA((n_col,)),
            pltpu.SemaphoreType.DMA((n_col,)),
        ],
        compiler_params=pltpu.CompilerParams(collective_id=2, has_side_effects=True),
    )(spread, parts, self_feature)


def local_kernel(rows_ref, cols_ref, count_ref, window_ref, tiles_ref, feat_ref, w_ref, ws_ref, cot_ref,
                 act_ref, parts_ref, self_ref, spread, acc, grad_agg):
    tile = tiles_ref.shape[-1]
    nodes = acc.shape[0]
    count = jnp.minimum(count_ref[0], tiles_ref.shape[0])
    acc[...] = jnp.zeros_like(acc)

    def forward(j, carry):
        at = pl.multiple_of(rows_ref[j] * tile, tile)
        acc[pl.ds(at, tile), :] += jnp.dot(
            tiles_ref[j], window_ref[cols_ref[j]], preferred_element_type=jnp.float32
        )
        return carry

    lax.fori_loop(0, count, forward, 0)
    aggregated = acc[...].astype(jnp.bfloat16)
    features = feat_ref[...]
    pre_act = jnp.dot(aggregated, w_ref[...], preferred_element_type=jnp.float32) + jnp.dot(
        features, ws_ref[...], preferred_element_type=jnp.float32
    )
    sigma = jax.nn.sigmoid(pre_act)
    act_ref[...] = (pre_act * sigma).astype(act_ref.dtype)
    grad_pre = (cot_ref[...].astype(jnp.float32) * sigma * (1.0 + pre_act * (1.0 - sigma))).astype(
        jnp.bfloat16
    )
    over_nodes = (((0,), (0,)), ((), ()))
    parts_ref[pl.ds(0, nodes), :] = lax.dot_general(
        aggregated, grad_pre, over_nodes, preferred_element_type=jnp.float32
    )
    parts_ref[pl.ds(nodes, nodes), :] = lax.dot_general(
        features, grad_pre, over_nodes, preferred_element_type=jnp.float32
    )
    by_rows = (((1,), (1,)), ((), ()))
    grad_agg[...] = lax.dot_general(
        grad_pre, w_ref[...], by_rows, preferred_element_type=jnp.float32
    ).astype(jnp.bfloat16)
    self_ref[...] = lax.dot_general(grad_pre, ws_ref[...], by_rows, preferred_element_type=jnp.float32)
    spread[...] = jnp.zeros_like(spread)

    def backward(j, carry):
        at = pl.multiple_of(rows_ref[j] * tile, tile)
        column = cols_ref[j]
        spread[column] += lax.dot_general(
            tiles_ref[j], grad_agg[pl.ds(at, tile), :], over_nodes, preferred_element_type=jnp.float32
        )
        return carry

    lax.fori_loop(0, count, backward, 0)


def local_math(slot_rows, slot_cols, count, window, tiles, features, weight, weight_self, cotangent):
    nodes, width = features.shape
    span = window.shape[0] // 3
    tile = tiles.shape[-1]
    smem = pl.BlockSpec(memory_space=pltpu.SMEM)
    vmem = pl.BlockSpec(memory_space=pltpu.VMEM)
    return pl.pallas_call(
        local_kernel,
        out_shape=(
            jax.ShapeDtypeStruct((nodes, width), jnp.bfloat16),
            jax.ShapeDtypeStruct((2 * width, width), jnp.float32),
            jax.ShapeDtypeStruct((nodes, width), jnp.float32),
            jax.ShapeDtypeStruct((3 * span, tile, width), jnp.float32),
        ),
        in_specs=[smem, smem, smem] + [vmem] * 6,
        out_specs=(vmem,) * 4,
        scratch_shapes=[
            pltpu.VMEM((nodes, width), jnp.float32),
            pltpu.VMEM((nodes, width), jnp.bfloat16),
        ],
    )(slot_rows, slot_cols, count, window, tiles, features, weight, weight_self, cotangent)


def shards(features, weight, weight_self, tile_values, tile_rows, tile_cols, tile_count, cotangent):
    tile_block = tile_values[0]
    slot_rows = tile_rows[0]
    slot_cols = tile_cols[0]
    live_count = tile_count[0, 0]
    slot_total = tile_block.shape[0]
    tile_side = tile_block.shape[-1]
    node_rows = features.shape[0]
    width = features.shape[1]
    per_block = node_rows // tile_side
    col_count = lax.axis_size("col")
    row_count = lax.axis_size("row")
    span = col_count * per_block
    window = gather_window(features, row_count, col_count)
    window_tiles = window.reshape(-1, tile_side, width)
    activations, parts, self_feature, spread = local_math(
        slot_rows,
        slot_cols,
        tile_count[0],
        window_tiles,
        tile_block,
        features,
        weight,
        weight_self,
        cotangent,
    )
    factor = 1.0 / math.sqrt(node_rows * col_count * row_count)
    feature_grad, summed_parts = reduce_spread(
        spread.reshape(3, col_count, node_rows, width),
        parts,
        self_feature,
        factor,
        row_count,
        col_count,
    )
    weight_total, self_total = summed_parts[:width], summed_parts[width:]
    return (activations, feature_grad, weight_total, self_total)


def solution(mesh):
    placed = (
        P(("row", "col"), None),
        P(),
        P(),
        P("row", "col", None, None),
        P("row", "col"),
        P("row", "col"),
        P("row", "col"),
        P(("row", "col"), None),
    )
    return jax.shard_map(
        shards,
        mesh=mesh,
        in_specs=placed,
        out_specs=(P(("row", "col"), None), P(("row", "col"), None), P(), P()),
        check_vma=False,
    )
```

```python
import functools
import math

import jax
import jax.numpy as jnp
from jax import lax
from jax.experimental import pallas as pl
from jax.experimental.pallas import tpu as pltpu
from jax.sharding import PartitionSpec as P

MESH = pl.DeviceIdType.MESH


def flip(index, stride):
    bit = (index // stride) % 2
    return index + stride - 2 * stride * bit, bit


def allreduce_partners(n_row, n_col, row, col):
    partners = [(row, peer) for peer in range(n_col)]
    for k in range(n_row.bit_length() - 1):
        partners.append((flip(row, 1 << k)[0], col))
    return partners


class Group:
    def __init__(self, copies, receipts, col):
        self.copies = copies
        self.receipts = receipts
        self.col = col

    def wait(self):
        for peer, (copy, receipt) in enumerate(zip(self.copies, self.receipts)):
            @pl.when(peer != self.col)
            def _():
                copy.wait_send()
                receipt.wait_recv()


def allreduce_steps(n_row, n_col, row, col, x_ref, o_ref, part, gath, rsend, rrecv, dsend, drecv, gsend, grecv):
    row_bits = n_row.bit_length() - 1
    chunk = x_ref.shape[0] // n_col
    mine = pl.ds(pl.multiple_of(col * chunk, 8), chunk)
    copies, receipts = [], []
    for peer in range(n_col):
        copies.append(pltpu.make_async_remote_copy(
            src_ref=x_ref.at[pl.ds(peer * chunk, chunk)],
            dst_ref=gath.at[0, col],
            send_sem=rsend.at[peer],
            recv_sem=rrecv.at[col],
            device_id=(row, peer),
            device_id_type=MESH,
        ))
        receipts.append(pltpu.make_async_remote_copy(
            src_ref=x_ref.at[pl.ds(peer * chunk, chunk)],
            dst_ref=gath.at[0, peer],
            send_sem=rsend.at[peer],
            recv_sem=rrecv.at[peer],
            device_id=(row, peer),
            device_id_type=MESH,
        ))
        pl.when(peer != col)(copies[-1].start)
    yield Group(copies, receipts, col)
    total = x_ref[mine, :]
    for peer in range(n_col):
        total = total + jnp.where(peer == col, jnp.zeros_like(total), gath[0, peer])
    for k in range(row_bits):
        other, _ = flip(row, 1 << k)
        hold = part.at[2 * k]
        hold[...] = total
        copy = pltpu.make_async_remote_copy(
            src_ref=hold,
            dst_ref=part.at[2 * k + 1],
            send_sem=dsend.at[k],
            recv_sem=drecv.at[k],
            device_id=(other, col),
            device_id_type=MESH,
        )
        copy.start()
        yield copy
        total = total + part[2 * k + 1]
    o_ref[mine, :] = total
    copies, receipts = [], []
    for peer in range(n_col):
        copies.append(pltpu.make_async_remote_copy(
            src_ref=o_ref.at[mine],
            dst_ref=o_ref.at[mine],
            send_sem=gsend.at[peer],
            recv_sem=grecv.at[col],
            device_id=(row, peer),
            device_id_type=MESH,
        ))
        receipts.append(pltpu.make_async_remote_copy(
            src_ref=o_ref.at[mine],
            dst_ref=o_ref.at[pl.ds(peer * chunk, chunk)],
            send_sem=gsend.at[peer],
            recv_sem=grecv.at[peer],
            device_id=(row, peer),
            device_id_type=MESH,
        ))
        pl.when(peer != col)(copies[-1].start)
    yield Group(copies, receipts, col)


def run_together(*chains):
    active = list(chains)
    while active:
        copies, kept = [], []
        for chain in active:
            try:
                copies.append(next(chain))
                kept.append(chain)
            except StopIteration:
                pass
        for copy in copies:
            copy.wait()
        active = kept


def ring_position(col, n):
    core = col % 2
    y = col // 2
    return y + core * (n - 1 - 2 * y)


def ring_col(p, n):
    q = p // (n // 2)
    y = p + q * (n - 1 - 2 * p)
    return 2 * y + q


def gather_kernel(n_row, n_col, x_ref, w_ref, ring_send, ring_recv, halo_send, halo_recv, local_sem):
    row = lax.axis_index("row")
    col = lax.axis_index("col")
    p = ring_position(col, n_col)
    succ = ring_col((p + 1) % n_col, n_col)
    pred = ring_col((p + n_col - 1) % n_col, n_col)
    up = (row + 1) % n_row
    down = (row + n_row - 1) % n_row
    half = max(n_row // 2, 1)
    far = {0: row % half == 0, 2: (row + 1) % half == 0}
    barrier = pltpu.get_barrier_semaphore()
    for device in ((row, succ), (row, pred), (up, col), (down, col)):
        pl.semaphore_signal(barrier, inc=1, device_id=device, device_id_type=MESH)
    pl.semaphore_wait(barrier, 4)
    local = pltpu.make_async_copy(x_ref, w_ref.at[1, col], local_sem.at[0])
    local.start()

    def halo(src, block, index):
        copies = {}
        for target, slot in ((up, 0), (down, 2)):
            copies[slot] = pltpu.make_async_remote_copy(
                src_ref=src,
                dst_ref=w_ref.at[slot, block],
                send_sem=halo_send.at[slot // 2, index],
                recv_sem=halo_recv.at[slot // 2, index],
                device_id=(target, col),
                device_id_type=MESH,
            )
        return copies

    halos = [(col, halo(x_ref, col, 0))]
    for copy in halos[0][1].values():
        copy.start()
    sent = col
    for step in range(1, n_col):
        copies = {}
        for group in (1, 0, 2):
            src = x_ref if (step == 1 and group == 1) else w_ref.at[group, sent]
            copies[group] = pltpu.make_async_remote_copy(
                src_ref=src,
                dst_ref=w_ref.at[group, sent],
                send_sem=ring_send.at[group, step - 1],
                recv_sem=ring_recv.at[group, step - 1],
                device_id=(row, succ),
                device_id_type=MESH,
            )
        copies[1].start()
        for group in (0, 2):
            @pl.when(far[group])
            def _():
                if step == 1:
                    halos[0][1][group].wait_recv()
                copies[group].start()
        copies[1].wait()
        for group in (0, 2):
            @pl.when(far[group])
            def _():
                copies[group].wait()
        sent = ring_col((p - step + n_col) % n_col, n_col)
        forward = halo(w_ref.at[1, sent], sent, step)
        halos.append((sent, forward))
        for slot in (0, 2):
            @pl.when(jnp.logical_not(far[2 - slot]))
            def _():
                forward[slot].start()
    for copy in halos[0][1].values():
        copy.wait_send()
    for slot in (0, 2):
        @pl.when(jnp.logical_not(far[slot]))
        def _():
            halos[0][1][slot].wait_recv()
    for _, copies in halos[1:]:
        for slot in (0, 2):
            @pl.when(jnp.logical_not(far[2 - slot]))
            def _():
                copies[slot].wait_send()

            @pl.when(jnp.logical_not(far[slot]))
            def _():
                copies[slot].wait_recv()
    local.wait()


def gather_window(block, n_row, n_col):
    rows, width = block.shape
    return pl.pallas_call(
        functools.partial(gather_kernel, n_row, n_col),
        out_shape=jax.ShapeDtypeStruct((3, n_col, rows, width), block.dtype),
        in_specs=[pl.BlockSpec(memory_space=pltpu.VMEM)],
        out_specs=pl.BlockSpec(memory_space=pltpu.VMEM),
        scratch_shapes=[
            pltpu.SemaphoreType.DMA((3, n_col - 1)),
            pltpu.SemaphoreType.DMA((3, n_col - 1)),
            pltpu.SemaphoreType.DMA((2, n_col)),
            pltpu.SemaphoreType.DMA((2, n_col)),
            pltpu.SemaphoreType.DMA((1,)),
        ],
        compiler_params=pltpu.CompilerParams(collective_id=1, has_side_effects=True),
    )(block)


class Gated:
    def __init__(self, copy, cond):
        self.copy = copy
        self.cond = cond

    def wait(self):
        pl.when(self.cond)(self.copy.wait)


def spread_kernel(n_row, n_col, scale, spread_ref, parts_ref, self_ref, o_ref, sums_ref, own,
                  up_bf, down_bf,
                  from_down, from_up, ring_in, ring_out, far_in, far_out, far_from, up_send, down_send,
                  from_down_sem, from_up_sem, ring_send, ring_recv, far_send, far_recv, last_send, last_recv,
                  part, gath, rsend, rrecv, dsend, drecv, gsend, grecv):
    row = lax.axis_index("row")
    col = lax.axis_index("col")
    p = ring_position(col, n_col)
    succ = ring_col((p + 1) % n_col, n_col)
    pred = ring_col((p + n_col - 1) % n_col, n_col)
    up = (row + 1) % n_row
    down = (row + n_row - 1) % n_row
    half = max(n_row // 2, 1)
    far_down = row % half == 0
    far_up = (row + 1) % half == 0
    partners = [(row, succ), (row, pred), (up, col), (down, col)]
    partners += allreduce_partners(n_row, n_col, row, col)
    barrier = pltpu.get_barrier_semaphore()
    for device in partners:
        def signal(device=device):
            pl.semaphore_signal(barrier, inc=1, device_id=device, device_id_type=MESH)

        pl.when(jnp.logical_or(device[0] != row, device[1] != col))(signal)
    pl.semaphore_wait(barrier, len(partners) - 1)
    mid_ref, up_ref, down_ref = spread_ref.at[1], spread_ref.at[2], spread_ref.at[0]
    up_bf[...] = up_ref[...].astype(up_bf.dtype)
    down_bf[...] = down_ref[...].astype(down_bf.dtype)
    halos = []
    starts = []
    lead = 3
    for step in range(1, n_col + 1):
        block = ring_col((p - step + 2 * n_col) % n_col, n_col)
        pair = []
        for src, dst, target, send, recv, far in (
            (up_bf, from_down, up, up_send, from_down_sem, far_up),
            (down_bf, from_up, down, down_send, from_up_sem, far_down),
        ):
            copy = pltpu.make_async_remote_copy(
                src_ref=src.at[block],
                dst_ref=dst.at[block],
                send_sem=send.at[step - 1],
                recv_sem=recv.at[step - 1],
                device_id=(target, col),
                device_id_type=MESH,
            )
            pair.append((copy, far))
        halos.append((block, [copy for copy, _ in pair]))
        starts.append(pair)

    def start_halo(index):
        if index < len(starts):
            for copy, far in starts[index]:
                pl.when(jnp.logical_not(far))(copy.start)

    for index in range(lead):
        start_halo(index)

    def local_total(index):
        block, (from_below, from_above) = halos[index]
        pl.when(jnp.logical_not(far_down))(from_below.wait_recv)
        pl.when(jnp.logical_not(far_up))(from_above.wait_recv)
        zero = jnp.zeros(mid_ref.shape[1:], jnp.float32)
        return (
            mid_ref[block]
            + jnp.where(far_down, zero, from_down[block].astype(jnp.float32))
            + jnp.where(far_up, zero, from_up[block].astype(jnp.float32))
        )

    def ring_steps():
        for step in range(1, n_col):
            start_halo(step - 1 + lead)
            value = local_total(step - 1)
            if step > 1:
                value = value + ring_in[step - 2].astype(jnp.float32)
            ring_out[step - 1] = value.astype(ring_out.dtype)
            copy = pltpu.make_async_remote_copy(
                src_ref=ring_out.at[step - 1],
                dst_ref=ring_in.at[step - 1],
                send_sem=ring_send.at[step - 1],
                recv_sem=ring_recv.at[step - 1],
                device_id=(row, succ),
                device_id_type=MESH,
            )
            copy.start()
            yield copy
        start_halo(n_col - 1 + lead)
        own[...] = local_total(n_col - 1) + ring_in[n_col - 2].astype(jnp.float32)

    def far_steps(side, part_ref, far):
        for step in range(1, n_col):
            block = ring_col((p - step + 2 * n_col) % n_col, n_col)
            copy = pltpu.make_async_remote_copy(
                src_ref=far_out.at[side, step - 1],
                dst_ref=far_in.at[side, step - 1],
                send_sem=far_send.at[side, step - 1],
                recv_sem=far_recv.at[side, step - 1],
                device_id=(row, succ),
                device_id_type=MESH,
            )

            def send(step=step, block=block, copy=copy):
                value = part_ref[block]
                if step > 1:
                    value = value + far_in[side, step - 2]
                far_out[side, step - 1] = value
                copy.start()

            pl.when(far)(send)
            yield Gated(copy, far)

        def finish():
            far_out[side, n_col - 1] = part_ref[col] + far_in[side, n_col - 2]

        pl.when(far)(finish)

    run_together(
        allreduce_steps(n_row, n_col, row, col, parts_ref, sums_ref, part, gath,
                        rsend, rrecv, dsend, drecv, gsend, grecv),
        ring_steps(),
        far_steps(0, up_ref, far_up),
        far_steps(1, down_ref, far_down),
    )
    lasts = []
    for side, target, slot, far in ((0, up, 0, far_up), (1, down, 1, far_down)):
        copy = pltpu.make_async_remote_copy(
            src_ref=far_out.at[side, n_col - 1],
            dst_ref=far_from.at[slot],
            send_sem=last_send.at[side],
            recv_sem=last_recv.at[slot],
            device_id=(target, col),
            device_id_type=MESH,
        )
        pl.when(far)(copy.start)
        lasts.append(copy)
    pl.when(far_up)(lasts[0].wait_send)
    pl.when(far_down)(lasts[1].wait_send)
    pl.when(far_down)(lasts[0].wait_recv)
    pl.when(far_up)(lasts[1].wait_recv)
    zero = jnp.zeros(o_ref.shape, jnp.float32)
    total = own[...] + jnp.where(far_down, far_from[0], zero) + jnp.where(far_up, far_from[1], zero)
    o_ref[...] = (total + self_ref[...]).astype(o_ref.dtype)
    sums_ref[...] = sums_ref[...] * scale
    for _, (to_up, to_down) in halos:
        pl.when(jnp.logical_not(far_up))(to_up.wait_send)
        pl.when(jnp.logical_not(far_down))(to_down.wait_send)


def reduce_spread(spread, parts, self_feature, scale, n_row, n_col):
    _, _, rows, width = spread.shape
    col_bits = n_col.bit_length() - 1
    row_bits = n_row.bit_length() - 1
    stacked, _ = parts.shape
    return pl.pallas_call(
        functools.partial(spread_kernel, n_row, n_col, scale),
        out_shape=(
            jax.ShapeDtypeStruct((rows, width), jnp.bfloat16),
            jax.ShapeDtypeStruct(parts.shape, jnp.float32),
        ),
        in_specs=[pl.BlockSpec(memory_space=pltpu.VMEM)] * 3,
        out_specs=(pl.BlockSpec(memory_space=pltpu.VMEM),) * 2,
        scratch_shapes=[
            pltpu.VMEM((rows, width), jnp.float32),
            pltpu.VMEM((n_col, rows, width), jnp.bfloat16),
            pltpu.VMEM((n_col, rows, width), jnp.bfloat16),
            pltpu.VMEM((n_col, rows, width), jnp.bfloat16),
            pltpu.VMEM((n_col, rows, width), jnp.bfloat16),
            pltpu.VMEM((n_col - 1, rows, width), jnp.bfloat16),
            pltpu.VMEM((n_col - 1, rows, width), jnp.bfloat16),
            pltpu.VMEM((2, n_col - 1, rows, width), jnp.float32),
            pltpu.VMEM((2, n_col, rows, width), jnp.float32),
            pltpu.VMEM((2, rows, width), jnp.float32),
            pltpu.SemaphoreType.DMA((n_col,)),
            pltpu.SemaphoreType.DMA((n_col,)),
            pltpu.SemaphoreType.DMA((n_col,)),
            pltpu.SemaphoreType.DMA((n_col,)),
            pltpu.SemaphoreType.DMA((n_col - 1,)),
            pltpu.SemaphoreType.DMA((n_col - 1,)),
            pltpu.SemaphoreType.DMA((2, n_col - 1)),
            pltpu.SemaphoreType.DMA((2, n_col - 1)),
            pltpu.SemaphoreType.DMA((2,)),
            pltpu.SemaphoreType.DMA((2,)),
            pltpu.VMEM((2 * row_bits, stacked // n_col, width), jnp.float32),
            pltpu.VMEM((1, n_col, stacked // n_col, width), jnp.float32),
            pltpu.SemaphoreType.DMA((n_col,)),
            pltpu.SemaphoreType.DMA((n_col,)),
            pltpu.SemaphoreType.DMA((row_bits,)),
            pltpu.SemaphoreType.DMA((row_bits,)),
            pltpu.SemaphoreType.DMA((n_col,)),
            pltpu.SemaphoreType.DMA((n_col,)),
        ],
        compiler_params=pltpu.CompilerParams(collective_id=2, has_side_effects=True),
    )(spread, parts, self_feature)


def local_kernel(rows_ref, cols_ref, count_ref, window_ref, tiles_ref, feat_ref, w_ref, ws_ref, cot_ref,
                 act_ref, parts_ref, self_ref, spread, acc, grad_agg):
    tile = tiles_ref.shape[-1]
    nodes = acc.shape[0]
    count = jnp.minimum(count_ref[0], tiles_ref.shape[0])
    acc[...] = jnp.zeros_like(acc)

    def forward(j, carry):
        at = pl.multiple_of(rows_ref[j] * tile, tile)
        acc[pl.ds(at, tile), :] += jnp.dot(
            tiles_ref[j], window_ref[cols_ref[j]], preferred_element_type=jnp.float32
        )
        return carry

    lax.fori_loop(0, count, forward, 0)
    aggregated = acc[...].astype(jnp.bfloat16)
    features = feat_ref[...]
    pre_act = jnp.dot(aggregated, w_ref[...], preferred_element_type=jnp.float32) + jnp.dot(
        features, ws_ref[...], preferred_element_type=jnp.float32
    )
    sigma = jax.nn.sigmoid(pre_act)
    act_ref[...] = (pre_act * sigma).astype(act_ref.dtype)
    grad_pre = (cot_ref[...].astype(jnp.float32) * sigma * (1.0 + pre_act * (1.0 - sigma))).astype(
        jnp.bfloat16
    )
    over_nodes = (((0,), (0,)), ((), ()))
    parts_ref[pl.ds(0, nodes), :] = lax.dot_general(
        aggregated, grad_pre, over_nodes, preferred_element_type=jnp.float32
    )
    parts_ref[pl.ds(nodes, nodes), :] = lax.dot_general(
        features, grad_pre, over_nodes, preferred_element_type=jnp.float32
    )
    by_rows = (((1,), (1,)), ((), ()))
    grad_agg[...] = lax.dot_general(
        grad_pre, w_ref[...], by_rows, preferred_element_type=jnp.float32
    ).astype(jnp.bfloat16)
    self_ref[...] = lax.dot_general(grad_pre, ws_ref[...], by_rows, preferred_element_type=jnp.float32)
    spread[...] = jnp.zeros_like(spread)

    def backward(j, carry):
        at = pl.multiple_of(rows_ref[j] * tile, tile)
        column = cols_ref[j]
        spread[column] += lax.dot_general(
            tiles_ref[j], grad_agg[pl.ds(at, tile), :], over_nodes, preferred_element_type=jnp.float32
        )
        return carry

    lax.fori_loop(0, count, backward, 0)


def local_math(slot_rows, slot_cols, count, window, tiles, features, weight, weight_self, cotangent):
    nodes, width = features.shape
    span = window.shape[0] // 3
    tile = tiles.shape[-1]
    smem = pl.BlockSpec(memory_space=pltpu.SMEM)
    vmem = pl.BlockSpec(memory_space=pltpu.VMEM)
    return pl.pallas_call(
        local_kernel,
        out_shape=(
            jax.ShapeDtypeStruct((nodes, width), jnp.bfloat16),
            jax.ShapeDtypeStruct((2 * width, width), jnp.float32),
            jax.ShapeDtypeStruct((nodes, width), jnp.float32),
            jax.ShapeDtypeStruct((3 * span, tile, width), jnp.float32),
        ),
        in_specs=[smem, smem, smem] + [vmem] * 6,
        out_specs=(vmem,) * 4,
        scratch_shapes=[
            pltpu.VMEM((nodes, width), jnp.float32),
            pltpu.VMEM((nodes, width), jnp.bfloat16),
        ],
    )(slot_rows, slot_cols, count, window, tiles, features, weight, weight_self, cotangent)


def shards(features, weight, weight_self, tile_values, tile_rows, tile_cols, tile_count, cotangent):
    tile_block = tile_values[0]
    slot_rows = tile_rows[0]
    slot_cols = tile_cols[0]
    live_count = tile_count[0, 0]
    slot_total = tile_block.shape[0]
    tile_side = tile_block.shape[-1]
    node_rows = features.shape[0]
    width = features.shape[1]
    per_block = node_rows // tile_side
    col_count = lax.axis_size("col")
    row_count = lax.axis_size("row")
    span = col_count * per_block
    window = gather_window(features, row_count, col_count)
    window_tiles = window.reshape(-1, tile_side, width)
    activations, parts, self_feature, spread = local_math(
        slot_rows,
        slot_cols,
        tile_count[0],
        window_tiles,
        tile_block,
        features,
        weight,
        weight_self,
        cotangent,
    )
    factor = 1.0 / math.sqrt(node_rows * col_count * row_count)
    feature_grad, summed_parts = reduce_spread(
        spread.reshape(3, col_count, node_rows, width),
        parts,
        self_feature,
        factor,
        row_count,
        col_count,
    )
    weight_total, self_total = summed_parts[:width], summed_parts[width:]
    return (activations, feature_grad, weight_total, self_total)


def solution(mesh):
    placed = (
        P(("row", "col"), None),
        P(),
        P(),
        P("row", "col", None, None),
        P("row", "col"),
        P("row", "col"),
        P("row", "col"),
        P(("row", "col"), None),
    )
    return jax.shard_map(
        shards,
        mesh=mesh,
        in_specs=placed,
        out_specs=(P(("row", "col"), None), P(("row", "col"), None), P(), P()),
        check_vma=False,
    )
```

```python
import functools
import math

import jax
import jax.numpy as jnp
from jax import lax
from jax.experimental import pallas as pl
from jax.experimental.pallas import tpu as pltpu
from jax.sharding import PartitionSpec as P

MESH = pl.DeviceIdType.MESH


def flip(index, stride):
    bit = (index // stride) % 2
    return index + stride - 2 * stride * bit, bit


def allreduce_partners(n_row, n_col, row, col):
    partners = [(row, peer) for peer in range(n_col)]
    for k in range(n_row.bit_length() - 1):
        partners.append((flip(row, 1 << k)[0], col))
    return partners


class Group:
    def __init__(self, copies, receipts, col):
        self.copies = copies
        self.receipts = receipts
        self.col = col

    def wait(self):
        for peer, (copy, receipt) in enumerate(zip(self.copies, self.receipts)):
            @pl.when(peer != self.col)
            def _():
                copy.wait_send()
                receipt.wait_recv()


def allreduce_steps(n_row, n_col, row, col, x_ref, o_ref, part, gath, rsend, rrecv, dsend, drecv, gsend, grecv):
    row_bits = n_row.bit_length() - 1
    chunk = x_ref.shape[0] // n_col
    mine = pl.ds(pl.multiple_of(col * chunk, 8), chunk)
    copies, receipts = [], []
    for peer in range(n_col):
        copies.append(pltpu.make_async_remote_copy(
            src_ref=x_ref.at[pl.ds(peer * chunk, chunk)],
            dst_ref=gath.at[0, col],
            send_sem=rsend.at[peer],
            recv_sem=rrecv.at[col],
            device_id=(row, peer),
            device_id_type=MESH,
        ))
        receipts.append(pltpu.make_async_remote_copy(
            src_ref=x_ref.at[pl.ds(peer * chunk, chunk)],
            dst_ref=gath.at[0, peer],
            send_sem=rsend.at[peer],
            recv_sem=rrecv.at[peer],
            device_id=(row, peer),
            device_id_type=MESH,
        ))
        pl.when(peer != col)(copies[-1].start)
    yield Group(copies, receipts, col)
    total = x_ref[mine, :]
    for peer in range(n_col):
        total = total + jnp.where(peer == col, jnp.zeros_like(total), gath[0, peer])
    for k in range(row_bits):
        other, _ = flip(row, 1 << k)
        hold = part.at[2 * k]
        hold[...] = total
        copy = pltpu.make_async_remote_copy(
            src_ref=hold,
            dst_ref=part.at[2 * k + 1],
            send_sem=dsend.at[k],
            recv_sem=drecv.at[k],
            device_id=(other, col),
            device_id_type=MESH,
        )
        copy.start()
        yield copy
        total = total + part[2 * k + 1]
    o_ref[mine, :] = total
    copies, receipts = [], []
    for peer in range(n_col):
        copies.append(pltpu.make_async_remote_copy(
            src_ref=o_ref.at[mine],
            dst_ref=o_ref.at[mine],
            send_sem=gsend.at[peer],
            recv_sem=grecv.at[col],
            device_id=(row, peer),
            device_id_type=MESH,
        ))
        receipts.append(pltpu.make_async_remote_copy(
            src_ref=o_ref.at[mine],
            dst_ref=o_ref.at[pl.ds(peer * chunk, chunk)],
            send_sem=gsend.at[peer],
            recv_sem=grecv.at[peer],
            device_id=(row, peer),
            device_id_type=MESH,
        ))
        pl.when(peer != col)(copies[-1].start)
    yield Group(copies, receipts, col)


def run_together(*chains):
    active = list(chains)
    while active:
        copies, kept = [], []
        for chain in active:
            try:
                copies.append(next(chain))
                kept.append(chain)
            except StopIteration:
                pass
        for copy in copies:
            copy.wait()
        active = kept


def ring_position(col, n):
    core = col % 2
    y = col // 2
    return y + core * (n - 1 - 2 * y)


def ring_col(p, n):
    q = p // (n // 2)
    y = p + q * (n - 1 - 2 * p)
    return 2 * y + q


def gather_kernel(n_row, n_col, x_ref, w_ref, ring_send, ring_recv, halo_send, halo_recv, local_sem):
    row = lax.axis_index("row")
    col = lax.axis_index("col")
    p = ring_position(col, n_col)
    succ = ring_col((p + 1) % n_col, n_col)
    pred = ring_col((p + n_col - 1) % n_col, n_col)
    up = (row + 1) % n_row
    down = (row + n_row - 1) % n_row
    half = max(n_row // 2, 1)
    far = {0: row % half == 0, 2: (row + 1) % half == 0}
    barrier = pltpu.get_barrier_semaphore()
    for device in ((row, succ), (row, pred), (up, col), (down, col)):
        pl.semaphore_signal(barrier, inc=1, device_id=device, device_id_type=MESH)
    pl.semaphore_wait(barrier, 4)
    local = pltpu.make_async_copy(x_ref, w_ref.at[1, col], local_sem.at[0])
    local.start()

    def halo(src, block, index):
        copies = {}
        for target, slot in ((up, 0), (down, 2)):
            copies[slot] = pltpu.make_async_remote_copy(
                src_ref=src,
                dst_ref=w_ref.at[slot, block],
                send_sem=halo_send.at[slot // 2, index],
                recv_sem=halo_recv.at[slot // 2, index],
                device_id=(target, col),
                device_id_type=MESH,
            )
        return copies

    halos = [(col, halo(x_ref, col, 0))]
    for copy in halos[0][1].values():
        copy.start()
    sent = col
    for step in range(1, n_col):
        copies = {}
        for group in (1, 0, 2):
            src = x_ref if (step == 1 and group == 1) else w_ref.at[group, sent]
            copies[group] = pltpu.make_async_remote_copy(
                src_ref=src,
                dst_ref=w_ref.at[group, sent],
                send_sem=ring_send.at[group, step - 1],
                recv_sem=ring_recv.at[group, step - 1],
                device_id=(row, succ),
                device_id_type=MESH,
            )
        copies[1].start()
        for group in (0, 2):
            @pl.when(far[group])
            def _():
                if step == 1:
                    halos[0][1][group].wait_recv()
                copies[group].start()
        copies[1].wait()
        for group in (0, 2):
            @pl.when(far[group])
            def _():
                copies[group].wait()
        sent = ring_col((p - step + n_col) % n_col, n_col)
        forward = halo(w_ref.at[1, sent], sent, step)
        halos.append((sent, forward))
        for slot in (0, 2):
            @pl.when(jnp.logical_not(far[2 - slot]))
            def _():
                forward[slot].start()
    for copy in halos[0][1].values():
        copy.wait_send()
    for slot in (0, 2):
        @pl.when(jnp.logical_not(far[slot]))
        def _():
            halos[0][1][slot].wait_recv()
    for _, copies in halos[1:]:
        for slot in (0, 2):
            @pl.when(jnp.logical_not(far[2 - slot]))
            def _():
                copies[slot].wait_send()

            @pl.when(jnp.logical_not(far[slot]))
            def _():
                copies[slot].wait_recv()
    local.wait()


def gather_window(block, n_row, n_col):
    rows, width = block.shape
    return pl.pallas_call(
        functools.partial(gather_kernel, n_row, n_col),
        out_shape=jax.ShapeDtypeStruct((3, n_col, rows, width), block.dtype),
        in_specs=[pl.BlockSpec(memory_space=pltpu.VMEM)],
        out_specs=pl.BlockSpec(memory_space=pltpu.VMEM),
        scratch_shapes=[
            pltpu.SemaphoreType.DMA((3, n_col - 1)),
            pltpu.SemaphoreType.DMA((3, n_col - 1)),
            pltpu.SemaphoreType.DMA((2, n_col)),
            pltpu.SemaphoreType.DMA((2, n_col)),
            pltpu.SemaphoreType.DMA((1,)),
        ],
        compiler_params=pltpu.CompilerParams(collective_id=1, has_side_effects=True),
    )(block)


class Gated:
    def __init__(self, copy, cond):
        self.copy = copy
        self.cond = cond

    def wait(self):
        pl.when(self.cond)(self.copy.wait)


def spread_kernel(n_row, n_col, scale, spread_ref, parts_ref, self_ref, o_ref, sums_ref, own,
                  up_bf, down_bf,
                  from_down, from_up, ring_in, ring_out, far_in, far_out, far_from, up_send, down_send,
                  from_down_sem, from_up_sem, ring_send, ring_recv, far_send, far_recv, last_send, last_recv,
                  part, gath, rsend, rrecv, dsend, drecv, gsend, grecv):
    row = lax.axis_index("row")
    col = lax.axis_index("col")
    p = ring_position(col, n_col)
    succ = ring_col((p + 1) % n_col, n_col)
    pred = ring_col((p + n_col - 1) % n_col, n_col)
    up = (row + 1) % n_row
    down = (row + n_row - 1) % n_row
    half = max(n_row // 2, 1)
    far_down = row % half == 0
    far_up = (row + 1) % half == 0
    partners = [(row, succ), (row, pred), (up, col), (down, col)]
    partners += allreduce_partners(n_row, n_col, row, col)
    barrier = pltpu.get_barrier_semaphore()
    for device in partners:
        def signal(device=device):
            pl.semaphore_signal(barrier, inc=1, device_id=device, device_id_type=MESH)

        pl.when(jnp.logical_or(device[0] != row, device[1] != col))(signal)
    pl.semaphore_wait(barrier, len(partners) - 1)
    mid_ref, up_ref, down_ref = spread_ref.at[1], spread_ref.at[2], spread_ref.at[0]
    up_bf[...] = up_ref[...].astype(up_bf.dtype)
    down_bf[...] = down_ref[...].astype(down_bf.dtype)
    halos = []
    starts = []
    lead = 1
    for step in range(1, n_col + 1):
        block = ring_col((p - step + 2 * n_col) % n_col, n_col)
        pair = []
        for src, dst, target, send, recv, far in (
            (up_bf, from_down, up, up_send, from_down_sem, far_up),
            (down_bf, from_up, down, down_send, from_up_sem, far_down),
        ):
            copy = pltpu.make_async_remote_copy(
                src_ref=src.at[block],
                dst_ref=dst.at[block],
                send_sem=send.at[step - 1],
                recv_sem=recv.at[step - 1],
                device_id=(target, col),
                device_id_type=MESH,
            )
            pair.append((copy, far))
        halos.append((block, [copy for copy, _ in pair]))
        starts.append(pair)

    def start_halo(index):
        if index < len(starts):
            for copy, far in starts[index]:
                pl.when(jnp.logical_not(far))(copy.start)

    for index in range(lead):
        start_halo(index)

    def local_total(index):
        block, (from_below, from_above) = halos[index]
        pl.when(jnp.logical_not(far_down))(from_below.wait_recv)
        pl.when(jnp.logical_not(far_up))(from_above.wait_recv)
        zero = jnp.zeros(mid_ref.shape[1:], jnp.float32)
        return (
            mid_ref[block]
            + jnp.where(far_down, zero, from_down[block].astype(jnp.float32))
            + jnp.where(far_up, zero, from_up[block].astype(jnp.float32))
        )

    def ring_steps():
        for step in range(1, n_col):
            start_halo(step - 1 + lead)
            value = local_total(step - 1)
            if step > 1:
                value = value + ring_in[step - 2].astype(jnp.float32)
            ring_out[step - 1] = value.astype(ring_out.dtype)
            copy = pltpu.make_async_remote_copy(
                src_ref=ring_out.at[step - 1],
                dst_ref=ring_in.at[step - 1],
                send_sem=ring_send.at[step - 1],
                recv_sem=ring_recv.at[step - 1],
                device_id=(row, succ),
                device_id_type=MESH,
            )
            copy.start()
            yield copy
        start_halo(n_col - 1 + lead)
        own[...] = local_total(n_col - 1) + ring_in[n_col - 2].astype(jnp.float32)

    def far_steps(side, part_ref, far):
        for step in range(1, n_col):
            block = ring_col((p - step + 2 * n_col) % n_col, n_col)
            copy = pltpu.make_async_remote_copy(
                src_ref=far_out.at[side, step - 1],
                dst_ref=far_in.at[side, step - 1],
                send_sem=far_send.at[side, step - 1],
                recv_sem=far_recv.at[side, step - 1],
                device_id=(row, succ),
                device_id_type=MESH,
            )

            def send(step=step, block=block, copy=copy):
                value = part_ref[block]
                if step > 1:
                    value = value + far_in[side, step - 2]
                far_out[side, step - 1] = value
                copy.start()

            pl.when(far)(send)
            yield Gated(copy, far)

        def finish():
            far_out[side, n_col - 1] = part_ref[col] + far_in[side, n_col - 2]

        pl.when(far)(finish)

    run_together(
        allreduce_steps(n_row, n_col, row, col, parts_ref, sums_ref, part, gath,
                        rsend, rrecv, dsend, drecv, gsend, grecv),
        ring_steps(),
        far_steps(0, up_ref, far_up),
        far_steps(1, down_ref, far_down),
    )
    lasts = []
    for side, target, slot, far in ((0, up, 0, far_up), (1, down, 1, far_down)):
        copy = pltpu.make_async_remote_copy(
            src_ref=far_out.at[side, n_col - 1],
            dst_ref=far_from.at[slot],
            send_sem=last_send.at[side],
            recv_sem=last_recv.at[slot],
            device_id=(target, col),
            device_id_type=MESH,
        )
        pl.when(far)(copy.start)
        lasts.append(copy)
    pl.when(far_up)(lasts[0].wait_send)
    pl.when(far_down)(lasts[1].wait_send)
    pl.when(far_down)(lasts[0].wait_recv)
    pl.when(far_up)(lasts[1].wait_recv)
    zero = jnp.zeros(o_ref.shape, jnp.float32)
    total = own[...] + jnp.where(far_down, far_from[0], zero) + jnp.where(far_up, far_from[1], zero)
    o_ref[...] = (total + self_ref[...]).astype(o_ref.dtype)
    sums_ref[...] = sums_ref[...] * scale
    for _, (to_up, to_down) in halos:
        pl.when(jnp.logical_not(far_up))(to_up.wait_send)
        pl.when(jnp.logical_not(far_down))(to_down.wait_send)


def reduce_spread(spread, parts, self_feature, scale, n_row, n_col):
    _, _, rows, width = spread.shape
    col_bits = n_col.bit_length() - 1
    row_bits = n_row.bit_length() - 1
    stacked, _ = parts.shape
    return pl.pallas_call(
        functools.partial(spread_kernel, n_row, n_col, scale),
        out_shape=(
            jax.ShapeDtypeStruct((rows, width), jnp.bfloat16),
            jax.ShapeDtypeStruct(parts.shape, jnp.float32),
        ),
        in_specs=[pl.BlockSpec(memory_space=pltpu.VMEM)] * 3,
        out_specs=(pl.BlockSpec(memory_space=pltpu.VMEM),) * 2,
        scratch_shapes=[
            pltpu.VMEM((rows, width), jnp.float32),
            pltpu.VMEM((n_col, rows, width), jnp.bfloat16),
            pltpu.VMEM((n_col, rows, width), jnp.bfloat16),
            pltpu.VMEM((n_col, rows, width), jnp.bfloat16),
            pltpu.VMEM((n_col, rows, width), jnp.bfloat16),
            pltpu.VMEM((n_col - 1, rows, width), jnp.bfloat16),
            pltpu.VMEM((n_col - 1, rows, width), jnp.bfloat16),
            pltpu.VMEM((2, n_col - 1, rows, width), jnp.float32),
            pltpu.VMEM((2, n_col, rows, width), jnp.float32),
            pltpu.VMEM((2, rows, width), jnp.float32),
            pltpu.SemaphoreType.DMA((n_col,)),
            pltpu.SemaphoreType.DMA((n_col,)),
            pltpu.SemaphoreType.DMA((n_col,)),
            pltpu.SemaphoreType.DMA((n_col,)),
            pltpu.SemaphoreType.DMA((n_col - 1,)),
            pltpu.SemaphoreType.DMA((n_col - 1,)),
            pltpu.SemaphoreType.DMA((2, n_col - 1)),
            pltpu.SemaphoreType.DMA((2, n_col - 1)),
            pltpu.SemaphoreType.DMA((2,)),
            pltpu.SemaphoreType.DMA((2,)),
            pltpu.VMEM((2 * row_bits, stacked // n_col, width), jnp.float32),
            pltpu.VMEM((1, n_col, stacked // n_col, width), jnp.float32),
            pltpu.SemaphoreType.DMA((n_col,)),
            pltpu.SemaphoreType.DMA((n_col,)),
            pltpu.SemaphoreType.DMA((row_bits,)),
            pltpu.SemaphoreType.DMA((row_bits,)),
            pltpu.SemaphoreType.DMA((n_col,)),
            pltpu.SemaphoreType.DMA((n_col,)),
        ],
        compiler_params=pltpu.CompilerParams(collective_id=2, has_side_effects=True),
    )(spread, parts, self_feature)


def local_kernel(rows_ref, cols_ref, count_ref, window_ref, tiles_ref, feat_ref, w_ref, ws_ref, cot_ref,
                 act_ref, parts_ref, self_ref, spread, acc, grad_agg):
    tile = tiles_ref.shape[-1]
    nodes = acc.shape[0]
    count = jnp.minimum(count_ref[0], tiles_ref.shape[0])
    acc[...] = jnp.zeros_like(acc)

    def forward(j, carry):
        at = pl.multiple_of(rows_ref[j] * tile, tile)
        acc[pl.ds(at, tile), :] += jnp.dot(
            tiles_ref[j], window_ref[cols_ref[j]], preferred_element_type=jnp.float32
        )
        return carry

    lax.fori_loop(0, count, forward, 0)
    aggregated = acc[...].astype(jnp.bfloat16)
    features = feat_ref[...]
    pre_act = jnp.dot(aggregated, w_ref[...], preferred_element_type=jnp.float32) + jnp.dot(
        features, ws_ref[...], preferred_element_type=jnp.float32
    )
    sigma = jax.nn.sigmoid(pre_act)
    act_ref[...] = (pre_act * sigma).astype(act_ref.dtype)
    grad_pre = (cot_ref[...].astype(jnp.float32) * sigma * (1.0 + pre_act * (1.0 - sigma))).astype(
        jnp.bfloat16
    )
    over_nodes = (((0,), (0,)), ((), ()))
    parts_ref[pl.ds(0, nodes), :] = lax.dot_general(
        aggregated, grad_pre, over_nodes, preferred_element_type=jnp.float32
    )
    parts_ref[pl.ds(nodes, nodes), :] = lax.dot_general(
        features, grad_pre, over_nodes, preferred_element_type=jnp.float32
    )
    by_rows = (((1,), (1,)), ((), ()))
    grad_agg[...] = lax.dot_general(
        grad_pre, w_ref[...], by_rows, preferred_element_type=jnp.float32
    ).astype(jnp.bfloat16)
    self_ref[...] = lax.dot_general(grad_pre, ws_ref[...], by_rows, preferred_element_type=jnp.float32)
    spread[...] = jnp.zeros_like(spread)

    def backward(j, carry):
        at = pl.multiple_of(rows_ref[j] * tile, tile)
        column = cols_ref[j]
        spread[column] += lax.dot_general(
            tiles_ref[j], grad_agg[pl.ds(at, tile), :], over_nodes, preferred_element_type=jnp.float32
        )
        return carry

    lax.fori_loop(0, count, backward, 0)


def local_math(slot_rows, slot_cols, count, window, tiles, features, weight, weight_self, cotangent):
    nodes, width = features.shape
    span = window.shape[0] // 3
    tile = tiles.shape[-1]
    smem = pl.BlockSpec(memory_space=pltpu.SMEM)
    vmem = pl.BlockSpec(memory_space=pltpu.VMEM)
    return pl.pallas_call(
        local_kernel,
        out_shape=(
            jax.ShapeDtypeStruct((nodes, width), jnp.bfloat16),
            jax.ShapeDtypeStruct((2 * width, width), jnp.float32),
            jax.ShapeDtypeStruct((nodes, width), jnp.float32),
            jax.ShapeDtypeStruct((3 * span, tile, width), jnp.float32),
        ),
        in_specs=[smem, smem, smem] + [vmem] * 6,
        out_specs=(vmem,) * 4,
        scratch_shapes=[
            pltpu.VMEM((nodes, width), jnp.float32),
            pltpu.VMEM((nodes, width), jnp.bfloat16),
        ],
    )(slot_rows, slot_cols, count, window, tiles, features, weight, weight_self, cotangent)


def shards(features, weight, weight_self, tile_values, tile_rows, tile_cols, tile_count, cotangent):
    tile_block = tile_values[0]
    slot_rows = tile_rows[0]
    slot_cols = tile_cols[0]
    live_count = tile_count[0, 0]
    slot_total = tile_block.shape[0]
    tile_side = tile_block.shape[-1]
    node_rows = features.shape[0]
    width = features.shape[1]
    per_block = node_rows // tile_side
    col_count = lax.axis_size("col")
    row_count = lax.axis_size("row")
    span = col_count * per_block
    window = gather_window(features, row_count, col_count)
    window_tiles = window.reshape(-1, tile_side, width)
    activations, parts, self_feature, spread = local_math(
        slot_rows,
        slot_cols,
        tile_count[0],
        window_tiles,
        tile_block,
        features,
        weight,
        weight_self,
        cotangent,
    )
    factor = 1.0 / math.sqrt(node_rows * col_count * row_count)
    feature_grad, summed_parts = reduce_spread(
        spread.reshape(3, col_count, node_rows, width),
        parts,
        self_feature,
        factor,
        row_count,
        col_count,
    )
    weight_total, self_total = summed_parts[:width], summed_parts[width:]
    return (activations, feature_grad, weight_total, self_total)


def solution(mesh):
    placed = (
        P(("row", "col"), None),
        P(),
        P(),
        P("row", "col", None, None),
        P("row", "col"),
        P("row", "col"),
        P("row", "col"),
        P(("row", "col"), None),
    )
    return jax.shard_map(
        shards,
        mesh=mesh,
        in_specs=placed,
        out_specs=(P(("row", "col"), None), P(("row", "col"), None), P(), P()),
        check_vma=False,
    )
```

```python
import functools
import math

import jax
import jax.numpy as jnp
from jax import lax
from jax.experimental import pallas as pl
from jax.experimental.pallas import tpu as pltpu
from jax.sharding import PartitionSpec as P

MESH = pl.DeviceIdType.MESH


def flip(index, stride):
    bit = (index // stride) % 2
    return index + stride - 2 * stride * bit, bit


def allreduce_partners(n_row, n_col, row, col):
    partners = [(row, peer) for peer in range(n_col)]
    for k in range(n_row.bit_length() - 1):
        partners.append((flip(row, 1 << k)[0], col))
    return partners


class Group:
    def __init__(self, copies, receipts, col):
        self.copies = copies
        self.receipts = receipts
        self.col = col

    def wait(self):
        for peer, (copy, receipt) in enumerate(zip(self.copies, self.receipts)):
            @pl.when(peer != self.col)
            def _():
                copy.wait_send()
                receipt.wait_recv()


def allreduce_steps(n_row, n_col, row, col, x_ref, o_ref, part, gath, rsend, rrecv, dsend, drecv, gsend, grecv):
    row_bits = n_row.bit_length() - 1
    chunk = x_ref.shape[0] // n_col
    mine = pl.ds(pl.multiple_of(col * chunk, 8), chunk)
    copies, receipts = [], []
    for peer in range(n_col):
        copies.append(pltpu.make_async_remote_copy(
            src_ref=x_ref.at[pl.ds(peer * chunk, chunk)],
            dst_ref=gath.at[0, col],
            send_sem=rsend.at[peer],
            recv_sem=rrecv.at[col],
            device_id=(row, peer),
            device_id_type=MESH,
        ))
        receipts.append(pltpu.make_async_remote_copy(
            src_ref=x_ref.at[pl.ds(peer * chunk, chunk)],
            dst_ref=gath.at[0, peer],
            send_sem=rsend.at[peer],
            recv_sem=rrecv.at[peer],
            device_id=(row, peer),
            device_id_type=MESH,
        ))
        pl.when(peer != col)(copies[-1].start)
    yield Group(copies, receipts, col)
    total = x_ref[mine, :]
    for peer in range(n_col):
        total = total + jnp.where(peer == col, jnp.zeros_like(total), gath[0, peer])
    for k in range(row_bits):
        other, _ = flip(row, 1 << k)
        hold = part.at[2 * k]
        hold[...] = total
        copy = pltpu.make_async_remote_copy(
            src_ref=hold,
            dst_ref=part.at[2 * k + 1],
            send_sem=dsend.at[k],
            recv_sem=drecv.at[k],
            device_id=(other, col),
            device_id_type=MESH,
        )
        copy.start()
        yield copy
        total = total + part[2 * k + 1]
    o_ref[mine, :] = total
    copies, receipts = [], []
    for peer in range(n_col):
        copies.append(pltpu.make_async_remote_copy(
            src_ref=o_ref.at[mine],
            dst_ref=o_ref.at[mine],
            send_sem=gsend.at[peer],
            recv_sem=grecv.at[col],
            device_id=(row, peer),
            device_id_type=MESH,
        ))
        receipts.append(pltpu.make_async_remote_copy(
            src_ref=o_ref.at[mine],
            dst_ref=o_ref.at[pl.ds(peer * chunk, chunk)],
            send_sem=gsend.at[peer],
            recv_sem=grecv.at[peer],
            device_id=(row, peer),
            device_id_type=MESH,
        ))
        pl.when(peer != col)(copies[-1].start)
    yield Group(copies, receipts, col)


def run_together(*chains):
    active = list(chains)
    while active:
        copies, kept = [], []
        for chain in active:
            try:
                copies.append(next(chain))
                kept.append(chain)
            except StopIteration:
                pass
        for copy in copies:
            copy.wait()
        active = kept


def ring_position(col, n):
    core = col % 2
    y = col // 2
    return y + core * (n - 1 - 2 * y)


def ring_col(p, n):
    q = p // (n // 2)
    y = p + q * (n - 1 - 2 * p)
    return 2 * y + q


def gather_kernel(n_row, n_col, x_ref, w_ref, ring_send, ring_recv, halo_send, halo_recv, local_sem):
    row = lax.axis_index("row")
    col = lax.axis_index("col")
    p = ring_position(col, n_col)
    succ = ring_col((p + 1) % n_col, n_col)
    pred = ring_col((p + n_col - 1) % n_col, n_col)
    up = (row + 1) % n_row
    down = (row + n_row - 1) % n_row
    half = max(n_row // 2, 1)
    far = {0: row % half == 0, 2: (row + 1) % half == 0}
    barrier = pltpu.get_barrier_semaphore()
    for device in ((row, succ), (row, pred), (up, col), (down, col)):
        pl.semaphore_signal(barrier, inc=1, device_id=device, device_id_type=MESH)
    pl.semaphore_wait(barrier, 4)
    local = pltpu.make_async_copy(x_ref, w_ref.at[1, col], local_sem.at[0])
    local.start()

    def halo(src, block, index):
        copies = {}
        for target, slot in ((up, 0), (down, 2)):
            copies[slot] = pltpu.make_async_remote_copy(
                src_ref=src,
                dst_ref=w_ref.at[slot, block],
                send_sem=halo_send.at[slot // 2, index],
                recv_sem=halo_recv.at[slot // 2, index],
                device_id=(target, col),
                device_id_type=MESH,
            )
        return copies

    halos = [(col, halo(x_ref, col, 0))]
    for copy in halos[0][1].values():
        copy.start()
    def start_forward(forward):
        for slot in (0, 2):
            pl.when(jnp.logical_not(far[2 - slot]))(forward[slot].start)

    sent = col
    deferred = None
    for step in range(1, n_col):
        copies = {}
        for group in (1, 0, 2):
            src = x_ref if (step == 1 and group == 1) else w_ref.at[group, sent]
            copies[group] = pltpu.make_async_remote_copy(
                src_ref=src,
                dst_ref=w_ref.at[group, sent],
                send_sem=ring_send.at[group, step - 1],
                recv_sem=ring_recv.at[group, step - 1],
                device_id=(row, succ),
                device_id_type=MESH,
            )
        copies[1].start()
        for group in (0, 2):
            @pl.when(far[group])
            def _():
                if step == 1:
                    halos[0][1][group].wait_recv()
                copies[group].start()
        if deferred is not None:
            start_forward(deferred)
        copies[1].wait()
        for group in (0, 2):
            @pl.when(far[group])
            def _():
                copies[group].wait()
        sent = ring_col((p - step + n_col) % n_col, n_col)
        deferred = halo(w_ref.at[1, sent], sent, step)
        halos.append((sent, deferred))
    start_forward(deferred)
    for copy in halos[0][1].values():
        copy.wait_send()
    for slot in (0, 2):
        @pl.when(jnp.logical_not(far[slot]))
        def _():
            halos[0][1][slot].wait_recv()
    for _, copies in halos[1:]:
        for slot in (0, 2):
            @pl.when(jnp.logical_not(far[2 - slot]))
            def _():
                copies[slot].wait_send()

            @pl.when(jnp.logical_not(far[slot]))
            def _():
                copies[slot].wait_recv()
    local.wait()


def gather_window(block, n_row, n_col):
    rows, width = block.shape
    return pl.pallas_call(
        functools.partial(gather_kernel, n_row, n_col),
        out_shape=jax.ShapeDtypeStruct((3, n_col, rows, width), block.dtype),
        in_specs=[pl.BlockSpec(memory_space=pltpu.VMEM)],
        out_specs=pl.BlockSpec(memory_space=pltpu.VMEM),
        scratch_shapes=[
            pltpu.SemaphoreType.DMA((3, n_col - 1)),
            pltpu.SemaphoreType.DMA((3, n_col - 1)),
            pltpu.SemaphoreType.DMA((2, n_col)),
            pltpu.SemaphoreType.DMA((2, n_col)),
            pltpu.SemaphoreType.DMA((1,)),
        ],
        compiler_params=pltpu.CompilerParams(collective_id=1, has_side_effects=True),
    )(block)


class Gated:
    def __init__(self, copy, cond):
        self.copy = copy
        self.cond = cond

    def wait(self):
        pl.when(self.cond)(self.copy.wait)


def spread_kernel(n_row, n_col, scale, spread_ref, parts_ref, self_ref, o_ref, sums_ref, own,
                  up_bf, down_bf,
                  from_down, from_up, ring_in, ring_out, far_in, far_out, far_from, up_send, down_send,
                  from_down_sem, from_up_sem, ring_send, ring_recv, far_send, far_recv, last_send, last_recv,
                  part, gath, rsend, rrecv, dsend, drecv, gsend, grecv):
    row = lax.axis_index("row")
    col = lax.axis_index("col")
    p = ring_position(col, n_col)
    succ = ring_col((p + 1) % n_col, n_col)
    pred = ring_col((p + n_col - 1) % n_col, n_col)
    up = (row + 1) % n_row
    down = (row + n_row - 1) % n_row
    half = max(n_row // 2, 1)
    far_down = row % half == 0
    far_up = (row + 1) % half == 0
    partners = [(row, succ), (row, pred), (up, col), (down, col)]
    partners += allreduce_partners(n_row, n_col, row, col)
    barrier = pltpu.get_barrier_semaphore()
    for device in partners:
        def signal(device=device):
            pl.semaphore_signal(barrier, inc=1, device_id=device, device_id_type=MESH)

        pl.when(jnp.logical_or(device[0] != row, device[1] != col))(signal)
    pl.semaphore_wait(barrier, len(partners) - 1)
    mid_ref, up_ref, down_ref = spread_ref.at[1], spread_ref.at[2], spread_ref.at[0]
    up_bf[...] = up_ref[...].astype(up_bf.dtype)
    down_bf[...] = down_ref[...].astype(down_bf.dtype)
    halos = []
    starts = []
    lead = 2
    for step in range(1, n_col + 1):
        block = ring_col((p - step + 2 * n_col) % n_col, n_col)
        pair = []
        for src, dst, target, send, recv, far in (
            (up_bf, from_down, up, up_send, from_down_sem, far_up),
            (down_bf, from_up, down, down_send, from_up_sem, far_down),
        ):
            copy = pltpu.make_async_remote_copy(
                src_ref=src.at[block],
                dst_ref=dst.at[block],
                send_sem=send.at[step - 1],
                recv_sem=recv.at[step - 1],
                device_id=(target, col),
                device_id_type=MESH,
            )
            pair.append((copy, far))
        halos.append((block, [copy for copy, _ in pair]))
        starts.append(pair)

    def start_halo(index):
        if index < len(starts):
            for copy, far in starts[index]:
                pl.when(jnp.logical_not(far))(copy.start)

    for index in range(lead):
        start_halo(index)

    def local_total(index):
        block, (from_below, from_above) = halos[index]
        pl.when(jnp.logical_not(far_down))(from_below.wait_recv)
        pl.when(jnp.logical_not(far_up))(from_above.wait_recv)
        zero = jnp.zeros(mid_ref.shape[1:], jnp.float32)
        return (
            mid_ref[block]
            + jnp.where(far_down, zero, from_down[block].astype(jnp.float32))
            + jnp.where(far_up, zero, from_up[block].astype(jnp.float32))
        )

    def ring_steps():
        for step in range(1, n_col):
            start_halo(step - 1 + lead)
            value = local_total(step - 1)
            if step > 1:
                value = value + ring_in[step - 2].astype(jnp.float32)
            ring_out[step - 1] = value.astype(ring_out.dtype)
            copy = pltpu.make_async_remote_copy(
                src_ref=ring_out.at[step - 1],
                dst_ref=ring_in.at[step - 1],
                send_sem=ring_send.at[step - 1],
                recv_sem=ring_recv.at[step - 1],
                device_id=(row, succ),
                device_id_type=MESH,
            )
            copy.start()
            yield copy
        start_halo(n_col - 1 + lead)
        own[...] = local_total(n_col - 1) + ring_in[n_col - 2].astype(jnp.float32)

    def far_steps(side, part_ref, far):
        for step in range(1, n_col):
            block = ring_col((p - step + 2 * n_col) % n_col, n_col)
            copy = pltpu.make_async_remote_copy(
                src_ref=far_out.at[side, step - 1],
                dst_ref=far_in.at[side, step - 1],
                send_sem=far_send.at[side, step - 1],
                recv_sem=far_recv.at[side, step - 1],
                device_id=(row, succ),
                device_id_type=MESH,
            )

            def send(step=step, block=block, copy=copy):
                value = part_ref[block]
                if step > 1:
                    value = value + far_in[side, step - 2]
                far_out[side, step - 1] = value
                copy.start()

            pl.when(far)(send)
            yield Gated(copy, far)

        def finish():
            far_out[side, n_col - 1] = part_ref[col] + far_in[side, n_col - 2]

        pl.when(far)(finish)

    run_together(
        allreduce_steps(n_row, n_col, row, col, parts_ref, sums_ref, part, gath,
                        rsend, rrecv, dsend, drecv, gsend, grecv),
        ring_steps(),
        far_steps(0, up_ref, far_up),
        far_steps(1, down_ref, far_down),
    )
    lasts = []
    for side, target, slot, far in ((0, up, 0, far_up), (1, down, 1, far_down)):
        copy = pltpu.make_async_remote_copy(
            src_ref=far_out.at[side, n_col - 1],
            dst_ref=far_from.at[slot],
            send_sem=last_send.at[side],
            recv_sem=last_recv.at[slot],
            device_id=(target, col),
            device_id_type=MESH,
        )
        pl.when(far)(copy.start)
        lasts.append(copy)
    pl.when(far_up)(lasts[0].wait_send)
    pl.when(far_down)(lasts[1].wait_send)
    pl.when(far_down)(lasts[0].wait_recv)
    pl.when(far_up)(lasts[1].wait_recv)
    zero = jnp.zeros(o_ref.shape, jnp.float32)
    total = own[...] + jnp.where(far_down, far_from[0], zero) + jnp.where(far_up, far_from[1], zero)
    o_ref[...] = (total + self_ref[...]).astype(o_ref.dtype)
    sums_ref[...] = sums_ref[...] * scale
    for _, (to_up, to_down) in halos:
        pl.when(jnp.logical_not(far_up))(to_up.wait_send)
        pl.when(jnp.logical_not(far_down))(to_down.wait_send)


def reduce_spread(spread, parts, self_feature, scale, n_row, n_col):
    _, _, rows, width = spread.shape
    col_bits = n_col.bit_length() - 1
    row_bits = n_row.bit_length() - 1
    stacked, _ = parts.shape
    return pl.pallas_call(
        functools.partial(spread_kernel, n_row, n_col, scale),
        out_shape=(
            jax.ShapeDtypeStruct((rows, width), jnp.bfloat16),
            jax.ShapeDtypeStruct(parts.shape, jnp.float32),
        ),
        in_specs=[pl.BlockSpec(memory_space=pltpu.VMEM)] * 3,
        out_specs=(pl.BlockSpec(memory_space=pltpu.VMEM),) * 2,
        scratch_shapes=[
            pltpu.VMEM((rows, width), jnp.float32),
            pltpu.VMEM((n_col, rows, width), jnp.bfloat16),
            pltpu.VMEM((n_col, rows, width), jnp.bfloat16),
            pltpu.VMEM((n_col, rows, width), jnp.bfloat16),
            pltpu.VMEM((n_col, rows, width), jnp.bfloat16),
            pltpu.VMEM((n_col - 1, rows, width), jnp.bfloat16),
            pltpu.VMEM((n_col - 1, rows, width), jnp.bfloat16),
            pltpu.VMEM((2, n_col - 1, rows, width), jnp.float32),
            pltpu.VMEM((2, n_col, rows, width), jnp.float32),
            pltpu.VMEM((2, rows, width), jnp.float32),
            pltpu.SemaphoreType.DMA((n_col,)),
            pltpu.SemaphoreType.DMA((n_col,)),
            pltpu.SemaphoreType.DMA((n_col,)),
            pltpu.SemaphoreType.DMA((n_col,)),
            pltpu.SemaphoreType.DMA((n_col - 1,)),
            pltpu.SemaphoreType.DMA((n_col - 1,)),
            pltpu.SemaphoreType.DMA((2, n_col - 1)),
            pltpu.SemaphoreType.DMA((2, n_col - 1)),
            pltpu.SemaphoreType.DMA((2,)),
            pltpu.SemaphoreType.DMA((2,)),
            pltpu.VMEM((2 * row_bits, stacked // n_col, width), jnp.float32),
            pltpu.VMEM((1, n_col, stacked // n_col, width), jnp.float32),
            pltpu.SemaphoreType.DMA((n_col,)),
            pltpu.SemaphoreType.DMA((n_col,)),
            pltpu.SemaphoreType.DMA((row_bits,)),
            pltpu.SemaphoreType.DMA((row_bits,)),
            pltpu.SemaphoreType.DMA((n_col,)),
            pltpu.SemaphoreType.DMA((n_col,)),
        ],
        compiler_params=pltpu.CompilerParams(collective_id=2, has_side_effects=True),
    )(spread, parts, self_feature)


def local_kernel(rows_ref, cols_ref, count_ref, window_ref, tiles_ref, feat_ref, w_ref, ws_ref, cot_ref,
                 act_ref, parts_ref, self_ref, spread, acc, grad_agg):
    tile = tiles_ref.shape[-1]
    nodes = acc.shape[0]
    count = jnp.minimum(count_ref[0], tiles_ref.shape[0])
    acc[...] = jnp.zeros_like(acc)

    def forward(j, carry):
        at = pl.multiple_of(rows_ref[j] * tile, tile)
        acc[pl.ds(at, tile), :] += jnp.dot(
            tiles_ref[j], window_ref[cols_ref[j]], preferred_element_type=jnp.float32
        )
        return carry

    lax.fori_loop(0, count, forward, 0)
    aggregated = acc[...].astype(jnp.bfloat16)
    features = feat_ref[...]
    pre_act = jnp.dot(aggregated, w_ref[...], preferred_element_type=jnp.float32) + jnp.dot(
        features, ws_ref[...], preferred_element_type=jnp.float32
    )
    sigma = jax.nn.sigmoid(pre_act)
    act_ref[...] = (pre_act * sigma).astype(act_ref.dtype)
    grad_pre = (cot_ref[...].astype(jnp.float32) * sigma * (1.0 + pre_act * (1.0 - sigma))).astype(
        jnp.bfloat16
    )
    over_nodes = (((0,), (0,)), ((), ()))
    parts_ref[pl.ds(0, nodes), :] = lax.dot_general(
        aggregated, grad_pre, over_nodes, preferred_element_type=jnp.float32
    )
    parts_ref[pl.ds(nodes, nodes), :] = lax.dot_general(
        features, grad_pre, over_nodes, preferred_element_type=jnp.float32
    )
    by_rows = (((1,), (1,)), ((), ()))
    grad_agg[...] = lax.dot_general(
        grad_pre, w_ref[...], by_rows, preferred_element_type=jnp.float32
    ).astype(jnp.bfloat16)
    self_ref[...] = lax.dot_general(grad_pre, ws_ref[...], by_rows, preferred_element_type=jnp.float32)
    spread[...] = jnp.zeros_like(spread)

    def backward(j, carry):
        at = pl.multiple_of(rows_ref[j] * tile, tile)
        column = cols_ref[j]
        spread[column] += lax.dot_general(
            tiles_ref[j], grad_agg[pl.ds(at, tile), :], over_nodes, preferred_element_type=jnp.float32
        )
        return carry

    lax.fori_loop(0, count, backward, 0)


def local_math(slot_rows, slot_cols, count, window, tiles, features, weight, weight_self, cotangent):
    nodes, width = features.shape
    span = window.shape[0] // 3
    tile = tiles.shape[-1]
    smem = pl.BlockSpec(memory_space=pltpu.SMEM)
    vmem = pl.BlockSpec(memory_space=pltpu.VMEM)
    return pl.pallas_call(
        local_kernel,
        out_shape=(
            jax.ShapeDtypeStruct((nodes, width), jnp.bfloat16),
            jax.ShapeDtypeStruct((2 * width, width), jnp.float32),
            jax.ShapeDtypeStruct((nodes, width), jnp.float32),
            jax.ShapeDtypeStruct((3 * span, tile, width), jnp.float32),
        ),
        in_specs=[smem, smem, smem] + [vmem] * 6,
        out_specs=(vmem,) * 4,
        scratch_shapes=[
            pltpu.VMEM((nodes, width), jnp.float32),
            pltpu.VMEM((nodes, width), jnp.bfloat16),
        ],
    )(slot_rows, slot_cols, count, window, tiles, features, weight, weight_self, cotangent)


def shards(features, weight, weight_self, tile_values, tile_rows, tile_cols, tile_count, cotangent):
    tile_block = tile_values[0]
    slot_rows = tile_rows[0]
    slot_cols = tile_cols[0]
    live_count = tile_count[0, 0]
    slot_total = tile_block.shape[0]
    tile_side = tile_block.shape[-1]
    node_rows = features.shape[0]
    width = features.shape[1]
    per_block = node_rows // tile_side
    col_count = lax.axis_size("col")
    row_count = lax.axis_size("row")
    span = col_count * per_block
    window = gather_window(features, row_count, col_count)
    window_tiles = window.reshape(-1, tile_side, width)
    activations, parts, self_feature, spread = local_math(
        slot_rows,
        slot_cols,
        tile_count[0],
        window_tiles,
        tile_block,
        features,
        weight,
        weight_self,
        cotangent,
    )
    factor = 1.0 / math.sqrt(node_rows * col_count * row_count)
    feature_grad, summed_parts = reduce_spread(
        spread.reshape(3, col_count, node_rows, width),
        parts,
        self_feature,
        factor,
        row_count,
        col_count,
    )
    weight_total, self_total = summed_parts[:width], summed_parts[width:]
    return (activations, feature_grad, weight_total, self_total)


def solution(mesh):
    placed = (
        P(("row", "col"), None),
        P(),
        P(),
        P("row", "col", None, None),
        P("row", "col"),
        P("row", "col"),
        P("row", "col"),
        P(("row", "col"), None),
    )
    return jax.shard_map(
        shards,
        mesh=mesh,
        in_specs=placed,
        out_specs=(P(("row", "col"), None), P(("row", "col"), None), P(), P()),
        check_vma=False,
    )
```

```python
import functools
import math

import jax
import jax.numpy as jnp
from jax import lax
from jax.experimental import pallas as pl
from jax.experimental.pallas import tpu as pltpu
from jax.sharding import PartitionSpec as P

MESH = pl.DeviceIdType.MESH


def flip(index, stride):
    bit = (index // stride) % 2
    return index + stride - 2 * stride * bit, bit


def allreduce_partners(n_row, n_col, row, col):
    partners = [(row, peer) for peer in range(n_col)]
    for k in range(n_row.bit_length() - 1):
        partners.append((flip(row, 1 << k)[0], col))
    return partners


class Group:
    def __init__(self, copies, receipts, col):
        self.copies = copies
        self.receipts = receipts
        self.col = col

    def wait(self):
        for peer, (copy, receipt) in enumerate(zip(self.copies, self.receipts)):
            @pl.when(peer != self.col)
            def _():
                copy.wait_send()
                receipt.wait_recv()


def allreduce_steps(n_row, n_col, row, col, x_ref, o_ref, part, gath, rsend, rrecv, dsend, drecv, gsend, grecv):
    row_bits = n_row.bit_length() - 1
    chunk = x_ref.shape[0] // n_col
    mine = pl.ds(pl.multiple_of(col * chunk, 8), chunk)
    copies, receipts = [], []
    for peer in range(n_col):
        copies.append(pltpu.make_async_remote_copy(
            src_ref=x_ref.at[pl.ds(peer * chunk, chunk)],
            dst_ref=gath.at[0, col],
            send_sem=rsend.at[peer],
            recv_sem=rrecv.at[col],
            device_id=(row, peer),
            device_id_type=MESH,
        ))
        receipts.append(pltpu.make_async_remote_copy(
            src_ref=x_ref.at[pl.ds(peer * chunk, chunk)],
            dst_ref=gath.at[0, peer],
            send_sem=rsend.at[peer],
            recv_sem=rrecv.at[peer],
            device_id=(row, peer),
            device_id_type=MESH,
        ))
        pl.when(peer != col)(copies[-1].start)
    yield Group(copies, receipts, col)
    total = x_ref[mine, :]
    for peer in range(n_col):
        total = total + jnp.where(peer == col, jnp.zeros_like(total), gath[0, peer])
    for k in range(row_bits):
        other, _ = flip(row, 1 << k)
        hold = part.at[2 * k]
        hold[...] = total
        copy = pltpu.make_async_remote_copy(
            src_ref=hold,
            dst_ref=part.at[2 * k + 1],
            send_sem=dsend.at[k],
            recv_sem=drecv.at[k],
            device_id=(other, col),
            device_id_type=MESH,
        )
        copy.start()
        yield copy
        total = total + part[2 * k + 1]
    o_ref[mine, :] = total
    copies, receipts = [], []
    for peer in range(n_col):
        copies.append(pltpu.make_async_remote_copy(
            src_ref=o_ref.at[mine],
            dst_ref=o_ref.at[mine],
            send_sem=gsend.at[peer],
            recv_sem=grecv.at[col],
            device_id=(row, peer),
            device_id_type=MESH,
        ))
        receipts.append(pltpu.make_async_remote_copy(
            src_ref=o_ref.at[mine],
            dst_ref=o_ref.at[pl.ds(peer * chunk, chunk)],
            send_sem=gsend.at[peer],
            recv_sem=grecv.at[peer],
            device_id=(row, peer),
            device_id_type=MESH,
        ))
        pl.when(peer != col)(copies[-1].start)
    yield Group(copies, receipts, col)


def run_together(*chains):
    active = list(chains)
    while active:
        copies, kept = [], []
        for chain in active:
            try:
                copies.append(next(chain))
                kept.append(chain)
            except StopIteration:
                pass
        for copy in copies:
            copy.wait()
        active = kept


def ring_position(col, n):
    core = col % 2
    y = col // 2
    return y + core * (n - 1 - 2 * y)


def ring_col(p, n):
    q = p // (n // 2)
    y = p + q * (n - 1 - 2 * p)
    return 2 * y + q


def gather_kernel(n_row, n_col, x_ref, w_ref, ring_send, ring_recv, halo_send, halo_recv, local_sem):
    row = lax.axis_index("row")
    col = lax.axis_index("col")
    p = ring_position(col, n_col)
    succ = ring_col((p + 1) % n_col, n_col)
    pred = ring_col((p + n_col - 1) % n_col, n_col)
    up = (row + 1) % n_row
    down = (row + n_row - 1) % n_row
    half = max(n_row // 2, 1)
    far = {0: row % half == 0, 2: (row + 1) % half == 0}
    barrier = pltpu.get_barrier_semaphore()
    for device in ((row, succ), (row, pred), (up, col), (down, col)):
        pl.semaphore_signal(barrier, inc=1, device_id=device, device_id_type=MESH)
    pl.semaphore_wait(barrier, 4)
    local = pltpu.make_async_copy(x_ref, w_ref.at[1, col], local_sem.at[0])
    local.start()

    def halo(src, block, index):
        copies = {}
        for target, slot in ((up, 0), (down, 2)):
            copies[slot] = pltpu.make_async_remote_copy(
                src_ref=src,
                dst_ref=w_ref.at[slot, block],
                send_sem=halo_send.at[slot // 2, index],
                recv_sem=halo_recv.at[slot // 2, index],
                device_id=(target, col),
                device_id_type=MESH,
            )
        return copies

    halos = [(col, halo(x_ref, col, 0))]
    for copy in halos[0][1].values():
        copy.start()
    sent = col
    for step in range(1, n_col):
        copies = {}
        for group in (1, 0, 2):
            src = x_ref if (step == 1 and group == 1) else w_ref.at[group, sent]
            copies[group] = pltpu.make_async_remote_copy(
                src_ref=src,
                dst_ref=w_ref.at[group, sent],
                send_sem=ring_send.at[group, step - 1],
                recv_sem=ring_recv.at[group, step - 1],
                device_id=(row, succ),
                device_id_type=MESH,
            )
        copies[1].start()
        for group in (0, 2):
            @pl.when(far[group])
            def _():
                if step == 1:
                    halos[0][1][group].wait_recv()
                copies[group].start()
        copies[1].wait()
        for group in (0, 2):
            @pl.when(far[group])
            def _():
                copies[group].wait()
        sent = ring_col((p - step + n_col) % n_col, n_col)
        forward = halo(w_ref.at[1, sent], sent, step)
        halos.append((sent, forward))
        for slot in (0, 2):
            @pl.when(jnp.logical_not(far[2 - slot]))
            def _():
                forward[slot].start()
    for copy in halos[0][1].values():
        copy.wait_send()
    for slot in (0, 2):
        @pl.when(jnp.logical_not(far[slot]))
        def _():
            halos[0][1][slot].wait_recv()
    for _, copies in halos[1:]:
        for slot in (0, 2):
            @pl.when(jnp.logical_not(far[2 - slot]))
            def _():
                copies[slot].wait_send()

            @pl.when(jnp.logical_not(far[slot]))
            def _():
                copies[slot].wait_recv()
    local.wait()


def gather_window(block, n_row, n_col):
    rows, width = block.shape
    return pl.pallas_call(
        functools.partial(gather_kernel, n_row, n_col),
        out_shape=jax.ShapeDtypeStruct((3, n_col, rows, width), block.dtype),
        in_specs=[pl.BlockSpec(memory_space=pltpu.VMEM)],
        out_specs=pl.BlockSpec(memory_space=pltpu.VMEM),
        scratch_shapes=[
            pltpu.SemaphoreType.DMA((3, n_col - 1)),
            pltpu.SemaphoreType.DMA((3, n_col - 1)),
            pltpu.SemaphoreType.DMA((2, n_col)),
            pltpu.SemaphoreType.DMA((2, n_col)),
            pltpu.SemaphoreType.DMA((1,)),
        ],
        compiler_params=pltpu.CompilerParams(collective_id=1, has_side_effects=True),
    )(block)


class Gated:
    def __init__(self, copy, cond):
        self.copy = copy
        self.cond = cond

    def wait(self):
        pl.when(self.cond)(self.copy.wait)


def spread_kernel(n_row, n_col, spread_ref, parts_ref, o_ref, sums_ref, own,
                  up_bf, down_bf,
                  from_down, from_up, ring_in, ring_out, far_in, far_out, far_from, up_send, down_send,
                  from_down_sem, from_up_sem, ring_send, ring_recv, far_send, far_recv, last_send, last_recv,
                  part, gath, rsend, rrecv, dsend, drecv, gsend, grecv):
    row = lax.axis_index("row")
    col = lax.axis_index("col")
    p = ring_position(col, n_col)
    succ = ring_col((p + 1) % n_col, n_col)
    pred = ring_col((p + n_col - 1) % n_col, n_col)
    up = (row + 1) % n_row
    down = (row + n_row - 1) % n_row
    half = max(n_row // 2, 1)
    far_down = row % half == 0
    far_up = (row + 1) % half == 0
    partners = [(row, succ), (row, pred), (up, col), (down, col)]
    partners += allreduce_partners(n_row, n_col, row, col)
    barrier = pltpu.get_barrier_semaphore()
    for device in partners:
        def signal(device=device):
            pl.semaphore_signal(barrier, inc=1, device_id=device, device_id_type=MESH)

        pl.when(jnp.logical_or(device[0] != row, device[1] != col))(signal)
    pl.semaphore_wait(barrier, len(partners) - 1)
    mid_ref, up_ref, down_ref = spread_ref.at[1], spread_ref.at[2], spread_ref.at[0]
    up_bf[...] = up_ref[...].astype(up_bf.dtype)
    down_bf[...] = down_ref[...].astype(down_bf.dtype)
    halos = []
    starts = []
    lead = 2
    for step in range(1, n_col + 1):
        block = ring_col((p - step + 2 * n_col) % n_col, n_col)
        pair = []
        for src, dst, target, send, recv, far in (
            (up_bf, from_down, up, up_send, from_down_sem, far_up),
            (down_bf, from_up, down, down_send, from_up_sem, far_down),
        ):
            copy = pltpu.make_async_remote_copy(
                src_ref=src.at[block],
                dst_ref=dst.at[block],
                send_sem=send.at[step - 1],
                recv_sem=recv.at[step - 1],
                device_id=(target, col),
                device_id_type=MESH,
            )
            pair.append((copy, far))
        halos.append((block, [copy for copy, _ in pair]))
        starts.append(pair)

    def start_halo(index):
        if index < len(starts):
            for copy, far in starts[index]:
                pl.when(jnp.logical_not(far))(copy.start)

    for index in range(lead):
        start_halo(index)

    def local_total(index):
        block, (from_below, from_above) = halos[index]
        pl.when(jnp.logical_not(far_down))(from_below.wait_recv)
        pl.when(jnp.logical_not(far_up))(from_above.wait_recv)
        zero = jnp.zeros(mid_ref.shape[1:], jnp.float32)
        return (
            mid_ref[block]
            + jnp.where(far_down, zero, from_down[block].astype(jnp.float32))
            + jnp.where(far_up, zero, from_up[block].astype(jnp.float32))
        )

    def ring_steps():
        for step in range(1, n_col):
            start_halo(step - 1 + lead)
            value = local_total(step - 1)
            if step > 1:
                value = value + ring_in[step - 2].astype(jnp.float32)
            ring_out[step - 1] = value.astype(ring_out.dtype)
            copy = pltpu.make_async_remote_copy(
                src_ref=ring_out.at[step - 1],
                dst_ref=ring_in.at[step - 1],
                send_sem=ring_send.at[step - 1],
                recv_sem=ring_recv.at[step - 1],
                device_id=(row, succ),
                device_id_type=MESH,
            )
            copy.start()
            yield copy
        start_halo(n_col - 1 + lead)
        own[...] = local_total(n_col - 1) + ring_in[n_col - 2].astype(jnp.float32)

    def far_steps(side, part_ref, far):
        for step in range(1, n_col):
            block = ring_col((p - step + 2 * n_col) % n_col, n_col)
            copy = pltpu.make_async_remote_copy(
                src_ref=far_out.at[side, step - 1],
                dst_ref=far_in.at[side, step - 1],
                send_sem=far_send.at[side, step - 1],
                recv_sem=far_recv.at[side, step - 1],
                device_id=(row, succ),
                device_id_type=MESH,
            )

            def send(step=step, block=block, copy=copy):
                value = part_ref[block]
                if step > 1:
                    value = value + far_in[side, step - 2]
                far_out[side, step - 1] = value
                copy.start()

            pl.when(far)(send)
            yield Gated(copy, far)

        def finish():
            far_out[side, n_col - 1] = part_ref[col] + far_in[side, n_col - 2]

        pl.when(far)(finish)

    run_together(
        allreduce_steps(n_row, n_col, row, col, parts_ref, sums_ref, part, gath,
                        rsend, rrecv, dsend, drecv, gsend, grecv),
        ring_steps(),
        far_steps(0, up_ref, far_up),
        far_steps(1, down_ref, far_down),
    )
    lasts = []
    for side, target, slot, far in ((0, up, 0, far_up), (1, down, 1, far_down)):
        copy = pltpu.make_async_remote_copy(
            src_ref=far_out.at[side, n_col - 1],
            dst_ref=far_from.at[slot],
            send_sem=last_send.at[side],
            recv_sem=last_recv.at[slot],
            device_id=(target, col),
            device_id_type=MESH,
        )
        pl.when(far)(copy.start)
        lasts.append(copy)
    pl.when(far_up)(lasts[0].wait_send)
    pl.when(far_down)(lasts[1].wait_send)
    pl.when(far_down)(lasts[0].wait_recv)
    pl.when(far_up)(lasts[1].wait_recv)
    zero = jnp.zeros(o_ref.shape, jnp.float32)
    total = own[...] + jnp.where(far_down, far_from[0], zero) + jnp.where(far_up, far_from[1], zero)
    o_ref[...] = total
    for _, (to_up, to_down) in halos:
        pl.when(jnp.logical_not(far_up))(to_up.wait_send)
        pl.when(jnp.logical_not(far_down))(to_down.wait_send)


def reduce_spread(spread, parts, n_row, n_col):
    _, _, rows, width = spread.shape
    col_bits = n_col.bit_length() - 1
    row_bits = n_row.bit_length() - 1
    stacked, _ = parts.shape
    return pl.pallas_call(
        functools.partial(spread_kernel, n_row, n_col),
        out_shape=(
            jax.ShapeDtypeStruct((rows, width), jnp.float32),
            jax.ShapeDtypeStruct(parts.shape, jnp.float32),
        ),
        in_specs=[pl.BlockSpec(memory_space=pltpu.VMEM)] * 2,
        out_specs=(pl.BlockSpec(memory_space=pltpu.VMEM),) * 2,
        scratch_shapes=[
            pltpu.VMEM((rows, width), jnp.float32),
            pltpu.VMEM((n_col, rows, width), jnp.bfloat16),
            pltpu.VMEM((n_col, rows, width), jnp.bfloat16),
            pltpu.VMEM((n_col, rows, width), jnp.bfloat16),
            pltpu.VMEM((n_col, rows, width), jnp.bfloat16),
            pltpu.VMEM((n_col - 1, rows, width), jnp.bfloat16),
            pltpu.VMEM((n_col - 1, rows, width), jnp.bfloat16),
            pltpu.VMEM((2, n_col - 1, rows, width), jnp.float32),
            pltpu.VMEM((2, n_col, rows, width), jnp.float32),
            pltpu.VMEM((2, rows, width), jnp.float32),
            pltpu.SemaphoreType.DMA((n_col,)),
            pltpu.SemaphoreType.DMA((n_col,)),
            pltpu.SemaphoreType.DMA((n_col,)),
            pltpu.SemaphoreType.DMA((n_col,)),
            pltpu.SemaphoreType.DMA((n_col - 1,)),
            pltpu.SemaphoreType.DMA((n_col - 1,)),
            pltpu.SemaphoreType.DMA((2, n_col - 1)),
            pltpu.SemaphoreType.DMA((2, n_col - 1)),
            pltpu.SemaphoreType.DMA((2,)),
            pltpu.SemaphoreType.DMA((2,)),
            pltpu.VMEM((2 * row_bits, stacked // n_col, width), jnp.float32),
            pltpu.VMEM((1, n_col, stacked // n_col, width), jnp.float32),
            pltpu.SemaphoreType.DMA((n_col,)),
            pltpu.SemaphoreType.DMA((n_col,)),
            pltpu.SemaphoreType.DMA((row_bits,)),
            pltpu.SemaphoreType.DMA((row_bits,)),
            pltpu.SemaphoreType.DMA((n_col,)),
            pltpu.SemaphoreType.DMA((n_col,)),
        ],
        compiler_params=pltpu.CompilerParams(collective_id=2, has_side_effects=True),
    )(spread, parts)


def local_kernel(rows_ref, cols_ref, count_ref, window_ref, tiles_ref, feat_ref, w_ref, ws_ref, cot_ref,
                 act_ref, parts_ref, self_ref, spread, acc, grad_agg):
    tile = tiles_ref.shape[-1]
    nodes = acc.shape[0]
    count = jnp.minimum(count_ref[0], tiles_ref.shape[0])
    acc[...] = jnp.zeros_like(acc)

    def forward(j, carry):
        at = pl.multiple_of(rows_ref[j] * tile, tile)
        acc[pl.ds(at, tile), :] += jnp.dot(
            tiles_ref[j], window_ref[cols_ref[j]], preferred_element_type=jnp.float32
        )
        return carry

    lax.fori_loop(0, count, forward, 0)
    aggregated = acc[...].astype(jnp.bfloat16)
    features = feat_ref[...]
    pre_act = jnp.dot(aggregated, w_ref[...], preferred_element_type=jnp.float32) + jnp.dot(
        features, ws_ref[...], preferred_element_type=jnp.float32
    )
    sigma = jax.nn.sigmoid(pre_act)
    act_ref[...] = (pre_act * sigma).astype(act_ref.dtype)
    grad_pre = (cot_ref[...].astype(jnp.float32) * sigma * (1.0 + pre_act * (1.0 - sigma))).astype(
        jnp.bfloat16
    )
    over_nodes = (((0,), (0,)), ((), ()))
    parts_ref[pl.ds(0, nodes), :] = lax.dot_general(
        aggregated, grad_pre, over_nodes, preferred_element_type=jnp.float32
    )
    parts_ref[pl.ds(nodes, nodes), :] = lax.dot_general(
        features, grad_pre, over_nodes, preferred_element_type=jnp.float32
    )
    by_rows = (((1,), (1,)), ((), ()))
    grad_agg[...] = lax.dot_general(
        grad_pre, w_ref[...], by_rows, preferred_element_type=jnp.float32
    ).astype(jnp.bfloat16)
    self_ref[...] = lax.dot_general(grad_pre, ws_ref[...], by_rows, preferred_element_type=jnp.float32)
    spread[...] = jnp.zeros_like(spread)

    def backward(j, carry):
        at = pl.multiple_of(rows_ref[j] * tile, tile)
        column = cols_ref[j]
        spread[column] += lax.dot_general(
            tiles_ref[j], grad_agg[pl.ds(at, tile), :], over_nodes, preferred_element_type=jnp.float32
        )
        return carry

    lax.fori_loop(0, count, backward, 0)


def local_math(slot_rows, slot_cols, count, window, tiles, features, weight, weight_self, cotangent):
    nodes, width = features.shape
    span = window.shape[0] // 3
    tile = tiles.shape[-1]
    smem = pl.BlockSpec(memory_space=pltpu.SMEM)
    vmem = pl.BlockSpec(memory_space=pltpu.VMEM)
    return pl.pallas_call(
        local_kernel,
        out_shape=(
            jax.ShapeDtypeStruct((nodes, width), jnp.bfloat16),
            jax.ShapeDtypeStruct((2 * width, width), jnp.float32),
            jax.ShapeDtypeStruct((nodes, width), jnp.float32),
            jax.ShapeDtypeStruct((3 * span, tile, width), jnp.float32),
        ),
        in_specs=[smem, smem, smem] + [vmem] * 6,
        out_specs=(vmem,) * 4,
        scratch_shapes=[
            pltpu.VMEM((nodes, width), jnp.float32),
            pltpu.VMEM((nodes, width), jnp.bfloat16),
        ],
    )(slot_rows, slot_cols, count, window, tiles, features, weight, weight_self, cotangent)


def shards(features, weight, weight_self, tile_values, tile_rows, tile_cols, tile_count, cotangent):
    tile_block = tile_values[0]
    slot_rows = tile_rows[0]
    slot_cols = tile_cols[0]
    live_count = tile_count[0, 0]
    slot_total = tile_block.shape[0]
    tile_side = tile_block.shape[-1]
    node_rows = features.shape[0]
    width = features.shape[1]
    per_block = node_rows // tile_side
    col_count = lax.axis_size("col")
    row_count = lax.axis_size("row")
    span = col_count * per_block
    window = gather_window(features, row_count, col_count)
    window_tiles = window.reshape(-1, tile_side, width)
    activations, parts, self_feature, spread = local_math(
        slot_rows,
        slot_cols,
        tile_count[0],
        window_tiles,
        tile_block,
        features,
        weight,
        weight_self,
        cotangent,
    )
    factor = 1.0 / math.sqrt(node_rows * col_count * row_count)
    own_share, summed_parts = reduce_spread(
        spread.reshape(3, col_count, node_rows, width),
        parts,
        row_count,
        col_count,
    )
    feature_grad = (own_share + self_feature).astype(jnp.bfloat16)
    weight_total, self_total = summed_parts[:width], summed_parts[width:]
    return (activations, feature_grad, weight_total * factor, self_total * factor)


def solution(mesh):
    placed = (
        P(("row", "col"), None),
        P(),
        P(),
        P("row", "col", None, None),
        P("row", "col"),
        P("row", "col"),
        P("row", "col"),
        P(("row", "col"), None),
    )
    return jax.shard_map(
        shards,
        mesh=mesh,
        in_specs=placed,
        out_specs=(P(("row", "col"), None), P(("row", "col"), None), P(), P()),
        check_vma=False,
    )
```

```python
import functools
import math

import jax
import jax.numpy as jnp
from jax import lax
from jax.experimental import pallas as pl
from jax.experimental.pallas import tpu as pltpu
from jax.sharding import PartitionSpec as P

MESH = pl.DeviceIdType.MESH


def flip(index, stride):
    bit = (index // stride) % 2
    return index + stride - 2 * stride * bit, bit


def allreduce_partners(n_row, n_col, row, col):
    partners = [(row, peer) for peer in range(n_col)]
    for k in range(n_row.bit_length() - 1):
        partners.append((flip(row, 1 << k)[0], col))
    return partners


class Group:
    def __init__(self, copies, receipts, col):
        self.copies = copies
        self.receipts = receipts
        self.col = col

    def wait(self):
        for peer, (copy, receipt) in enumerate(zip(self.copies, self.receipts)):
            @pl.when(peer != self.col)
            def _():
                copy.wait_send()
                receipt.wait_recv()


def allreduce_steps(n_row, n_col, row, col, x_ref, o_ref, part, gath, rsend, rrecv, dsend, drecv, gsend, grecv):
    row_bits = n_row.bit_length() - 1
    chunk = x_ref.shape[0] // n_col
    mine = pl.ds(pl.multiple_of(col * chunk, 8), chunk)
    copies, receipts = [], []
    for peer in range(n_col):
        copies.append(pltpu.make_async_remote_copy(
            src_ref=x_ref.at[pl.ds(peer * chunk, chunk)],
            dst_ref=gath.at[0, col],
            send_sem=rsend.at[peer],
            recv_sem=rrecv.at[col],
            device_id=(row, peer),
            device_id_type=MESH,
        ))
        receipts.append(pltpu.make_async_remote_copy(
            src_ref=x_ref.at[pl.ds(peer * chunk, chunk)],
            dst_ref=gath.at[0, peer],
            send_sem=rsend.at[peer],
            recv_sem=rrecv.at[peer],
            device_id=(row, peer),
            device_id_type=MESH,
        ))
        pl.when(peer != col)(copies[-1].start)
    yield Group(copies, receipts, col)
    total = x_ref[mine, :]
    for peer in range(n_col):
        total = total + jnp.where(peer == col, jnp.zeros_like(total), gath[0, peer])
    for k in range(row_bits):
        other, _ = flip(row, 1 << k)
        hold = part.at[2 * k]
        hold[...] = total
        copy = pltpu.make_async_remote_copy(
            src_ref=hold,
            dst_ref=part.at[2 * k + 1],
            send_sem=dsend.at[k],
            recv_sem=drecv.at[k],
            device_id=(other, col),
            device_id_type=MESH,
        )
        copy.start()
        yield copy
        total = total + part[2 * k + 1]
    o_ref[mine, :] = total
    copies, receipts = [], []
    for peer in range(n_col):
        copies.append(pltpu.make_async_remote_copy(
            src_ref=o_ref.at[mine],
            dst_ref=o_ref.at[mine],
            send_sem=gsend.at[peer],
            recv_sem=grecv.at[col],
            device_id=(row, peer),
            device_id_type=MESH,
        ))
        receipts.append(pltpu.make_async_remote_copy(
            src_ref=o_ref.at[mine],
            dst_ref=o_ref.at[pl.ds(peer * chunk, chunk)],
            send_sem=gsend.at[peer],
            recv_sem=grecv.at[peer],
            device_id=(row, peer),
            device_id_type=MESH,
        ))
        pl.when(peer != col)(copies[-1].start)
    yield Group(copies, receipts, col)


def run_together(*chains):
    active = list(chains)
    while active:
        copies, kept = [], []
        for chain in active:
            try:
                copies.append(next(chain))
                kept.append(chain)
            except StopIteration:
                pass
        for copy in copies:
            copy.wait()
        active = kept


def ring_position(col, n):
    core = col % 2
    y = col // 2
    return y + core * (n - 1 - 2 * y)


def ring_col(p, n):
    q = p // (n // 2)
    y = p + q * (n - 1 - 2 * p)
    return 2 * y + q


def gather_kernel(n_row, n_col, x_ref, w_ref, ring_send, ring_recv, halo_send, halo_recv, local_sem):
    row = lax.axis_index("row")
    col = lax.axis_index("col")
    p = ring_position(col, n_col)
    succ = ring_col((p + 1) % n_col, n_col)
    pred = ring_col((p + n_col - 1) % n_col, n_col)
    up = (row + 1) % n_row
    down = (row + n_row - 1) % n_row
    half = max(n_row // 2, 1)
    far = {0: row % half == 0, 2: (row + 1) % half == 0}
    barrier = pltpu.get_barrier_semaphore()
    for device in ((row, succ), (row, pred), (up, col), (down, col)):
        pl.semaphore_signal(barrier, inc=1, device_id=device, device_id_type=MESH)
    pl.semaphore_wait(barrier, 4)
    local = pltpu.make_async_copy(x_ref, w_ref.at[1, col], local_sem.at[0])
    local.start()

    def halo(src, block, index):
        copies = {}
        for target, slot in ((up, 0), (down, 2)):
            copies[slot] = pltpu.make_async_remote_copy(
                src_ref=src,
                dst_ref=w_ref.at[slot, block],
                send_sem=halo_send.at[slot // 2, index],
                recv_sem=halo_recv.at[slot // 2, index],
                device_id=(target, col),
                device_id_type=MESH,
            )
        return copies

    halos = [(col, halo(x_ref, col, 0))]
    for copy in halos[0][1].values():
        copy.start()
    sent = col
    for step in range(1, n_col):
        copies = {}
        for group in (1, 0, 2):
            src = x_ref if (step == 1 and group == 1) else w_ref.at[group, sent]
            copies[group] = pltpu.make_async_remote_copy(
                src_ref=src,
                dst_ref=w_ref.at[group, sent],
                send_sem=ring_send.at[group, step - 1],
                recv_sem=ring_recv.at[group, step - 1],
                device_id=(row, succ),
                device_id_type=MESH,
            )
        copies[1].start()
        for group in (0, 2):
            @pl.when(far[group])
            def _():
                if step == 1:
                    halos[0][1][group].wait_recv()
                copies[group].start()
        copies[1].wait()
        for group in (0, 2):
            @pl.when(far[group])
            def _():
                copies[group].wait()
        sent = ring_col((p - step + n_col) % n_col, n_col)
        forward = halo(w_ref.at[1, sent], sent, step)
        halos.append((sent, forward))
        for slot in (0, 2):
            @pl.when(jnp.logical_not(far[2 - slot]))
            def _():
                forward[slot].start()
    for copy in halos[0][1].values():
        copy.wait_send()
    for slot in (0, 2):
        @pl.when(jnp.logical_not(far[slot]))
        def _():
            halos[0][1][slot].wait_recv()
    for _, copies in halos[1:]:
        for slot in (0, 2):
            @pl.when(jnp.logical_not(far[2 - slot]))
            def _():
                copies[slot].wait_send()

            @pl.when(jnp.logical_not(far[slot]))
            def _():
                copies[slot].wait_recv()
    local.wait()


def gather_window(block, n_row, n_col):
    rows, width = block.shape
    return pl.pallas_call(
        functools.partial(gather_kernel, n_row, n_col),
        out_shape=jax.ShapeDtypeStruct((3, n_col, rows, width), block.dtype),
        in_specs=[pl.BlockSpec(memory_space=pltpu.VMEM)],
        out_specs=pl.BlockSpec(memory_space=pltpu.VMEM),
        scratch_shapes=[
            pltpu.SemaphoreType.DMA((3, n_col - 1)),
            pltpu.SemaphoreType.DMA((3, n_col - 1)),
            pltpu.SemaphoreType.DMA((2, n_col)),
            pltpu.SemaphoreType.DMA((2, n_col)),
            pltpu.SemaphoreType.DMA((1,)),
        ],
        compiler_params=pltpu.CompilerParams(collective_id=1, has_side_effects=True),
    )(block)


class Gated:
    def __init__(self, copy, cond):
        self.copy = copy
        self.cond = cond

    def wait(self):
        pl.when(self.cond)(self.copy.wait)


def spread_kernel(n_row, n_col, spread_ref, parts_ref, o_ref, sums_ref, own,
                  up_bf, down_bf,
                  from_down, from_up, ring_in, ring_out, far_in, far_out, far_from, up_send, down_send,
                  from_down_sem, from_up_sem, ring_send, ring_recv, far_send, far_recv, last_send, last_recv,
                  part, gath, rsend, rrecv, dsend, drecv, gsend, grecv):
    row = lax.axis_index("row")
    col = lax.axis_index("col")
    p = ring_position(col, n_col)
    succ = ring_col((p + 1) % n_col, n_col)
    pred = ring_col((p + n_col - 1) % n_col, n_col)
    up = (row + 1) % n_row
    down = (row + n_row - 1) % n_row
    half = max(n_row // 2, 1)
    far_down = row % half == 0
    far_up = (row + 1) % half == 0
    partners = [(row, succ), (row, pred), (up, col), (down, col)]
    partners += allreduce_partners(n_row, n_col, row, col)
    barrier = pltpu.get_barrier_semaphore()
    for device in partners:
        def signal(device=device):
            pl.semaphore_signal(barrier, inc=1, device_id=device, device_id_type=MESH)

        pl.when(jnp.logical_or(device[0] != row, device[1] != col))(signal)
    pl.semaphore_wait(barrier, len(partners) - 1)
    mid_ref, up_ref, down_ref = spread_ref.at[1], spread_ref.at[2], spread_ref.at[0]
    up_bf[...] = up_ref[...].astype(up_bf.dtype)
    down_bf[...] = down_ref[...].astype(down_bf.dtype)
    halos = []
    starts = []
    lead = 2
    for step in range(1, n_col + 1):
        block = ring_col((p - step + 2 * n_col) % n_col, n_col)
        pair = []
        for src, dst, target, send, recv, far in (
            (up_bf, from_down, up, up_send, from_down_sem, far_up),
            (down_bf, from_up, down, down_send, from_up_sem, far_down),
        ):
            copy = pltpu.make_async_remote_copy(
                src_ref=src.at[block],
                dst_ref=dst.at[block],
                send_sem=send.at[step - 1],
                recv_sem=recv.at[step - 1],
                device_id=(target, col),
                device_id_type=MESH,
            )
            pair.append((copy, far))
        halos.append((block, [copy for copy, _ in pair]))
        starts.append(pair)

    def start_halo(index):
        if index < len(starts):
            for copy, far in starts[index]:
                pl.when(jnp.logical_not(far))(copy.start)

    for index in range(lead):
        start_halo(index)

    def local_total(index):
        block, (from_below, from_above) = halos[index]
        pl.when(jnp.logical_not(far_down))(from_below.wait_recv)
        pl.when(jnp.logical_not(far_up))(from_above.wait_recv)
        zero = jnp.zeros(mid_ref.shape[1:], jnp.float32)
        return (
            mid_ref[block]
            + jnp.where(far_down, zero, from_down[block].astype(jnp.float32))
            + jnp.where(far_up, zero, from_up[block].astype(jnp.float32))
        )

    def ring_steps():
        for step in range(1, n_col):
            start_halo(step - 1 + lead)
            value = local_total(step - 1)
            if step > 1:
                value = value + ring_in[step - 2].astype(jnp.float32)
            ring_out[step - 1] = value.astype(ring_out.dtype)
            copy = pltpu.make_async_remote_copy(
                src_ref=ring_out.at[step - 1],
                dst_ref=ring_in.at[step - 1],
                send_sem=ring_send.at[step - 1],
                recv_sem=ring_recv.at[step - 1],
                device_id=(row, succ),
                device_id_type=MESH,
            )
            copy.start()
            yield copy
        start_halo(n_col - 1 + lead)
        own[...] = local_total(n_col - 1) + ring_in[n_col - 2].astype(jnp.float32)

    def far_steps(side, part_ref, far):
        for step in range(1, n_col):
            block = ring_col((p - step + 2 * n_col) % n_col, n_col)
            copy = pltpu.make_async_remote_copy(
                src_ref=far_out.at[side, step - 1],
                dst_ref=far_in.at[side, step - 1],
                send_sem=far_send.at[side, step - 1],
                recv_sem=far_recv.at[side, step - 1],
                device_id=(row, succ),
                device_id_type=MESH,
            )

            def send(step=step, block=block, copy=copy):
                value = part_ref[block]
                if step > 1:
                    value = value + far_in[side, step - 2]
                far_out[side, step - 1] = value
                copy.start()

            pl.when(far)(send)
            yield Gated(copy, far)

        def finish():
            far_out[side, n_col - 1] = part_ref[col] + far_in[side, n_col - 2]

        pl.when(far)(finish)

    run_together(
        allreduce_steps(n_row, n_col, row, col, parts_ref, sums_ref, part, gath,
                        rsend, rrecv, dsend, drecv, gsend, grecv),
        ring_steps(),
        far_steps(0, up_ref, far_up),
        far_steps(1, down_ref, far_down),
    )
    lasts = []
    for side, target, slot, far in ((0, up, 0, far_up), (1, down, 1, far_down)):
        copy = pltpu.make_async_remote_copy(
            src_ref=far_out.at[side, n_col - 1],
            dst_ref=far_from.at[slot],
            send_sem=last_send.at[side],
            recv_sem=last_recv.at[slot],
            device_id=(target, col),
            device_id_type=MESH,
        )
        pl.when(far)(copy.start)
        lasts.append(copy)
    pl.when(far_up)(lasts[0].wait_send)
    pl.when(far_down)(lasts[1].wait_send)
    pl.when(far_down)(lasts[0].wait_recv)
    pl.when(far_up)(lasts[1].wait_recv)
    zero = jnp.zeros(o_ref.shape, jnp.float32)
    total = own[...] + jnp.where(far_down, far_from[0], zero) + jnp.where(far_up, far_from[1], zero)
    o_ref[...] = total
    for _, (to_up, to_down) in halos:
        pl.when(jnp.logical_not(far_up))(to_up.wait_send)
        pl.when(jnp.logical_not(far_down))(to_down.wait_send)


def reduce_spread(spread, parts, n_row, n_col):
    _, _, rows, width = spread.shape
    col_bits = n_col.bit_length() - 1
    row_bits = n_row.bit_length() - 1
    stacked, _ = parts.shape
    return pl.pallas_call(
        functools.partial(spread_kernel, n_row, n_col),
        out_shape=(
            jax.ShapeDtypeStruct((rows, width), jnp.float32),
            jax.ShapeDtypeStruct(parts.shape, jnp.float32),
        ),
        in_specs=[pl.BlockSpec(memory_space=pltpu.VMEM)] * 2,
        out_specs=(pl.BlockSpec(memory_space=pltpu.VMEM),) * 2,
        scratch_shapes=[
            pltpu.VMEM((rows, width), jnp.float32),
            pltpu.VMEM((n_col, rows, width), jnp.bfloat16),
            pltpu.VMEM((n_col, rows, width), jnp.bfloat16),
            pltpu.VMEM((n_col, rows, width), jnp.bfloat16),
            pltpu.VMEM((n_col, rows, width), jnp.bfloat16),
            pltpu.VMEM((n_col - 1, rows, width), jnp.bfloat16),
            pltpu.VMEM((n_col - 1, rows, width), jnp.bfloat16),
            pltpu.VMEM((2, n_col - 1, rows, width), jnp.float32),
            pltpu.VMEM((2, n_col, rows, width), jnp.float32),
            pltpu.VMEM((2, rows, width), jnp.float32),
            pltpu.SemaphoreType.DMA((n_col,)),
            pltpu.SemaphoreType.DMA((n_col,)),
            pltpu.SemaphoreType.DMA((n_col,)),
            pltpu.SemaphoreType.DMA((n_col,)),
            pltpu.SemaphoreType.DMA((n_col - 1,)),
            pltpu.SemaphoreType.DMA((n_col - 1,)),
            pltpu.SemaphoreType.DMA((2, n_col - 1)),
            pltpu.SemaphoreType.DMA((2, n_col - 1)),
            pltpu.SemaphoreType.DMA((2,)),
            pltpu.SemaphoreType.DMA((2,)),
            pltpu.VMEM((2 * row_bits, stacked // n_col, width), jnp.float32),
            pltpu.VMEM((1, n_col, stacked // n_col, width), jnp.float32),
            pltpu.SemaphoreType.DMA((n_col,)),
            pltpu.SemaphoreType.DMA((n_col,)),
            pltpu.SemaphoreType.DMA((row_bits,)),
            pltpu.SemaphoreType.DMA((row_bits,)),
            pltpu.SemaphoreType.DMA((n_col,)),
            pltpu.SemaphoreType.DMA((n_col,)),
        ],
        compiler_params=pltpu.CompilerParams(collective_id=2, has_side_effects=True),
    )(spread, parts)


def local_kernel(rows_ref, cols_ref, count_ref, window_ref, tiles_ref, feat_ref, w_ref, ws_ref, cot_ref,
                 act_ref, parts_ref, self_ref, spread, acc, grad_agg):
    tile = tiles_ref.shape[-1]
    nodes = acc.shape[0]
    count = jnp.minimum(count_ref[0], tiles_ref.shape[0])
    acc[...] = jnp.zeros_like(acc)

    last = tiles_ref.shape[0] - 1

    def forward(i, carry):
        j = 2 * i
        k = jnp.minimum(j + 1, last)
        first = jnp.dot(tiles_ref[j], window_ref[cols_ref[j]], preferred_element_type=jnp.float32)
        second = jnp.dot(tiles_ref[k], window_ref[cols_ref[k]], preferred_element_type=jnp.float32)
        at = pl.multiple_of(rows_ref[j] * tile, tile)
        acc[pl.ds(at, tile), :] += first

        @pl.when(j + 1 < count)
        def _():
            at = pl.multiple_of(rows_ref[k] * tile, tile)
            acc[pl.ds(at, tile), :] += second

        return carry

    lax.fori_loop(0, (count + 1) // 2, forward, 0)
    aggregated = acc[...].astype(jnp.bfloat16)
    features = feat_ref[...]
    pre_act = jnp.dot(aggregated, w_ref[...], preferred_element_type=jnp.float32) + jnp.dot(
        features, ws_ref[...], preferred_element_type=jnp.float32
    )
    sigma = jax.nn.sigmoid(pre_act)
    act_ref[...] = (pre_act * sigma).astype(act_ref.dtype)
    grad_pre = (cot_ref[...].astype(jnp.float32) * sigma * (1.0 + pre_act * (1.0 - sigma))).astype(
        jnp.bfloat16
    )
    over_nodes = (((0,), (0,)), ((), ()))
    parts_ref[pl.ds(0, nodes), :] = lax.dot_general(
        aggregated, grad_pre, over_nodes, preferred_element_type=jnp.float32
    )
    parts_ref[pl.ds(nodes, nodes), :] = lax.dot_general(
        features, grad_pre, over_nodes, preferred_element_type=jnp.float32
    )
    by_rows = (((1,), (1,)), ((), ()))
    grad_agg[...] = lax.dot_general(
        grad_pre, w_ref[...], by_rows, preferred_element_type=jnp.float32
    ).astype(jnp.bfloat16)
    self_ref[...] = lax.dot_general(grad_pre, ws_ref[...], by_rows, preferred_element_type=jnp.float32)
    spread[...] = jnp.zeros_like(spread)

    def backward(i, carry):
        j = 2 * i
        k = jnp.minimum(j + 1, last)
        at = pl.multiple_of(rows_ref[j] * tile, tile)
        first = lax.dot_general(
            tiles_ref[j], grad_agg[pl.ds(at, tile), :], over_nodes, preferred_element_type=jnp.float32
        )
        at = pl.multiple_of(rows_ref[k] * tile, tile)
        second = lax.dot_general(
            tiles_ref[k], grad_agg[pl.ds(at, tile), :], over_nodes, preferred_element_type=jnp.float32
        )
        spread[cols_ref[j]] += first

        @pl.when(j + 1 < count)
        def _():
            spread[cols_ref[k]] += second

        return carry

    lax.fori_loop(0, (count + 1) // 2, backward, 0)


def local_math(slot_rows, slot_cols, count, window, tiles, features, weight, weight_self, cotangent):
    nodes, width = features.shape
    span = window.shape[0] // 3
    tile = tiles.shape[-1]
    smem = pl.BlockSpec(memory_space=pltpu.SMEM)
    vmem = pl.BlockSpec(memory_space=pltpu.VMEM)
    return pl.pallas_call(
        local_kernel,
        out_shape=(
            jax.ShapeDtypeStruct((nodes, width), jnp.bfloat16),
            jax.ShapeDtypeStruct((2 * width, width), jnp.float32),
            jax.ShapeDtypeStruct((nodes, width), jnp.float32),
            jax.ShapeDtypeStruct((3 * span, tile, width), jnp.float32),
        ),
        in_specs=[smem, smem, smem] + [vmem] * 6,
        out_specs=(vmem,) * 4,
        scratch_shapes=[
            pltpu.VMEM((nodes, width), jnp.float32),
            pltpu.VMEM((nodes, width), jnp.bfloat16),
        ],
    )(slot_rows, slot_cols, count, window, tiles, features, weight, weight_self, cotangent)


def shards(features, weight, weight_self, tile_values, tile_rows, tile_cols, tile_count, cotangent):
    tile_block = tile_values[0]
    slot_rows = tile_rows[0]
    slot_cols = tile_cols[0]
    live_count = tile_count[0, 0]
    slot_total = tile_block.shape[0]
    tile_side = tile_block.shape[-1]
    node_rows = features.shape[0]
    width = features.shape[1]
    per_block = node_rows // tile_side
    col_count = lax.axis_size("col")
    row_count = lax.axis_size("row")
    span = col_count * per_block
    window = gather_window(features, row_count, col_count)
    window_tiles = window.reshape(-1, tile_side, width)
    activations, parts, self_feature, spread = local_math(
        slot_rows,
        slot_cols,
        tile_count[0],
        window_tiles,
        tile_block,
        features,
        weight,
        weight_self,
        cotangent,
    )
    factor = 1.0 / math.sqrt(node_rows * col_count * row_count)
    own_share, summed_parts = reduce_spread(
        spread.reshape(3, col_count, node_rows, width),
        parts,
        row_count,
        col_count,
    )
    feature_grad = (own_share + self_feature).astype(jnp.bfloat16)
    weight_total, self_total = summed_parts[:width], summed_parts[width:]
    return (activations, feature_grad, weight_total * factor, self_total * factor)


def solution(mesh):
    placed = (
        P(("row", "col"), None),
        P(),
        P(),
        P("row", "col", None, None),
        P("row", "col"),
        P("row", "col"),
        P("row", "col"),
        P(("row", "col"), None),
    )
    return jax.shard_map(
        shards,
        mesh=mesh,
        in_specs=placed,
        out_specs=(P(("row", "col"), None), P(("row", "col"), None), P(), P()),
        check_vma=False,
    )
```

```python
import functools
import math

import jax
import jax.numpy as jnp
from jax import lax
from jax.experimental import pallas as pl
from jax.experimental.pallas import tpu as pltpu
from jax.sharding import PartitionSpec as P

MESH = pl.DeviceIdType.MESH


def flip(index, stride):
    bit = (index // stride) % 2
    return index + stride - 2 * stride * bit, bit


def allreduce_partners(n_row, n_col, row, col):
    partners = [(row, peer) for peer in range(n_col)]
    for k in range(n_row.bit_length() - 1):
        partners.append((flip(row, 1 << k)[0], col))
    return partners


class Group:
    def __init__(self, copies, receipts, col):
        self.copies = copies
        self.receipts = receipts
        self.col = col

    def wait(self):
        for peer, (copy, receipt) in enumerate(zip(self.copies, self.receipts)):
            @pl.when(peer != self.col)
            def _():
                copy.wait_send()
                receipt.wait_recv()


def allreduce_steps(n_row, n_col, row, col, x_ref, o_ref, part, gath, rsend, rrecv, dsend, drecv, gsend, grecv):
    row_bits = n_row.bit_length() - 1
    chunk = x_ref.shape[0] // n_col
    mine = pl.ds(pl.multiple_of(col * chunk, 8), chunk)
    copies, receipts = [], []
    for peer in range(n_col):
        copies.append(pltpu.make_async_remote_copy(
            src_ref=x_ref.at[pl.ds(peer * chunk, chunk)],
            dst_ref=gath.at[0, col],
            send_sem=rsend.at[peer],
            recv_sem=rrecv.at[col],
            device_id=(row, peer),
            device_id_type=MESH,
        ))
        receipts.append(pltpu.make_async_remote_copy(
            src_ref=x_ref.at[pl.ds(peer * chunk, chunk)],
            dst_ref=gath.at[0, peer],
            send_sem=rsend.at[peer],
            recv_sem=rrecv.at[peer],
            device_id=(row, peer),
            device_id_type=MESH,
        ))
        pl.when(peer != col)(copies[-1].start)
    yield Group(copies, receipts, col)
    total = x_ref[mine, :]
    for peer in range(n_col):
        total = total + jnp.where(peer == col, jnp.zeros_like(total), gath[0, peer])
    for k in range(row_bits):
        other, _ = flip(row, 1 << k)
        hold = part.at[2 * k]
        hold[...] = total
        copy = pltpu.make_async_remote_copy(
            src_ref=hold,
            dst_ref=part.at[2 * k + 1],
            send_sem=dsend.at[k],
            recv_sem=drecv.at[k],
            device_id=(other, col),
            device_id_type=MESH,
        )
        copy.start()
        yield copy
        total = total + part[2 * k + 1]
    o_ref[mine, :] = total
    copies, receipts = [], []
    for peer in range(n_col):
        copies.append(pltpu.make_async_remote_copy(
            src_ref=o_ref.at[mine],
            dst_ref=o_ref.at[mine],
            send_sem=gsend.at[peer],
            recv_sem=grecv.at[col],
            device_id=(row, peer),
            device_id_type=MESH,
        ))
        receipts.append(pltpu.make_async_remote_copy(
            src_ref=o_ref.at[mine],
            dst_ref=o_ref.at[pl.ds(peer * chunk, chunk)],
            send_sem=gsend.at[peer],
            recv_sem=grecv.at[peer],
            device_id=(row, peer),
            device_id_type=MESH,
        ))
        pl.when(peer != col)(copies[-1].start)
    yield Group(copies, receipts, col)


def run_together(*chains):
    active = list(chains)
    while active:
        copies, kept = [], []
        for chain in active:
            try:
                copies.append(next(chain))
                kept.append(chain)
            except StopIteration:
                pass
        for copy in copies:
            copy.wait()
        active = kept


def ring_position(col, n):
    core = col % 2
    y = col // 2
    return y + core * (n - 1 - 2 * y)


def ring_col(p, n):
    q = p // (n // 2)
    y = p + q * (n - 1 - 2 * p)
    return 2 * y + q


def gather_kernel(n_row, n_col, x_ref, w_ref, ring_send, ring_recv, halo_send, halo_recv, local_sem):
    row = lax.axis_index("row")
    col = lax.axis_index("col")
    p = ring_position(col, n_col)
    succ = ring_col((p + 1) % n_col, n_col)
    pred = ring_col((p + n_col - 1) % n_col, n_col)
    up = (row + 1) % n_row
    down = (row + n_row - 1) % n_row
    half = max(n_row // 2, 1)
    far = {0: row % half == 0, 2: (row + 1) % half == 0}
    barrier = pltpu.get_barrier_semaphore()
    for device in ((row, succ), (row, pred), (up, col), (down, col)):
        pl.semaphore_signal(barrier, inc=1, device_id=device, device_id_type=MESH)
    pl.semaphore_wait(barrier, 4)
    local = pltpu.make_async_copy(x_ref, w_ref.at[1, col], local_sem.at[0])
    local.start()

    def halo(src, block, index):
        copies = {}
        for target, slot in ((up, 0), (down, 2)):
            copies[slot] = pltpu.make_async_remote_copy(
                src_ref=src,
                dst_ref=w_ref.at[slot, block],
                send_sem=halo_send.at[slot // 2, index],
                recv_sem=halo_recv.at[slot // 2, index],
                device_id=(target, col),
                device_id_type=MESH,
            )
        return copies

    halos = [(col, halo(x_ref, col, 0))]
    for copy in halos[0][1].values():
        copy.start()
    sent = col
    for step in range(1, n_col):
        copies = {}
        for group in (1, 0, 2):
            src = x_ref if (step == 1 and group == 1) else w_ref.at[group, sent]
            copies[group] = pltpu.make_async_remote_copy(
                src_ref=src,
                dst_ref=w_ref.at[group, sent],
                send_sem=ring_send.at[group, step - 1],
                recv_sem=ring_recv.at[group, step - 1],
                device_id=(row, succ),
                device_id_type=MESH,
            )
        copies[1].start()
        for group in (0, 2):
            @pl.when(far[group])
            def _():
                if step == 1:
                    halos[0][1][group].wait_recv()
                copies[group].start()
        copies[1].wait()
        for group in (0, 2):
            @pl.when(far[group])
            def _():
                copies[group].wait()
        sent = ring_col((p - step + n_col) % n_col, n_col)
        forward = halo(w_ref.at[1, sent], sent, step)
        halos.append((sent, forward))
        for slot in (0, 2):
            @pl.when(jnp.logical_not(far[2 - slot]))
            def _():
                forward[slot].start()
    for copy in halos[0][1].values():
        copy.wait_send()
    for slot in (0, 2):
        @pl.when(jnp.logical_not(far[slot]))
        def _():
            halos[0][1][slot].wait_recv()
    for _, copies in halos[1:]:
        for slot in (0, 2):
            @pl.when(jnp.logical_not(far[2 - slot]))
            def _():
                copies[slot].wait_send()

            @pl.when(jnp.logical_not(far[slot]))
            def _():
                copies[slot].wait_recv()
    local.wait()


def gather_window(block, n_row, n_col):
    rows, width = block.shape
    return pl.pallas_call(
        functools.partial(gather_kernel, n_row, n_col),
        out_shape=jax.ShapeDtypeStruct((3, n_col, rows, width), block.dtype),
        in_specs=[pl.BlockSpec(memory_space=pltpu.VMEM)],
        out_specs=pl.BlockSpec(memory_space=pltpu.VMEM),
        scratch_shapes=[
            pltpu.SemaphoreType.DMA((3, n_col - 1)),
            pltpu.SemaphoreType.DMA((3, n_col - 1)),
            pltpu.SemaphoreType.DMA((2, n_col)),
            pltpu.SemaphoreType.DMA((2, n_col)),
            pltpu.SemaphoreType.DMA((1,)),
        ],
        compiler_params=pltpu.CompilerParams(collective_id=1, has_side_effects=True),
    )(block)


class Gated:
    def __init__(self, copy, cond):
        self.copy = copy
        self.cond = cond

    def wait(self):
        pl.when(self.cond)(self.copy.wait)


def spread_kernel(n_row, n_col, scale, spread_ref, parts_ref, self_ref, o_ref, sums_ref, own,
                  up_bf, down_bf,
                  from_down, from_up, ring_in, ring_out, far_in, far_out, far_from, up_send, down_send,
                  from_down_sem, from_up_sem, ring_send, ring_recv, far_send, far_recv, last_send, last_recv,
                  part, gath, rsend, rrecv, dsend, drecv, gsend, grecv):
    row = lax.axis_index("row")
    col = lax.axis_index("col")
    p = ring_position(col, n_col)
    succ = ring_col((p + 1) % n_col, n_col)
    pred = ring_col((p + n_col - 1) % n_col, n_col)
    up = (row + 1) % n_row
    down = (row + n_row - 1) % n_row
    half = max(n_row // 2, 1)
    far_down = row % half == 0
    far_up = (row + 1) % half == 0
    partners = [(row, succ), (row, pred), (up, col), (down, col)]
    partners += allreduce_partners(n_row, n_col, row, col)
    barrier = pltpu.get_barrier_semaphore()
    for device in partners:
        def signal(device=device):
            pl.semaphore_signal(barrier, inc=1, device_id=device, device_id_type=MESH)

        pl.when(jnp.logical_or(device[0] != row, device[1] != col))(signal)
    pl.semaphore_wait(barrier, len(partners) - 1)
    mid_ref, up_ref, down_ref = spread_ref.at[1], spread_ref.at[2], spread_ref.at[0]
    up_bf[...] = up_ref[...].astype(up_bf.dtype)
    down_bf[...] = down_ref[...].astype(down_bf.dtype)
    halos = []
    starts = []
    lead = 2
    for step in range(1, n_col + 1):
        block = ring_col((p - step + 2 * n_col) % n_col, n_col)
        pair = []
        for src, dst, target, send, recv, far in (
            (up_bf, from_down, up, up_send, from_down_sem, far_up),
            (down_bf, from_up, down, down_send, from_up_sem, far_down),
        ):
            copy = pltpu.make_async_remote_copy(
                src_ref=src.at[block],
                dst_ref=dst.at[block],
                send_sem=send.at[step - 1],
                recv_sem=recv.at[step - 1],
                device_id=(target, col),
                device_id_type=MESH,
            )
            pair.append((copy, far))
        halos.append((block, [copy for copy, _ in pair]))
        starts.append(pair)

    def start_halo(index):
        if index < len(starts):
            for copy, far in starts[index]:
                pl.when(jnp.logical_not(far))(copy.start)

    for index in range(lead):
        start_halo(index)

    def local_total(index):
        block, (from_below, from_above) = halos[index]
        pl.when(jnp.logical_not(far_down))(from_below.wait_recv)
        pl.when(jnp.logical_not(far_up))(from_above.wait_recv)
        zero = jnp.zeros(mid_ref.shape[1:], jnp.float32)
        return (
            mid_ref[block]
            + jnp.where(far_down, zero, from_down[block].astype(jnp.float32))
            + jnp.where(far_up, zero, from_up[block].astype(jnp.float32))
        )

    def ring_steps():
        for step in range(1, n_col):
            start_halo(step - 1 + lead)
            value = local_total(step - 1)
            if step > 1:
                value = value + ring_in[step - 2].astype(jnp.float32)
            ring_out[step - 1] = value.astype(ring_out.dtype)
            copy = pltpu.make_async_remote_copy(
                src_ref=ring_out.at[step - 1],
                dst_ref=ring_in.at[step - 1],
                send_sem=ring_send.at[step - 1],
                recv_sem=ring_recv.at[step - 1],
                device_id=(row, succ),
                device_id_type=MESH,
            )
            copy.start()
            yield copy
        start_halo(n_col - 1 + lead)
        own[...] = local_total(n_col - 1) + ring_in[n_col - 2].astype(jnp.float32)

    def far_steps(side, part_ref, far):
        for step in range(1, n_col):
            block = ring_col((p - step + 2 * n_col) % n_col, n_col)
            copy = pltpu.make_async_remote_copy(
                src_ref=far_out.at[side, step - 1],
                dst_ref=far_in.at[side, step - 1],
                send_sem=far_send.at[side, step - 1],
                recv_sem=far_recv.at[side, step - 1],
                device_id=(row, succ),
                device_id_type=MESH,
            )

            def send(step=step, block=block, copy=copy):
                value = part_ref[block]
                if step > 1:
                    value = value + far_in[side, step - 2]
                far_out[side, step - 1] = value
                copy.start()

            pl.when(far)(send)
            yield Gated(copy, far)

        def finish():
            far_out[side, n_col - 1] = part_ref[col] + far_in[side, n_col - 2]

        pl.when(far)(finish)

    run_together(
        ring_steps(),
        far_steps(0, up_ref, far_up),
        far_steps(1, down_ref, far_down),
        allreduce_steps(n_row, n_col, row, col, parts_ref, sums_ref, part, gath,
                        rsend, rrecv, dsend, drecv, gsend, grecv),
    )
    lasts = []
    for side, target, slot, far in ((0, up, 0, far_up), (1, down, 1, far_down)):
        copy = pltpu.make_async_remote_copy(
            src_ref=far_out.at[side, n_col - 1],
            dst_ref=far_from.at[slot],
            send_sem=last_send.at[side],
            recv_sem=last_recv.at[slot],
            device_id=(target, col),
            device_id_type=MESH,
        )
        pl.when(far)(copy.start)
        lasts.append(copy)
    pl.when(far_up)(lasts[0].wait_send)
    pl.when(far_down)(lasts[1].wait_send)
    pl.when(far_down)(lasts[0].wait_recv)
    pl.when(far_up)(lasts[1].wait_recv)
    zero = jnp.zeros(o_ref.shape, jnp.float32)
    total = own[...] + jnp.where(far_down, far_from[0], zero) + jnp.where(far_up, far_from[1], zero)
    o_ref[...] = (total + self_ref[...]).astype(o_ref.dtype)
    sums_ref[...] = sums_ref[...] * scale
    for _, (to_up, to_down) in halos:
        pl.when(jnp.logical_not(far_up))(to_up.wait_send)
        pl.when(jnp.logical_not(far_down))(to_down.wait_send)


def reduce_spread(spread, parts, self_feature, scale, n_row, n_col):
    _, _, rows, width = spread.shape
    col_bits = n_col.bit_length() - 1
    row_bits = n_row.bit_length() - 1
    stacked, _ = parts.shape
    return pl.pallas_call(
        functools.partial(spread_kernel, n_row, n_col, scale),
        out_shape=(
            jax.ShapeDtypeStruct((rows, width), jnp.bfloat16),
            jax.ShapeDtypeStruct(parts.shape, jnp.float32),
        ),
        in_specs=[pl.BlockSpec(memory_space=pltpu.VMEM)] * 3,
        out_specs=(pl.BlockSpec(memory_space=pltpu.VMEM),) * 2,
        scratch_shapes=[
            pltpu.VMEM((rows, width), jnp.float32),
            pltpu.VMEM((n_col, rows, width), jnp.bfloat16),
            pltpu.VMEM((n_col, rows, width), jnp.bfloat16),
            pltpu.VMEM((n_col, rows, width), jnp.bfloat16),
            pltpu.VMEM((n_col, rows, width), jnp.bfloat16),
            pltpu.VMEM((n_col - 1, rows, width), jnp.bfloat16),
            pltpu.VMEM((n_col - 1, rows, width), jnp.bfloat16),
            pltpu.VMEM((2, n_col - 1, rows, width), jnp.float32),
            pltpu.VMEM((2, n_col, rows, width), jnp.float32),
            pltpu.VMEM((2, rows, width), jnp.float32),
            pltpu.SemaphoreType.DMA((n_col,)),
            pltpu.SemaphoreType.DMA((n_col,)),
            pltpu.SemaphoreType.DMA((n_col,)),
            pltpu.SemaphoreType.DMA((n_col,)),
            pltpu.SemaphoreType.DMA((n_col - 1,)),
            pltpu.SemaphoreType.DMA((n_col - 1,)),
            pltpu.SemaphoreType.DMA((2, n_col - 1)),
            pltpu.SemaphoreType.DMA((2, n_col - 1)),
            pltpu.SemaphoreType.DMA((2,)),
            pltpu.SemaphoreType.DMA((2,)),
            pltpu.VMEM((2 * row_bits, stacked // n_col, width), jnp.float32),
            pltpu.VMEM((1, n_col, stacked // n_col, width), jnp.float32),
            pltpu.SemaphoreType.DMA((n_col,)),
            pltpu.SemaphoreType.DMA((n_col,)),
            pltpu.SemaphoreType.DMA((row_bits,)),
            pltpu.SemaphoreType.DMA((row_bits,)),
            pltpu.SemaphoreType.DMA((n_col,)),
            pltpu.SemaphoreType.DMA((n_col,)),
        ],
        compiler_params=pltpu.CompilerParams(collective_id=2, has_side_effects=True),
    )(spread, parts, self_feature)


def local_kernel(rows_ref, cols_ref, count_ref, window_ref, tiles_ref, feat_ref, w_ref, ws_ref, cot_ref,
                 act_ref, parts_ref, self_ref, spread, acc, grad_agg):
    tile = tiles_ref.shape[-1]
    nodes = acc.shape[0]
    count = jnp.minimum(count_ref[0], tiles_ref.shape[0])
    acc[...] = jnp.zeros_like(acc)

    def forward(j, carry):
        at = pl.multiple_of(rows_ref[j] * tile, tile)
        acc[pl.ds(at, tile), :] += jnp.dot(
            tiles_ref[j], window_ref[cols_ref[j]], preferred_element_type=jnp.float32
        )
        return carry

    lax.fori_loop(0, count, forward, 0)
    aggregated = acc[...].astype(jnp.bfloat16)
    features = feat_ref[...]
    pre_act = jnp.dot(aggregated, w_ref[...], preferred_element_type=jnp.float32) + jnp.dot(
        features, ws_ref[...], preferred_element_type=jnp.float32
    )
    sigma = jax.nn.sigmoid(pre_act)
    act_ref[...] = (pre_act * sigma).astype(act_ref.dtype)
    grad_pre = (cot_ref[...].astype(jnp.float32) * sigma * (1.0 + pre_act * (1.0 - sigma))).astype(
        jnp.bfloat16
    )
    over_nodes = (((0,), (0,)), ((), ()))
    parts_ref[pl.ds(0, nodes), :] = lax.dot_general(
        aggregated, grad_pre, over_nodes, preferred_element_type=jnp.float32
    )
    parts_ref[pl.ds(nodes, nodes), :] = lax.dot_general(
        features, grad_pre, over_nodes, preferred_element_type=jnp.float32
    )
    by_rows = (((1,), (1,)), ((), ()))
    grad_agg[...] = lax.dot_general(
        grad_pre, w_ref[...], by_rows, preferred_element_type=jnp.float32
    ).astype(jnp.bfloat16)
    self_ref[...] = lax.dot_general(grad_pre, ws_ref[...], by_rows, preferred_element_type=jnp.float32)
    spread[...] = jnp.zeros_like(spread)

    def backward(j, carry):
        at = pl.multiple_of(rows_ref[j] * tile, tile)
        column = cols_ref[j]
        spread[column] += lax.dot_general(
            tiles_ref[j], grad_agg[pl.ds(at, tile), :], over_nodes, preferred_element_type=jnp.float32
        )
        return carry

    lax.fori_loop(0, count, backward, 0)


def local_math(slot_rows, slot_cols, count, window, tiles, features, weight, weight_self, cotangent):
    nodes, width = features.shape
    span = window.shape[0] // 3
    tile = tiles.shape[-1]
    smem = pl.BlockSpec(memory_space=pltpu.SMEM)
    vmem = pl.BlockSpec(memory_space=pltpu.VMEM)
    return pl.pallas_call(
        local_kernel,
        out_shape=(
            jax.ShapeDtypeStruct((nodes, width), jnp.bfloat16),
            jax.ShapeDtypeStruct((2 * width, width), jnp.float32),
            jax.ShapeDtypeStruct((nodes, width), jnp.float32),
            jax.ShapeDtypeStruct((3 * span, tile, width), jnp.float32),
        ),
        in_specs=[smem, smem, smem] + [vmem] * 6,
        out_specs=(vmem,) * 4,
        scratch_shapes=[
            pltpu.VMEM((nodes, width), jnp.float32),
            pltpu.VMEM((nodes, width), jnp.bfloat16),
        ],
    )(slot_rows, slot_cols, count, window, tiles, features, weight, weight_self, cotangent)


def shards(features, weight, weight_self, tile_values, tile_rows, tile_cols, tile_count, cotangent):
    tile_block = tile_values[0]
    slot_rows = tile_rows[0]
    slot_cols = tile_cols[0]
    live_count = tile_count[0, 0]
    slot_total = tile_block.shape[0]
    tile_side = tile_block.shape[-1]
    node_rows = features.shape[0]
    width = features.shape[1]
    per_block = node_rows // tile_side
    col_count = lax.axis_size("col")
    row_count = lax.axis_size("row")
    span = col_count * per_block
    window = gather_window(features, row_count, col_count)
    window_tiles = window.reshape(-1, tile_side, width)
    activations, parts, self_feature, spread = local_math(
        slot_rows,
        slot_cols,
        tile_count[0],
        window_tiles,
        tile_block,
        features,
        weight,
        weight_self,
        cotangent,
    )
    factor = 1.0 / math.sqrt(node_rows * col_count * row_count)
    feature_grad, summed_parts = reduce_spread(
        spread.reshape(3, col_count, node_rows, width),
        parts,
        self_feature,
        factor,
        row_count,
        col_count,
    )
    weight_total, self_total = summed_parts[:width], summed_parts[width:]
    return (activations, feature_grad, weight_total, self_total)


def solution(mesh):
    placed = (
        P(("row", "col"), None),
        P(),
        P(),
        P("row", "col", None, None),
        P("row", "col"),
        P("row", "col"),
        P("row", "col"),
        P(("row", "col"), None),
    )
    return jax.shard_map(
        shards,
        mesh=mesh,
        in_specs=placed,
        out_specs=(P(("row", "col"), None), P(("row", "col"), None), P(), P()),
        check_vma=False,
    )
```

```python
import functools
import math

import jax
import jax.numpy as jnp
from jax import lax
from jax.experimental import pallas as pl
from jax.experimental.pallas import tpu as pltpu
from jax.sharding import PartitionSpec as P

MESH = pl.DeviceIdType.MESH


def flip(index, stride):
    bit = (index // stride) % 2
    return index + stride - 2 * stride * bit, bit


def allreduce_partners(n_row, n_col, row, col):
    partners = [(row, peer) for peer in range(n_col)]
    for k in range(n_row.bit_length() - 1):
        partners.append((flip(row, 1 << k)[0], col))
    return partners


class Group:
    def __init__(self, copies, receipts, col):
        self.copies = copies
        self.receipts = receipts
        self.col = col

    def wait(self):
        for peer, (copy, receipt) in enumerate(zip(self.copies, self.receipts)):
            @pl.when(peer != self.col)
            def _():
                copy.wait_send()
                receipt.wait_recv()


def allreduce_steps(n_row, n_col, row, col, x_ref, o_ref, part, gath, rsend, rrecv, dsend, drecv, gsend, grecv):
    row_bits = n_row.bit_length() - 1
    chunk = x_ref.shape[0] // n_col
    mine = pl.ds(pl.multiple_of(col * chunk, 8), chunk)
    copies, receipts = [], []
    for peer in range(n_col):
        copies.append(pltpu.make_async_remote_copy(
            src_ref=x_ref.at[pl.ds(peer * chunk, chunk)],
            dst_ref=gath.at[0, col],
            send_sem=rsend.at[peer],
            recv_sem=rrecv.at[col],
            device_id=(row, peer),
            device_id_type=MESH,
        ))
        receipts.append(pltpu.make_async_remote_copy(
            src_ref=x_ref.at[pl.ds(peer * chunk, chunk)],
            dst_ref=gath.at[0, peer],
            send_sem=rsend.at[peer],
            recv_sem=rrecv.at[peer],
            device_id=(row, peer),
            device_id_type=MESH,
        ))
        pl.when(peer != col)(copies[-1].start)
    yield Group(copies, receipts, col)
    total = x_ref[mine, :]
    for peer in range(n_col):
        total = total + jnp.where(peer == col, jnp.zeros_like(total), gath[0, peer])
    for k in range(row_bits):
        other, _ = flip(row, 1 << k)
        hold = part.at[2 * k]
        hold[...] = total
        copy = pltpu.make_async_remote_copy(
            src_ref=hold,
            dst_ref=part.at[2 * k + 1],
            send_sem=dsend.at[k],
            recv_sem=drecv.at[k],
            device_id=(other, col),
            device_id_type=MESH,
        )
        copy.start()
        yield copy
        total = total + part[2 * k + 1]
    o_ref[mine, :] = total
    copies, receipts = [], []
    for peer in range(n_col):
        copies.append(pltpu.make_async_remote_copy(
            src_ref=o_ref.at[mine],
            dst_ref=o_ref.at[mine],
            send_sem=gsend.at[peer],
            recv_sem=grecv.at[col],
            device_id=(row, peer),
            device_id_type=MESH,
        ))
        receipts.append(pltpu.make_async_remote_copy(
            src_ref=o_ref.at[mine],
            dst_ref=o_ref.at[pl.ds(peer * chunk, chunk)],
            send_sem=gsend.at[peer],
            recv_sem=grecv.at[peer],
            device_id=(row, peer),
            device_id_type=MESH,
        ))
        pl.when(peer != col)(copies[-1].start)
    yield Group(copies, receipts, col)


def run_together(*chains):
    active = list(chains)
    while active:
        copies, kept = [], []
        for chain in active:
            try:
                copies.append(next(chain))
                kept.append(chain)
            except StopIteration:
                pass
        for copy in copies:
            copy.wait()
        active = kept


def ring_position(col, n):
    core = col % 2
    y = col // 2
    return y + core * (n - 1 - 2 * y)


def ring_col(p, n):
    q = p // (n // 2)
    y = p + q * (n - 1 - 2 * p)
    return 2 * y + q


def gather_kernel(n_row, n_col, x_ref, w_ref, ring_send, ring_recv, halo_send, halo_recv, local_sem):
    row = lax.axis_index("row")
    col = lax.axis_index("col")
    p = ring_position(col, n_col)
    succ = ring_col((p + 1) % n_col, n_col)
    pred = ring_col((p + n_col - 1) % n_col, n_col)
    up = (row + 1) % n_row
    down = (row + n_row - 1) % n_row
    half = max(n_row // 2, 1)
    far = {0: row % half == 0, 2: (row + 1) % half == 0}
    barrier = pltpu.get_barrier_semaphore()
    for device in ((row, succ), (row, pred), (up, col), (down, col)):
        pl.semaphore_signal(barrier, inc=1, device_id=device, device_id_type=MESH)
    pl.semaphore_wait(barrier, 4)
    local = pltpu.make_async_copy(x_ref, w_ref.at[1, col], local_sem.at[0])
    local.start()

    def halo(src, block, index):
        copies = {}
        for target, slot in ((up, 0), (down, 2)):
            copies[slot] = pltpu.make_async_remote_copy(
                src_ref=src,
                dst_ref=w_ref.at[slot, block],
                send_sem=halo_send.at[slot // 2, index],
                recv_sem=halo_recv.at[slot // 2, index],
                device_id=(target, col),
                device_id_type=MESH,
            )
        return copies

    halos = [(col, halo(x_ref, col, 0))]
    for copy in halos[0][1].values():
        copy.start()
    sent = col
    for step in range(1, n_col):
        copies = {}
        for group in (1, 0, 2):
            src = x_ref if (step == 1 and group == 1) else w_ref.at[group, sent]
            copies[group] = pltpu.make_async_remote_copy(
                src_ref=src,
                dst_ref=w_ref.at[group, sent],
                send_sem=ring_send.at[group, step - 1],
                recv_sem=ring_recv.at[group, step - 1],
                device_id=(row, succ),
                device_id_type=MESH,
            )
        copies[1].start()
        for group in (0, 2):
            @pl.when(far[group])
            def _():
                if step == 1:
                    halos[0][1][group].wait_recv()
                copies[group].start()
        copies[1].wait()
        for group in (0, 2):
            @pl.when(far[group])
            def _():
                copies[group].wait()
        sent = ring_col((p - step + n_col) % n_col, n_col)
        forward = halo(w_ref.at[1, sent], sent, step)
        halos.append((sent, forward))
        for slot in (0, 2):
            @pl.when(jnp.logical_not(far[2 - slot]))
            def _():
                forward[slot].start()
    for copy in halos[0][1].values():
        copy.wait_send()
    for slot in (0, 2):
        @pl.when(jnp.logical_not(far[slot]))
        def _():
            halos[0][1][slot].wait_recv()
    for _, copies in halos[1:]:
        for slot in (0, 2):
            @pl.when(jnp.logical_not(far[2 - slot]))
            def _():
                copies[slot].wait_send()

            @pl.when(jnp.logical_not(far[slot]))
            def _():
                copies[slot].wait_recv()
    local.wait()


def gather_window(block, n_row, n_col):
    rows, width = block.shape
    return pl.pallas_call(
        functools.partial(gather_kernel, n_row, n_col),
        out_shape=jax.ShapeDtypeStruct((3, n_col, rows, width), block.dtype),
        in_specs=[pl.BlockSpec(memory_space=pltpu.VMEM)],
        out_specs=pl.BlockSpec(memory_space=pltpu.VMEM),
        scratch_shapes=[
            pltpu.SemaphoreType.DMA((3, n_col - 1)),
            pltpu.SemaphoreType.DMA((3, n_col - 1)),
            pltpu.SemaphoreType.DMA((2, n_col)),
            pltpu.SemaphoreType.DMA((2, n_col)),
            pltpu.SemaphoreType.DMA((1,)),
        ],
        compiler_params=pltpu.CompilerParams(collective_id=1, has_side_effects=True),
    )(block)


class Gated:
    def __init__(self, copy, cond):
        self.copy = copy
        self.cond = cond

    def wait(self):
        pl.when(self.cond)(self.copy.wait)


def spread_kernel(n_row, n_col, scale, spread_ref, parts_ref, self_ref, o_ref, sums_ref, own,
                  up_bf, down_bf,
                  from_down, from_up, ring_in, ring_out, far_in, far_out, far_from, up_send, down_send,
                  from_down_sem, from_up_sem, ring_send, ring_recv, far_send, far_recv, last_send, last_recv,
                  part, gath, rsend, rrecv, dsend, drecv, gsend, grecv):
    row = lax.axis_index("row")
    col = lax.axis_index("col")
    p = ring_position(col, n_col)
    succ = ring_col((p + 1) % n_col, n_col)
    pred = ring_col((p + n_col - 1) % n_col, n_col)
    up = (row + 1) % n_row
    down = (row + n_row - 1) % n_row
    half = max(n_row // 2, 1)
    far_down = row % half == 0
    far_up = (row + 1) % half == 0
    partners = [(row, succ), (row, pred), (up, col), (down, col)]
    partners += allreduce_partners(n_row, n_col, row, col)
    barrier = pltpu.get_barrier_semaphore()
    for device in partners:
        def signal(device=device):
            pl.semaphore_signal(barrier, inc=1, device_id=device, device_id_type=MESH)

        pl.when(jnp.logical_or(device[0] != row, device[1] != col))(signal)
    pl.semaphore_wait(barrier, len(partners) - 1)
    mid_ref, up_ref, down_ref = spread_ref.at[1], spread_ref.at[2], spread_ref.at[0]
    up_bf[...] = up_ref[...].astype(up_bf.dtype)
    down_bf[...] = down_ref[...].astype(down_bf.dtype)
    halos = []
    starts = []
    lead = 2
    for step in range(1, n_col + 1):
        block = ring_col((p - step + 2 * n_col) % n_col, n_col)
        pair = []
        for src, dst, target, send, recv, far in (
            (up_bf, from_down, up, up_send, from_down_sem, far_up),
            (down_bf, from_up, down, down_send, from_up_sem, far_down),
        ):
            copy = pltpu.make_async_remote_copy(
                src_ref=src.at[block],
                dst_ref=dst.at[block],
                send_sem=send.at[step - 1],
                recv_sem=recv.at[step - 1],
                device_id=(target, col),
                device_id_type=MESH,
            )
            pair.append((copy, far))
        halos.append((block, [copy for copy, _ in pair]))
        starts.append(pair)

    def start_halo(index):
        if index < len(starts):
            for copy, far in starts[index]:
                pl.when(jnp.logical_not(far))(copy.start)

    for index in range(lead):
        start_halo(index)

    def local_total(index):
        block, (from_below, from_above) = halos[index]
        pl.when(jnp.logical_not(far_down))(from_below.wait_recv)
        pl.when(jnp.logical_not(far_up))(from_above.wait_recv)
        zero = jnp.zeros(mid_ref.shape[1:], jnp.float32)
        return (
            mid_ref[block]
            + jnp.where(far_down, zero, from_down[block].astype(jnp.float32))
            + jnp.where(far_up, zero, from_up[block].astype(jnp.float32))
        )

    def ring_steps():
        for step in range(1, n_col):
            value = local_total(step - 1)
            if step > 1:
                value = value + ring_in[step - 2].astype(jnp.float32)
            ring_out[step - 1] = value.astype(ring_out.dtype)
            copy = pltpu.make_async_remote_copy(
                src_ref=ring_out.at[step - 1],
                dst_ref=ring_in.at[step - 1],
                send_sem=ring_send.at[step - 1],
                recv_sem=ring_recv.at[step - 1],
                device_id=(row, succ),
                device_id_type=MESH,
            )
            copy.start()
            start_halo(step - 1 + lead)
            yield copy
        start_halo(n_col - 1 + lead)
        own[...] = local_total(n_col - 1) + ring_in[n_col - 2].astype(jnp.float32)

    def far_steps(side, part_ref, far):
        for step in range(1, n_col):
            block = ring_col((p - step + 2 * n_col) % n_col, n_col)
            copy = pltpu.make_async_remote_copy(
                src_ref=far_out.at[side, step - 1],
                dst_ref=far_in.at[side, step - 1],
                send_sem=far_send.at[side, step - 1],
                recv_sem=far_recv.at[side, step - 1],
                device_id=(row, succ),
                device_id_type=MESH,
            )

            def send(step=step, block=block, copy=copy):
                value = part_ref[block]
                if step > 1:
                    value = value + far_in[side, step - 2]
                far_out[side, step - 1] = value
                copy.start()

            pl.when(far)(send)
            yield Gated(copy, far)

        def finish():
            far_out[side, n_col - 1] = part_ref[col] + far_in[side, n_col - 2]

        pl.when(far)(finish)

    run_together(
        allreduce_steps(n_row, n_col, row, col, parts_ref, sums_ref, part, gath,
                        rsend, rrecv, dsend, drecv, gsend, grecv),
        ring_steps(),
        far_steps(0, up_ref, far_up),
        far_steps(1, down_ref, far_down),
    )
    lasts = []
    for side, target, slot, far in ((0, up, 0, far_up), (1, down, 1, far_down)):
        copy = pltpu.make_async_remote_copy(
            src_ref=far_out.at[side, n_col - 1],
            dst_ref=far_from.at[slot],
            send_sem=last_send.at[side],
            recv_sem=last_recv.at[slot],
            device_id=(target, col),
            device_id_type=MESH,
        )
        pl.when(far)(copy.start)
        lasts.append(copy)
    pl.when(far_up)(lasts[0].wait_send)
    pl.when(far_down)(lasts[1].wait_send)
    pl.when(far_down)(lasts[0].wait_recv)
    pl.when(far_up)(lasts[1].wait_recv)
    zero = jnp.zeros(o_ref.shape, jnp.float32)
    total = own[...] + jnp.where(far_down, far_from[0], zero) + jnp.where(far_up, far_from[1], zero)
    o_ref[...] = (total + self_ref[...]).astype(o_ref.dtype)
    sums_ref[...] = sums_ref[...] * scale
    for _, (to_up, to_down) in halos:
        pl.when(jnp.logical_not(far_up))(to_up.wait_send)
        pl.when(jnp.logical_not(far_down))(to_down.wait_send)


def reduce_spread(spread, parts, self_feature, scale, n_row, n_col):
    _, _, rows, width = spread.shape
    col_bits = n_col.bit_length() - 1
    row_bits = n_row.bit_length() - 1
    stacked, _ = parts.shape
    return pl.pallas_call(
        functools.partial(spread_kernel, n_row, n_col, scale),
        out_shape=(
            jax.ShapeDtypeStruct((rows, width), jnp.bfloat16),
            jax.ShapeDtypeStruct(parts.shape, jnp.float32),
        ),
        in_specs=[pl.BlockSpec(memory_space=pltpu.VMEM)] * 3,
        out_specs=(pl.BlockSpec(memory_space=pltpu.VMEM),) * 2,
        scratch_shapes=[
            pltpu.VMEM((rows, width), jnp.float32),
            pltpu.VMEM((n_col, rows, width), jnp.bfloat16),
            pltpu.VMEM((n_col, rows, width), jnp.bfloat16),
            pltpu.VMEM((n_col, rows, width), jnp.bfloat16),
            pltpu.VMEM((n_col, rows, width), jnp.bfloat16),
            pltpu.VMEM((n_col - 1, rows, width), jnp.bfloat16),
            pltpu.VMEM((n_col - 1, rows, width), jnp.bfloat16),
            pltpu.VMEM((2, n_col - 1, rows, width), jnp.float32),
            pltpu.VMEM((2, n_col, rows, width), jnp.float32),
            pltpu.VMEM((2, rows, width), jnp.float32),
            pltpu.SemaphoreType.DMA((n_col,)),
            pltpu.SemaphoreType.DMA((n_col,)),
            pltpu.SemaphoreType.DMA((n_col,)),
            pltpu.SemaphoreType.DMA((n_col,)),
            pltpu.SemaphoreType.DMA((n_col - 1,)),
            pltpu.SemaphoreType.DMA((n_col - 1,)),
            pltpu.SemaphoreType.DMA((2, n_col - 1)),
            pltpu.SemaphoreType.DMA((2, n_col - 1)),
            pltpu.SemaphoreType.DMA((2,)),
            pltpu.SemaphoreType.DMA((2,)),
            pltpu.VMEM((2 * row_bits, stacked // n_col, width), jnp.float32),
            pltpu.VMEM((1, n_col, stacked // n_col, width), jnp.float32),
            pltpu.SemaphoreType.DMA((n_col,)),
            pltpu.SemaphoreType.DMA((n_col,)),
            pltpu.SemaphoreType.DMA((row_bits,)),
            pltpu.SemaphoreType.DMA((row_bits,)),
            pltpu.SemaphoreType.DMA((n_col,)),
            pltpu.SemaphoreType.DMA((n_col,)),
        ],
        compiler_params=pltpu.CompilerParams(collective_id=2, has_side_effects=True),
    )(spread, parts, self_feature)


def local_kernel(rows_ref, cols_ref, count_ref, window_ref, tiles_ref, feat_ref, w_ref, ws_ref, cot_ref,
                 act_ref, parts_ref, self_ref, spread, acc, grad_agg):
    tile = tiles_ref.shape[-1]
    nodes = acc.shape[0]
    count = jnp.minimum(count_ref[0], tiles_ref.shape[0])
    acc[...] = jnp.zeros_like(acc)

    def forward(j, carry):
        at = pl.multiple_of(rows_ref[j] * tile, tile)
        acc[pl.ds(at, tile), :] += jnp.dot(
            tiles_ref[j], window_ref[cols_ref[j]], preferred_element_type=jnp.float32
        )
        return carry

    lax.fori_loop(0, count, forward, 0)
    aggregated = acc[...].astype(jnp.bfloat16)
    features = feat_ref[...]
    pre_act = jnp.dot(aggregated, w_ref[...], preferred_element_type=jnp.float32) + jnp.dot(
        features, ws_ref[...], preferred_element_type=jnp.float32
    )
    sigma = jax.nn.sigmoid(pre_act)
    act_ref[...] = (pre_act * sigma).astype(act_ref.dtype)
    grad_pre = (cot_ref[...].astype(jnp.float32) * sigma * (1.0 + pre_act * (1.0 - sigma))).astype(
        jnp.bfloat16
    )
    over_nodes = (((0,), (0,)), ((), ()))
    parts_ref[pl.ds(0, nodes), :] = lax.dot_general(
        aggregated, grad_pre, over_nodes, preferred_element_type=jnp.float32
    )
    parts_ref[pl.ds(nodes, nodes), :] = lax.dot_general(
        features, grad_pre, over_nodes, preferred_element_type=jnp.float32
    )
    by_rows = (((1,), (1,)), ((), ()))
    grad_agg[...] = lax.dot_general(
        grad_pre, w_ref[...], by_rows, preferred_element_type=jnp.float32
    ).astype(jnp.bfloat16)
    self_ref[...] = lax.dot_general(grad_pre, ws_ref[...], by_rows, preferred_element_type=jnp.float32)
    spread[...] = jnp.zeros_like(spread)

    def backward(j, carry):
        at = pl.multiple_of(rows_ref[j] * tile, tile)
        column = cols_ref[j]
        spread[column] += lax.dot_general(
            tiles_ref[j], grad_agg[pl.ds(at, tile), :], over_nodes, preferred_element_type=jnp.float32
        )
        return carry

    lax.fori_loop(0, count, backward, 0)


def local_math(slot_rows, slot_cols, count, window, tiles, features, weight, weight_self, cotangent):
    nodes, width = features.shape
    span = window.shape[0] // 3
    tile = tiles.shape[-1]
    smem = pl.BlockSpec(memory_space=pltpu.SMEM)
    vmem = pl.BlockSpec(memory_space=pltpu.VMEM)
    return pl.pallas_call(
        local_kernel,
        out_shape=(
            jax.ShapeDtypeStruct((nodes, width), jnp.bfloat16),
            jax.ShapeDtypeStruct((2 * width, width), jnp.float32),
            jax.ShapeDtypeStruct((nodes, width), jnp.float32),
            jax.ShapeDtypeStruct((3 * span, tile, width), jnp.float32),
        ),
        in_specs=[smem, smem, smem] + [vmem] * 6,
        out_specs=(vmem,) * 4,
        scratch_shapes=[
            pltpu.VMEM((nodes, width), jnp.float32),
            pltpu.VMEM((nodes, width), jnp.bfloat16),
        ],
    )(slot_rows, slot_cols, count, window, tiles, features, weight, weight_self, cotangent)


def shards(features, weight, weight_self, tile_values, tile_rows, tile_cols, tile_count, cotangent):
    tile_block = tile_values[0]
    slot_rows = tile_rows[0]
    slot_cols = tile_cols[0]
    live_count = tile_count[0, 0]
    slot_total = tile_block.shape[0]
    tile_side = tile_block.shape[-1]
    node_rows = features.shape[0]
    width = features.shape[1]
    per_block = node_rows // tile_side
    col_count = lax.axis_size("col")
    row_count = lax.axis_size("row")
    span = col_count * per_block
    window = gather_window(features, row_count, col_count)
    window_tiles = window.reshape(-1, tile_side, width)
    activations, parts, self_feature, spread = local_math(
        slot_rows,
        slot_cols,
        tile_count[0],
        window_tiles,
        tile_block,
        features,
        weight,
        weight_self,
        cotangent,
    )
    factor = 1.0 / math.sqrt(node_rows * col_count * row_count)
    feature_grad, summed_parts = reduce_spread(
        spread.reshape(3, col_count, node_rows, width),
        parts,
        self_feature,
        factor,
        row_count,
        col_count,
    )
    weight_total, self_total = summed_parts[:width], summed_parts[width:]
    return (activations, feature_grad, weight_total, self_total)


def solution(mesh):
    placed = (
        P(("row", "col"), None),
        P(),
        P(),
        P("row", "col", None, None),
        P("row", "col"),
        P("row", "col"),
        P("row", "col"),
        P(("row", "col"), None),
    )
    return jax.shard_map(
        shards,
        mesh=mesh,
        in_specs=placed,
        out_specs=(P(("row", "col"), None), P(("row", "col"), None), P(), P()),
        check_vma=False,
    )
```
